32 devices in a mesh: dp: 8 (over z, x), vocab: 4 (over y, core).
Axes of the slice: x: 2, y: 2, z: 4, core: 2. Of those that a mesh axis runs over, the one named last changes fastest.
Arguments:
- token_ids: int32 [32, 1024], P(('dp', 'vocab')), may hold values from 0 to 51199
- scored: int32 [32, 512], P(('dp', 'vocab')), may hold values from 0 to 1023, as said below
- lengths: int32 [32], P(('dp', 'vocab')), may hold values from 768 to 1024, as said below
- times: int32 [32], P(('dp', 'vocab')), may hold values from 0 to 19
- step_count: int32 [1], replicated, may hold values from 1 to 20
- layer_w: float32 [768, 9216], P(('dp', 'vocab'))
- layer_m: float32 [768, 9216], P(('dp', 'vocab')), may hold values from -1.1444092e-05 to 1.1444092e-05
- layer_v: float32 [768, 9216], P(('dp', 'vocab')), may hold values from 8.477105e-12 to 1.3693785e-10
- layer_ema: float32 [768, 9216], P(('dp', 'vocab'))
- ada_w: float32 [128, 4608], P(('dp', 'vocab')), may hold values from -1 to 1
- ada_m: float32 [128, 4608], P(('dp', 'vocab')), may hold values from -1.1444092e-05 to 1.1444092e-05
- ada_v: float32 [128, 4608], P(('dp', 'vocab')), may hold values from 8.477105e-12 to 1.3693785e-10
- ada_ema: float32 [128, 4608], P(('dp', 'vocab')), may hold values from -1 to 1
- gains_w: float32 [4, 768], P(None, ('dp', 'vocab'))
- gains_m: float32 [4, 768], P(None, ('dp', 'vocab')), may hold values from -4.5776367e-05 to 4.5776367e-05
- gains_v: float32 [4, 768], P(None, ('dp', 'vocab')), may hold values from 1.3563368e-10 to 2.1910056e-09
- gains_ema: float32 [4, 768], P(None, ('dp', 'vocab'))
- embed_w: float32 [51200, 768], P('vocab', 'dp'), may hold values from -6 to 6
- embed_m: float32 [51200, 768], P('vocab', 'dp'), may hold values from -4.7683716e-07 to 4.7683716e-07
- embed_v: float32 [51200, 768], P('vocab', 'dp'), may hold values from 1.3563368e-14 to 2.1910056e-13
- embed_ema: float32 [51200, 768], P('vocab', 'dp'), may hold values from -6 to 6
- head_w: float32 [768, 51200], P('dp', 'vocab'), may hold values from -0.5 to 0.5
- head_m: float32 [768, 51200], P('dp', 'vocab'), may hold values from -4.7683716e-07 to 4.7683716e-07
- head_v: float32 [768, 51200], P('dp', 'vocab'), may hold values from 1.3563368e-14 to 2.1910056e-13
- head_ema: float32 [768, 51200], P('dp', 'vocab'), may hold values from -0.5 to 0.5
Outputs:
- loss: float32 [], replicated
- grad_norm: float32 [], replicated
- layer_first: float32 [768, 9216], P(('dp', 'vocab'))
- layer_second: float32 [768, 9216], P(('dp', 'vocab'))
- layer_new: float32 [768, 9216], P(('dp', 'vocab'))
- layer_avg: float32 [768, 9216], P(('dp', 'vocab'))
- ada_first: float32 [128, 4608], P(('dp', 'vocab'))
- ada_second: float32 [128, 4608], P(('dp', 'vocab'))
- ada_new: float32 [128, 4608], P(('dp', 'vocab'))
- ada_avg: float32 [128, 4608], P(('dp', 'vocab'))
- gains_first: float32 [4, 768], P(None, ('dp', 'vocab'))
- gains_second: float32 [4, 768], P(None, ('dp', 'vocab'))
- gains_new: float32 [4, 768], P(None, ('dp', 'vocab'))
- gains_avg: float32 [4, 768], P(None, ('dp', 'vocab'))
- embed_first: float32 [51200, 768], P('vocab', 'dp')
- embed_second: float32 [51200, 768], P('vocab', 'dp')
- embed_new: float32 [51200, 768], P('vocab', 'dp')
- embed_avg: float32 [51200, 768], P('vocab', 'dp')
- head_first: float32 [768, 51200], P('dp', 'vocab')
- head_second: float32 [768, 51200], P('dp', 'vocab')
- head_new: float32 [768, 51200], P('dp', 'vocab')
- head_avg: float32 [768, 51200], P('dp', 'vocab')
The draws below stay inside these ranges and needn't reach their ends.
Inputs may be any that keep to these rules, and one draw needn't show every extreme that they name: `lengths`: each sequence has at least 768 tokens; the first sequence has exactly 1024. `scored`: each row holds 512 distinct positions in ascending order, each below that sequence's length.
All inputs are finite; a program needn't handle non-finite values.
Results may differ from the reference program's by a relative error of at most 0.0044.
The reference program's roundings to bfloat16 on the way count: a program that leaves them out, or rounds other values in their place, can miss the bound.
Values may be sent and summed in bfloat16 or wider, within the bound.
A program may use at most 448 MiB of HBM per device.

```python
import math
import jax
import jax.numpy as jnp
import numpy as np
from jax import lax

D = 768
H = 12
HD = 64
FF = 3072
V = 51200
C = 128
LEN = 1024
SCORE = 512
TSTEPS = 20
SEQS = 32


def layer_draw(key):
    columns = jnp.arange(4 * D + 2 * FF)
    column_scale = jnp.where(columns < 3 * D, D ** (-0.5), jnp.where(columns < 4 * D, 4.0 * D ** (-0.5), jnp.where(columns < 4 * D + FF, D ** (-0.5), FF ** (-0.5))))
    base_draw = jax.random.normal(key, (D, 4 * D + 2 * FF), jnp.float32)
    return (base_draw * column_scale[None, :].astype(jnp.float32)).astype(jnp.float32)


def draw_layer_w(key, part):
    return layer_draw(jax.random.fold_in(key, 11))


def draw_layer_ema(key, part):
    return layer_draw(jax.random.fold_in(key, 12))


def gains_draw(key):
    row_index = jnp.arange(4)[:, None]
    noise = jnp.clip(jax.random.normal(key, (4, D), jnp.float32), -5.0, 5.0)
    return jnp.where(row_index < 3, 1.0 + 0.1 * noise, noise).astype(jnp.float32)


def draw_gains_w(key, part):
    return gains_draw(jax.random.fold_in(key, 31))


def draw_gains_ema(key, part):
    return gains_draw(jax.random.fold_in(key, 32))


def length_draw(key):
    drawn_lengths = jax.random.randint(jax.random.fold_in(key, 21), (SEQS,), 3 * LEN // 4, LEN + 1)
    return drawn_lengths.at[0].set(LEN).astype(jnp.int32)


def draw_lengths(key, part):
    return length_draw(key)


def draw_scored(key, part):
    seq_lengths = length_draw(key)
    positions = jnp.arange(LEN)
    jitter = jax.random.randint(jax.random.fold_in(key, 22), (SEQS, LEN), 0, 1024)
    rank_keys = (jitter + jnp.where(positions[None, :] >= seq_lengths[:, None], 2048, 0)) * LEN + positions[None, :]
    chosen = jnp.argsort(rank_keys, axis=1)[:, :SCORE]
    return jnp.sort(chosen, axis=1).astype(jnp.int32)


def plant(values, stream_key, smallest, largest):
    index_at = [jax.random.randint(jax.random.fold_in(stream_key, axis), (), 0, length) for axis, length in enumerate(values.shape)]
    main_axis = values.shape.index(max(values.shape))
    beside = index_at[:main_axis] + [(index_at[main_axis] + 1) % values.shape[main_axis]] + index_at[main_axis + 1:]
    return values.at[tuple(index_at)].set(smallest).at[tuple(beside)].set(largest)


def shard_levels(own_key, dims, cuts, smallest, top_value):
    loudness, own = 1.0, jax.random.fold_in(own_key, 6)
    for axis_at, blocks in cuts:
        heights = jnp.exp(jax.random.uniform(jax.random.fold_in(own, axis_at), (blocks,), jnp.float32, smallest / len(cuts), top_value / len(cuts)))
        loudness = loudness * jnp.repeat(heights, dims[axis_at] // blocks).reshape([-1 if axis == axis_at else 1 for axis in range(len(dims))])
    return loudness


def rank_bounds(number_of, slope):
    portions = [(1 << 20) // math.isqrt(rank ** slope) + 1 for rank in range(1, number_of + 1)]
    scale = 1 + sum(portions) // (1 << 30)
    return np.cumsum(np.array([max(1, weight // scale) for weight in portions]))


def skewed_ids(own_key, dims, amount, skew):
    table = rank_bounds(amount, skew)
    ticket = jax.random.randint(jax.random.fold_in(own_key, 1), dims, 0, int(table[amount - 1]))
    standing = jnp.searchsorted(jnp.asarray(table, jnp.int32), ticket, side="right")
    return jax.random.permutation(jax.random.fold_in(own_key, 2), amount)[standing].astype(jnp.int32)


def gaussian(stream_key, extent, scale, reach, cuts=(), kind=jnp.bfloat16):
    gain = shard_levels(stream_key, extent, cuts, -0.22, 0.18) if cuts else 1.0
    entries = jax.random.normal(stream_key, extent, jnp.float32) * scale * gain
    return jnp.minimum(jnp.maximum(entries, -reach), reach).astype(kind)


def setup_inputs(seed: int = 0) -> dict:
    key_list = jax.random.split(jax.random.key(seed), 26)
    return {
        "token_ids": plant(skewed_ids(key_list[0], (SEQS, LEN), V, 2), jax.random.fold_in(key_list[0], 3), 0, V - 1).astype(jnp.int32),
        "scored": draw_scored(jax.random.fold_in(key_list[25], 71), 0),
        "lengths": draw_lengths(jax.random.fold_in(key_list[25], 71), 0),
        "times": plant(jax.random.randint(key_list[3], (SEQS,), 0, TSTEPS), jax.random.fold_in(key_list[3], 1), 0, TSTEPS - 1).astype(jnp.int32),
        "step_count": jax.random.randint(key_list[4], (1,), 1, 21).astype(jnp.int32),
        "layer_w": draw_layer_w(jax.random.fold_in(key_list[25], 71), 0),
        "layer_m": gaussian(key_list[6], (D, 4 * D + 2 * FF), (0.0055 / (D * (4 * D + 2 * FF) + 6 * C * D) ** 0.5), 1.1444091796875e-05, ((0, 32),), jnp.float32),
        "layer_v": jnp.clip(jnp.exp(math.log(1.3693784994828206e-10) - 2.7821581 * jax.random.uniform(key_list[7], (D, 4 * D + 2 * FF), jnp.float32) ** shard_levels(key_list[7], (D, 4 * D + 2 * FF), ((0, 32),), -0.2, 0.2)), 8.477105302440169e-12, 1.3693784994828206e-10),
        "layer_ema": draw_layer_ema(jax.random.fold_in(key_list[25], 71), 0),
        "ada_w": gaussian(key_list[9], (C, 6 * D), (C // 4) ** -0.5, 1.0, ((0, 32),), jnp.float32),
        "ada_m": gaussian(key_list[10], (C, 6 * D), (0.0055 / (D * (4 * D + 2 * FF) + 6 * C * D) ** 0.5), 1.1444091796875e-05, ((0, 32),), jnp.float32),
        "ada_v": jnp.clip(jnp.exp(math.log(1.3693784994828206e-10) - 2.7821581 * jax.random.uniform(key_list[11], (C, 6 * D), jnp.float32) ** shard_levels(key_list[11], (C, 6 * D), ((0, 32),), -0.2, 0.2)), 8.477105302440169e-12, 1.3693784994828206e-10),
        "ada_ema": gaussian(key_list[12], (C, 6 * D), (C // 4) ** -0.5, 1.0, ((0, 32),), jnp.float32),
        "gains_w": draw_gains_w(jax.random.fold_in(key_list[25], 71), 0),
        "gains_m": gaussian(key_list[14], (4, D), (0.022 / (D * (4 * D + 2 * FF) + 6 * C * D) ** 0.5), 4.57763671875e-05, ((1, 32),), jnp.float32),
        "gains_v": jnp.clip(jnp.exp(math.log(2.191005599172513e-09) - 2.7821581 * jax.random.uniform(key_list[15], (4, D), jnp.float32) ** shard_levels(key_list[15], (4, D), ((1, 32),), -0.2, 0.2)), 1.356336848390427e-10, 2.191005599172513e-09),
        "gains_ema": draw_gains_ema(jax.random.fold_in(key_list[25], 71), 0),
        "embed_w": gaussian(key_list[17], (V, D), 1.0, 6.0, ((0, 4), (1, 8)), jnp.float32),
        "embed_m": gaussian(key_list[18], (V, D), (0.00022 / (D * (4 * D + 2 * FF) + 6 * C * D) ** 0.5), 4.76837158203125e-07, ((0, 4), (1, 8)), jnp.float32),
        "embed_v": jnp.clip(jnp.exp(math.log(2.1910056234586417e-13) - 2.7821582 * jax.random.uniform(key_list[19], (V, D), jnp.float32) ** shard_levels(key_list[19], (V, D), ((0, 4), (1, 8)), -0.2, 0.2)), 1.3563368330760713e-14, 2.1910056234586417e-13),
        "embed_ema": gaussian(key_list[20], (V, D), 1.0, 6.0, ((0, 4), (1, 8)), jnp.float32),
        "head_w": gaussian(key_list[21], (D, V), (D // 6) ** -0.5, 0.5, ((0, 8), (1, 4)), jnp.float32),
        "head_m": gaussian(key_list[22], (D, V), (0.00022 / (D * (4 * D + 2 * FF) + 6 * C * D) ** 0.5), 4.76837158203125e-07, ((0, 8), (1, 4)), jnp.float32),
        "head_v": jnp.clip(jnp.exp(math.log(2.1910056234586417e-13) - 2.7821582 * jax.random.uniform(key_list[23], (D, V), jnp.float32) ** shard_levels(key_list[23], (D, V), ((0, 8), (1, 4)), -0.2, 0.2)), 1.3563368330760713e-14, 2.1910056234586417e-13),
        "head_ema": gaussian(key_list[24], (D, V), (D // 6) ** -0.5, 0.5, ((0, 8), (1, 4)), jnp.float32),
    }


@jax.custom_vjp
def low(v):
    return lax.optimization_barrier(v.astype(jnp.bfloat16)).astype(jnp.float32)

@jax.custom_vjp
def low_back(v):
    return v

def low_keep(v):
    return (low(v), None)

def low_pass(kept, grad):
    return (grad,)

def back_keep(v):
    return (v, None)

def back_low(kept, grad):
    return (low(grad),)
low.defvjp(low_keep, low_pass)
low_back.defvjp(back_keep, back_low)
NORM_EPS = 1e-05
CLIP_NORM = 0.05
BETA_ONE = 0.9
BETA_TWO = 0.95
ADAM_EPS = 1e-08
EMA_DECAY = 0.9999
LEARN_RATES = (0.03, 0.1, 0.1, 0.5, 0.05)
WEIGHT_DECAYS = (0.01, 0.01, 0.0, 0.01, 0.01)
HIGHEST = lax.Precision.HIGHEST

def layer_norm(values):
    center = values - lax.optimization_barrier(jnp.mean(values, axis=-1, keepdims=True))
    spread = lax.optimization_barrier(jnp.mean(center * center, axis=-1, keepdims=True))
    return center * lax.rsqrt(spread + NORM_EPS)

def time_features(time_index, width, steps):
    t_value = (time_index.astype(jnp.float32) + 1.0) / steps
    half_width = width // 2
    frequencies = jnp.exp(-math.log(10000.0) * jnp.arange(half_width, dtype=jnp.float32) / half_width)
    angles = 1000.0 * t_value[:, None] * frequencies[None, :]
    return jax.nn.silu(jnp.concatenate([jnp.cos(angles), jnp.sin(angles)], axis=1))

def rope_tables(length, head_size):
    half_size = head_size // 2
    inverse = jnp.exp(-math.log(10000.0) * jnp.arange(half_size, dtype=jnp.float32) * 2.0 / head_size)
    angles = jnp.arange(length, dtype=jnp.float32)[:, None] * inverse[None, :]
    return (jnp.cos(angles)[:, None, :], jnp.sin(angles)[:, None, :])

def rotate(values, cosine_table, sine_table):
    half_size = values.shape[-1] // 2
    front_half = values[..., :half_size]
    back_half = values[..., half_size:]
    return jnp.concatenate([front_half * cosine_table - back_half * sine_table, back_half * cosine_table + front_half * sine_table], axis=-1)

def attention(queries, key_vecs, value_vecs, key_valid):
    block_size = min(512, LEN)
    block_count = LEN // block_size
    scale_factor = HD ** (-0.5)

    def one_block(query_block):
        raw_scores = low_back(jnp.einsum('qhd,khd->hqk', query_block, key_vecs, precision=HIGHEST))
        scores = jnp.where(key_valid[None, None, :], raw_scores * scale_factor, -1e+30)
        row_max = lax.optimization_barrier(jnp.max(scores, axis=-1, keepdims=True))
        weights = jnp.exp(scores - row_max)
        probabilities = weights / lax.optimization_barrier(jnp.sum(weights, axis=-1, keepdims=True))
        return jnp.einsum('hqk,khd->qhd', low(probabilities), value_vecs, precision=HIGHEST)
    mixed_out = lax.map(jax.checkpoint(one_block), queries.reshape(block_count, block_size, H, HD))
    return mixed_out.reshape(LEN, H, HD)

def sequence_forward(input_row, length_value, modulation, positions, embed_low, layer_low, gains_low, cosine_table, sine_table):
    table_rows = jnp.take(embed_low, jnp.maximum(input_row, 0), axis=0)
    hidden0 = jnp.where(input_row[:, None] < 0, gains_low[3][None, :], table_rows)
    shift_a, scale_a, gate_a, shift_m, scale_m, gate_m = [modulation[part_index * D:(part_index + 1) * D] for part_index in range(6)]
    att_in = low(layer_norm(hidden0) * gains_low[0] * (1.0 + scale_a) + shift_a)
    qkv_raw = low_back(jnp.dot(att_in, layer_low[:, :3 * D], precision=HIGHEST)).reshape(LEN, 3, H, HD)
    queries = low(rotate(qkv_raw[:, 0], cosine_table, sine_table))
    key_vecs = low(rotate(qkv_raw[:, 1], cosine_table, sine_table))
    value_vecs = low(qkv_raw[:, 2])
    key_valid = jnp.arange(LEN) < length_value
    att_out = low(low_back(attention(queries, key_vecs, value_vecs, key_valid))).reshape(LEN, D)
    branch = low_back(jnp.dot(att_out, layer_low[:, 3 * D:4 * D], precision=HIGHEST))
    hidden1 = hidden0 + gate_a * branch
    mlp_in = low(layer_norm(hidden1) * gains_low[1] * (1.0 + scale_m) + shift_m)
    pre_act = low_back(jnp.dot(mlp_in, layer_low[:, 4 * D:4 * D + FF], precision=HIGHEST))
    activation = low(jax.nn.gelu(pre_act, approximate=True))
    mlp_out = low_back(jnp.dot(activation, layer_low[:, 4 * D + FF:].T, precision=HIGHEST))
    hidden2 = hidden1 + gate_m * mlp_out
    picked = jnp.take(hidden2, positions, axis=0)
    return low(layer_norm(picked) * gains_low[2])

def tile_loss(rows_tile, target_tile, weight_tile, head_low):
    logits = low_back(jnp.dot(rows_tile, head_low, precision=HIGHEST))
    row_max = lax.optimization_barrier(jnp.max(logits, axis=1, keepdims=True))
    log_total = jnp.log(lax.optimization_barrier(jnp.sum(jnp.exp(logits - row_max), axis=1))) + row_max[:, 0]
    target_logit = jnp.take_along_axis(logits, target_tile[:, None], axis=1)[:, 0]
    return jnp.sum(weight_tile * (log_total - target_logit))

def adam_step(weight, first, second, ema_copy, gradient, step_value, learn_rate, decay_rate):
    first_new = BETA_ONE * first + (1.0 - BETA_ONE) * gradient
    second_new = BETA_TWO * second + (1.0 - BETA_TWO) * gradient * gradient
    first_hat = first_new / (1.0 - BETA_ONE ** step_value)
    second_hat = second_new / (1.0 - BETA_TWO ** step_value)
    weight_new = weight - learn_rate * (first_hat / (jnp.sqrt(second_hat) + ADAM_EPS) + decay_rate * weight)
    ema_rate = jnp.minimum(EMA_DECAY, (1.0 + step_value) / (10.0 + step_value))
    ema_new = ema_rate * ema_copy + (1.0 - ema_rate) * weight_new
    return (first_new, second_new, weight_new, ema_new)

def reference(token_ids, scored, lengths, times, step_count, layer_w, layer_m, layer_v, layer_ema, ada_w, ada_m, ada_v, ada_ema, gains_w, gains_m, gains_v, gains_ema, embed_w, embed_m, embed_v, embed_ema, head_w, head_m, head_v, head_ema):
    is_scored = jnp.any(scored[:, :, None] == jnp.arange(LEN, dtype=jnp.int32)[None, None, :], axis=1)
    input_ids = jnp.where(is_scored, -1, token_ids).astype(jnp.int32)
    targets = jnp.take_along_axis(token_ids, scored, axis=1).reshape(-1)
    row_weights = jnp.repeat(TSTEPS / (times.astype(jnp.float32) + 1.0) / (SEQS * SCORE), SCORE)
    condition = low(time_features(times, C, TSTEPS))
    cosine_table, sine_table = rope_tables(LEN, HD)
    tile_size = min(512, SEQS * SCORE)
    tile_count = SEQS * SCORE // tile_size

    def loss_fn(layer_f, ada_f, gains_f, embed_f, head_f):
        layer_low = low(layer_f)
        gains_low = low(gains_f)
        embed_low = low(embed_f)
        head_low = low(head_f)
        modulation = jnp.dot(condition, low(ada_f), precision=HIGHEST)

        def per_sequence(seq_items):
            return sequence_forward(seq_items[0], seq_items[1], seq_items[2], seq_items[3], embed_low, layer_low, gains_low, cosine_table, sine_table)
        picked_rows = lax.map(jax.checkpoint(per_sequence), (input_ids, lengths, modulation, scored)).reshape(tile_count, tile_size, D)

        def per_tile(tile_items):
            return tile_loss(tile_items[0], tile_items[1], tile_items[2], head_low)
        return jnp.sum(lax.map(jax.checkpoint(per_tile), (picked_rows, targets.reshape(tile_count, tile_size), row_weights.reshape(tile_count, tile_size))))
    total_loss, pullback = jax.vjp(loss_fn, layer_w, ada_w, gains_w, embed_w, head_w)
    gradients = pullback(jnp.ones_like(total_loss))
    squares = jnp.sum(gradients[0] * gradients[0]) + jnp.sum(gradients[1] * gradients[1]) + jnp.sum(gradients[2] * gradients[2]) + jnp.sum(gradients[3] * gradients[3]) + jnp.sum(gradients[4] * gradients[4])
    grad_norm = jnp.sqrt(squares)
    factor = jnp.minimum(1.0, CLIP_NORM / grad_norm)
    step_value = step_count[0].astype(jnp.float32)
    layer_out = adam_step(layer_w, layer_m, layer_v, layer_ema, gradients[0] * factor, step_value, LEARN_RATES[0], WEIGHT_DECAYS[0])
    ada_out = adam_step(ada_w, ada_m, ada_v, ada_ema, gradients[1] * factor, step_value, LEARN_RATES[1], WEIGHT_DECAYS[1])
    gains_out = adam_step(gains_w, gains_m, gains_v, gains_ema, gradients[2] * factor, step_value, LEARN_RATES[2], WEIGHT_DECAYS[2])
    embed_out = adam_step(embed_w, embed_m, embed_v, embed_ema, gradients[3] * factor, step_value, LEARN_RATES[3], WEIGHT_DECAYS[3])
    head_out = adam_step(head_w, head_m, head_v, head_ema, gradients[4] * factor, step_value, LEARN_RATES[4], WEIGHT_DECAYS[4])
    return (total_loss, grad_norm, layer_out[0], layer_out[1], layer_out[2], layer_out[3], ada_out[0], ada_out[1], ada_out[2], ada_out[3], gains_out[0], gains_out[1], gains_out[2], gains_out[3], embed_out[0], embed_out[1], embed_out[2], embed_out[3], head_out[0], head_out[1], head_out[2], head_out[3])
```

```python
import functools
import math

import jax
import jax.numpy as jnp
from jax import lax
from jax.experimental import pallas as pl
from jax.experimental.pallas import tpu as pltpu
from jax.sharding import Mesh, PartitionSpec as P

D = 768
H = 12
HD = 64
FF = 3072
V = 51200
C = 128
TSTEPS = 20
SEGMENT = 3200
LANES = 128

NORM_EPS = 1e-05
CLIP_NORM = 0.05
BETA_ONE = 0.9
BETA_TWO = 0.95
ADAM_EPS = 1e-08
EMA_DECAY = 0.9999
LEARN_RATES = (0.03, 0.1, 0.1, 0.5, 0.05)
WEIGHT_DECAYS = (0.01, 0.01, 0.0, 0.01, 0.01)

ALL = ("z", "x", "y", "c")
BF = jnp.bfloat16
F32 = jnp.float32
MESH = pl.DeviceIdType.MESH
VMEM_LIMIT = 60 * 1024 * 1024


def dot(a, b, contract):
    return lax.dot_general(a, b, ((contract[0], contract[1]), ((), ())), preferred_element_type=F32)


def matmul(a, b):
    return dot(a, b, ((1,), (0,)))


def matmul_nt(a, b):
    return dot(a, b, ((1,), (1,)))


def matmul_tn(a, b):
    return dot(a, b, ((0,), (0,)))


def share_kernel(sizes, count, *refs):
    nz, nx, ny, nc = sizes
    n = nz * nx * ny * nc
    ins, outs = refs[:count], refs[count : 2 * count]
    send, recv, near = refs[2 * count :]
    me = ((lax.axis_index("z") * nx + lax.axis_index("x")) * ny + lax.axis_index("y")) * nc
    me = me + lax.axis_index("c")

    def device(k):
        peer = lax.rem(me + k, n)
        return (
            peer // (nx * ny * nc),
            lax.rem(peer // (ny * nc), nx),
            lax.rem(peer // nc, ny),
            lax.rem(peer, nc),
        )

    def remote(i, k):
        return pltpu.make_async_remote_copy(
            src_ref=ins[i],
            dst_ref=outs[i].at[me],
            send_sem=send.at[i, k],
            recv_sem=recv.at[i, k],
            device_id=device(k),
            device_id_type=MESH,
        )

    barrier = pltpu.get_barrier_semaphore()

    @pl.loop(1, n)
    def _(k):
        pl.semaphore_signal(barrier, inc=1, device_id=device(k), device_id_type=MESH)

    pl.semaphore_wait(barrier, n - 1)

    @pl.loop(1, n)
    def _(k):
        for i in range(count):
            remote(i, k).start()

    for i in range(count):
        pltpu.make_async_copy(ins[i], outs[i].at[me], near.at[i]).start()
    for i in range(count):
        pltpu.make_async_copy(ins[i], outs[i].at[me], near.at[i]).wait()

    @pl.loop(1, n)
    def _(k):
        for i in range(count):
            remote(i, k).wait()


def share(sizes, collective_id, *arrays):
    n = math.prod(sizes)
    count = len(arrays)
    return pl.pallas_call(
        functools.partial(share_kernel, sizes, count),
        out_shape=[jax.ShapeDtypeStruct((n,) + a.shape, a.dtype) for a in arrays],
        in_specs=[pl.BlockSpec(memory_space=pltpu.VMEM)] * count,
        out_specs=[pl.BlockSpec(memory_space=pltpu.VMEM)] * count,
        scratch_shapes=[
            pltpu.SemaphoreType.DMA((count, n)),
            pltpu.SemaphoreType.DMA((count, n)),
            pltpu.SemaphoreType.DMA((count,)),
        ],
        compiler_params=pltpu.CompilerParams(
            collective_id=collective_id, has_side_effects=True
        ),
        name=f"share{collective_id}",
    )(*arrays)


def axis_place(axes):
    index, size = 0, 1
    for axis in axes:
        index = index * lax.axis_size(axis) + lax.axis_index(axis)
        size = size * lax.axis_size(axis)
    return index, size


def exchange(piece_for, axes):
    me, n = axis_place(axes)
    got = [(me, piece_for(me))]
    for step in range(1, n):
        piece = piece_for(lax.rem(me + step, n))
        moved = lax.ppermute(piece, axes, [(i, (i + step) % n) for i in range(n)])
        got.append((lax.rem(me + n - step, n), moved))
    return got


def in_order(got):
    out = jnp.zeros((len(got),) + got[0][1].shape, got[0][1].dtype)
    for sender, piece in got:
        out = lax.dynamic_update_index_in_dim(out, piece, sender, 0)
    return out


def pick(values, index):
    return lax.dynamic_index_in_dim(values, index, 0, keepdims=False)


def gather_kernel(low_ref, high_ref, ids_ref, table_ref, out_ref, rows_ref):
    source = pl.program_id(0)
    low, high = low_ref[source], high_ref[source]
    rows_ref[...] = jnp.zeros_like(rows_ref)

    def chunk(k, carry):
        base = pl.multiple_of(k * 8, 8)
        rows = []
        for i in range(8):
            place = base + i
            valid = jnp.logical_and(place >= low, place < high)
            row = jnp.where(valid, ids_ref[source, place], 0)
            value = table_ref[pl.ds(row, 1), :]
            rows.append(jnp.where(valid, value, 0.0))
        rows_ref[pl.ds(base, 8), :] = jnp.concatenate(rows, axis=0)
        return carry

    lax.fori_loop(low // 8, (high + 7) // 8, chunk, 0)
    out_ref[0] = rows_ref[...].astype(BF)


def gather_rows(table, ids, low, high):
    sources, count = ids.shape
    width = table.shape[1]
    return pl.pallas_call(
        gather_kernel,
        out_shape=jax.ShapeDtypeStruct((sources, count, width), BF),
        grid_spec=pltpu.PrefetchScalarGridSpec(
            num_scalar_prefetch=3,
            grid=(sources,),
            in_specs=[
                pl.BlockSpec(table.shape, lambda i, *_: (0, 0), pipeline_mode=pl.Buffered(1))
            ],
            out_specs=pl.BlockSpec((1, count, width), lambda i, *_: (i, 0, 0)),
            scratch_shapes=[pltpu.VMEM((count, width), F32)],
        ),
        compiler_params=pltpu.CompilerParams(vmem_limit_bytes=VMEM_LIMIT),
        name="gather_rows",
    )(low, high, ids, table)


def scatter_kernel(low_ref, high_ref, ids_ref, rows_ref, out_ref, wide_ref):
    source = pl.program_id(0)

    @pl.when(source == 0)
    def _():
        out_ref[...] = jnp.zeros_like(out_ref)

    low, high = low_ref[source], high_ref[source]
    wide_ref[...] = rows_ref[0].astype(F32)

    def chunk(k, carry):
        base = pl.multiple_of(k * 8, 8)
        block = wide_ref[pl.ds(base, 8), :]
        for i in range(8):
            place = base + i
            valid = jnp.logical_and(place >= low, place < high)
            row = jnp.where(valid, ids_ref[source, place], 0)
            addend = jnp.where(valid, block[i : i + 1, :], 0.0)
            out_ref[pl.ds(row, 1), :] = out_ref[pl.ds(row, 1), :] + addend
        return carry

    lax.fori_loop(low // 8, (high + 7) // 8, chunk, 0)


def scatter_rows(rows, ids, low, high, table_rows):
    sources, count, width = rows.shape
    return pl.pallas_call(
        scatter_kernel,
        out_shape=jax.ShapeDtypeStruct((table_rows, width), F32),
        grid_spec=pltpu.PrefetchScalarGridSpec(
            num_scalar_prefetch=3,
            grid=(sources,),
            in_specs=[pl.BlockSpec((1, count, width), lambda i, *_: (i, 0, 0))],
            out_specs=pl.BlockSpec((table_rows, width), lambda i, *_: (0, 0)),
            scratch_shapes=[pltpu.VMEM((count, width), F32)],
        ),
        compiler_params=pltpu.CompilerParams(vmem_limit_bytes=VMEM_LIMIT),
        name="scatter_rows",
    )(low, high, ids, rows)


def swap_halves(values):
    lane = lax.broadcasted_iota(jnp.int32, values.shape, 1)
    half = HD // 2
    up = pltpu.roll(values, LANES - half, 1)
    down = pltpu.roll(values, half, 1)
    return jnp.where(lax.rem(lane, HD) < half, up, down)


def turn(values, cosine, sine):
    return values * cosine + swap_halves(values) * sine


def turn_back(values, cosine, sine):
    return values * cosine - swap_halves(values) * sine


def attend_kernel(kv_ref, vv_ref, qm_ref, km_ref, vm_ref, cu_ref, su_ref, cm_ref, sm_ref,
                  mask_ref, q_out, ku_out, km_out, att_out, lse_out):
    rows = cm_ref.shape[0]
    wide = (rows, LANES)
    cm, sm = cm_ref[...], sm_ref[...]
    q = turn(jnp.broadcast_to(qm_ref[0:1, :], wide), cm, sm).astype(BF)
    k_m = turn(jnp.broadcast_to(km_ref[0:1, :], wide), cm, sm).astype(BF)
    k_u = turn(kv_ref[...], cu_ref[...], su_ref[...]).astype(BF)
    v_u = vv_ref[...].astype(BF)
    v_m = vm_ref[0:1, :].astype(BF).astype(F32)
    q_out[...] = q
    ku_out[...] = k_u
    km_out[...] = k_m
    mask = mask_ref[0:1, :]
    outs, totals = [], []
    for head in range(LANES // HD):
        part = slice(head * HD, (head + 1) * HD)
        s_u = matmul_nt(q[:, part], k_u[:, part]) * HD ** (-0.5) + mask
        s_m = matmul_nt(q[:, part], k_m[:, part]) * HD ** (-0.5)
        top = jnp.maximum(
            jnp.max(s_u, axis=1, keepdims=True), jnp.max(s_m, axis=1, keepdims=True)
        )
        e_u = jnp.exp(s_u - top)
        e_m = jnp.exp(s_m - top)
        total = jnp.sum(e_u, axis=1, keepdims=True) + jnp.sum(e_m, axis=1, keepdims=True)
        inverse = 1.0 / total
        p_u = (e_u * inverse).astype(BF)
        p_m = (e_m * inverse).astype(BF).astype(F32)
        mixed = matmul(p_u, v_u[:, part]) + jnp.sum(p_m, axis=1, keepdims=True) * v_m[:, part]
        outs.append(mixed)
        totals.append(top + jnp.log(total))
    att_out[...] = jnp.concatenate(outs, axis=1).astype(BF)
    lse_out[0] = jnp.concatenate(totals, axis=1)


def attend(kv_u, qkv_m, tables, mask):
    count, rows = kv_u.shape[0], tables[2].shape[0]
    blocks = D // LANES
    per = LANES // HD
    row = lambda offset: pl.BlockSpec((qkv_m.shape[0], LANES), lambda i: (0, offset * blocks + i))
    column = lambda n: pl.BlockSpec((n, LANES), lambda i: (0, i))
    whole = lambda a: pl.BlockSpec(a.shape, lambda i: (0, 0))
    return pl.pallas_call(
        attend_kernel,
        grid=(blocks,),
        out_shape=[
            jax.ShapeDtypeStruct((rows, D), BF),
            jax.ShapeDtypeStruct((count, D), BF),
            jax.ShapeDtypeStruct((rows, D), BF),
            jax.ShapeDtypeStruct((rows, D), BF),
            jax.ShapeDtypeStruct((blocks, rows, per), F32),
        ],
        in_specs=[
            pl.BlockSpec((count, LANES), lambda i: (0, i)),
            pl.BlockSpec((count, LANES), lambda i: (0, blocks + i)),
            row(0), row(1), row(2),
            *[whole(t) for t in tables],
            whole(mask),
        ],
        out_specs=[column(rows), column(count), column(rows), column(rows),
                   pl.BlockSpec((1, rows, per), lambda i: (i, 0, 0))],
        compiler_params=pltpu.CompilerParams(vmem_limit_bytes=VMEM_LIMIT),
        cost_estimate=pl.CostEstimate(
            flops=2 * 3 * rows * count * D, bytes_accessed=12 * rows * D,
            transcendentals=2 * rows * count * H,
        ),
        name="attend",
    )(kv_u, kv_u, qkv_m, qkv_m, qkv_m, *tables, mask)


def attend_back_kernel(q_ref, ku_ref, km_ref, vv_ref, vm_ref, cu_ref, su_ref, cm_ref, sm_ref,
                       mask_ref, lse_ref, datt_ref, dk_out, dv_out, dm_out):
    q, k_u, k_m, datt = q_ref[...], ku_ref[...], km_ref[...], datt_ref[...]
    v_u = vv_ref[...].astype(BF)
    v_m = vm_ref[0:1, :].astype(BF).astype(F32)
    datt_f = datt.astype(F32)
    mask = mask_ref[0:1, :]
    scale = HD ** (-0.5)
    dq, dk_u, dk_m, dv_u, dv_m = [], [], [], [], []
    for head in range(LANES // HD):
        part = slice(head * HD, (head + 1) * HD)
        lse = lse_ref[0, :, head : head + 1]
        p_u = jnp.exp(matmul_nt(q[:, part], k_u[:, part]) * scale + mask - lse)
        p_m = jnp.exp(matmul_nt(q[:, part], k_m[:, part]) * scale - lse)
        dp_u = matmul_nt(datt[:, part], v_u[:, part])
        dp_m = jnp.sum(datt_f[:, part] * v_m[:, part], axis=1, keepdims=True)
        inner = jnp.sum(p_u * dp_u, axis=1, keepdims=True) + dp_m * jnp.sum(
            p_m, axis=1, keepdims=True
        )
        ds_u = (p_u * (dp_u - inner) * scale).astype(BF)
        ds_m = (p_m * ((dp_m - inner) * scale)).astype(BF)
        dq.append(matmul(ds_u, k_u[:, part]) + matmul(ds_m, k_m[:, part]))
        dk_u.append(matmul_tn(ds_u, q[:, part]))
        dk_m.append(matmul_tn(ds_m, q[:, part]))
        dv_u.append(matmul_tn(p_u.astype(BF), datt[:, part]))
        mass = jnp.sum(p_m.astype(BF).astype(F32), axis=1, keepdims=True)
        dv_m.append(jnp.sum(mass * datt_f[:, part], axis=0, keepdims=True))
    cm, sm = cm_ref[...], sm_ref[...]
    join = lambda parts: jnp.concatenate(parts, axis=1)
    low = lambda a: a.astype(BF).astype(F32)
    dk_out[...] = turn_back(join(dk_u), cu_ref[...], su_ref[...]).astype(BF)
    dv_out[...] = join(dv_u).astype(BF)
    dq_sum = jnp.sum(low(turn_back(join(dq), cm, sm)), axis=0, keepdims=True)
    dk_sum = jnp.sum(low(turn_back(join(dk_m), cm, sm)), axis=0, keepdims=True)
    filler = jnp.zeros((5, LANES), F32)
    dm_out[...] = jnp.concatenate([dq_sum, dk_sum, join(dv_m), filler], axis=0)


def attend_back(q, k_u, k_m, kv_u, qkv_m, tables, mask, lse, datt):
    count, rows = kv_u.shape[0], q.shape[0]
    blocks = D // LANES
    per = LANES // HD
    column = lambda n: pl.BlockSpec((n, LANES), lambda i: (0, i))
    whole = lambda a: pl.BlockSpec(a.shape, lambda i: (0, 0))
    return pl.pallas_call(
        attend_back_kernel,
        grid=(blocks,),
        out_shape=[
            jax.ShapeDtypeStruct((count, D), BF),
            jax.ShapeDtypeStruct((count, D), BF),
            jax.ShapeDtypeStruct((8, D), F32),
        ],
        in_specs=[
            column(rows), column(count), column(rows),
            pl.BlockSpec((count, LANES), lambda i: (0, blocks + i)),
            pl.BlockSpec((qkv_m.shape[0], LANES), lambda i: (0, 2 * blocks + i)),
            *[whole(t) for t in tables],
            whole(mask),
            pl.BlockSpec((1, rows, per), lambda i: (i, 0, 0)),
            column(rows),
        ],
        out_specs=[column(count), column(count), column(8)],
        compiler_params=pltpu.CompilerParams(vmem_limit_bytes=VMEM_LIMIT),
        cost_estimate=pl.CostEstimate(
            flops=2 * 8 * rows * count * D, bytes_accessed=14 * rows * D,
            transcendentals=2 * rows * count * H,
        ),
        name="attend_back",
    )(q, k_u, k_m, kv_u, qkv_m, *tables, mask, lse, datt)


def tile_of(segments):
    return max(16, 512 // segments)


def chunk_of(width):
    return next(n for n in (640, 400, 128, width) if width % n == 0)


def logits_kernel(x_ref, w_ref, target_ref, e_ref, stats_ref, logits_ref):
    segments, _, width = w_ref.shape
    chunk = chunk_of(width)
    rows = x_ref.shape[0]
    x = x_ref[...]
    spots = [(y, at) for y in range(segments) for at in range(0, width, chunk)]
    best = None
    for place, (y, at) in enumerate(spots):
        logits = matmul(x, w_ref[y, :, at : at + chunk])
        logits_ref[:, place * chunk : (place + 1) * chunk] = logits
        best = logits if best is None else jnp.maximum(best, logits)
    top = jnp.max(best, axis=1, keepdims=True)
    lane = lax.broadcasted_iota(jnp.int32, (rows, chunk), 1)
    total = jnp.zeros((rows, chunk), F32)
    chosen = jnp.zeros((rows, chunk), F32)
    target = target_ref[...]
    for place, (y, at) in enumerate(spots):
        logits = logits_ref[:, place * chunk : (place + 1) * chunk]
        e = jnp.exp(logits - top)
        total = total + e
        chosen = chosen + jnp.where(lane == target - place * chunk, logits, 0.0)
        e_ref[y, :, at : at + chunk] = e.astype(BF)
    stats_ref[...] = jnp.concatenate(
        [top, jnp.sum(total, axis=1, keepdims=True), jnp.sum(chosen, axis=1, keepdims=True), top],
        axis=1,
    )


def head_logits(rows, weights, targets):
    count = rows.shape[0]
    segments, _, width = weights.shape
    tile = tile_of(segments)
    return pl.pallas_call(
        logits_kernel,
        grid=(count // tile,),
        out_shape=[
            jax.ShapeDtypeStruct((segments, count, width), BF),
            jax.ShapeDtypeStruct((count, 4), F32),
        ],
        in_specs=[
            pl.BlockSpec((tile, D), lambda i: (i, 0)),
            pl.BlockSpec(weights.shape, lambda i: (0, 0, 0), pipeline_mode=pl.Buffered(1)),
            pl.BlockSpec((tile, 1), lambda i: (i, 0)),
        ],
        out_specs=[
            pl.BlockSpec((segments, tile, width), lambda i: (0, i, 0)),
            pl.BlockSpec((tile, 4), lambda i: (i, 0)),
        ],
        scratch_shapes=[pltpu.VMEM((tile, segments * width), F32)],
        compiler_params=pltpu.CompilerParams(vmem_limit_bytes=VMEM_LIMIT),
        cost_estimate=pl.CostEstimate(
            flops=2 * count * D * segments * width,
            bytes_accessed=2 * count * segments * width,
            transcendentals=count * segments * width,
        ),
        name="head_logits",
    )(rows, weights, targets)


def rows_back_kernel(e_ref, w_ref, target_ref, factor_ref, d_ref, dx_ref):
    segments, _, width = w_ref.shape
    chunk = chunk_of(width)
    rows = e_ref.shape[1]
    lane = lax.broadcasted_iota(jnp.int32, (rows, chunk), 1)
    target = target_ref[...]
    factor = factor_ref[:, 0:1]
    special = factor_ref[:, 1:2]
    total = None
    for y in range(segments):
        for at in range(0, width, chunk):
            e = e_ref[y, :, at : at + chunk].astype(F32)
            hit = lane == target - (y * width + at)
            d_ref[y, :, at : at + chunk] = jnp.where(hit, special, e * factor).astype(BF)
        part = matmul_nt(d_ref[y], w_ref[y])
        total = part if total is None else total + part
    dx_ref[...] = total


def head_rows_back(e, weights, targets, factors):
    segments, count, width = e.shape
    tile = tile_of(segments)
    return pl.pallas_call(
        rows_back_kernel,
        grid=(count // tile,),
        out_shape=[
            jax.ShapeDtypeStruct(e.shape, BF),
            jax.ShapeDtypeStruct((count, D), F32),
        ],
        in_specs=[
            pl.BlockSpec((segments, tile, width), lambda i: (0, i, 0)),
            pl.BlockSpec(weights.shape, lambda i: (0, 0, 0), pipeline_mode=pl.Buffered(1)),
            pl.BlockSpec((tile, 1), lambda i: (i, 0)),
            pl.BlockSpec((tile, 2), lambda i: (i, 0)),
        ],
        out_specs=[
            pl.BlockSpec((segments, tile, width), lambda i: (0, i, 0)),
            pl.BlockSpec((tile, D), lambda i: (i, 0)),
        ],
        input_output_aliases={0: 0},
        compiler_params=pltpu.CompilerParams(vmem_limit_bytes=VMEM_LIMIT),
        cost_estimate=pl.CostEstimate(
            flops=2 * count * D * segments * width,
            bytes_accessed=4 * count * segments * width,
            transcendentals=0,
        ),
        name="head_rows_back",
    )(e, weights, targets, factors)


def layer_norm(values):
    center = values - jnp.mean(values, axis=-1, keepdims=True)
    spread = jnp.mean(center * center, axis=-1, keepdims=True)
    inv_std = lax.rsqrt(spread + NORM_EPS)
    return (center * inv_std, inv_std)


def norm_back(d_normed, normed, inv_std):
    return inv_std * (
        d_normed
        - jnp.mean(d_normed, axis=-1, keepdims=True)
        - normed * jnp.mean(d_normed * normed, axis=-1, keepdims=True)
    )


def time_features(time_index, width, steps):
    t_value = (time_index.astype(F32) + 1.0) / steps
    half_width = width // 2
    frequencies = jnp.exp(-math.log(10000.0) * jnp.arange(half_width, dtype=F32) / half_width)
    angles = 1000.0 * t_value[:, None] * frequencies[None, :]
    return jax.nn.silu(jnp.concatenate([jnp.cos(angles), jnp.sin(angles)], axis=1))


def rope_rows(positions):
    half = HD // 2
    inverse = jnp.exp(-math.log(10000.0) * jnp.arange(half, dtype=F32) * 2.0 / HD)
    angles = positions.astype(F32)[:, None] * inverse[None, :]
    cosine, sine = jnp.cos(angles), jnp.sin(angles)
    return (jnp.tile(cosine, (1, LANES // half)),
            jnp.tile(jnp.concatenate([-sine, sine], axis=1), (1, LANES // HD)))


def gelu_tanh(values):
    return jax.nn.gelu(values, approximate=True)


def adam_step(weight, first, second, ema_copy, gradient, step_value, learn_rate, decay_rate):
    first_new = BETA_ONE * first + (1.0 - BETA_ONE) * gradient
    second_new = BETA_TWO * second + (1.0 - BETA_TWO) * gradient * gradient
    first_hat = first_new / (1.0 - BETA_ONE**step_value)
    second_hat = second_new / (1.0 - BETA_TWO**step_value)
    weight_new = weight - learn_rate * (
        first_hat / (jnp.sqrt(second_hat) + ADAM_EPS) + decay_rate * weight
    )
    ema_rate = jnp.minimum(EMA_DECAY, (1.0 + step_value) / (10.0 + step_value))
    ema_new = ema_rate * ema_copy + (1.0 - ema_rate) * weight_new
    return (first_new, second_new, weight_new, ema_new)


def split3(row):
    parts, rest = [], row
    for _ in range(3):
        part = lax.reduce_precision(rest, 8, 7)
        parts.append(part.astype(BF))
        rest = rest - part
    return parts


def local(sizes, token_ids, scored, lengths, times, step_count, layer_w, layer_m, layer_v, layer_ema,
          ada_w, ada_m, ada_v, ada_ema, gains_w, gains_m, gains_v, gains_ema,
          embed_w, embed_m, embed_v, embed_ema, head_w, head_m, head_v, head_ema):
    nz, nx, ny, nc = sizes
    n = nz * nx * ny * nc
    length, score_count = token_ids.shape[1], scored.shape[1]
    free_count = length - score_count
    total_rows = n * score_count
    table_rows, table_width = embed_w.shape
    iz, ix, iy, ic = [lax.axis_index(a) for a in ALL]
    vocab_index = iy * nc + ic
    vocab_start = vocab_index * table_rows
    me = (iz * nx + ix) * (ny * nc) + vocab_index

    layer_all = lax.all_gather(layer_w.astype(BF), ALL, axis=0, tiled=True)

    tokens, masked = token_ids[0], scored[0]
    positions = jnp.arange(length, dtype=jnp.int32)
    hits = masked[:, None] == positions[None, :]
    is_masked = jnp.any(hits, axis=0)
    targets = jnp.sum(jnp.where(hits, tokens[None, :], 0), axis=1)
    keys = jnp.where(is_masked, n * V, (tokens // table_rows) * length + positions)
    rank = jnp.sum((keys[None, :] < keys[:, None]).astype(jnp.int32), axis=1)
    rank = jnp.where(is_masked, length, rank)
    slots = rank[None, :] == jnp.arange(free_count, dtype=jnp.int32)[:, None]
    free_tokens = jnp.sum(jnp.where(slots, tokens[None, :], 0), axis=1)
    free_positions = jnp.sum(jnp.where(slots, positions[None, :], 0), axis=1)

    ints = jnp.concatenate([free_tokens.reshape(-1, LANES), targets.reshape(-1, LANES),
                            jnp.broadcast_to(times[:, None], (1, LANES))], axis=0)
    ints = jnp.pad(ints, ((0, -ints.shape[0] % 8), (0, 0)))
    gain_part = jnp.pad(gains_w.astype(BF).astype(F32),
                        ((0, 8 - gains_w.shape[0]), (0, LANES - gains_w.shape[1])))
    ada_part = ada_w.astype(BF).reshape(-1, LANES)
    ints_all, gains_all, ada_all = share(sizes, 0, ints, gain_part, ada_part)
    gains = jnp.moveaxis(gains_all[:, : gains_w.shape[0], : gains_w.shape[1]], 0, 1).reshape(4, D)
    ada = ada_all.reshape(C, 6 * D)
    free_rows = free_count // LANES
    score_rows = score_count // LANES
    all_tokens = ints_all[:, :free_rows].reshape(nz * nx, ny * nc, free_count)
    all_targets = ints_all[:, free_rows : free_rows + score_rows].reshape(
        nz, nx, ny, nc, score_count)
    all_times = ints_all[:, free_rows + score_rows, 0]

    wanted = jnp.swapaxes(all_tokens, 0, 1).reshape(n, free_count)
    owners = wanted // table_rows
    low = jnp.sum((owners < vocab_index).astype(jnp.int32), axis=1)
    high = jnp.sum((owners <= vocab_index).astype(jnp.int32), axis=1)
    local_ids = wanted - vocab_start
    looked_up = gather_rows(embed_w, local_ids, low, high)
    looked_up = looked_up.reshape(ny * nc, nz * nx * free_count, table_width)
    got = exchange(lambda k: pick(looked_up, k), ("y", "c"))
    mine = got[0][1].astype(F32)
    for _, piece in got[1:]:
        mine = mine + piece.astype(F32)
    mine = mine.astype(BF).reshape(nz * nx, free_count, table_width)
    columns = in_order(exchange(lambda k: pick(mine, k), ("z", "x")))
    x0_u = jnp.swapaxes(columns, 0, 1).reshape(free_count, D).astype(F32)

    head_low = head_w.astype(BF)
    piece_for = lambda k: lax.dynamic_slice_in_dim(head_low, k * SEGMENT, SEGMENT, 1)
    head_part = in_order(exchange(piece_for, ("z",))).reshape(-1, SEGMENT)

    mask_row = gains[3:4]
    condition = time_features(times, C, TSTEPS).astype(BF)
    modulation = matmul(condition, ada)
    shift_a, scale_a, gate_a, shift_m, scale_m, gate_m = [
        modulation[:, i * D : (i + 1) * D] for i in range(6)]
    normed_u, inv_u = layer_norm(x0_u)
    a_u = (normed_u * gains[0:1] * (1.0 + scale_a) + shift_a).astype(BF)
    normed_0, inv_0 = layer_norm(mask_row)
    a_m = (normed_0 * gains[0:1] * (1.0 + scale_a) + shift_a).astype(BF)
    w_qkv, w_o = layer_all[:, : 3 * D], layer_all[:, 3 * D : 4 * D]
    w_up, w_down = layer_all[:, 4 * D : 4 * D + FF], layer_all[:, 4 * D + FF :]
    qkv_m = matmul(jnp.broadcast_to(a_m, (16, D)), w_qkv)
    kv_u = matmul(a_u, w_qkv[:, D:])
    tables = (*rope_rows(free_positions), *rope_rows(masked))
    mask = jnp.where(free_positions[None, :] < lengths[:, None], 0.0, -1e30)
    mask = jnp.broadcast_to(mask, (8, free_count)).astype(F32)
    q, k_u, k_m, att, lse_a = attend(kv_u, qkv_m, tables, mask)
    branch = matmul(att, w_o)
    x1 = mask_row + gate_a * branch
    normed_m, inv_m = layer_norm(x1)
    b = (normed_m * gains[1:2] * (1.0 + scale_m) + shift_m).astype(BF)
    pre = matmul(b, w_up)
    act = gelu_tanh(pre).astype(BF)
    mlp = matmul_nt(act, w_down)
    x2 = x1 + gate_m * mlp
    normed_f, inv_f = layer_norm(x2)
    final = (normed_f * gains[2:3]).astype(BF)

    final_turned = jnp.swapaxes(final.reshape(score_count, nz, nx, -1), 1, 2).reshape(score_count, D)
    head_all = lax.all_gather(head_part, ("y", "x"), axis=0, tiled=True).reshape(ny, D, SEGMENT)
    rows = lax.all_gather(final_turned, ("z", "c"), axis=0, tiled=True)
    group = rows.shape[0]
    row_targets = pick(jnp.moveaxis(jnp.moveaxis(all_targets, 3, 1), (2, 3), (0, 1)).reshape(
        nx * ny, group), ix * ny + iy)
    row_times = pick(jnp.moveaxis(jnp.moveaxis(all_times.reshape(nz, nx, ny, nc), 3, 1), (2, 3), (0, 1))
                     .reshape(nx * ny, nz * nc), ix * ny + iy)
    row_weights = jnp.repeat(TSTEPS / (row_times.astype(F32) + 1.0) / total_rows, score_count)
    owner, within = row_targets // table_rows, row_targets % table_rows
    owned = jnp.logical_and(owner % nc == ic, within // SEGMENT == iz)
    column_of = jnp.where(owned, (owner // nc) * SEGMENT + within % SEGMENT, -1)[:, None]
    e, stats = head_logits(rows, head_all, column_of)
    top = stats[:, 0]
    every = lax.all_gather(stats.T, ("z", "c"), axis=0)
    best = jnp.max(every[:, 0], axis=0)
    log_total = best + jnp.log(jnp.sum(every[:, 1] * jnp.exp(every[:, 0] - best), axis=0))
    chosen = jnp.sum(every[:, 2], axis=0)
    own_start = (iz * nc + ic) * score_count
    own_terms = lax.dynamic_slice_in_dim(row_weights * (log_total - chosen), own_start, score_count)
    loss_part = jnp.sum(own_terms)
    factors = jnp.stack([row_weights * jnp.exp(top - log_total),
                         row_weights * (jnp.exp(chosen - log_total) - 1.0)], axis=1)
    d_logits, d_rows = head_rows_back(e, head_all, column_of, factors)
    d_final = lax.psum_scatter(d_rows, ("z", "c"), scatter_dimension=0, tiled=True)
    d_final = jnp.swapaxes(d_final.reshape(score_count, nx, nz, -1), 1, 2).reshape(score_count, D)

    d_head = jnp.einsum("rd,yrv->ydv", rows, d_logits, preferred_element_type=F32)
    d_head = d_head.reshape(ny * nx, -1, SEGMENT)
    block_for = lambda k: pick(d_head, lax.rem(k, ny) * nx + k // ny)
    got = exchange(lambda k: block_for(k).astype(BF), ("x", "y"))
    g_part = block_for(got[0][0])
    for _, piece in got[1:]:
        g_part = g_part + piece.astype(F32)
    g_part = g_part.reshape(nz, -1, SEGMENT)
    g_head = in_order(exchange(lambda k: pick(g_part, k), ("z",)))
    g_head = jnp.swapaxes(g_head, 0, 1).reshape(head_w.shape)

    d_gain_f = jnp.sum(d_final * normed_f, axis=0)
    d_x2 = norm_back(d_final * gains[2:3], normed_f, inv_f)
    d_gate_m = jnp.sum(d_x2 * mlp, axis=0)
    d_out = (d_x2 * gate_m).astype(BF)
    d_down = matmul_tn(d_out, act)
    d_act = matmul(d_out, w_down)
    d_pre = jax.vjp(gelu_tanh, pre)[1](d_act)[0].astype(BF)
    d_up = matmul_tn(b, d_pre)
    d_b = matmul_nt(d_pre, w_up)
    d_shift_m = jnp.sum(d_b, axis=0)
    product = jnp.sum(d_b * normed_m, axis=0)
    d_scale_m = product * gains[1]
    d_gain_m = product * (1.0 + scale_m[0])
    d_x1 = d_x2 + norm_back(d_b * ((1.0 + scale_m) * gains[1:2]), normed_m, inv_m)
    d_gate_a = jnp.sum(d_x1 * branch, axis=0)
    d_branch = (d_x1 * gate_a).astype(BF)
    d_wout = matmul_tn(att, d_branch)
    d_att = matmul_nt(d_branch, w_o).astype(BF)
    d_k, d_v, d_qkv_m = attend_back(q, k_u, k_m, kv_u, qkv_m, tables, mask, lse_a, d_att)
    d_kv = jnp.concatenate([d_k, d_v], axis=1)
    d_wkv = matmul_tn(a_u, d_kv)
    d_row_m = d_qkv_m[:3].reshape(3 * D)
    d_a_u = matmul_nt(d_kv, w_qkv[:, D:])
    d_parts = matmul_nt(jnp.pad(jnp.stack(split3(d_row_m)), ((0, 13), (0, 0))), w_qkv)
    d_a_m = jnp.sum(d_parts[:3], axis=0, keepdims=True)
    d_shift_a = jnp.sum(d_a_u, axis=0) + d_a_m[0]
    product = jnp.sum(d_a_u * normed_u, axis=0) + (d_a_m * normed_0)[0]
    d_scale_a = product * gains[0]
    d_gain_a = product * (1.0 + scale_a[0])
    scaling = (1.0 + scale_a) * gains[0:1]
    d_x0_u = norm_back(d_a_u * scaling, normed_u, inv_u)
    d_mask = jnp.sum(d_x1, axis=0) + norm_back(d_a_m * scaling, normed_0, inv_0)[0]

    sent = jnp.swapaxes(d_x0_u.astype(BF).reshape(free_count, nz * nx, -1), 0, 1)
    arrived = in_order(exchange(lambda k: pick(sent, k), ("z", "x")))
    arrived = in_order(exchange(lambda k: arrived, ("y", "c")))
    g_embed = scatter_rows(arrived.reshape(n, free_count, table_width), local_ids, low, high,
                           table_rows)

    small = jnp.concatenate([d_shift_a, d_scale_a, d_gate_a, d_shift_m, d_scale_m, d_gate_m,
                             d_gain_a, d_gain_m, d_gain_f, d_mask,
                             a_m[0].astype(F32), d_row_m, jnp.broadcast_to(loss_part, (LANES,))])
    small = small.reshape(-1, LANES)
    count_small = small.shape[0]
    small_all = share(sizes, 1, jnp.pad(small, ((0, -count_small % 8), (0, 0))))[0]
    small_all = small_all[:, :count_small].reshape(n, -1)
    d_mod_all = small_all[:, : 6 * D]
    d_gains = jnp.sum(small_all[:, 6 * D : 10 * D], axis=0).reshape(4, D)
    g_gains = lax.dynamic_slice_in_dim(d_gains, me * gains_w.shape[1], gains_w.shape[1], 1)
    total_loss = jnp.sum(small_all[:, 14 * D])
    condition_all = time_features(all_times, C, TSTEPS).astype(BF).astype(F32)
    condition_rows = lax.dynamic_slice_in_dim(condition_all, me * ada_w.shape[0], ada_w.shape[0], 1)
    exact = lambda a, b: jnp.einsum("nr,nc->rc", a, b, precision=lax.Precision.HIGHEST)
    g_ada = exact(condition_rows, d_mod_all)
    a_rows = lax.dynamic_slice_in_dim(small_all[:, 10 * D : 11 * D], me * layer_w.shape[0],
                                      layer_w.shape[0], 1)
    g_outer = exact(a_rows, small_all[:, 11 * D : 14 * D])

    scatter = lambda a: lax.psum_scatter(a, ALL, scatter_dimension=0, tiled=True)
    g_down, g_up = scatter(d_down), scatter(d_up)
    g_wout, g_wkv = scatter(d_wout), scatter(d_wkv)
    g_layer = jnp.concatenate(
        [g_outer[:, :D], g_outer[:, D:] + g_wkv, g_wout, g_up, g_down], axis=1)

    squares = sum(jnp.sum(g * g) for g in (g_layer, g_ada, g_gains, g_embed, g_head))
    squares_all = share(sizes, 2, jnp.broadcast_to(squares, (8, LANES)))[0]
    grad_norm = jnp.sqrt(jnp.sum(squares_all[:, 0, 0]))
    factor = jnp.minimum(1.0, CLIP_NORM / grad_norm)
    step_value = step_count[0].astype(F32)
    updates = (
        (layer_w, layer_m, layer_v, layer_ema, g_layer),
        (ada_w, ada_m, ada_v, ada_ema, g_ada),
        (gains_w, gains_m, gains_v, gains_ema, g_gains),
        (embed_w, embed_m, embed_v, embed_ema, g_embed),
        (head_w, head_m, head_v, head_ema, g_head),
    )
    results = []
    for (w, m, v, ema, g), rate, decay in zip(updates, LEARN_RATES, WEIGHT_DECAYS):
        results.extend(adam_step(w, m, v, ema, g * factor, step_value, rate, decay))
    return (total_loss, grad_norm, *results)


def solution(mesh):
    dp, vocab = mesh.shape["dp"], mesh.shape["vocab"]
    nz, nc = V // vocab // SEGMENT, 2
    sizes = (nz, dp // nz, vocab // nc, nc)
    fine = Mesh(mesh.devices.reshape(sizes), ALL)
    rows_all, columns_all = P(ALL, None), P(None, ALL)
    table, head = P(("y", "c"), ("z", "x")), P(("z", "x"), ("y", "c"))
    weights = [rows_all] * 8 + [columns_all] * 4 + [table] * 4 + [head] * 4
    return jax.shard_map(
        functools.partial(local, sizes),
        mesh=fine,
        in_specs=(rows_all, rows_all, P(ALL), P(ALL), P(), *weights),
        out_specs=(P(), P(), *weights),
        check_vma=False,
    )
```

```python
import functools
import math

import jax
import jax.numpy as jnp
from jax import lax
from jax.experimental import pallas as pl
from jax.experimental.pallas import tpu as pltpu
from jax.sharding import Mesh, PartitionSpec as P

D = 768
H = 12
HD = 64
FF = 3072
V = 51200
C = 128
TSTEPS = 20
SEGMENT = 3200
LANES = 128

NORM_EPS = 1e-05
CLIP_NORM = 0.05
BETA_ONE = 0.9
BETA_TWO = 0.95
ADAM_EPS = 1e-08
EMA_DECAY = 0.9999
LEARN_RATES = (0.03, 0.1, 0.1, 0.5, 0.05)
WEIGHT_DECAYS = (0.01, 0.01, 0.0, 0.01, 0.01)

ALL = ("z", "x", "y", "c")
BF = jnp.bfloat16
F32 = jnp.float32
MESH = pl.DeviceIdType.MESH
VMEM_LIMIT = 60 * 1024 * 1024


def dot(a, b, contract):
    return lax.dot_general(a, b, ((contract[0], contract[1]), ((), ())), preferred_element_type=F32)


def matmul(a, b):
    return dot(a, b, ((1,), (0,)))


def matmul_nt(a, b):
    return dot(a, b, ((1,), (1,)))


def matmul_tn(a, b):
    return dot(a, b, ((0,), (0,)))


def share_kernel(sizes, count, *refs):
    nz, nx, ny, nc = sizes
    n = nz * nx * ny * nc
    ins, outs = refs[:count], refs[count : 2 * count]
    send, recv, near = refs[2 * count :]
    me = ((lax.axis_index("z") * nx + lax.axis_index("x")) * ny + lax.axis_index("y")) * nc
    me = me + lax.axis_index("c")

    def device(k):
        peer = lax.rem(me + k, n)
        return (
            peer // (nx * ny * nc),
            lax.rem(peer // (ny * nc), nx),
            lax.rem(peer // nc, ny),
            lax.rem(peer, nc),
        )

    def remote(i, k):
        return pltpu.make_async_remote_copy(
            src_ref=ins[i],
            dst_ref=outs[i].at[me],
            send_sem=send.at[i, k],
            recv_sem=recv.at[i, k],
            device_id=device(k),
            device_id_type=MESH,
        )

    barrier = pltpu.get_barrier_semaphore()

    @pl.loop(1, n)
    def _(k):
        pl.semaphore_signal(barrier, inc=1, device_id=device(k), device_id_type=MESH)

    pl.semaphore_wait(barrier, n - 1)

    @pl.loop(1, n)
    def _(k):
        for i in range(count):
            remote(i, k).start()

    for i in range(count):
        pltpu.make_async_copy(ins[i], outs[i].at[me], near.at[i]).start()
    for i in range(count):
        pltpu.make_async_copy(ins[i], outs[i].at[me], near.at[i]).wait()

    @pl.loop(1, n)
    def _(k):
        for i in range(count):
            remote(i, k).wait()


def share(sizes, collective_id, *arrays):
    n = math.prod(sizes)
    count = len(arrays)
    return pl.pallas_call(
        functools.partial(share_kernel, sizes, count),
        out_shape=[jax.ShapeDtypeStruct((n,) + a.shape, a.dtype) for a in arrays],
        in_specs=[pl.BlockSpec(memory_space=pltpu.VMEM)] * count,
        out_specs=[pl.BlockSpec(memory_space=pltpu.VMEM)] * count,
        scratch_shapes=[
            pltpu.SemaphoreType.DMA((count, n)),
            pltpu.SemaphoreType.DMA((count, n)),
            pltpu.SemaphoreType.DMA((count,)),
        ],
        compiler_params=pltpu.CompilerParams(
            collective_id=collective_id, has_side_effects=True
        ),
        name=f"share{collective_id}",
    )(*arrays)


def axis_place(axes):
    index, size = 0, 1
    for axis in axes:
        index = index * lax.axis_size(axis) + lax.axis_index(axis)
        size = size * lax.axis_size(axis)
    return index, size


def exchange(piece_for, axes):
    me, n = axis_place(axes)
    got = [(me, piece_for(me))]
    for step in range(1, n):
        piece = piece_for(lax.rem(me + step, n))
        moved = lax.ppermute(piece, axes, [(i, (i + step) % n) for i in range(n)])
        got.append((lax.rem(me + n - step, n), moved))
    return got


def in_order(got):
    out = jnp.zeros((len(got),) + got[0][1].shape, got[0][1].dtype)
    for sender, piece in got:
        out = lax.dynamic_update_index_in_dim(out, piece, sender, 0)
    return out


def together(*values):
    return lax.optimization_barrier(values)


def pick(values, index):
    return lax.dynamic_index_in_dim(values, index, 0, keepdims=False)


def gather_kernel(low_ref, high_ref, ids_ref, table_ref, out_ref, rows_ref):
    source = pl.program_id(0)
    low, high = low_ref[source], high_ref[source]
    rows_ref[...] = jnp.zeros_like(rows_ref)

    def chunk(k, carry):
        base = pl.multiple_of(k * 8, 8)
        rows = []
        for i in range(8):
            place = base + i
            valid = jnp.logical_and(place >= low, place < high)
            row = jnp.where(valid, ids_ref[source, place], 0)
            value = table_ref[pl.ds(row, 1), :]
            rows.append(jnp.where(valid, value, 0.0))
        rows_ref[pl.ds(base, 8), :] = jnp.concatenate(rows, axis=0)
        return carry

    lax.fori_loop(low // 8, (high + 7) // 8, chunk, 0)
    out_ref[0] = rows_ref[...].astype(BF)


def gather_rows(table, ids, low, high):
    sources, count = ids.shape
    width = table.shape[1]
    return pl.pallas_call(
        gather_kernel,
        out_shape=jax.ShapeDtypeStruct((sources, count, width), BF),
        grid_spec=pltpu.PrefetchScalarGridSpec(
            num_scalar_prefetch=3,
            grid=(sources,),
            in_specs=[
                pl.BlockSpec(table.shape, lambda i, *_: (0, 0), pipeline_mode=pl.Buffered(1))
            ],
            out_specs=pl.BlockSpec((1, count, width), lambda i, *_: (i, 0, 0)),
            scratch_shapes=[pltpu.VMEM((count, width), F32)],
        ),
        compiler_params=pltpu.CompilerParams(vmem_limit_bytes=VMEM_LIMIT),
        name="gather_rows",
    )(low, high, ids, table)


def scatter_kernel(low_ref, high_ref, ids_ref, rows_ref, out_ref, wide_ref):
    source = pl.program_id(0)

    @pl.when(source == 0)
    def _():
        out_ref[...] = jnp.zeros_like(out_ref)

    low, high = low_ref[source], high_ref[source]
    wide_ref[...] = rows_ref[0].astype(F32)

    def chunk(k, carry):
        base = pl.multiple_of(k * 8, 8)
        block = wide_ref[pl.ds(base, 8), :]
        for i in range(8):
            place = base + i
            valid = jnp.logical_and(place >= low, place < high)
            row = jnp.where(valid, ids_ref[source, place], 0)
            addend = jnp.where(valid, block[i : i + 1, :], 0.0)
            out_ref[pl.ds(row, 1), :] = out_ref[pl.ds(row, 1), :] + addend
        return carry

    lax.fori_loop(low // 8, (high + 7) // 8, chunk, 0)


def scatter_rows(rows, ids, low, high, table_rows):
    sources, count, width = rows.shape
    return pl.pallas_call(
        scatter_kernel,
        out_shape=jax.ShapeDtypeStruct((table_rows, width), F32),
        grid_spec=pltpu.PrefetchScalarGridSpec(
            num_scalar_prefetch=3,
            grid=(sources,),
            in_specs=[pl.BlockSpec((1, count, width), lambda i, *_: (i, 0, 0))],
            out_specs=pl.BlockSpec((table_rows, width), lambda i, *_: (0, 0)),
            scratch_shapes=[pltpu.VMEM((count, width), F32)],
        ),
        compiler_params=pltpu.CompilerParams(vmem_limit_bytes=VMEM_LIMIT),
        name="scatter_rows",
    )(low, high, ids, rows)


def swap_halves(values):
    lane = lax.broadcasted_iota(jnp.int32, values.shape, 1)
    half = HD // 2
    up = pltpu.roll(values, LANES - half, 1)
    down = pltpu.roll(values, half, 1)
    return jnp.where(lax.rem(lane, HD) < half, up, down)


def turn(values, cosine, sine):
    return values * cosine + swap_halves(values) * sine


def turn_back(values, cosine, sine):
    return values * cosine - swap_halves(values) * sine


def attend_kernel(kv_ref, vv_ref, qm_ref, km_ref, vm_ref, cu_ref, su_ref, cm_ref, sm_ref,
                  mask_ref, q_out, ku_out, km_out, att_out, lse_out):
    rows = cm_ref.shape[0]
    wide = (rows, LANES)
    cm, sm = cm_ref[...], sm_ref[...]
    q = turn(jnp.broadcast_to(qm_ref[0:1, :], wide), cm, sm).astype(BF)
    k_m = turn(jnp.broadcast_to(km_ref[0:1, :], wide), cm, sm).astype(BF)
    k_u = turn(kv_ref[...], cu_ref[...], su_ref[...]).astype(BF)
    v_u = vv_ref[...].astype(BF)
    v_m = vm_ref[0:1, :].astype(BF).astype(F32)
    q_out[...] = q
    ku_out[...] = k_u
    km_out[...] = k_m
    mask = mask_ref[0:1, :]
    outs, totals = [], []
    for head in range(LANES // HD):
        part = slice(head * HD, (head + 1) * HD)
        s_u = matmul_nt(q[:, part], k_u[:, part]) * HD ** (-0.5) + mask
        s_m = matmul_nt(q[:, part], k_m[:, part]) * HD ** (-0.5)
        top = jnp.maximum(
            jnp.max(s_u, axis=1, keepdims=True), jnp.max(s_m, axis=1, keepdims=True)
        )
        e_u = jnp.exp(s_u - top)
        e_m = jnp.exp(s_m - top)
        total = jnp.sum(e_u, axis=1, keepdims=True) + jnp.sum(e_m, axis=1, keepdims=True)
        inverse = 1.0 / total
        p_u = (e_u * inverse).astype(BF)
        p_m = (e_m * inverse).astype(BF).astype(F32)
        mixed = matmul(p_u, v_u[:, part]) + jnp.sum(p_m, axis=1, keepdims=True) * v_m[:, part]
        outs.append(mixed)
        totals.append(top + jnp.log(total))
    att_out[...] = jnp.concatenate(outs, axis=1).astype(BF)
    lse_out[0] = jnp.concatenate(totals, axis=1)


def attend(kv_u, qkv_m, tables, mask):
    count, rows = kv_u.shape[0], tables[2].shape[0]
    blocks = D // LANES
    per = LANES // HD
    row = lambda offset: pl.BlockSpec((qkv_m.shape[0], LANES), lambda i: (0, offset * blocks + i))
    column = lambda n: pl.BlockSpec((n, LANES), lambda i: (0, i))
    whole = lambda a: pl.BlockSpec(a.shape, lambda i: (0, 0))
    return pl.pallas_call(
        attend_kernel,
        grid=(blocks,),
        out_shape=[
            jax.ShapeDtypeStruct((rows, D), BF),
            jax.ShapeDtypeStruct((count, D), BF),
            jax.ShapeDtypeStruct((rows, D), BF),
            jax.ShapeDtypeStruct((rows, D), BF),
            jax.ShapeDtypeStruct((blocks, rows, per), F32),
        ],
        in_specs=[
            pl.BlockSpec((count, LANES), lambda i: (0, i)),
            pl.BlockSpec((count, LANES), lambda i: (0, blocks + i)),
            row(0), row(1), row(2),
            *[whole(t) for t in tables],
            whole(mask),
        ],
        out_specs=[column(rows), column(count), column(rows), column(rows),
                   pl.BlockSpec((1, rows, per), lambda i: (i, 0, 0))],
        compiler_params=pltpu.CompilerParams(vmem_limit_bytes=VMEM_LIMIT),
        cost_estimate=pl.CostEstimate(
            flops=2 * 3 * rows * count * D, bytes_accessed=12 * rows * D,
            transcendentals=2 * rows * count * H,
        ),
        name="attend",
    )(kv_u, kv_u, qkv_m, qkv_m, qkv_m, *tables, mask)


def attend_back_kernel(q_ref, ku_ref, km_ref, vv_ref, vm_ref, cu_ref, su_ref, cm_ref, sm_ref,
                       mask_ref, lse_ref, datt_ref, dk_out, dv_out, dm_out):
    q, k_u, k_m, datt = q_ref[...], ku_ref[...], km_ref[...], datt_ref[...]
    v_u = vv_ref[...].astype(BF)
    v_m = vm_ref[0:1, :].astype(BF).astype(F32)
    datt_f = datt.astype(F32)
    mask = mask_ref[0:1, :]
    scale = HD ** (-0.5)
    dq, dk_u, dk_m, dv_u, dv_m = [], [], [], [], []
    for head in range(LANES // HD):
        part = slice(head * HD, (head + 1) * HD)
        lse = lse_ref[0, :, head : head + 1]
        p_u = jnp.exp(matmul_nt(q[:, part], k_u[:, part]) * scale + mask - lse)
        p_m = jnp.exp(matmul_nt(q[:, part], k_m[:, part]) * scale - lse)
        dp_u = matmul_nt(datt[:, part], v_u[:, part])
        dp_m = jnp.sum(datt_f[:, part] * v_m[:, part], axis=1, keepdims=True)
        inner = jnp.sum(p_u * dp_u, axis=1, keepdims=True) + dp_m * jnp.sum(
            p_m, axis=1, keepdims=True
        )
        ds_u = (p_u * (dp_u - inner) * scale).astype(BF)
        ds_m = (p_m * ((dp_m - inner) * scale)).astype(BF)
        dq.append(matmul(ds_u, k_u[:, part]) + matmul(ds_m, k_m[:, part]))
        dk_u.append(matmul_tn(ds_u, q[:, part]))
        dk_m.append(matmul_tn(ds_m, q[:, part]))
        dv_u.append(matmul_tn(p_u.astype(BF), datt[:, part]))
        mass = jnp.sum(p_m.astype(BF).astype(F32), axis=1, keepdims=True)
        dv_m.append(jnp.sum(mass * datt_f[:, part], axis=0, keepdims=True))
    cm, sm = cm_ref[...], sm_ref[...]
    join = lambda parts: jnp.concatenate(parts, axis=1)
    low = lambda a: a.astype(BF).astype(F32)
    dk_out[...] = turn_back(join(dk_u), cu_ref[...], su_ref[...]).astype(BF)
    dv_out[...] = join(dv_u).astype(BF)
    dq_sum = jnp.sum(low(turn_back(join(dq), cm, sm)), axis=0, keepdims=True)
    dk_sum = jnp.sum(low(turn_back(join(dk_m), cm, sm)), axis=0, keepdims=True)
    filler = jnp.zeros((5, LANES), F32)
    dm_out[...] = jnp.concatenate([dq_sum, dk_sum, join(dv_m), filler], axis=0)


def attend_back(q, k_u, k_m, kv_u, qkv_m, tables, mask, lse, datt):
    count, rows = kv_u.shape[0], q.shape[0]
    blocks = D // LANES
    per = LANES // HD
    column = lambda n: pl.BlockSpec((n, LANES), lambda i: (0, i))
    whole = lambda a: pl.BlockSpec(a.shape, lambda i: (0, 0))
    return pl.pallas_call(
        attend_back_kernel,
        grid=(blocks,),
        out_shape=[
            jax.ShapeDtypeStruct((count, D), BF),
            jax.ShapeDtypeStruct((count, D), BF),
            jax.ShapeDtypeStruct((8, D), F32),
        ],
        in_specs=[
            column(rows), column(count), column(rows),
            pl.BlockSpec((count, LANES), lambda i: (0, blocks + i)),
            pl.BlockSpec((qkv_m.shape[0], LANES), lambda i: (0, 2 * blocks + i)),
            *[whole(t) for t in tables],
            whole(mask),
            pl.BlockSpec((1, rows, per), lambda i: (i, 0, 0)),
            column(rows),
        ],
        out_specs=[column(count), column(count), column(8)],
        compiler_params=pltpu.CompilerParams(vmem_limit_bytes=VMEM_LIMIT),
        cost_estimate=pl.CostEstimate(
            flops=2 * 8 * rows * count * D, bytes_accessed=14 * rows * D,
            transcendentals=2 * rows * count * H,
        ),
        name="attend_back",
    )(q, k_u, k_m, kv_u, qkv_m, *tables, mask, lse, datt)


def tile_of(segments):
    return max(16, 512 // segments)


def chunk_of(width):
    return next(n for n in (640, 400, 128, width) if width % n == 0)


def logits_kernel(x_ref, w_ref, target_ref, e_ref, stats_ref, logits_ref):
    segments, _, width = w_ref.shape
    chunk = chunk_of(width)
    rows = x_ref.shape[0]
    x = x_ref[...]
    spots = [(y, at) for y in range(segments) for at in range(0, width, chunk)]
    best = None
    for place, (y, at) in enumerate(spots):
        logits = matmul(x, w_ref[y, :, at : at + chunk])
        logits_ref[:, place * chunk : (place + 1) * chunk] = logits
        best = logits if best is None else jnp.maximum(best, logits)
    top = jnp.max(best, axis=1, keepdims=True)
    lane = lax.broadcasted_iota(jnp.int32, (rows, chunk), 1)
    total = jnp.zeros((rows, chunk), F32)
    chosen = jnp.zeros((rows, chunk), F32)
    target = target_ref[...]
    for place, (y, at) in enumerate(spots):
        logits = logits_ref[:, place * chunk : (place + 1) * chunk]
        e = jnp.exp(logits - top)
        total = total + e
        chosen = chosen + jnp.where(lane == target - place * chunk, logits, 0.0)
        e_ref[y, :, at : at + chunk] = e.astype(BF)
    stats_ref[...] = jnp.concatenate(
        [top, jnp.sum(total, axis=1, keepdims=True), jnp.sum(chosen, axis=1, keepdims=True), top],
        axis=1,
    )


def head_logits(rows, weights, targets):
    count = rows.shape[0]
    segments, _, width = weights.shape
    tile = tile_of(segments)
    return pl.pallas_call(
        logits_kernel,
        grid=(count // tile,),
        out_shape=[
            jax.ShapeDtypeStruct((segments, count, width), BF),
            jax.ShapeDtypeStruct((count, 4), F32),
        ],
        in_specs=[
            pl.BlockSpec((tile, D), lambda i: (i, 0)),
            pl.BlockSpec(weights.shape, lambda i: (0, 0, 0), pipeline_mode=pl.Buffered(1)),
            pl.BlockSpec((tile, 1), lambda i: (i, 0)),
        ],
        out_specs=[
            pl.BlockSpec((segments, tile, width), lambda i: (0, i, 0)),
            pl.BlockSpec((tile, 4), lambda i: (i, 0)),
        ],
        scratch_shapes=[pltpu.VMEM((tile, segments * width), F32)],
        compiler_params=pltpu.CompilerParams(vmem_limit_bytes=VMEM_LIMIT),
        cost_estimate=pl.CostEstimate(
            flops=2 * count * D * segments * width,
            bytes_accessed=2 * count * segments * width,
            transcendentals=count * segments * width,
        ),
        name="head_logits",
    )(rows, weights, targets)


def rows_back_kernel(e_ref, w_ref, target_ref, factor_ref, d_ref, dx_ref):
    segments, _, width = w_ref.shape
    chunk = chunk_of(width)
    rows = e_ref.shape[1]
    lane = lax.broadcasted_iota(jnp.int32, (rows, chunk), 1)
    target = target_ref[...]
    factor = factor_ref[:, 0:1]
    special = factor_ref[:, 1:2]
    total = None
    for y in range(segments):
        for at in range(0, width, chunk):
            e = e_ref[y, :, at : at + chunk].astype(F32)
            hit = lane == target - (y * width + at)
            d_ref[y, :, at : at + chunk] = jnp.where(hit, special, e * factor).astype(BF)
        part = matmul_nt(d_ref[y], w_ref[y])
        total = part if total is None else total + part
    dx_ref[...] = total


def head_rows_back(e, weights, targets, factors):
    segments, count, width = e.shape
    tile = tile_of(segments)
    return pl.pallas_call(
        rows_back_kernel,
        grid=(count // tile,),
        out_shape=[
            jax.ShapeDtypeStruct(e.shape, BF),
            jax.ShapeDtypeStruct((count, D), F32),
        ],
        in_specs=[
            pl.BlockSpec((segments, tile, width), lambda i: (0, i, 0)),
            pl.BlockSpec(weights.shape, lambda i: (0, 0, 0), pipeline_mode=pl.Buffered(1)),
            pl.BlockSpec((tile, 1), lambda i: (i, 0)),
            pl.BlockSpec((tile, 2), lambda i: (i, 0)),
        ],
        out_specs=[
            pl.BlockSpec((segments, tile, width), lambda i: (0, i, 0)),
            pl.BlockSpec((tile, D), lambda i: (i, 0)),
        ],
        input_output_aliases={0: 0},
        compiler_params=pltpu.CompilerParams(vmem_limit_bytes=VMEM_LIMIT),
        cost_estimate=pl.CostEstimate(
            flops=2 * count * D * segments * width,
            bytes_accessed=4 * count * segments * width,
            transcendentals=0,
        ),
        name="head_rows_back",
    )(e, weights, targets, factors)


def layer_norm(values):
    center = values - jnp.mean(values, axis=-1, keepdims=True)
    spread = jnp.mean(center * center, axis=-1, keepdims=True)
    inv_std = lax.rsqrt(spread + NORM_EPS)
    return (center * inv_std, inv_std)


def norm_back(d_normed, normed, inv_std):
    return inv_std * (
        d_normed
        - jnp.mean(d_normed, axis=-1, keepdims=True)
        - normed * jnp.mean(d_normed * normed, axis=-1, keepdims=True)
    )


def time_features(time_index, width, steps):
    t_value = (time_index.astype(F32) + 1.0) / steps
    half_width = width // 2
    frequencies = jnp.exp(-math.log(10000.0) * jnp.arange(half_width, dtype=F32) / half_width)
    angles = 1000.0 * t_value[:, None] * frequencies[None, :]
    return jax.nn.silu(jnp.concatenate([jnp.cos(angles), jnp.sin(angles)], axis=1))


def rope_rows(positions):
    half = HD // 2
    inverse = jnp.exp(-math.log(10000.0) * jnp.arange(half, dtype=F32) * 2.0 / HD)
    angles = positions.astype(F32)[:, None] * inverse[None, :]
    cosine, sine = jnp.cos(angles), jnp.sin(angles)
    return (jnp.tile(cosine, (1, LANES // half)),
            jnp.tile(jnp.concatenate([-sine, sine], axis=1), (1, LANES // HD)))


def gelu_tanh(values):
    return jax.nn.gelu(values, approximate=True)


def adam_step(weight, first, second, ema_copy, gradient, step_value, learn_rate, decay_rate):
    first_new = BETA_ONE * first + (1.0 - BETA_ONE) * gradient
    second_new = BETA_TWO * second + (1.0 - BETA_TWO) * gradient * gradient
    first_hat = first_new / (1.0 - BETA_ONE**step_value)
    second_hat = second_new / (1.0 - BETA_TWO**step_value)
    weight_new = weight - learn_rate * (
        first_hat / (jnp.sqrt(second_hat) + ADAM_EPS) + decay_rate * weight
    )
    ema_rate = jnp.minimum(EMA_DECAY, (1.0 + step_value) / (10.0 + step_value))
    ema_new = ema_rate * ema_copy + (1.0 - ema_rate) * weight_new
    return (first_new, second_new, weight_new, ema_new)


def split3(row):
    parts, rest = [], row
    for _ in range(3):
        part = lax.reduce_precision(rest, 8, 7)
        parts.append(part.astype(BF))
        rest = rest - part
    return parts


def local(sizes, token_ids, scored, lengths, times, step_count, layer_w, layer_m, layer_v, layer_ema,
          ada_w, ada_m, ada_v, ada_ema, gains_w, gains_m, gains_v, gains_ema,
          embed_w, embed_m, embed_v, embed_ema, head_w, head_m, head_v, head_ema):
    nz, nx, ny, nc = sizes
    n = nz * nx * ny * nc
    length, score_count = token_ids.shape[1], scored.shape[1]
    free_count = length - score_count
    total_rows = n * score_count
    table_rows, table_width = embed_w.shape
    iz, ix, iy, ic = [lax.axis_index(a) for a in ALL]
    vocab_index = iy * nc + ic
    vocab_start = vocab_index * table_rows
    me = (iz * nx + ix) * (ny * nc) + vocab_index

    tokens, masked = token_ids[0], scored[0]
    positions = jnp.arange(length, dtype=jnp.int32)
    hits = masked[:, None] == positions[None, :]
    is_masked = jnp.any(hits, axis=0)
    targets = jnp.sum(jnp.where(hits, tokens[None, :], 0), axis=1)
    keys = jnp.where(is_masked, n * V, (tokens // table_rows) * length + positions)
    rank = jnp.sum((keys[None, :] < keys[:, None]).astype(jnp.int32), axis=1)
    rank = jnp.where(is_masked, length, rank)
    slots = rank[None, :] == jnp.arange(free_count, dtype=jnp.int32)[:, None]
    free_tokens = jnp.sum(jnp.where(slots, tokens[None, :], 0), axis=1)
    free_positions = jnp.sum(jnp.where(slots, positions[None, :], 0), axis=1)

    ints = jnp.concatenate([free_tokens.reshape(-1, LANES), targets.reshape(-1, LANES),
                            jnp.broadcast_to(times[:, None], (1, LANES))], axis=0)
    ints = jnp.pad(ints, ((0, -ints.shape[0] % 8), (0, 0)))
    gain_part = jnp.pad(gains_w.astype(BF).astype(F32),
                        ((0, 8 - gains_w.shape[0]), (0, LANES - gains_w.shape[1])))
    ada_part = ada_w.astype(BF).reshape(-1, LANES)
    ints_all, gains_all, ada_all = share(sizes, 0, ints, gain_part, ada_part)

    layer_low, head_low, ints_all = together(layer_w.astype(BF), head_w.astype(BF), ints_all)
    layer_all = lax.all_gather(layer_low, ALL, axis=0, tiled=True)

    piece_for = lambda k: lax.dynamic_slice_in_dim(head_low, k * SEGMENT, SEGMENT, 1)
    head_parts = exchange(piece_for, ("z",))

    gains = jnp.moveaxis(gains_all[:, : gains_w.shape[0], : gains_w.shape[1]], 0, 1).reshape(4, D)
    ada = ada_all.reshape(C, 6 * D)
    free_rows = free_count // LANES
    score_rows = score_count // LANES
    all_tokens = ints_all[:, :free_rows].reshape(nz * nx, ny * nc, free_count)
    all_targets = ints_all[:, free_rows : free_rows + score_rows].reshape(
        nz, nx, ny, nc, score_count)
    all_times = ints_all[:, free_rows + score_rows, 0]

    wanted = jnp.swapaxes(all_tokens, 0, 1).reshape(n, free_count)
    owners = wanted // table_rows
    low = jnp.sum((owners < vocab_index).astype(jnp.int32), axis=1)
    high = jnp.sum((owners <= vocab_index).astype(jnp.int32), axis=1)
    local_ids = wanted - vocab_start
    looked_up = gather_rows(embed_w, local_ids, low, high)
    looked_up = looked_up.reshape(ny * nc, nz * nx * free_count, table_width)
    got = exchange(lambda k: pick(looked_up, k), ("y", "c"))
    mine = got[0][1].astype(F32)
    for _, piece in got[1:]:
        mine = mine + piece.astype(F32)
    mine = mine.astype(BF).reshape(nz * nx, free_count, table_width)
    columns = in_order(exchange(lambda k: pick(mine, k), ("z", "x")))
    x0_u = jnp.swapaxes(columns, 0, 1).reshape(free_count, D).astype(F32)

    senders = [sender for sender, _ in head_parts]
    x0_u, *pieces = together(x0_u, *[piece for _, piece in head_parts])
    head_part = in_order(list(zip(senders, pieces))).reshape(-1, SEGMENT)

    mask_row = gains[3:4]
    condition = time_features(times, C, TSTEPS).astype(BF)
    modulation = matmul(condition, ada)
    shift_a, scale_a, gate_a, shift_m, scale_m, gate_m = [
        modulation[:, i * D : (i + 1) * D] for i in range(6)]
    normed_u, inv_u = layer_norm(x0_u)
    a_u = (normed_u * gains[0:1] * (1.0 + scale_a) + shift_a).astype(BF)
    normed_0, inv_0 = layer_norm(mask_row)
    a_m = (normed_0 * gains[0:1] * (1.0 + scale_a) + shift_a).astype(BF)
    w_qkv, w_o = layer_all[:, : 3 * D], layer_all[:, 3 * D : 4 * D]
    w_up, w_down = layer_all[:, 4 * D : 4 * D + FF], layer_all[:, 4 * D + FF :]
    qkv_m = matmul(jnp.broadcast_to(a_m, (16, D)), w_qkv)
    kv_u = matmul(a_u, w_qkv[:, D:])
    tables = (*rope_rows(free_positions), *rope_rows(masked))
    mask = jnp.where(free_positions[None, :] < lengths[:, None], 0.0, -1e30)
    mask = jnp.broadcast_to(mask, (8, free_count)).astype(F32)
    q, k_u, k_m, att, lse_a = attend(kv_u, qkv_m, tables, mask)
    branch = matmul(att, w_o)
    x1 = mask_row + gate_a * branch
    normed_m, inv_m = layer_norm(x1)
    b = (normed_m * gains[1:2] * (1.0 + scale_m) + shift_m).astype(BF)
    pre = matmul(b, w_up)
    act = gelu_tanh(pre).astype(BF)
    mlp = matmul_nt(act, w_down)
    x2 = x1 + gate_m * mlp
    normed_f, inv_f = layer_norm(x2)
    final = (normed_f * gains[2:3]).astype(BF)

    final_turned = jnp.swapaxes(final.reshape(score_count, nz, nx, -1), 1, 2).reshape(score_count, D)
    head_all = lax.all_gather(head_part, ("y", "x"), axis=0, tiled=True).reshape(ny, D, SEGMENT)
    rows = lax.all_gather(final_turned, ("z", "c"), axis=0, tiled=True)
    group = rows.shape[0]
    row_targets = pick(jnp.moveaxis(jnp.moveaxis(all_targets, 3, 1), (2, 3), (0, 1)).reshape(
        nx * ny, group), ix * ny + iy)
    row_times = pick(jnp.moveaxis(jnp.moveaxis(all_times.reshape(nz, nx, ny, nc), 3, 1), (2, 3), (0, 1))
                     .reshape(nx * ny, nz * nc), ix * ny + iy)
    row_weights = jnp.repeat(TSTEPS / (row_times.astype(F32) + 1.0) / total_rows, score_count)
    owner, within = row_targets // table_rows, row_targets % table_rows
    owned = jnp.logical_and(owner % nc == ic, within // SEGMENT == iz)
    column_of = jnp.where(owned, (owner // nc) * SEGMENT + within % SEGMENT, -1)[:, None]
    e, stats = head_logits(rows, head_all, column_of)
    top = stats[:, 0]
    every = lax.all_gather(stats.T, ("z", "c"), axis=0)
    best = jnp.max(every[:, 0], axis=0)
    log_total = best + jnp.log(jnp.sum(every[:, 1] * jnp.exp(every[:, 0] - best), axis=0))
    chosen = jnp.sum(every[:, 2], axis=0)
    own_start = (iz * nc + ic) * score_count
    own_terms = lax.dynamic_slice_in_dim(row_weights * (log_total - chosen), own_start, score_count)
    loss_part = jnp.sum(own_terms)
    factors = jnp.stack([row_weights * jnp.exp(top - log_total),
                         row_weights * (jnp.exp(chosen - log_total) - 1.0)], axis=1)
    d_logits, d_rows = head_rows_back(e, head_all, column_of, factors)
    d_final = lax.psum_scatter(d_rows.astype(BF), ("z", "c"), scatter_dimension=0, tiled=True)

    d_head = jnp.einsum("rd,yrv->ydv", rows, d_logits, preferred_element_type=F32)
    d_head = d_head.reshape(ny * nx, -1, SEGMENT)
    d_final, d_head = together(d_final, d_head)
    d_final = d_final.astype(F32)
    d_final = jnp.swapaxes(d_final.reshape(score_count, nx, nz, -1), 1, 2).reshape(score_count, D)
    block_for = lambda k: pick(d_head, lax.rem(k, ny) * nx + k // ny)
    head_sums = exchange(lambda k: block_for(k).astype(BF), ("x", "y"))
    head_own = block_for(head_sums[0][0])

    d_gain_f = jnp.sum(d_final * normed_f, axis=0)
    d_x2 = norm_back(d_final * gains[2:3], normed_f, inv_f)
    d_gate_m = jnp.sum(d_x2 * mlp, axis=0)
    d_out = (d_x2 * gate_m).astype(BF)
    d_down = matmul_tn(d_out, act)
    d_act = matmul(d_out, w_down)
    d_pre = jax.vjp(gelu_tanh, pre)[1](d_act)[0].astype(BF)
    d_up = matmul_tn(b, d_pre)
    d_b = matmul_nt(d_pre, w_up)
    d_b, d_mlp = together(d_b, jnp.concatenate([d_up.astype(BF), d_down.astype(BF)], axis=1))
    scatter = lambda a: lax.psum_scatter(a, ALL, scatter_dimension=0, tiled=True).astype(F32)
    g_mlp = scatter(d_mlp)
    d_shift_m = jnp.sum(d_b, axis=0)
    product = jnp.sum(d_b * normed_m, axis=0)
    d_scale_m = product * gains[1]
    d_gain_m = product * (1.0 + scale_m[0])
    d_x1 = d_x2 + norm_back(d_b * ((1.0 + scale_m) * gains[1:2]), normed_m, inv_m)
    d_gate_a = jnp.sum(d_x1 * branch, axis=0)
    d_branch = (d_x1 * gate_a).astype(BF)
    d_wout = matmul_tn(att, d_branch)
    d_att = matmul_nt(d_branch, w_o).astype(BF)
    d_k, d_v, d_qkv_m = attend_back(q, k_u, k_m, kv_u, qkv_m, tables, mask, lse_a, d_att)
    d_k, *head_pieces = together(d_k, *[piece for _, piece in head_sums[1:]])
    d_kv = jnp.concatenate([d_k, d_v], axis=1)
    d_wkv = matmul_tn(a_u, d_kv)
    d_row_m = d_qkv_m[:3].reshape(3 * D)
    d_a_u = matmul_nt(d_kv, w_qkv[:, D:])
    d_parts = matmul_nt(jnp.pad(jnp.stack(split3(d_row_m)), ((0, 13), (0, 0))), w_qkv)
    d_a_m = jnp.sum(d_parts[:3], axis=0, keepdims=True)
    d_shift_a = jnp.sum(d_a_u, axis=0) + d_a_m[0]
    product = jnp.sum(d_a_u * normed_u, axis=0) + (d_a_m * normed_0)[0]
    d_scale_a = product * gains[0]
    d_gain_a = product * (1.0 + scale_a[0])
    scaling = (1.0 + scale_a) * gains[0:1]
    d_x0_u = norm_back(d_a_u * scaling, normed_u, inv_u)
    d_mask = jnp.sum(d_x1, axis=0) + norm_back(d_a_m * scaling, normed_0, inv_0)[0]

    sent = jnp.swapaxes(d_x0_u.astype(BF).reshape(free_count, nz * nx, -1), 0, 1)
    arrived = in_order(exchange(lambda k: pick(sent, k), ("z", "x")))
    arrived = in_order(exchange(lambda k: arrived, ("y", "c")))
    g_embed = scatter_rows(arrived.reshape(n, free_count, table_width), local_ids, low, high,
                           table_rows).T

    g_part = head_own
    for piece in head_pieces:
        g_part = g_part + piece.astype(F32)
    g_part = g_part.reshape(nz, -1, SEGMENT)
    g_head = together(in_order(exchange(lambda k: pick(g_part, k), ("z",))))[0]
    g_head = jnp.swapaxes(g_head, 0, 1).reshape(head_w.shape)

    small = jnp.concatenate([d_shift_a, d_scale_a, d_gate_a, d_shift_m, d_scale_m, d_gate_m,
                             d_gain_a, d_gain_m, d_gain_f, d_mask,
                             a_m[0].astype(F32), d_row_m, jnp.broadcast_to(loss_part, (LANES,))])
    small = small.reshape(-1, LANES)
    count_small = small.shape[0]
    small_all = share(sizes, 1, jnp.pad(small, ((0, -count_small % 8), (0, 0))))[0]
    small_all = small_all[:, :count_small].reshape(n, -1)
    d_mod_all = small_all[:, : 6 * D]
    d_gains = jnp.sum(small_all[:, 6 * D : 10 * D], axis=0).reshape(4, D)
    g_gains = lax.dynamic_slice_in_dim(d_gains, me * gains_w.shape[1], gains_w.shape[1], 1)
    total_loss = jnp.sum(small_all[:, 14 * D])
    condition_all = time_features(all_times, C, TSTEPS).astype(BF).astype(F32)
    condition_rows = lax.dynamic_slice_in_dim(condition_all, me * ada_w.shape[0], ada_w.shape[0], 1)
    exact = lambda a, b: jnp.einsum("nr,nc->rc", a, b, precision=lax.Precision.HIGHEST)
    g_ada = exact(condition_rows, d_mod_all)
    a_rows = lax.dynamic_slice_in_dim(small_all[:, 10 * D : 11 * D], me * layer_w.shape[0],
                                      layer_w.shape[0], 1)
    g_outer = exact(a_rows, small_all[:, 11 * D : 14 * D])

    g_rest = scatter(jnp.concatenate([d_wkv.astype(BF), d_wout.astype(BF)], axis=1))
    g_layer = jnp.concatenate(
        [g_outer[:, :D], g_outer[:, D:] + g_rest[:, : 2 * D], g_rest[:, 2 * D :], g_mlp], axis=1)

    squares = sum(jnp.sum(g * g) for g in (g_layer, g_ada, g_gains, g_embed, g_head))
    squares_all = share(sizes, 2, jnp.broadcast_to(squares, (8, LANES)))[0]
    grad_norm = jnp.sqrt(jnp.sum(squares_all[:, 0, 0]))
    factor = jnp.minimum(1.0, CLIP_NORM / grad_norm)
    step_value = step_count[0].astype(F32)
    updates = (
        (layer_w, layer_m, layer_v, layer_ema, g_layer),
        (ada_w, ada_m, ada_v, ada_ema, g_ada),
        (gains_w, gains_m, gains_v, gains_ema, g_gains),
        (embed_w.T, embed_m.T, embed_v.T, embed_ema.T, g_embed),
        (head_w, head_m, head_v, head_ema, g_head),
    )
    results = []
    for (w, m, v, ema, g), rate, decay in zip(updates, LEARN_RATES, WEIGHT_DECAYS):
        results.extend(adam_step(w, m, v, ema, g * factor, step_value, rate, decay))
    results[12:16] = [a.T for a in results[12:16]]
    return (total_loss, grad_norm, *results)


def solution(mesh):
    dp, vocab = mesh.shape["dp"], mesh.shape["vocab"]
    nz, nc = V // vocab // SEGMENT, 2
    sizes = (nz, dp // nz, vocab // nc, nc)
    fine = Mesh(mesh.devices.reshape(sizes), ALL)
    rows_all, columns_all = P(ALL, None), P(None, ALL)
    table, head = P(("y", "c"), ("z", "x")), P(("z", "x"), ("y", "c"))
    weights = [rows_all] * 8 + [columns_all] * 4 + [table] * 4 + [head] * 4
    return jax.shard_map(
        functools.partial(local, sizes),
        mesh=fine,
        in_specs=(rows_all, rows_all, P(ALL), P(ALL), P(), *weights),
        out_specs=(P(), P(), *weights),
        check_vma=False,
    )
```

```python
import functools
import math

import jax
import jax.numpy as jnp
from jax import lax
from jax.experimental import pallas as pl
from jax.experimental.pallas import tpu as pltpu
from jax.sharding import Mesh, PartitionSpec as P

D = 768
H = 12
HD = 64
FF = 3072
V = 51200
C = 128
TSTEPS = 20
SEGMENT = 3200
LANES = 128

NORM_EPS = 1e-05
CLIP_NORM = 0.05
BETA_ONE = 0.9
BETA_TWO = 0.95
ADAM_EPS = 1e-08
EMA_DECAY = 0.9999
LEARN_RATES = (0.03, 0.1, 0.1, 0.5, 0.05)
WEIGHT_DECAYS = (0.01, 0.01, 0.0, 0.01, 0.01)

ALL = ("z", "x", "y", "c")
BF = jnp.bfloat16
F32 = jnp.float32
MESH = pl.DeviceIdType.MESH
VMEM_LIMIT = 60 * 1024 * 1024


def dot(a, b, contract):
    return lax.dot_general(a, b, ((contract[0], contract[1]), ((), ())), preferred_element_type=F32)


def matmul(a, b):
    return dot(a, b, ((1,), (0,)))


def matmul_nt(a, b):
    return dot(a, b, ((1,), (1,)))


def matmul_tn(a, b):
    return dot(a, b, ((0,), (0,)))


def neighbours(axes, sizes):
    found = []
    for place, (axis, size) in enumerate(zip(axes, sizes)):
        for step in range(1, size):
            found.append((place, step, {axis: lax.rem(lax.axis_index(axis) + step, size)}))
    return found


def meet(devices):
    barrier = pltpu.get_barrier_semaphore()
    for device in devices:
        pl.semaphore_signal(barrier, inc=1, device_id=device, device_id_type=MESH)
    pl.semaphore_wait(barrier, len(devices))


def share_kernel(axes, sizes, count, *refs):
    ins, outs = refs[:count], refs[count : 2 * count]
    send, recv, near = refs[2 * count :]
    index = tuple(lax.axis_index(a) for a in axes)
    peers = neighbours(axes, sizes)
    meet([device for _, _, device in peers])
    for i in range(count):
        pltpu.make_async_copy(ins[i], outs[i].at[index], near.at[i]).start()
    for i in range(count):
        pltpu.make_async_copy(ins[i], outs[i].at[index], near.at[i]).wait()
    for place in range(len(axes)):
        view = (slice(None),) * place + index[place:]
        copies = []
        for number, (at, _, device) in enumerate(peers):
            if at == place:
                for i in range(count):
                    copies.append(
                        pltpu.make_async_remote_copy(
                            src_ref=outs[i].at[view],
                            dst_ref=outs[i].at[view],
                            send_sem=send.at[i, number],
                            recv_sem=recv.at[i, number],
                            device_id=device,
                            device_id_type=MESH,
                        )
                    )
        for copy in copies:
            copy.start()
        for copy in copies:
            copy.wait()


def share(axes, collective_id, *arrays):
    sizes = tuple(lax.axis_size(a) for a in axes)
    count, peers = len(arrays), sum(sizes) - len(sizes)
    return pl.pallas_call(
        functools.partial(share_kernel, axes, sizes, count),
        out_shape=[jax.ShapeDtypeStruct(sizes + a.shape, a.dtype) for a in arrays],
        in_specs=[pl.BlockSpec(memory_space=pltpu.VMEM)] * count,
        out_specs=[pl.BlockSpec(memory_space=pltpu.VMEM)] * count,
        scratch_shapes=[
            pltpu.SemaphoreType.DMA((count, peers)),
            pltpu.SemaphoreType.DMA((count, peers)),
            pltpu.SemaphoreType.DMA((count,)),
        ],
        compiler_params=pltpu.CompilerParams(
            collective_id=collective_id, has_side_effects=True
        ),
        name=f"share{collective_id}",
    )(*arrays)


def remote(src, dst, send, recv, device):
    return pltpu.make_async_remote_copy(
        src_ref=src, dst_ref=dst, send_sem=send, recv_sem=recv, device_id=device,
        device_id_type=MESH,
    )


def run_all(copies):
    for copy in copies:
        copy.start()
    for copy in copies:
        copy.wait()


def block_peer(sizes, step):
    nz, nx = sizes[:2]
    me = lax.axis_index("z") * nx + lax.axis_index("x")
    peer = lax.rem(me + step, nz * nx)
    return me, peer, {"z": peer // nx, "x": lax.rem(peer, nx)}


def fetch_kernel(sizes, in_ref, out_ref, from_c, from_y, half, total, sems_c, sems_y, sems_b):
    nz, nx, ny, nc = sizes
    blocks = nz * nx
    iy, ic = lax.axis_index("y"), lax.axis_index("c")
    along_y = [d for _, _, d in neighbours(("y",), (ny,))]
    along_c = [d for _, _, d in neighbours(("c",), (nc,))]
    along_b = [block_peer(sizes, step)[2] for step in range(1, blocks)]
    meet(along_c + along_y + along_b)
    run_all([
        remote(in_ref.at[:, d["c"]], from_c.at[i], sems_c.at[0, i], sems_c.at[1, i], d)
        for i, d in enumerate(along_c)
    ])

    @pl.loop(0, ny)
    def _(y):
        @pl.loop(0, blocks)
        def _(k):
            value = in_ref[y, ic, k]
            for i in range(nc - 1):
                value = value + from_c[i, y, k]
            half[y, k] = value

    run_all([
        remote(half.at[d["y"]], from_y.at[i], sems_y.at[0, i], sems_y.at[1, i], d)
        for i, d in enumerate(along_y)
    ])

    @pl.loop(0, blocks)
    def _(k):
        value = half[iy, k]
        for i in range(ny - 1):
            value = value + from_y[i, k]
        total[k] = value

    me = block_peer(sizes, 0)[0]
    copies = []
    for step in range(1, blocks):
        _, peer, device = block_peer(sizes, step)
        copies.append(
            remote(total.at[peer], out_ref.at[me], sems_b.at[0, step], sems_b.at[1, step], device)
        )
    for copy in copies:
        copy.start()
    out_ref[me] = total[me]
    for copy in copies:
        copy.wait()


def fetch_blocks(sizes, looked_up, collective_id):
    nz, nx, ny, nc = sizes
    block = looked_up.shape[3:]
    blocks = nz * nx
    return pl.pallas_call(
        functools.partial(fetch_kernel, sizes),
        out_shape=jax.ShapeDtypeStruct((blocks,) + block, BF),
        in_specs=[pl.BlockSpec(memory_space=pltpu.VMEM)],
        out_specs=pl.BlockSpec(memory_space=pltpu.VMEM),
        scratch_shapes=[
            pltpu.VMEM((nc - 1, ny, blocks) + block, BF),
            pltpu.VMEM((ny - 1, blocks) + block, BF),
            pltpu.VMEM((ny, blocks) + block, BF),
            pltpu.VMEM((blocks,) + block, BF),
            pltpu.SemaphoreType.DMA((2, nc - 1)),
            pltpu.SemaphoreType.DMA((2, ny - 1)),
            pltpu.SemaphoreType.DMA((2, blocks)),
        ],
        compiler_params=pltpu.CompilerParams(
            collective_id=collective_id, has_side_effects=True, vmem_limit_bytes=VMEM_LIMIT
        ),
        name="fetch_blocks",
    )(looked_up)


def spread_kernel(sizes, in_ref, out_ref, sems_c, sems_y, sems_b):
    nz, nx, ny, nc = sizes
    blocks = nz * nx
    iy, ic = lax.axis_index("y"), lax.axis_index("c")
    along_y = [d for _, _, d in neighbours(("y",), (ny,))]
    along_c = [d for _, _, d in neighbours(("c",), (nc,))]
    along_b = [block_peer(sizes, step)[2] for step in range(1, blocks)]
    meet(along_c + along_y + along_b)
    me = block_peer(sizes, 0)[0]
    copies = []
    for step in range(1, blocks):
        _, peer, device = block_peer(sizes, step)
        copies.append(
            remote(in_ref.at[peer], out_ref.at[iy, ic, me], sems_b.at[0, step],
                   sems_b.at[1, step], device)
        )
    for copy in copies:
        copy.start()
    out_ref[iy, ic, me] = in_ref[me]
    for copy in copies:
        copy.wait()
    run_all([
        remote(out_ref.at[iy, ic], out_ref.at[iy, ic], sems_y.at[0, i], sems_y.at[1, i], d)
        for i, d in enumerate(along_y)
    ])
    run_all([
        remote(out_ref.at[:, ic], out_ref.at[:, ic], sems_c.at[0, i], sems_c.at[1, i], d)
        for i, d in enumerate(along_c)
    ])


def spread_blocks(sizes, parts, collective_id):
    nz, nx, ny, nc = sizes
    return pl.pallas_call(
        functools.partial(spread_kernel, sizes),
        out_shape=jax.ShapeDtypeStruct((ny, nc) + parts.shape, parts.dtype),
        in_specs=[pl.BlockSpec(memory_space=pltpu.VMEM)],
        out_specs=pl.BlockSpec(memory_space=pltpu.VMEM),
        scratch_shapes=[
            pltpu.SemaphoreType.DMA((2, nc - 1)),
            pltpu.SemaphoreType.DMA((2, ny - 1)),
            pltpu.SemaphoreType.DMA((2, nz * nx)),
        ],
        compiler_params=pltpu.CompilerParams(
            collective_id=collective_id, has_side_effects=True, vmem_limit_bytes=VMEM_LIMIT
        ),
        name="spread_blocks",
    )(parts)


def axis_place(axes):
    index, size = 0, 1
    for axis in axes:
        index = index * lax.axis_size(axis) + lax.axis_index(axis)
        size = size * lax.axis_size(axis)
    return index, size


def exchange(piece_for, axes):
    me, n = axis_place(axes)
    got = [(me, piece_for(me))]
    for step in range(1, n):
        piece = piece_for(lax.rem(me + step, n))
        moved = lax.ppermute(piece, axes, [(i, (i + step) % n) for i in range(n)])
        got.append((lax.rem(me + n - step, n), moved))
    return got


def in_order(got):
    out = jnp.zeros((len(got),) + got[0][1].shape, got[0][1].dtype)
    for sender, piece in got:
        out = lax.dynamic_update_index_in_dim(out, piece, sender, 0)
    return out


def together(*values):
    return lax.optimization_barrier(values)


def pick(values, index):
    return lax.dynamic_index_in_dim(values, index, 0, keepdims=False)


def gather_kernel(low_ref, high_ref, ids_ref, table_ref, out_ref, turned_ref, rows_ref):
    source = pl.program_id(0)

    @pl.when(source == 0)
    def _():
        @pl.loop(0, table_ref.shape[1] // LANES)
        def _(k):
            at = pl.multiple_of(k * LANES, LANES)
            turned_ref[pl.ds(at, LANES), :] = table_ref[:, pl.ds(at, LANES)].T

    low, high = low_ref[source], high_ref[source]
    rows_ref[...] = jnp.zeros_like(rows_ref)

    def chunk(k, carry):
        base = pl.multiple_of(k * 8, 8)
        rows = []
        for i in range(8):
            place = base + i
            valid = jnp.logical_and(place >= low, place < high)
            row = jnp.where(valid, ids_ref[source, place], 0)
            value = turned_ref[pl.ds(row, 1), :]
            rows.append(jnp.where(valid, value, 0.0))
        rows_ref[pl.ds(base, 8), :] = jnp.concatenate(rows, axis=0)
        return carry

    lax.fori_loop(low // 8, (high + 7) // 8, chunk, 0)
    out_ref[0] = rows_ref[...].T.astype(BF)


def gather_rows(table, ids, low, high):
    sources, count = ids.shape
    width = table.shape[0]
    return pl.pallas_call(
        gather_kernel,
        out_shape=jax.ShapeDtypeStruct((sources, width, count), BF),
        grid_spec=pltpu.PrefetchScalarGridSpec(
            num_scalar_prefetch=3,
            grid=(sources,),
            in_specs=[
                pl.BlockSpec(table.shape, lambda i, *_: (0, 0), pipeline_mode=pl.Buffered(1))
            ],
            out_specs=pl.BlockSpec((1, width, count), lambda i, *_: (i, 0, 0)),
            scratch_shapes=[
                pltpu.VMEM((table.shape[1], width), F32),
                pltpu.VMEM((count, width), F32),
            ],
        ),
        compiler_params=pltpu.CompilerParams(vmem_limit_bytes=VMEM_LIMIT),
        name="gather_rows",
    )(low, high, ids, table)


def scatter_kernel(low_ref, high_ref, ids_ref, rows_ref, out_ref, total_ref, wide_ref):
    source = pl.program_id(0)

    @pl.when(source == 0)
    def _():
        total_ref[...] = jnp.zeros_like(total_ref)

    low, high = low_ref[source], high_ref[source]
    wide_ref[...] = rows_ref[0].astype(F32).T

    def chunk(k, carry):
        base = pl.multiple_of(k * 8, 8)
        block = wide_ref[pl.ds(base, 8), :]
        for i in range(8):
            place = base + i
            valid = jnp.logical_and(place >= low, place < high)
            row = jnp.where(valid, ids_ref[source, place], 0)
            addend = jnp.where(valid, block[i : i + 1, :], 0.0)
            total_ref[pl.ds(row, 1), :] = total_ref[pl.ds(row, 1), :] + addend
        return carry

    lax.fori_loop(low // 8, (high + 7) // 8, chunk, 0)

    @pl.when(source == pl.num_programs(0) - 1)
    def _():
        @pl.loop(0, out_ref.shape[1] // LANES)
        def _(k):
            at = pl.multiple_of(k * LANES, LANES)
            out_ref[:, pl.ds(at, LANES)] = total_ref[pl.ds(at, LANES), :].T


def scatter_rows(rows, ids, low, high, table_rows):
    sources, width, count = rows.shape
    return pl.pallas_call(
        scatter_kernel,
        out_shape=jax.ShapeDtypeStruct((width, table_rows), F32),
        grid_spec=pltpu.PrefetchScalarGridSpec(
            num_scalar_prefetch=3,
            grid=(sources,),
            in_specs=[pl.BlockSpec((1, width, count), lambda i, *_: (i, 0, 0))],
            out_specs=pl.BlockSpec((width, table_rows), lambda i, *_: (0, 0)),
            scratch_shapes=[
                pltpu.VMEM((table_rows, width), F32),
                pltpu.VMEM((count, width), F32),
            ],
        ),
        compiler_params=pltpu.CompilerParams(vmem_limit_bytes=VMEM_LIMIT),
        name="scatter_rows",
    )(low, high, ids, rows)


def swap_halves(values):
    lane = lax.broadcasted_iota(jnp.int32, values.shape, 1)
    half = HD // 2
    up = pltpu.roll(values, LANES - half, 1)
    down = pltpu.roll(values, half, 1)
    return jnp.where(lax.rem(lane, HD) < half, up, down)


def turn(values, cosine, sine):
    return values * cosine + swap_halves(values) * sine


def turn_back(values, cosine, sine):
    return values * cosine - swap_halves(values) * sine


def attend_kernel(kv_ref, vv_ref, qm_ref, km_ref, vm_ref, cu_ref, su_ref, cm_ref, sm_ref,
                  mask_ref, q_out, ku_out, km_out, att_out, lse_out):
    rows = cm_ref.shape[0]
    wide = (rows, LANES)
    cm, sm = cm_ref[...], sm_ref[...]
    q = turn(jnp.broadcast_to(qm_ref[0:1, :], wide), cm, sm).astype(BF)
    k_m = turn(jnp.broadcast_to(km_ref[0:1, :], wide), cm, sm).astype(BF)
    k_u = turn(kv_ref[...], cu_ref[...], su_ref[...]).astype(BF)
    v_u = vv_ref[...].astype(BF)
    v_m = vm_ref[0:1, :].astype(BF).astype(F32)
    q_out[...] = q
    ku_out[...] = k_u
    km_out[...] = k_m
    mask = mask_ref[0:1, :]
    outs, totals = [], []
    for head in range(LANES // HD):
        part = slice(head * HD, (head + 1) * HD)
        s_u = matmul_nt(q[:, part], k_u[:, part]) * HD ** (-0.5) + mask
        s_m = matmul_nt(q[:, part], k_m[:, part]) * HD ** (-0.5)
        top = jnp.maximum(
            jnp.max(s_u, axis=1, keepdims=True), jnp.max(s_m, axis=1, keepdims=True)
        )
        e_u = jnp.exp(s_u - top)
        e_m = jnp.exp(s_m - top)
        total = jnp.sum(e_u, axis=1, keepdims=True) + jnp.sum(e_m, axis=1, keepdims=True)
        inverse = 1.0 / total
        p_u = (e_u * inverse).astype(BF)
        p_m = (e_m * inverse).astype(BF).astype(F32)
        mixed = matmul(p_u, v_u[:, part]) + jnp.sum(p_m, axis=1, keepdims=True) * v_m[:, part]
        outs.append(mixed)
        totals.append(top + jnp.log(total))
    att_out[...] = jnp.concatenate(outs, axis=1).astype(BF)
    lse_out[0] = jnp.concatenate(totals, axis=1)


def attend(kv_u, qkv_m, tables, mask):
    count, rows = kv_u.shape[0], tables[2].shape[0]
    blocks = D // LANES
    per = LANES // HD
    row = lambda offset: pl.BlockSpec((qkv_m.shape[0], LANES), lambda i: (0, offset * blocks + i))
    column = lambda n: pl.BlockSpec((n, LANES), lambda i: (0, i))
    whole = lambda a: pl.BlockSpec(a.shape, lambda i: (0, 0))
    return pl.pallas_call(
        attend_kernel,
        grid=(blocks,),
        out_shape=[
            jax.ShapeDtypeStruct((rows, D), BF),
            jax.ShapeDtypeStruct((count, D), BF),
            jax.ShapeDtypeStruct((rows, D), BF),
            jax.ShapeDtypeStruct((rows, D), BF),
            jax.ShapeDtypeStruct((blocks, rows, per), F32),
        ],
        in_specs=[
            pl.BlockSpec((count, LANES), lambda i: (0, i)),
            pl.BlockSpec((count, LANES), lambda i: (0, blocks + i)),
            row(0), row(1), row(2),
            *[whole(t) for t in tables],
            whole(mask),
        ],
        out_specs=[column(rows), column(count), column(rows), column(rows),
                   pl.BlockSpec((1, rows, per), lambda i: (i, 0, 0))],
        compiler_params=pltpu.CompilerParams(vmem_limit_bytes=VMEM_LIMIT),
        cost_estimate=pl.CostEstimate(
            flops=2 * 3 * rows * count * D, bytes_accessed=12 * rows * D,
            transcendentals=2 * rows * count * H,
        ),
        name="attend",
    )(kv_u, kv_u, qkv_m, qkv_m, qkv_m, *tables, mask)


def attend_back_kernel(q_ref, ku_ref, km_ref, vv_ref, vm_ref, cu_ref, su_ref, cm_ref, sm_ref,
                       mask_ref, lse_ref, datt_ref, dk_out, dv_out, dm_out):
    q, k_u, k_m, datt = q_ref[...], ku_ref[...], km_ref[...], datt_ref[...]
    v_u = vv_ref[...].astype(BF)
    v_m = vm_ref[0:1, :].astype(BF).astype(F32)
    datt_f = datt.astype(F32)
    mask = mask_ref[0:1, :]
    scale = HD ** (-0.5)
    dq, dk_u, dk_m, dv_u, dv_m = [], [], [], [], []
    for head in range(LANES // HD):
        part = slice(head * HD, (head + 1) * HD)
        lse = lse_ref[0, :, head : head + 1]
        p_u = jnp.exp(matmul_nt(q[:, part], k_u[:, part]) * scale + mask - lse)
        p_m = jnp.exp(matmul_nt(q[:, part], k_m[:, part]) * scale - lse)
        dp_u = matmul_nt(datt[:, part], v_u[:, part])
        dp_m = jnp.sum(datt_f[:, part] * v_m[:, part], axis=1, keepdims=True)
        inner = jnp.sum(p_u * dp_u, axis=1, keepdims=True) + dp_m * jnp.sum(
            p_m, axis=1, keepdims=True
        )
        ds_u = (p_u * (dp_u - inner) * scale).astype(BF)
        ds_m = (p_m * ((dp_m - inner) * scale)).astype(BF)
        dq.append(matmul(ds_u, k_u[:, part]) + matmul(ds_m, k_m[:, part]))
        dk_u.append(matmul_tn(ds_u, q[:, part]))
        dk_m.append(matmul_tn(ds_m, q[:, part]))
        dv_u.append(matmul_tn(p_u.astype(BF), datt[:, part]))
        mass = jnp.sum(p_m.astype(BF).astype(F32), axis=1, keepdims=True)
        dv_m.append(jnp.sum(mass * datt_f[:, part], axis=0, keepdims=True))
    cm, sm = cm_ref[...], sm_ref[...]
    join = lambda parts: jnp.concatenate(parts, axis=1)
    low = lambda a: a.astype(BF).astype(F32)
    dk_out[...] = turn_back(join(dk_u), cu_ref[...], su_ref[...]).astype(BF)
    dv_out[...] = join(dv_u).astype(BF)
    dq_sum = jnp.sum(low(turn_back(join(dq), cm, sm)), axis=0, keepdims=True)
    dk_sum = jnp.sum(low(turn_back(join(dk_m), cm, sm)), axis=0, keepdims=True)
    filler = jnp.zeros((5, LANES), F32)
    dm_out[...] = jnp.concatenate([dq_sum, dk_sum, join(dv_m), filler], axis=0)


def attend_back(q, k_u, k_m, kv_u, qkv_m, tables, mask, lse, datt):
    count, rows = kv_u.shape[0], q.shape[0]
    blocks = D // LANES
    per = LANES // HD
    column = lambda n: pl.BlockSpec((n, LANES), lambda i: (0, i))
    whole = lambda a: pl.BlockSpec(a.shape, lambda i: (0, 0))
    return pl.pallas_call(
        attend_back_kernel,
        grid=(blocks,),
        out_shape=[
            jax.ShapeDtypeStruct((count, D), BF),
            jax.ShapeDtypeStruct((count, D), BF),
            jax.ShapeDtypeStruct((8, D), F32),
        ],
        in_specs=[
            column(rows), column(count), column(rows),
            pl.BlockSpec((count, LANES), lambda i: (0, blocks + i)),
            pl.BlockSpec((qkv_m.shape[0], LANES), lambda i: (0, 2 * blocks + i)),
            *[whole(t) for t in tables],
            whole(mask),
            pl.BlockSpec((1, rows, per), lambda i: (i, 0, 0)),
            column(rows),
        ],
        out_specs=[column(count), column(count), column(8)],
        compiler_params=pltpu.CompilerParams(vmem_limit_bytes=VMEM_LIMIT),
        cost_estimate=pl.CostEstimate(
            flops=2 * 8 * rows * count * D, bytes_accessed=14 * rows * D,
            transcendentals=2 * rows * count * H,
        ),
        name="attend_back",
    )(q, k_u, k_m, kv_u, qkv_m, *tables, mask, lse, datt)


def tile_of(segments):
    return max(16, 512 // segments)


def chunk_of(width):
    return next(n for n in (640, 400, 128, width) if width % n == 0)


def logits_kernel(x_ref, w_ref, target_ref, e_ref, stats_ref, logits_ref):
    segments, _, width = w_ref.shape
    chunk = chunk_of(width)
    rows = x_ref.shape[0]
    x = x_ref[...]
    spots = [(y, at) for y in range(segments) for at in range(0, width, chunk)]
    best = None
    for place, (y, at) in enumerate(spots):
        logits = matmul(x, w_ref[y, :, at : at + chunk])
        logits_ref[:, place * chunk : (place + 1) * chunk] = logits
        best = logits if best is None else jnp.maximum(best, logits)
    top = jnp.max(best, axis=1, keepdims=True)
    lane = lax.broadcasted_iota(jnp.int32, (rows, chunk), 1)
    total = jnp.zeros((rows, chunk), F32)
    chosen = jnp.zeros((rows, chunk), F32)
    target = target_ref[...]
    for place, (y, at) in enumerate(spots):
        logits = logits_ref[:, place * chunk : (place + 1) * chunk]
        e = jnp.exp(logits - top)
        total = total + e
        chosen = chosen + jnp.where(lane == target - place * chunk, logits, 0.0)
        e_ref[y, :, at : at + chunk] = e.astype(BF)
    stats_ref[...] = jnp.concatenate(
        [top, jnp.sum(total, axis=1, keepdims=True), jnp.sum(chosen, axis=1, keepdims=True), top],
        axis=1,
    )


def head_logits(rows, weights, targets):
    count = rows.shape[0]
    segments, _, width = weights.shape
    tile = tile_of(segments)
    return pl.pallas_call(
        logits_kernel,
        grid=(count // tile,),
        out_shape=[
            jax.ShapeDtypeStruct((segments, count, width), BF),
            jax.ShapeDtypeStruct((count, 4), F32),
        ],
        in_specs=[
            pl.BlockSpec((tile, D), lambda i: (i, 0)),
            pl.BlockSpec(weights.shape, lambda i: (0, 0, 0), pipeline_mode=pl.Buffered(1)),
            pl.BlockSpec((tile, 1), lambda i: (i, 0)),
        ],
        out_specs=[
            pl.BlockSpec((segments, tile, width), lambda i: (0, i, 0)),
            pl.BlockSpec((tile, 4), lambda i: (i, 0)),
        ],
        scratch_shapes=[pltpu.VMEM((tile, segments * width), F32)],
        compiler_params=pltpu.CompilerParams(vmem_limit_bytes=VMEM_LIMIT),
        cost_estimate=pl.CostEstimate(
            flops=2 * count * D * segments * width,
            bytes_accessed=2 * count * segments * width,
            transcendentals=count * segments * width,
        ),
        name="head_logits",
    )(rows, weights, targets)


def rows_back_kernel(e_ref, w_ref, target_ref, factor_ref, d_ref, dx_ref):
    segments, _, width = w_ref.shape
    chunk = chunk_of(width)
    rows = e_ref.shape[1]
    lane = lax.broadcasted_iota(jnp.int32, (rows, chunk), 1)
    target = target_ref[...]
    factor = factor_ref[:, 0:1]
    special = factor_ref[:, 1:2]
    total = None
    for y in range(segments):
        for at in range(0, width, chunk):
            e = e_ref[y, :, at : at + chunk].astype(F32)
            hit = lane == target - (y * width + at)
            d_ref[y, :, at : at + chunk] = jnp.where(hit, special, e * factor).astype(BF)
        part = matmul_nt(d_ref[y], w_ref[y])
        total = part if total is None else total + part
    dx_ref[...] = total


def head_rows_back(e, weights, targets, factors):
    segments, count, width = e.shape
    tile = tile_of(segments)
    return pl.pallas_call(
        rows_back_kernel,
        grid=(count // tile,),
        out_shape=[
            jax.ShapeDtypeStruct(e.shape, BF),
            jax.ShapeDtypeStruct((count, D), F32),
        ],
        in_specs=[
            pl.BlockSpec((segments, tile, width), lambda i: (0, i, 0)),
            pl.BlockSpec(weights.shape, lambda i: (0, 0, 0), pipeline_mode=pl.Buffered(1)),
            pl.BlockSpec((tile, 1), lambda i: (i, 0)),
            pl.BlockSpec((tile, 2), lambda i: (i, 0)),
        ],
        out_specs=[
            pl.BlockSpec((segments, tile, width), lambda i: (0, i, 0)),
            pl.BlockSpec((tile, D), lambda i: (i, 0)),
        ],
        input_output_aliases={0: 0},
        compiler_params=pltpu.CompilerParams(vmem_limit_bytes=VMEM_LIMIT),
        cost_estimate=pl.CostEstimate(
            flops=2 * count * D * segments * width,
            bytes_accessed=4 * count * segments * width,
            transcendentals=0,
        ),
        name="head_rows_back",
    )(e, weights, targets, factors)


def layer_norm(values):
    center = values - jnp.mean(values, axis=-1, keepdims=True)
    spread = jnp.mean(center * center, axis=-1, keepdims=True)
    inv_std = lax.rsqrt(spread + NORM_EPS)
    return (center * inv_std, inv_std)


def norm_back(d_normed, normed, inv_std):
    return inv_std * (
        d_normed
        - jnp.mean(d_normed, axis=-1, keepdims=True)
        - normed * jnp.mean(d_normed * normed, axis=-1, keepdims=True)
    )


def time_features(time_index, width, steps):
    t_value = (time_index.astype(F32) + 1.0) / steps
    half_width = width // 2
    frequencies = jnp.exp(-math.log(10000.0) * jnp.arange(half_width, dtype=F32) / half_width)
    angles = 1000.0 * t_value[:, None] * frequencies[None, :]
    return jax.nn.silu(jnp.concatenate([jnp.cos(angles), jnp.sin(angles)], axis=1))


def rope_rows(positions):
    half = HD // 2
    inverse = jnp.exp(-math.log(10000.0) * jnp.arange(half, dtype=F32) * 2.0 / HD)
    angles = positions.astype(F32)[:, None] * inverse[None, :]
    cosine, sine = jnp.cos(angles), jnp.sin(angles)
    return (jnp.tile(cosine, (1, LANES // half)),
            jnp.tile(jnp.concatenate([-sine, sine], axis=1), (1, LANES // HD)))


def gelu_tanh(values):
    return jax.nn.gelu(values, approximate=True)


def adam_step(weight, first, second, ema_copy, gradient, step_value, learn_rate, decay_rate):
    first_new = BETA_ONE * first + (1.0 - BETA_ONE) * gradient
    second_new = BETA_TWO * second + (1.0 - BETA_TWO) * gradient * gradient
    first_hat = first_new / (1.0 - BETA_ONE**step_value)
    second_hat = second_new / (1.0 - BETA_TWO**step_value)
    weight_new = weight - learn_rate * (
        first_hat / (jnp.sqrt(second_hat) + ADAM_EPS) + decay_rate * weight
    )
    ema_rate = jnp.minimum(EMA_DECAY, (1.0 + step_value) / (10.0 + step_value))
    ema_new = ema_rate * ema_copy + (1.0 - ema_rate) * weight_new
    return (first_new, second_new, weight_new, ema_new)


def split3(row):
    parts, rest = [], row
    for _ in range(3):
        part = lax.reduce_precision(rest, 8, 7)
        parts.append(part.astype(BF))
        rest = rest - part
    return parts


def local(sizes, token_ids, scored, lengths, times, step_count, layer_w, layer_m, layer_v, layer_ema,
          ada_w, ada_m, ada_v, ada_ema, gains_w, gains_m, gains_v, gains_ema,
          embed_w, embed_m, embed_v, embed_ema, head_w, head_m, head_v, head_ema):
    nz, nx, ny, nc = sizes
    n = nz * nx * ny * nc
    length, score_count = token_ids.shape[1], scored.shape[1]
    free_count = length - score_count
    total_rows = n * score_count
    table_rows, table_width = embed_w.shape
    iz, ix, iy, ic = [lax.axis_index(a) for a in ALL]
    vocab_index = iy * nc + ic
    vocab_start = vocab_index * table_rows
    me = (iz * nx + ix) * (ny * nc) + vocab_index

    tokens, masked = token_ids[0], scored[0]
    positions = jnp.arange(length, dtype=jnp.int32)
    hits = masked[:, None] == positions[None, :]
    is_masked = jnp.any(hits, axis=0)
    targets = jnp.sum(jnp.where(hits, tokens[None, :], 0), axis=1)
    keys = jnp.where(is_masked, n * V, (tokens // table_rows) * length + positions)
    rank = jnp.sum((keys[None, :] < keys[:, None]).astype(jnp.int32), axis=1)
    rank = jnp.where(is_masked, length, rank)
    slots = rank[None, :] == jnp.arange(free_count, dtype=jnp.int32)[:, None]
    free_tokens = jnp.sum(jnp.where(slots, tokens[None, :], 0), axis=1)
    free_positions = jnp.sum(jnp.where(slots, positions[None, :], 0), axis=1)

    ints = jnp.concatenate([free_tokens.reshape(-1, LANES), targets.reshape(-1, LANES),
                            jnp.broadcast_to(times[:, None], (1, LANES))], axis=0)
    ints = jnp.pad(ints, ((0, -ints.shape[0] % 8), (0, 0)))
    gain_part = jnp.pad(gains_w.astype(BF).astype(F32),
                        ((0, 8 - gains_w.shape[0]), (0, LANES - gains_w.shape[1])))
    ints_all, gains_all = share(ALL, 0, ints, gain_part)
    ints_all = ints_all.reshape((n,) + ints.shape)
    gains_all = gains_all.reshape((n,) + gain_part.shape)

    block_low = jnp.concatenate(
        [layer_w.astype(BF), ada_w.astype(BF).reshape(layer_w.shape[0], -1)], axis=1)
    block_low, head_low, ints_all = together(block_low, head_w.astype(BF), ints_all)
    layer_all = lax.all_gather(block_low, ALL, axis=0, tiled=True)

    piece_for = lambda k: lax.dynamic_slice_in_dim(head_low, k * SEGMENT, SEGMENT, 1)
    head_parts = exchange(piece_for, ("z",))

    gains = jnp.moveaxis(gains_all[:, : gains_w.shape[0], : gains_w.shape[1]], 0, 1).reshape(4, D)
    free_rows = free_count // LANES
    score_rows = score_count // LANES
    all_tokens = ints_all[:, :free_rows].reshape(nz * nx, ny * nc, free_count)
    all_targets = ints_all[:, free_rows : free_rows + score_rows].reshape(
        nz, nx, ny, nc, score_count)
    all_times = ints_all[:, free_rows + score_rows, 0]

    wanted = jnp.swapaxes(all_tokens, 0, 1).reshape(n, free_count)
    owners = wanted // table_rows
    low = jnp.sum((owners < vocab_index).astype(jnp.int32), axis=1)
    high = jnp.sum((owners <= vocab_index).astype(jnp.int32), axis=1)
    local_ids = wanted - vocab_start
    looked_up = gather_rows(embed_w.T, local_ids, low, high)
    looked_up = looked_up.reshape((ny, nc, nz * nx) + looked_up.shape[1:])
    x0_u = fetch_blocks(sizes, looked_up, 3).reshape(D, free_count).T.astype(F32)
    senders = [sender for sender, _ in head_parts]
    x0_u, *pieces = together(x0_u, *[piece for _, piece in head_parts])
    head_part = in_order(list(zip(senders, pieces))).reshape(-1, SEGMENT)

    mask_row = gains[3:4]
    condition = time_features(times, C, TSTEPS).astype(BF)
    modulation = matmul(condition, layer_all[:, layer_w.shape[1] :].reshape(C, 6 * D))
    shift_a, scale_a, gate_a, shift_m, scale_m, gate_m = [
        modulation[:, i * D : (i + 1) * D] for i in range(6)]
    normed_u, inv_u = layer_norm(x0_u)
    a_u = (normed_u * gains[0:1] * (1.0 + scale_a) + shift_a).astype(BF)
    normed_0, inv_0 = layer_norm(mask_row)
    a_m = (normed_0 * gains[0:1] * (1.0 + scale_a) + shift_a).astype(BF)
    w_qkv, w_o = layer_all[:, : 3 * D], layer_all[:, 3 * D : 4 * D]
    w_up, w_down = layer_all[:, 4 * D : 4 * D + FF], layer_all[:, 4 * D + FF : 4 * D + 2 * FF]
    qkv_m = matmul(jnp.broadcast_to(a_m, (16, D)), w_qkv)
    kv_u = matmul(a_u, w_qkv[:, D:])
    tables = (*rope_rows(free_positions), *rope_rows(masked))
    mask = jnp.where(free_positions[None, :] < lengths[:, None], 0.0, -1e30)
    mask = jnp.broadcast_to(mask, (8, free_count)).astype(F32)
    q, k_u, k_m, att, lse_a = attend(kv_u, qkv_m, tables, mask)
    branch = matmul(att, w_o)
    x1 = mask_row + gate_a * branch
    normed_m, inv_m = layer_norm(x1)
    b = (normed_m * gains[1:2] * (1.0 + scale_m) + shift_m).astype(BF)
    pre = matmul(b, w_up)
    act = gelu_tanh(pre).astype(BF)
    mlp = matmul_nt(act, w_down)
    x2 = x1 + gate_m * mlp
    normed_f, inv_f = layer_norm(x2)
    final = (normed_f * gains[2:3]).astype(BF)

    final_turned = jnp.swapaxes(final.reshape(score_count, nz, nx, -1), 1, 2).reshape(score_count, D)
    head_all = lax.all_gather(head_part, ("y", "x"), axis=0, tiled=True).reshape(ny, D, SEGMENT)
    rows = lax.all_gather(final_turned, ("z", "c"), axis=0, tiled=True)
    group = rows.shape[0]
    row_targets = pick(jnp.moveaxis(jnp.moveaxis(all_targets, 3, 1), (2, 3), (0, 1)).reshape(
        nx * ny, group), ix * ny + iy)
    row_times = pick(jnp.moveaxis(jnp.moveaxis(all_times.reshape(nz, nx, ny, nc), 3, 1), (2, 3), (0, 1))
                     .reshape(nx * ny, nz * nc), ix * ny + iy)
    row_weights = jnp.repeat(TSTEPS / (row_times.astype(F32) + 1.0) / total_rows, score_count)
    owner, within = row_targets // table_rows, row_targets % table_rows
    owned = jnp.logical_and(owner % nc == ic, within // SEGMENT == iz)
    column_of = jnp.where(owned, (owner // nc) * SEGMENT + within % SEGMENT, -1)[:, None]
    e, stats = head_logits(rows, head_all, column_of)
    top = stats[:, 0]
    every = share(("z", "c"), 4, stats.T.reshape(4, -1, LANES))[0].reshape(nz * nc, 4, group)
    best = jnp.max(every[:, 0], axis=0)
    log_total = best + jnp.log(jnp.sum(every[:, 1] * jnp.exp(every[:, 0] - best), axis=0))
    chosen = jnp.sum(every[:, 2], axis=0)
    own_start = (iz * nc + ic) * score_count
    own_terms = lax.dynamic_slice_in_dim(row_weights * (log_total - chosen), own_start, score_count)
    loss_part = jnp.sum(own_terms)
    factors = jnp.stack([row_weights * jnp.exp(top - log_total),
                         row_weights * (jnp.exp(chosen - log_total) - 1.0)], axis=1)
    d_logits, d_rows = head_rows_back(e, head_all, column_of, factors)
    d_final = lax.psum_scatter(d_rows.astype(BF), ("z", "c"), scatter_dimension=0, tiled=True)

    d_head = jnp.einsum("rd,yrv->ydv", rows, d_logits, preferred_element_type=F32)
    d_head = d_head.reshape(ny * nx, -1, SEGMENT)
    d_final, d_head = together(d_final, d_head)
    d_final = d_final.astype(F32)
    d_final = jnp.swapaxes(d_final.reshape(score_count, nx, nz, -1), 1, 2).reshape(score_count, D)
    block_for = lambda k: pick(d_head, lax.rem(k, ny) * nx + k // ny)
    head_sums = exchange(lambda k: block_for(k).astype(BF), ("x", "y"))
    head_own = block_for(head_sums[0][0])

    d_gain_f = jnp.sum(d_final * normed_f, axis=0)
    d_x2 = norm_back(d_final * gains[2:3], normed_f, inv_f)
    d_gate_m = jnp.sum(d_x2 * mlp, axis=0)
    d_out = (d_x2 * gate_m).astype(BF)
    d_down = matmul_tn(d_out, act)
    d_act = matmul(d_out, w_down)
    d_pre = jax.vjp(gelu_tanh, pre)[1](d_act)[0].astype(BF)
    d_up = matmul_tn(b, d_pre)
    d_b = matmul_nt(d_pre, w_up)
    d_shift_m = jnp.sum(d_b, axis=0)
    product = jnp.sum(d_b * normed_m, axis=0)
    d_scale_m = product * gains[1]
    d_gain_m = product * (1.0 + scale_m[0])
    d_x1 = d_x2 + norm_back(d_b * ((1.0 + scale_m) * gains[1:2]), normed_m, inv_m)
    d_gate_a = jnp.sum(d_x1 * branch, axis=0)
    d_branch = (d_x1 * gate_a).astype(BF)
    d_wout = matmul_tn(att, d_branch)
    d_att = matmul_nt(d_branch, w_o).astype(BF)
    d_k, d_v, d_qkv_m = attend_back(q, k_u, k_m, kv_u, qkv_m, tables, mask, lse_a, d_att)
    arrivals = [piece for _, piece in head_sums[1:]]
    d_k, *arrivals[:-1] = together(d_k, *arrivals[:-1])
    d_kv = jnp.concatenate([d_k, d_v], axis=1)
    d_wkv = matmul_tn(a_u, d_kv)
    d_row_m = d_qkv_m[:3].reshape(3 * D)
    d_a_u = matmul_nt(d_kv, w_qkv[:, D:])
    d_parts = matmul_nt(jnp.pad(jnp.stack(split3(d_row_m)), ((0, 13), (0, 0))), w_qkv)
    d_a_m = jnp.sum(d_parts[:3], axis=0, keepdims=True)
    d_shift_a = jnp.sum(d_a_u, axis=0) + d_a_m[0]
    product = jnp.sum(d_a_u * normed_u, axis=0) + (d_a_m * normed_0)[0]
    d_scale_a = product * gains[0]
    d_gain_a = product * (1.0 + scale_a[0])
    scaling = (1.0 + scale_a) * gains[0:1]
    d_x0_u = norm_back(d_a_u * scaling, normed_u, inv_u)
    d_mask = jnp.sum(d_x1, axis=0) + norm_back(d_a_m * scaling, normed_0, inv_0)[0]

    d_block = jnp.concatenate(
        [d_wkv.astype(BF), d_wout.astype(BF), d_up.astype(BF), d_down.astype(BF)], axis=1)
    width = d_block.shape[1]
    d_block = jnp.transpose(d_block.reshape(nz, nx, ny, nc, -1, width), (3, 1, 2, 0, 4, 5))
    d_block = d_block.reshape(nc, -1, width)
    got = exchange(lambda k: pick(d_block, k), ("c",))
    chip_sum = sum(piece.astype(F32) for _, piece in got).astype(BF)
    plane_sum = lax.psum_scatter(chip_sum, ("x", "y"), scatter_dimension=0, tiled=True)

    sent, chip_sum, *head_pieces = together(
        d_x0_u.astype(BF).T.reshape(nz * nx, table_width, free_count), chip_sum, *arrivals)
    g_part = head_own
    for piece in head_pieces:
        g_part = g_part + piece.astype(F32)
    g_part = g_part.reshape(nz, -1, SEGMENT)
    sent, g_part = together(sent, g_part)
    head_got = exchange(lambda k: pick(g_part, k), ("z",))

    arrived = spread_blocks(sizes, sent, 5).reshape(n, table_width, free_count)
    g_embed = scatter_rows(arrived, local_ids, low, high, table_rows)

    small = jnp.concatenate([d_shift_a, d_scale_a, d_gate_a, d_shift_m, d_scale_m, d_gate_m,
                             d_gain_a, d_gain_m, d_gain_f, d_mask,
                             a_m[0].astype(F32), d_row_m, jnp.broadcast_to(loss_part, (LANES,))])
    small = small.reshape(-1, LANES)
    count_small = small.shape[0]
    small = jnp.pad(small, ((0, -count_small % 8), (0, 0)))
    small_all = share(ALL, 1, small)[0].reshape((n,) + small.shape)
    small_all = small_all[:, :count_small].reshape(n, -1)
    d_mod_all = small_all[:, : 6 * D]
    d_gains = jnp.sum(small_all[:, 6 * D : 10 * D], axis=0).reshape(4, D)
    g_gains = lax.dynamic_slice_in_dim(d_gains, me * gains_w.shape[1], gains_w.shape[1], 1)
    total_loss = jnp.sum(small_all[:, 14 * D])
    condition_all = time_features(all_times, C, TSTEPS).astype(BF).astype(F32)
    condition_rows = lax.dynamic_slice_in_dim(condition_all, me * ada_w.shape[0], ada_w.shape[0], 1)
    exact = lambda a, b: jnp.einsum("nr,nc->rc", a, b, precision=lax.Precision.HIGHEST)
    g_ada = exact(condition_rows, d_mod_all)
    a_rows = lax.dynamic_slice_in_dim(small_all[:, 10 * D : 11 * D], me * layer_w.shape[0],
                                      layer_w.shape[0], 1)
    g_outer = exact(a_rows, small_all[:, 11 * D : 14 * D])

    plane_sum = plane_sum.reshape(nz, -1, width)
    g_rest = sum(p.astype(F32) for _, p in exchange(lambda k: pick(plane_sum, k), ("z",)))
    g_layer = jnp.concatenate(
        [g_outer[:, :D], g_outer[:, D:] + g_rest[:, : 2 * D], g_rest[:, 2 * D :]], axis=1)

    segments = []
    for k in range(nz):
        segment = head_got[0][1]
        for sender, piece in head_got[1:]:
            segment = jnp.where(sender == k, piece, segment)
        segments.append(segment)
    g_head = jnp.concatenate(segments, axis=1)

    squares = sum(jnp.sum(g * g) for g in (g_layer, g_ada, g_gains, g_embed, g_head))
    squares_all = share(ALL, 2, jnp.broadcast_to(squares, (8, LANES)))[0]
    grad_norm = jnp.sqrt(jnp.sum(squares_all[..., 0, 0]))
    factor = jnp.minimum(1.0, CLIP_NORM / grad_norm)
    step_value = step_count[0].astype(F32)
    updates = (
        (layer_w, layer_m, layer_v, layer_ema, g_layer),
        (ada_w, ada_m, ada_v, ada_ema, g_ada),
        (gains_w, gains_m, gains_v, gains_ema, g_gains),
        (embed_w.T, embed_m.T, embed_v.T, embed_ema.T, g_embed),
        (head_w, head_m, head_v, head_ema, g_head),
    )
    results = []
    for (w, m, v, ema, g), rate, decay in zip(updates, LEARN_RATES, WEIGHT_DECAYS):
        results.extend(adam_step(w, m, v, ema, g * factor, step_value, rate, decay))
    results[12:16] = [a.T for a in results[12:16]]
    return (total_loss, grad_norm, *results)


def solution(mesh):
    dp, vocab = mesh.shape["dp"], mesh.shape["vocab"]
    nz, nc = V // vocab // SEGMENT, 2
    sizes = (nz, dp // nz, vocab // nc, nc)
    fine = Mesh(mesh.devices.reshape(sizes), ALL)
    rows_all, columns_all = P(ALL, None), P(None, ALL)
    table, head = P(("y", "c"), ("z", "x")), P(("z", "x"), ("y", "c"))
    weights = [rows_all] * 8 + [columns_all] * 4 + [table] * 4 + [head] * 4
    return jax.shard_map(
        functools.partial(local, sizes),
        mesh=fine,
        in_specs=(rows_all, rows_all, P(ALL), P(ALL), P(), *weights),
        out_specs=(P(), P(), *weights),
        check_vma=False,
    )
```

```python
import functools
import math

import jax
import jax.numpy as jnp
from jax import lax
from jax.experimental import pallas as pl
from jax.experimental.pallas import tpu as pltpu
from jax.sharding import Mesh, PartitionSpec as P

D = 768
H = 12
HD = 64
FF = 3072
V = 51200
C = 128
TSTEPS = 20
SEGMENT = 3200
LANES = 128
ROWS = 64

NORM_EPS = 1e-05
CLIP_NORM = 0.05
BETA_ONE = 0.9
BETA_TWO = 0.95
ADAM_EPS = 1e-08
EMA_DECAY = 0.9999
LEARN_RATES = (0.03, 0.1, 0.1, 0.5, 0.05)
WEIGHT_DECAYS = (0.01, 0.01, 0.0, 0.01, 0.01)

ALL = ("z", "x", "y", "c")
BF = jnp.bfloat16
F32 = jnp.float32
MESH = pl.DeviceIdType.MESH
VMEM_LIMIT = 60 * 1024 * 1024


def dot(a, b, contract):
    return lax.dot_general(a, b, ((contract[0], contract[1]), ((), ())), preferred_element_type=F32)


def matmul(a, b):
    return dot(a, b, ((1,), (0,)))


def matmul_nt(a, b):
    return dot(a, b, ((1,), (1,)))


def matmul_tn(a, b):
    return dot(a, b, ((0,), (0,)))


def neighbours(axes, sizes):
    found = []
    for place, (axis, size) in enumerate(zip(axes, sizes)):
        for step in range(1, size):
            found.append((place, step, {axis: lax.rem(lax.axis_index(axis) + step, size)}))
    return found


def meet(devices):
    barrier = pltpu.get_barrier_semaphore()
    for device in devices:
        pl.semaphore_signal(barrier, inc=1, device_id=device, device_id_type=MESH)
    pl.semaphore_wait(barrier, len(devices))


def share_kernel(axes, sizes, count, *refs):
    ins, outs = refs[:count], refs[count : 2 * count]
    send, recv, near = refs[2 * count :]
    index = tuple(lax.axis_index(a) for a in axes)
    peers = neighbours(axes, sizes)
    meet([device for _, _, device in peers])
    for i in range(count):
        pltpu.make_async_copy(ins[i], outs[i].at[index], near.at[i]).start()
    for i in range(count):
        pltpu.make_async_copy(ins[i], outs[i].at[index], near.at[i]).wait()
    for place in range(len(axes)):
        view = (slice(None),) * place + index[place:]
        copies = []
        for number, (at, _, device) in enumerate(peers):
            if at == place:
                for i in range(count):
                    copies.append(
                        pltpu.make_async_remote_copy(
                            src_ref=outs[i].at[view],
                            dst_ref=outs[i].at[view],
                            send_sem=send.at[i, number],
                            recv_sem=recv.at[i, number],
                            device_id=device,
                            device_id_type=MESH,
                        )
                    )
        for copy in copies:
            copy.start()
        for copy in copies:
            copy.wait()


def share(axes, collective_id, *arrays):
    sizes = tuple(lax.axis_size(a) for a in axes)
    count, peers = len(arrays), sum(sizes) - len(sizes)
    return pl.pallas_call(
        functools.partial(share_kernel, axes, sizes, count),
        out_shape=[jax.ShapeDtypeStruct(sizes + a.shape, a.dtype) for a in arrays],
        in_specs=[pl.BlockSpec(memory_space=pltpu.VMEM)] * count,
        out_specs=[pl.BlockSpec(memory_space=pltpu.VMEM)] * count,
        scratch_shapes=[
            pltpu.SemaphoreType.DMA((count, peers)),
            pltpu.SemaphoreType.DMA((count, peers)),
            pltpu.SemaphoreType.DMA((count,)),
        ],
        compiler_params=pltpu.CompilerParams(
            collective_id=collective_id, has_side_effects=True
        ),
        name=f"share{collective_id}",
    )(*arrays)


def remote(src, dst, send, recv, device):
    return pltpu.make_async_remote_copy(
        src_ref=src, dst_ref=dst, send_sem=send, recv_sem=recv, device_id=device,
        device_id_type=MESH,
    )


def run_all(copies):
    for copy in copies:
        copy.start()
    for copy in copies:
        copy.wait()


def block_peer(sizes, step):
    nz, nx = sizes[:2]
    me = lax.axis_index("z") * nx + lax.axis_index("x")
    peer = lax.rem(me + step, nz * nx)
    return me, peer, {"z": peer // nx, "x": lax.rem(peer, nx)}


def fetch_kernel(sizes, in_ref, out_ref, from_c, from_y, half, total, sems_c, sems_y, sems_b):
    nz, nx, ny, nc = sizes
    blocks = nz * nx
    iy, ic = lax.axis_index("y"), lax.axis_index("c")
    along_y = [d for _, _, d in neighbours(("y",), (ny,))]
    along_c = [d for _, _, d in neighbours(("c",), (nc,))]
    along_b = [block_peer(sizes, step)[2] for step in range(1, blocks)]
    meet(along_c + along_y + along_b)
    run_all([
        remote(in_ref.at[:, d["c"]], from_c.at[i], sems_c.at[0, i], sems_c.at[1, i], d)
        for i, d in enumerate(along_c)
    ])

    @pl.loop(0, ny)
    def _(y):
        @pl.loop(0, blocks)
        def _(k):
            value = in_ref[y, ic, k]
            for i in range(nc - 1):
                value = value + from_c[i, y, k]
            half[y, k] = value

    run_all([
        remote(half.at[d["y"]], from_y.at[i], sems_y.at[0, i], sems_y.at[1, i], d)
        for i, d in enumerate(along_y)
    ])

    @pl.loop(0, blocks)
    def _(k):
        value = half[iy, k]
        for i in range(ny - 1):
            value = value + from_y[i, k]
        total[k] = value

    me = block_peer(sizes, 0)[0]
    copies = []
    for step in range(1, blocks):
        _, peer, device = block_peer(sizes, step)
        copies.append(
            remote(total.at[peer], out_ref.at[me], sems_b.at[0, step], sems_b.at[1, step], device)
        )
    for copy in copies:
        copy.start()
    out_ref[me] = total[me]
    for copy in copies:
        copy.wait()


def fetch_blocks(sizes, looked_up, collective_id):
    nz, nx, ny, nc = sizes
    block = looked_up.shape[3:]
    blocks = nz * nx
    return pl.pallas_call(
        functools.partial(fetch_kernel, sizes),
        out_shape=jax.ShapeDtypeStruct((blocks,) + block, BF),
        in_specs=[pl.BlockSpec(memory_space=pltpu.VMEM)],
        out_specs=pl.BlockSpec(memory_space=pltpu.VMEM),
        scratch_shapes=[
            pltpu.VMEM((nc - 1, ny, blocks) + block, BF),
            pltpu.VMEM((ny - 1, blocks) + block, BF),
            pltpu.VMEM((ny, blocks) + block, BF),
            pltpu.VMEM((blocks,) + block, BF),
            pltpu.SemaphoreType.DMA((2, nc - 1)),
            pltpu.SemaphoreType.DMA((2, ny - 1)),
            pltpu.SemaphoreType.DMA((2, blocks)),
        ],
        compiler_params=pltpu.CompilerParams(
            collective_id=collective_id, has_side_effects=True, vmem_limit_bytes=VMEM_LIMIT
        ),
        cost_estimate=pl.CostEstimate(flops=0, bytes_accessed=1 << 27, transcendentals=0),
        name="fetch_blocks",
    )(looked_up)


def spread_kernel(sizes, in_ref, out_ref, sems_c, sems_y, sems_b):
    nz, nx, ny, nc = sizes
    blocks = nz * nx
    iy, ic = lax.axis_index("y"), lax.axis_index("c")
    along_y = [d for _, _, d in neighbours(("y",), (ny,))]
    along_c = [d for _, _, d in neighbours(("c",), (nc,))]
    along_b = [block_peer(sizes, step)[2] for step in range(1, blocks)]
    meet(along_c + along_y + along_b)
    me = block_peer(sizes, 0)[0]
    copies = []
    for step in range(1, blocks):
        _, peer, device = block_peer(sizes, step)
        copies.append(
            remote(in_ref.at[peer], out_ref.at[iy, ic, me], sems_b.at[0, step],
                   sems_b.at[1, step], device)
        )
    for copy in copies:
        copy.start()
    out_ref[iy, ic, me] = in_ref[me]
    for copy in copies:
        copy.wait()
    run_all([
        remote(out_ref.at[iy, ic], out_ref.at[iy, ic], sems_y.at[0, i], sems_y.at[1, i], d)
        for i, d in enumerate(along_y)
    ])
    run_all([
        remote(out_ref.at[:, ic], out_ref.at[:, ic], sems_c.at[0, i], sems_c.at[1, i], d)
        for i, d in enumerate(along_c)
    ])


def spread_blocks(sizes, parts, collective_id):
    nz, nx, ny, nc = sizes
    return pl.pallas_call(
        functools.partial(spread_kernel, sizes),
        out_shape=jax.ShapeDtypeStruct((ny, nc) + parts.shape, parts.dtype),
        in_specs=[pl.BlockSpec(memory_space=pltpu.VMEM)],
        out_specs=pl.BlockSpec(memory_space=pltpu.VMEM),
        scratch_shapes=[
            pltpu.SemaphoreType.DMA((2, nc - 1)),
            pltpu.SemaphoreType.DMA((2, ny - 1)),
            pltpu.SemaphoreType.DMA((2, nz * nx)),
        ],
        compiler_params=pltpu.CompilerParams(
            collective_id=collective_id, has_side_effects=True, vmem_limit_bytes=VMEM_LIMIT
        ),
        cost_estimate=pl.CostEstimate(flops=0, bytes_accessed=1 << 27, transcendentals=0),
        name="spread_blocks",
    )(parts)


def axis_place(axes):
    index, size = 0, 1
    for axis in axes:
        index = index * lax.axis_size(axis) + lax.axis_index(axis)
        size = size * lax.axis_size(axis)
    return index, size


def exchange(piece_for, axes):
    me, n = axis_place(axes)
    got = [(me, piece_for(me))]
    for step in range(1, n):
        piece = piece_for(lax.rem(me + step, n))
        moved = lax.ppermute(piece, axes, [(i, (i + step) % n) for i in range(n)])
        got.append((lax.rem(me + n - step, n), moved))
    return got


def in_order(got):
    out = jnp.zeros((len(got),) + got[0][1].shape, got[0][1].dtype)
    for sender, piece in got:
        out = lax.dynamic_update_index_in_dim(out, piece, sender, 0)
    return out


def together(*values):
    return lax.optimization_barrier(values)


def pick(values, index, dim=0):
    return lax.dynamic_index_in_dim(values, index, dim, keepdims=False)


def spread_parts(values, dim, axis):
    got = exchange(lambda k: pick(values, k, dim).astype(jnp.float16), (axis,))
    return pick(values, got[0][0], dim), [piece for _, piece in got[1:]]


def added(own, pieces):
    for piece in pieces:
        own = own + piece.astype(F32)
    return own


def gather_kernel(low_ref, high_ref, ids_ref, table_ref, out_ref, turned_ref, rows_ref):
    source = pl.program_id(0)

    @pl.when(source == 0)
    def _():
        @pl.loop(0, table_ref.shape[1] // LANES)
        def _(k):
            at = pl.multiple_of(k * LANES, LANES)
            turned_ref[pl.ds(at, LANES), :] = table_ref[:, pl.ds(at, LANES)].T

    low, high = low_ref[source], high_ref[source]
    rows_ref[...] = jnp.zeros_like(rows_ref)

    def chunk(k, carry):
        base = pl.multiple_of(k * 8, 8)
        rows = []
        for i in range(8):
            place = base + i
            valid = jnp.logical_and(place >= low, place < high)
            row = jnp.where(valid, ids_ref[source, place], 0)
            value = turned_ref[pl.ds(row, 1), :]
            rows.append(jnp.where(valid, value, 0.0))
        rows_ref[pl.ds(base, 8), :] = jnp.concatenate(rows, axis=0)
        return carry

    lax.fori_loop(low // 8, (high + 7) // 8, chunk, 0)
    out_ref[0] = rows_ref[...].T.astype(BF)


def gather_rows(table, ids, low, high):
    sources, count = ids.shape
    width = table.shape[0]
    return pl.pallas_call(
        gather_kernel,
        out_shape=jax.ShapeDtypeStruct((sources, width, count), BF),
        grid_spec=pltpu.PrefetchScalarGridSpec(
            num_scalar_prefetch=3,
            grid=(sources,),
            in_specs=[
                pl.BlockSpec(table.shape, lambda i, *_: (0, 0), pipeline_mode=pl.Buffered(1))
            ],
            out_specs=pl.BlockSpec((1, width, count), lambda i, *_: (i, 0, 0)),
            scratch_shapes=[
                pltpu.VMEM((table.shape[1], width), F32),
                pltpu.VMEM((count, width), F32),
            ],
        ),
        compiler_params=pltpu.CompilerParams(vmem_limit_bytes=VMEM_LIMIT),
        cost_estimate=pl.CostEstimate(flops=0, bytes_accessed=1 << 27, transcendentals=0),
        name="gather_rows",
    )(low, high, ids, table)


def scatter_kernel(low_ref, high_ref, ids_ref, rows_ref, out_ref, total_ref, wide_ref):
    source = pl.program_id(0)

    @pl.when(source == 0)
    def _():
        total_ref[...] = jnp.zeros_like(total_ref)

    low, high = low_ref[source], high_ref[source]
    wide_ref[...] = rows_ref[0].astype(F32).T

    def chunk(k, carry):
        base = pl.multiple_of(k * 8, 8)
        block = wide_ref[pl.ds(base, 8), :]
        for i in range(8):
            place = base + i
            valid = jnp.logical_and(place >= low, place < high)
            row = jnp.where(valid, ids_ref[source, place], 0)
            addend = jnp.where(valid, block[i : i + 1, :], 0.0)
            total_ref[pl.ds(row, 1), :] = total_ref[pl.ds(row, 1), :] + addend
        return carry

    lax.fori_loop(low // 8, (high + 7) // 8, chunk, 0)

    @pl.when(source == pl.num_programs(0) - 1)
    def _():
        @pl.loop(0, out_ref.shape[1] // LANES)
        def _(k):
            at = pl.multiple_of(k * LANES, LANES)
            out_ref[:, pl.ds(at, LANES)] = total_ref[pl.ds(at, LANES), :].T


def scatter_rows(rows, ids, low, high, table_rows):
    sources, width, count = rows.shape
    return pl.pallas_call(
        scatter_kernel,
        out_shape=jax.ShapeDtypeStruct((width, table_rows), F32),
        grid_spec=pltpu.PrefetchScalarGridSpec(
            num_scalar_prefetch=3,
            grid=(sources,),
            in_specs=[pl.BlockSpec((1, width, count), lambda i, *_: (i, 0, 0))],
            out_specs=pl.BlockSpec((width, table_rows), lambda i, *_: (0, 0)),
            scratch_shapes=[
                pltpu.VMEM((table_rows, width), F32),
                pltpu.VMEM((count, width), F32),
            ],
        ),
        compiler_params=pltpu.CompilerParams(vmem_limit_bytes=VMEM_LIMIT),
        cost_estimate=pl.CostEstimate(flops=0, bytes_accessed=1 << 27, transcendentals=0),
        name="scatter_rows",
    )(low, high, ids, rows)


def swap_halves(values):
    lane = lax.broadcasted_iota(jnp.int32, values.shape, 1)
    half = HD // 2
    up = pltpu.roll(values, LANES - half, 1)
    down = pltpu.roll(values, half, 1)
    return jnp.where(lax.rem(lane, HD) < half, up, down)


def turn(values, cosine, sine):
    return values * cosine + swap_halves(values) * sine


def turn_back(values, cosine, sine):
    return values * cosine - swap_halves(values) * sine


def attend_kernel(kv_ref, vv_ref, qm_ref, km_ref, vm_ref, cu_ref, su_ref, cm_ref, sm_ref,
                  mask_ref, q_out, ku_out, km_out, att_out, lse_out):
    rows = cm_ref.shape[0]
    wide = (rows, LANES)
    cm, sm = cm_ref[...], sm_ref[...]
    q = turn(jnp.broadcast_to(qm_ref[0:1, :], wide), cm, sm).astype(BF)
    k_m = turn(jnp.broadcast_to(km_ref[0:1, :], wide), cm, sm).astype(BF)
    k_u = turn(kv_ref[...], cu_ref[...], su_ref[...]).astype(BF)
    v_u = vv_ref[...].astype(BF)
    v_m = vm_ref[0:1, :].astype(BF).astype(F32)
    q_out[...] = q
    ku_out[...] = k_u
    km_out[...] = k_m
    mask = mask_ref[0:1, :]
    outs, totals = [], []
    for head in range(LANES // HD):
        part = slice(head * HD, (head + 1) * HD)
        s_u = matmul_nt(q[:, part], k_u[:, part]) * HD ** (-0.5) + mask
        s_m = matmul_nt(q[:, part], k_m[:, part]) * HD ** (-0.5)
        top = jnp.maximum(
            jnp.max(s_u, axis=1, keepdims=True), jnp.max(s_m, axis=1, keepdims=True)
        )
        e_u = jnp.exp(s_u - top)
        e_m = jnp.exp(s_m - top)
        total = jnp.sum(e_u, axis=1, keepdims=True) + jnp.sum(e_m, axis=1, keepdims=True)
        inverse = 1.0 / total
        p_u = (e_u * inverse).astype(BF)
        p_m = (e_m * inverse).astype(BF).astype(F32)
        mixed = matmul(p_u, v_u[:, part]) + jnp.sum(p_m, axis=1, keepdims=True) * v_m[:, part]
        outs.append(mixed)
        totals.append(top + jnp.log(total))
    att_out[...] = jnp.concatenate(outs, axis=1).astype(BF)
    lse_out[0] = jnp.concatenate(totals, axis=1)


def attend(kv_u, qkv_m, tables, mask):
    count, rows = kv_u.shape[0], tables[2].shape[0]
    blocks = D // LANES
    per = LANES // HD
    row = lambda offset: pl.BlockSpec((qkv_m.shape[0], LANES), lambda i: (0, offset * blocks + i))
    column = lambda n: pl.BlockSpec((n, LANES), lambda i: (0, i))
    whole = lambda a: pl.BlockSpec(a.shape, lambda i: (0, 0))
    return pl.pallas_call(
        attend_kernel,
        grid=(blocks,),
        out_shape=[
            jax.ShapeDtypeStruct((rows, D), BF),
            jax.ShapeDtypeStruct((count, D), BF),
            jax.ShapeDtypeStruct((rows, D), BF),
            jax.ShapeDtypeStruct((rows, D), BF),
            jax.ShapeDtypeStruct((blocks, rows, per), F32),
        ],
        in_specs=[
            pl.BlockSpec((count, LANES), lambda i: (0, i)),
            pl.BlockSpec((count, LANES), lambda i: (0, blocks + i)),
            row(0), row(1), row(2),
            *[whole(t) for t in tables],
            whole(mask),
        ],
        out_specs=[column(rows), column(count), column(rows), column(rows),
                   pl.BlockSpec((1, rows, per), lambda i: (i, 0, 0))],
        compiler_params=pltpu.CompilerParams(vmem_limit_bytes=VMEM_LIMIT),
        cost_estimate=pl.CostEstimate(
            flops=2 * 3 * rows * count * D, bytes_accessed=12 * rows * D,
            transcendentals=2 * rows * count * H,
        ),
        name="attend",
    )(kv_u, kv_u, qkv_m, qkv_m, qkv_m, *tables, mask)


def attend_back_kernel(q_ref, ku_ref, km_ref, vv_ref, vm_ref, cu_ref, su_ref, cm_ref, sm_ref,
                       mask_ref, lse_ref, datt_ref, dk_out, dv_out, dm_out):
    q, k_u, k_m, datt = q_ref[...], ku_ref[...], km_ref[...], datt_ref[...]
    v_u = vv_ref[...].astype(BF)
    v_m = vm_ref[0:1, :].astype(BF).astype(F32)
    datt_f = datt.astype(F32)
    mask = mask_ref[0:1, :]
    scale = HD ** (-0.5)
    dq, dk_u, dk_m, dv_u, dv_m = [], [], [], [], []
    for head in range(LANES // HD):
        part = slice(head * HD, (head + 1) * HD)
        lse = lse_ref[0, :, head : head + 1]
        p_u = jnp.exp(matmul_nt(q[:, part], k_u[:, part]) * scale + mask - lse)
        p_m = jnp.exp(matmul_nt(q[:, part], k_m[:, part]) * scale - lse)
        dp_u = matmul_nt(datt[:, part], v_u[:, part])
        dp_m = jnp.sum(datt_f[:, part] * v_m[:, part], axis=1, keepdims=True)
        inner = jnp.sum(p_u * dp_u, axis=1, keepdims=True) + dp_m * jnp.sum(
            p_m, axis=1, keepdims=True
        )
        ds_u = (p_u * (dp_u - inner) * scale).astype(BF)
        ds_m = (p_m * ((dp_m - inner) * scale)).astype(BF)
        dq.append(matmul(ds_u, k_u[:, part]) + matmul(ds_m, k_m[:, part]))
        dk_u.append(matmul_tn(ds_u, q[:, part]))
        dk_m.append(matmul_tn(ds_m, q[:, part]))
        dv_u.append(matmul_tn(p_u.astype(BF), datt[:, part]))
        mass = jnp.sum(p_m.astype(BF).astype(F32), axis=1, keepdims=True)
        dv_m.append(jnp.sum(mass * datt_f[:, part], axis=0, keepdims=True))
    cm, sm = cm_ref[...], sm_ref[...]
    join = lambda parts: jnp.concatenate(parts, axis=1)
    low = lambda a: a.astype(BF).astype(F32)
    dk_out[...] = turn_back(join(dk_u), cu_ref[...], su_ref[...]).astype(BF)
    dv_out[...] = join(dv_u).astype(BF)
    dq_sum = jnp.sum(low(turn_back(join(dq), cm, sm)), axis=0, keepdims=True)
    dk_sum = jnp.sum(low(turn_back(join(dk_m), cm, sm)), axis=0, keepdims=True)
    filler = jnp.zeros((5, LANES), F32)
    dm_out[...] = jnp.concatenate([dq_sum, dk_sum, join(dv_m), filler], axis=0)


def attend_back(q, k_u, k_m, kv_u, qkv_m, tables, mask, lse, datt):
    count, rows = kv_u.shape[0], q.shape[0]
    blocks = D // LANES
    per = LANES // HD
    column = lambda n: pl.BlockSpec((n, LANES), lambda i: (0, i))
    whole = lambda a: pl.BlockSpec(a.shape, lambda i: (0, 0))
    return pl.pallas_call(
        attend_back_kernel,
        grid=(blocks,),
        out_shape=[
            jax.ShapeDtypeStruct((count, D), BF),
            jax.ShapeDtypeStruct((count, D), BF),
            jax.ShapeDtypeStruct((8, D), F32),
        ],
        in_specs=[
            column(rows), column(count), column(rows),
            pl.BlockSpec((count, LANES), lambda i: (0, blocks + i)),
            pl.BlockSpec((qkv_m.shape[0], LANES), lambda i: (0, 2 * blocks + i)),
            *[whole(t) for t in tables],
            whole(mask),
            pl.BlockSpec((1, rows, per), lambda i: (i, 0, 0)),
            column(rows),
        ],
        out_specs=[column(count), column(count), column(8)],
        compiler_params=pltpu.CompilerParams(vmem_limit_bytes=VMEM_LIMIT),
        cost_estimate=pl.CostEstimate(
            flops=2 * 8 * rows * count * D, bytes_accessed=14 * rows * D,
            transcendentals=2 * rows * count * H,
        ),
        name="attend_back",
    )(q, k_u, k_m, kv_u, qkv_m, *tables, mask, lse, datt)


def tile_of(segments):
    return max(16, 1024 // segments)


def chunk_of(width):
    return next(n for n in (640, 400, 128, width) if width % n == 0)


def logits_kernel(places_ref, x_ref, w_ref, target_ref, *refs):
    e_ref, stats_ref, logits_ref = refs[-3:]
    segments, _, width = w_ref.shape
    chunk = chunk_of(width)
    rows = x_ref.shape[0]
    x = x_ref[...]
    spots = [(y, at) for y in range(segments) for at in range(0, width, chunk)]
    best = None
    for place, (y, at) in enumerate(spots):
        logits = matmul(x, w_ref[y, :, at : at + chunk])
        logits_ref[:, place * chunk : (place + 1) * chunk] = logits
        best = logits if best is None else jnp.maximum(best, logits)
    top = jnp.max(best, axis=1, keepdims=True)
    lane = lax.broadcasted_iota(jnp.int32, (rows, chunk), 1)
    total = jnp.zeros((rows, chunk), F32)
    chosen = jnp.zeros((rows, chunk), F32)
    target = target_ref[...]
    for place, (y, at) in enumerate(spots):
        logits = logits_ref[:, place * chunk : (place + 1) * chunk]
        e = jnp.exp(logits - top)
        total = total + e
        chosen = chosen + jnp.where(lane == target - place * chunk, logits, 0.0)
        e_ref[y, :, at : at + chunk] = e.astype(BF)
    stats_ref[...] = jnp.concatenate(
        [top, jnp.sum(total, axis=1, keepdims=True), jnp.sum(chosen, axis=1, keepdims=True), top],
        axis=1,
    )


def head_logits(rows, weights, targets, places, block, so_far):
    count, group = rows.shape[0], targets.shape[0]
    segments, _, width = weights.shape
    tile = tile_of(segments)
    per = group // places.shape[0] // tile
    first = block * (count // tile)

    def place(i, places):
        return places[(first + i) // per] * per + lax.rem(first + i, per)

    return pl.pallas_call(
        logits_kernel,
        out_shape=[
            jax.ShapeDtypeStruct((segments, group, width), BF),
            jax.ShapeDtypeStruct((group, 4), F32),
        ],
        grid_spec=pltpu.PrefetchScalarGridSpec(
            num_scalar_prefetch=1,
            grid=(count // tile,),
            in_specs=[
                pl.BlockSpec((tile, D), lambda i, p: (i, 0)),
                pl.BlockSpec(weights.shape, lambda i, p: (0, 0, 0), pipeline_mode=pl.Buffered(1)),
                pl.BlockSpec((tile, 1), lambda i, p: (place(i, p), 0)),
            ] + [pl.BlockSpec(memory_space=pl.ANY)] * len(so_far),
            out_specs=[
                pl.BlockSpec((segments, tile, width), lambda i, p: (0, first + i, 0)),
                pl.BlockSpec((tile, 4), lambda i, p: (place(i, p), 0)),
            ],
            scratch_shapes=[pltpu.VMEM((tile, segments * width), F32)],
        ),
        input_output_aliases={4 + i: i for i in range(len(so_far))},
        compiler_params=pltpu.CompilerParams(vmem_limit_bytes=VMEM_LIMIT),
        cost_estimate=pl.CostEstimate(
            flops=2 * count * D * segments * width,
            bytes_accessed=2 * count * segments * width,
            transcendentals=count * segments * width,
        ),
        name="head_logits",
    )(places, rows, weights, targets, *so_far)


def rows_back_kernel(places_ref, e_ref, w_ref, target_ref, factor_ref, d_ref, dx_ref):
    segments, _, width = w_ref.shape
    rows = e_ref.shape[1]
    lane = lax.broadcasted_iota(jnp.int32, (ROWS, LANES), 1)
    wide = lambda a: jnp.broadcast_to(a, (ROWS, LANES))
    total = None
    for y in range(segments):
        for r in range(0, rows, ROWS):
            place = target_ref[r : r + ROWS, :] - (lane + y * width)
            factor = wide(factor_ref[r : r + ROWS, 0:1])
            special = wide(factor_ref[r : r + ROWS, 1:2])
            for at in range(0, width, LANES):
                e = e_ref[y, r : r + ROWS, at : at + LANES].astype(F32)
                d_ref[y, r : r + ROWS, at : at + LANES] = jnp.where(
                    place == at, special, e * factor).astype(BF)
        part = matmul_nt(d_ref[y], w_ref[y])
        total = part if total is None else total + part
    dx_ref[...] = total.astype(BF)


def head_rows_back(e, weights, targets, factors, places):
    segments, count, width = e.shape
    tile = tile_of(segments)
    per = count // places.shape[0] // tile

    def placed(i, places):
        return (places[i // per] * per + lax.rem(i, per), 0)

    return pl.pallas_call(
        rows_back_kernel,
        out_shape=[
            jax.ShapeDtypeStruct(e.shape, BF),
            jax.ShapeDtypeStruct((count, D), BF),
        ],
        grid_spec=pltpu.PrefetchScalarGridSpec(
            num_scalar_prefetch=1,
            grid=(count // tile,),
            in_specs=[
                pl.BlockSpec((segments, tile, width), lambda i, p: (0, i, 0)),
                pl.BlockSpec(weights.shape, lambda i, p: (0, 0, 0), pipeline_mode=pl.Buffered(1)),
                pl.BlockSpec((tile, 1), placed),
                pl.BlockSpec((tile, 2), placed),
            ],
            out_specs=[
                pl.BlockSpec((segments, tile, width), lambda i, p: (0, i, 0)),
                pl.BlockSpec((tile, D), placed),
            ],
        ),
        input_output_aliases={1: 0},
        compiler_params=pltpu.CompilerParams(vmem_limit_bytes=VMEM_LIMIT),
        cost_estimate=pl.CostEstimate(
            flops=2 * count * D * segments * width,
            bytes_accessed=4 * count * segments * width,
            transcendentals=0,
        ),
        name="head_rows_back",
    )(places, e, weights, targets, factors)


def layer_norm(values):
    center = values - jnp.mean(values, axis=-1, keepdims=True)
    spread = jnp.mean(center * center, axis=-1, keepdims=True)
    inv_std = lax.rsqrt(spread + NORM_EPS)
    return (center * inv_std, inv_std)


def norm_back(d_normed, normed, inv_std):
    return inv_std * (
        d_normed
        - jnp.mean(d_normed, axis=-1, keepdims=True)
        - normed * jnp.mean(d_normed * normed, axis=-1, keepdims=True)
    )


def time_features(time_index, width, steps):
    t_value = (time_index.astype(F32) + 1.0) / steps
    half_width = width // 2
    frequencies = jnp.exp(-math.log(10000.0) * jnp.arange(half_width, dtype=F32) / half_width)
    angles = 1000.0 * t_value[:, None] * frequencies[None, :]
    return jax.nn.silu(jnp.concatenate([jnp.cos(angles), jnp.sin(angles)], axis=1))


def rope_rows(positions):
    half = HD // 2
    inverse = jnp.exp(-math.log(10000.0) * jnp.arange(half, dtype=F32) * 2.0 / HD)
    angles = positions.astype(F32)[:, None] * inverse[None, :]
    cosine, sine = jnp.cos(angles), jnp.sin(angles)
    return (jnp.tile(cosine, (1, LANES // half)),
            jnp.tile(jnp.concatenate([-sine, sine], axis=1), (1, LANES // HD)))


def gelu_tanh(values):
    return jax.nn.gelu(values, approximate=True)


def adam_step(weight, first, second, ema_copy, gradient, step_value, learn_rate, decay_rate):
    first_new = BETA_ONE * first + (1.0 - BETA_ONE) * gradient
    second_new = BETA_TWO * second + (1.0 - BETA_TWO) * gradient * gradient
    first_hat = first_new / (1.0 - BETA_ONE**step_value)
    second_hat = second_new / (1.0 - BETA_TWO**step_value)
    weight_new = weight - learn_rate * (
        first_hat / (jnp.sqrt(second_hat) + ADAM_EPS) + decay_rate * weight
    )
    ema_rate = jnp.minimum(EMA_DECAY, (1.0 + step_value) / (10.0 + step_value))
    ema_new = ema_rate * ema_copy + (1.0 - ema_rate) * weight_new
    return (first_new, second_new, weight_new, ema_new)


def split3(row):
    parts, rest = [], row
    for _ in range(3):
        part = lax.reduce_precision(rest, 8, 7)
        parts.append(part.astype(BF))
        rest = rest - part
    return parts


def local(sizes, token_ids, scored, lengths, times, step_count, layer_w, layer_m, layer_v, layer_ema,
          ada_w, ada_m, ada_v, ada_ema, gains_w, gains_m, gains_v, gains_ema,
          embed_w, embed_m, embed_v, embed_ema, head_w, head_m, head_v, head_ema):
    nz, nx, ny, nc = sizes
    n = nz * nx * ny * nc
    length, score_count = token_ids.shape[1], scored.shape[1]
    free_count = length - score_count
    total_rows = n * score_count
    table_rows, table_width = embed_w.shape
    iz, ix, iy, ic = [lax.axis_index(a) for a in ALL]
    vocab_index = iy * nc + ic
    vocab_start = vocab_index * table_rows
    me = (iz * nx + ix) * (ny * nc) + vocab_index

    tokens, masked = token_ids[0], scored[0]
    positions = jnp.arange(length, dtype=jnp.int32)
    hits = masked[:, None] == positions[None, :]
    is_masked = jnp.any(hits, axis=0)
    targets = jnp.sum(jnp.where(hits, tokens[None, :], 0), axis=1)
    keys = jnp.where(is_masked, n * V, (tokens // table_rows) * length + positions)
    rank = jnp.sum((keys[None, :] < keys[:, None]).astype(jnp.int32), axis=1)
    rank = jnp.where(is_masked, length, rank)
    slots = rank[None, :] == jnp.arange(free_count, dtype=jnp.int32)[:, None]
    free_tokens = jnp.sum(jnp.where(slots, tokens[None, :], 0), axis=1)
    free_positions = jnp.sum(jnp.where(slots, positions[None, :], 0), axis=1)

    ints = jnp.concatenate([free_tokens.reshape(-1, LANES), targets.reshape(-1, LANES),
                            jnp.broadcast_to(times[:, None], (1, LANES))], axis=0)
    ints = jnp.pad(ints, ((0, -ints.shape[0] % 8), (0, 0)))
    gain_part = jnp.pad(gains_w.astype(BF).astype(F32),
                        ((0, 8 - gains_w.shape[0]), (0, LANES - gains_w.shape[1])))
    ints_all, gains_all = share(ALL, 0, ints, gain_part)
    ints_all = ints_all.reshape((n,) + ints.shape)
    gains_all = gains_all.reshape((n,) + gain_part.shape)

    block_low = jnp.concatenate(
        [layer_w.astype(BF), ada_w.astype(BF).reshape(layer_w.shape[0], -1)], axis=1)
    block_low, head_low, ints_all = together(block_low, head_w.astype(BF), ints_all)
    layer_all = lax.all_gather(block_low, ALL, axis=0, tiled=True)

    piece_for = lambda k: lax.dynamic_slice_in_dim(head_low, k * SEGMENT, SEGMENT, 1)
    head_parts = exchange(piece_for, ("z",))

    gains = jnp.moveaxis(gains_all[:, : gains_w.shape[0], : gains_w.shape[1]], 0, 1).reshape(4, D)
    free_rows = free_count // LANES
    score_rows = score_count // LANES
    all_tokens = ints_all[:, :free_rows].reshape(nz * nx, ny * nc, free_count)
    all_targets = ints_all[:, free_rows : free_rows + score_rows].reshape(
        nz, nx, ny, nc, score_count)
    all_times = ints_all[:, free_rows + score_rows, 0]

    wanted = jnp.swapaxes(all_tokens, 0, 1).reshape(n, free_count)
    owners = wanted // table_rows
    low = jnp.sum((owners < vocab_index).astype(jnp.int32), axis=1)
    high = jnp.sum((owners <= vocab_index).astype(jnp.int32), axis=1)
    local_ids = wanted - vocab_start
    looked_up = gather_rows(embed_w.T, local_ids, low, high)
    looked_up = looked_up.reshape((ny, nc, nz * nx) + looked_up.shape[1:])
    x0_u = fetch_blocks(sizes, looked_up, 3).reshape(D, free_count).T.astype(F32)
    senders = [sender for sender, _ in head_parts]
    x0_u, *pieces = together(x0_u, *[piece for _, piece in head_parts])
    head_part = in_order(list(zip(senders, pieces))).reshape(-1, SEGMENT)

    mask_row = gains[3:4]
    condition = time_features(times, C, TSTEPS).astype(BF)
    modulation = matmul(condition, layer_all[:, layer_w.shape[1] :].reshape(C, 6 * D))
    shift_a, scale_a, gate_a, shift_m, scale_m, gate_m = [
        modulation[:, i * D : (i + 1) * D] for i in range(6)]
    normed_u, inv_u = layer_norm(x0_u)
    a_u = (normed_u * gains[0:1] * (1.0 + scale_a) + shift_a).astype(BF)
    normed_0, inv_0 = layer_norm(mask_row)
    a_m = (normed_0 * gains[0:1] * (1.0 + scale_a) + shift_a).astype(BF)
    w_qkv, w_o = layer_all[:, : 3 * D], layer_all[:, 3 * D : 4 * D]
    w_up, w_down = layer_all[:, 4 * D : 4 * D + FF], layer_all[:, 4 * D + FF : 4 * D + 2 * FF]
    qkv_m = matmul(jnp.broadcast_to(a_m, (16, D)), w_qkv)
    kv_u = matmul(a_u, w_qkv[:, D:])
    tables = (*rope_rows(free_positions), *rope_rows(masked))
    mask = jnp.where(free_positions[None, :] < lengths[:, None], 0.0, -1e30)
    mask = jnp.broadcast_to(mask, (8, free_count)).astype(F32)
    q, k_u, k_m, att, lse_a = attend(kv_u, qkv_m, tables, mask)
    branch = matmul(att, w_o)
    x1 = mask_row + gate_a * branch
    normed_m, inv_m = layer_norm(x1)
    b = (normed_m * gains[1:2] * (1.0 + scale_m) + shift_m).astype(BF)
    pre = matmul(b, w_up)
    act = gelu_tanh(pre).astype(BF)
    mlp = matmul_nt(act, w_down)
    x2 = x1 + gate_m * mlp
    normed_f, inv_f = layer_norm(x2)
    final = (normed_f * gains[2:3]).astype(BF)

    final_turned = jnp.swapaxes(final.reshape(score_count, nz, nx, -1), 1, 2).reshape(score_count, D)
    head_all = lax.all_gather(head_part, ("y", "x"), axis=0, tiled=True).reshape(ny, D, SEGMENT)
    group = nz * nc * score_count
    blocks, places = [], []
    for sender, piece in exchange(lambda k: final_turned, ("z",)):
        for place, part in exchange(lambda k: piece, ("c",)):
            blocks.append(part)
            places.append(sender * nc + place)
    places = jnp.stack(places).astype(jnp.int32)
    row_targets = pick(jnp.moveaxis(jnp.moveaxis(all_targets, 3, 1), (2, 3), (0, 1)).reshape(
        nx * ny, group), ix * ny + iy)
    row_times = pick(jnp.moveaxis(jnp.moveaxis(all_times.reshape(nz, nx, ny, nc), 3, 1), (2, 3), (0, 1))
                     .reshape(nx * ny, nz * nc), ix * ny + iy)
    row_weights = jnp.repeat(TSTEPS / (row_times.astype(F32) + 1.0) / total_rows, score_count)
    owner, within = row_targets // table_rows, row_targets % table_rows
    owned = jnp.logical_and(owner % nc == ic, within // SEGMENT == iz)
    column_of = jnp.where(owned, (owner // nc) * SEGMENT + within % SEGMENT, -1)[:, None]
    so_far = ()
    for block in range(nz):
        part = jnp.concatenate(blocks[block * nc : (block + 1) * nc], axis=0)
        so_far = head_logits(part, head_all, column_of, places, block, so_far)
    e, stats = so_far
    rows = jnp.concatenate(blocks, axis=0)
    top = stats[:, 0]
    every = share(("z", "c"), 4, stats.T.reshape(4, -1, LANES))[0].reshape(nz * nc, 4, group)
    best = jnp.max(every[:, 0], axis=0)
    log_total = best + jnp.log(jnp.sum(every[:, 1] * jnp.exp(every[:, 0] - best), axis=0))
    chosen = jnp.sum(every[:, 2], axis=0)
    own_start = (iz * nc + ic) * score_count
    own_terms = lax.dynamic_slice_in_dim(row_weights * (log_total - chosen), own_start, score_count)
    loss_part = jnp.sum(own_terms)
    factors = jnp.stack([row_weights * jnp.exp(top - log_total),
                         row_weights * (jnp.exp(chosen - log_total) - 1.0)], axis=1)
    d_logits, d_rows = head_rows_back(e, head_all, column_of, factors, places)
    d_final = lax.psum_scatter(d_rows, ("z", "c"), scatter_dimension=0, tiled=True)

    bound = D**0.5 * jnp.max(jnp.abs(gains[2])) * 1.02
    bound = bound * score_count * jnp.sum(TSTEPS / (all_times.astype(F32) + 1.0) / total_rows)
    enlarge = 60000.0 / jnp.maximum(bound, 1e-30)
    d_head = jnp.einsum("rd,yrv->ydv", rows, d_logits, preferred_element_type=F32) * enlarge
    d_final, d_head = together(d_final, d_head.reshape(ny, nx, nz, -1, SEGMENT))
    cut = nz // 2
    own_x, from_x = spread_parts(d_head[:, :, :cut], 1, "x")
    own_y, from_y = spread_parts(d_head[:, :, cut:], 0, "y")
    d_final = d_final.astype(F32)
    d_final = jnp.swapaxes(d_final.reshape(score_count, nx, nz, -1), 1, 2).reshape(score_count, D)

    d_gain_f = jnp.sum(d_final * normed_f, axis=0)
    d_x2 = norm_back(d_final * gains[2:3], normed_f, inv_f)
    d_gate_m = jnp.sum(d_x2 * mlp, axis=0)
    d_out = (d_x2 * gate_m).astype(BF)
    d_down = matmul_tn(d_out, act)
    d_act = matmul(d_out, w_down)
    d_pre = jax.vjp(gelu_tanh, pre)[1](d_act)[0].astype(BF)
    d_up = matmul_tn(b, d_pre)
    d_b = matmul_nt(d_pre, w_up)
    d_shift_m = jnp.sum(d_b, axis=0)
    product = jnp.sum(d_b * normed_m, axis=0)
    d_scale_m = product * gains[1]
    d_gain_m = product * (1.0 + scale_m[0])
    d_x1 = d_x2 + norm_back(d_b * ((1.0 + scale_m) * gains[1:2]), normed_m, inv_m)
    d_gate_a = jnp.sum(d_x1 * branch, axis=0)
    d_branch = (d_x1 * gate_a).astype(BF)
    d_wout = matmul_tn(att, d_branch)
    d_att, *from_xy = together(matmul_nt(d_branch, w_o).astype(BF), *from_x, *from_y)
    own_xy, from_xy = (
        spread_parts(added(own_x, from_xy[: nx - 1]), 0, "y"),
        spread_parts(added(own_y, from_xy[nx - 1 :]), 0, "x"),
    )
    d_k, d_v, d_qkv_m = attend_back(q, k_u, k_m, kv_u, qkv_m, tables, mask, lse_a, d_att)
    d_k, *arrivals = together(d_k, *own_xy[1], *from_xy[1])
    d_kv = jnp.concatenate([d_k, d_v], axis=1)
    d_wkv = matmul_tn(a_u, d_kv)
    d_row_m = d_qkv_m[:3].reshape(3 * D)
    d_a_u = matmul_nt(d_kv, w_qkv[:, D:])
    d_parts = matmul_nt(jnp.pad(jnp.stack(split3(d_row_m)), ((0, 13), (0, 0))), w_qkv)
    d_a_m = jnp.sum(d_parts[:3], axis=0, keepdims=True)
    d_shift_a = jnp.sum(d_a_u, axis=0) + d_a_m[0]
    product = jnp.sum(d_a_u * normed_u, axis=0) + (d_a_m * normed_0)[0]
    d_scale_a = product * gains[0]
    d_gain_a = product * (1.0 + scale_a[0])
    scaling = (1.0 + scale_a) * gains[0:1]
    d_x0_u = norm_back(d_a_u * scaling, normed_u, inv_u)
    d_mask = jnp.sum(d_x1, axis=0) + norm_back(d_a_m * scaling, normed_0, inv_0)[0]

    d_block = jnp.concatenate(
        [d_wkv.astype(BF), d_wout.astype(BF), d_up.astype(BF), d_down.astype(BF)], axis=1)
    width = d_block.shape[1]
    d_block = jnp.transpose(d_block.reshape(nz, nx, ny, nc, -1, width), (3, 1, 2, 0, 4, 5))
    d_block = d_block.reshape(nc, -1, width)
    got = exchange(lambda k: pick(d_block, k), ("c",))
    chip_sum = sum(piece.astype(F32) for _, piece in got).astype(BF)
    plane_sum = lax.psum_scatter(chip_sum, ("x", "y"), scatter_dimension=0, tiled=True)

    sent, chip_sum = together(
        d_x0_u.astype(BF).T.reshape(nz * nx, table_width, free_count), chip_sum)
    head_sum = jnp.concatenate(
        [added(own_xy[0], arrivals[: ny - 1]), added(from_xy[0], arrivals[ny - 1 :])], axis=0)
    sent, head_sum = together(sent, head_sum)
    head_own, head_parts = spread_parts(head_sum, 0, "z")

    arrived = spread_blocks(sizes, sent, 5).reshape(n, table_width, free_count)
    arrived, plane_sum, *head_parts = together(arrived, plane_sum, *head_parts)
    plane_sum = plane_sum.reshape(nz, -1, width)
    block_got = exchange(lambda k: pick(plane_sum, k), ("z",))
    g_embed = scatter_rows(arrived, local_ids, low, high, table_rows)

    small = jnp.concatenate([d_shift_a, d_scale_a, d_gate_a, d_shift_m, d_scale_m, d_gate_m,
                             d_gain_a, d_gain_m, d_gain_f, d_mask,
                             a_m[0].astype(F32), d_row_m, jnp.broadcast_to(loss_part, (LANES,))])
    small = small.reshape(-1, LANES)
    count_small = small.shape[0]
    small = jnp.pad(small, ((0, -count_small % 8), (0, 0)))
    small, g_embed, *block_parts = together(small, g_embed, *[p for _, p in block_got])
    small_all = share(ALL, 1, small)[0].reshape((n,) + small.shape)
    small_all = small_all[:, :count_small].reshape(n, -1)
    d_mod_all = small_all[:, : 6 * D]
    d_gains = jnp.sum(small_all[:, 6 * D : 10 * D], axis=0).reshape(4, D)
    g_gains = lax.dynamic_slice_in_dim(d_gains, me * gains_w.shape[1], gains_w.shape[1], 1)
    total_loss = jnp.sum(small_all[:, 14 * D])
    condition_all = time_features(all_times, C, TSTEPS).astype(BF).astype(F32)
    condition_rows = lax.dynamic_slice_in_dim(condition_all, me * ada_w.shape[0], ada_w.shape[0], 1)
    exact = lambda a, b: jnp.einsum("nr,nc->rc", a, b, precision=lax.Precision.HIGHEST)
    g_ada = exact(condition_rows, d_mod_all)
    a_rows = lax.dynamic_slice_in_dim(small_all[:, 10 * D : 11 * D], me * layer_w.shape[0],
                                      layer_w.shape[0], 1)
    g_outer = exact(a_rows, small_all[:, 11 * D : 14 * D])

    g_rest = sum(p.astype(F32) for p in block_parts)
    g_layer = jnp.concatenate(
        [g_outer[:, :D], g_outer[:, D:] + g_rest[:, : 2 * D], g_rest[:, 2 * D :]], axis=1)

    segments = []
    for k in range(nz):
        segment = head_own
        for step, piece in enumerate(head_parts, 1):
            segment = jnp.where(lax.rem(iz + nz - step, nz) == k, piece.astype(F32), segment)
        segments.append(segment)
    g_head = jnp.concatenate(segments, axis=1) / enlarge

    squares = sum(jnp.sum(g * g) for g in (g_layer, g_ada, g_gains, g_embed, g_head))
    squares_all = share(ALL, 2, jnp.broadcast_to(squares, (8, LANES)))[0]
    grad_norm = jnp.sqrt(jnp.sum(squares_all[..., 0, 0]))
    factor = jnp.minimum(1.0, CLIP_NORM / grad_norm)
    step_value = step_count[0].astype(F32)
    updates = (
        (layer_w, layer_m, layer_v, layer_ema, g_layer),
        (ada_w, ada_m, ada_v, ada_ema, g_ada),
        (gains_w, gains_m, gains_v, gains_ema, g_gains),
        (embed_w.T, embed_m.T, embed_v.T, embed_ema.T, g_embed),
        (head_w, head_m, head_v, head_ema, g_head),
    )
    results = []
    for (w, m, v, ema, g), rate, decay in zip(updates, LEARN_RATES, WEIGHT_DECAYS):
        results.extend(adam_step(w, m, v, ema, g * factor, step_value, rate, decay))
    results[12:16] = [a.T for a in results[12:16]]
    return (total_loss, grad_norm, *results)


def solution(mesh):
    dp, vocab = mesh.shape["dp"], mesh.shape["vocab"]
    nz, nc = V // vocab // SEGMENT, 2
    sizes = (nz, dp // nz, vocab // nc, nc)
    fine = Mesh(mesh.devices.reshape(sizes), ALL)
    rows_all, columns_all = P(ALL, None), P(None, ALL)
    table, head = P(("y", "c"), ("z", "x")), P(("z", "x"), ("y", "c"))
    weights = [rows_all] * 8 + [columns_all] * 4 + [table] * 4 + [head] * 4
    return jax.shard_map(
        functools.partial(local, sizes),
        mesh=fine,
        in_specs=(rows_all, rows_all, P(ALL), P(ALL), P(), *weights),
        out_specs=(P(), P(), *weights),
        check_vma=False,
    )
```

```python
import functools
import math

import jax
import jax.numpy as jnp
from jax import lax
from jax.experimental import pallas as pl
from jax.experimental.pallas import tpu as pltpu
from jax.sharding import Mesh, PartitionSpec as P

D = 768
H = 12
HD = 64
FF = 3072
V = 51200
C = 128
TSTEPS = 20
SEGMENT = 3200
LANES = 128
ROWS = 64

NORM_EPS = 1e-05
CLIP_NORM = 0.05
BETA_ONE = 0.9
BETA_TWO = 0.95
ADAM_EPS = 1e-08
EMA_DECAY = 0.9999
LEARN_RATES = (0.03, 0.1, 0.1, 0.5, 0.05)
WEIGHT_DECAYS = (0.01, 0.01, 0.0, 0.01, 0.01)

ALL = ("z", "x", "y", "c")
BF = jnp.bfloat16
F32 = jnp.float32
MESH = pl.DeviceIdType.MESH
VMEM_LIMIT = 60 * 1024 * 1024


def dot(a, b, contract):
    return lax.dot_general(a, b, ((contract[0], contract[1]), ((), ())), preferred_element_type=F32)


def matmul(a, b):
    return dot(a, b, ((1,), (0,)))


def matmul_nt(a, b):
    return dot(a, b, ((1,), (1,)))


def matmul_tn(a, b):
    return dot(a, b, ((0,), (0,)))


def neighbours(axes, sizes):
    found = []
    for place, (axis, size) in enumerate(zip(axes, sizes)):
        for step in range(1, size):
            found.append((place, step, {axis: lax.rem(lax.axis_index(axis) + step, size)}))
    return found


def meet(devices):
    barrier = pltpu.get_barrier_semaphore()
    for device in devices:
        pl.semaphore_signal(barrier, inc=1, device_id=device, device_id_type=MESH)
    pl.semaphore_wait(barrier, len(devices))


def share_kernel(axes, sizes, count, *refs):
    ins, outs = refs[:count], refs[count : 2 * count]
    send, recv, near = refs[2 * count :]
    index = tuple(lax.axis_index(a) for a in axes)
    peers = neighbours(axes, sizes)
    meet([device for _, _, device in peers])
    for i in range(count):
        pltpu.make_async_copy(ins[i], outs[i].at[index], near.at[i]).start()
    for i in range(count):
        pltpu.make_async_copy(ins[i], outs[i].at[index], near.at[i]).wait()
    for place in range(len(axes)):
        view = (slice(None),) * place + index[place:]
        copies = []
        for number, (at, _, device) in enumerate(peers):
            if at == place:
                for i in range(count):
                    copies.append(
                        pltpu.make_async_remote_copy(
                            src_ref=outs[i].at[view],
                            dst_ref=outs[i].at[view],
                            send_sem=send.at[i, number],
                            recv_sem=recv.at[i, number],
                            device_id=device,
                            device_id_type=MESH,
                        )
                    )
        for copy in copies:
            copy.start()
        for copy in copies:
            copy.wait()


def share(axes, collective_id, *arrays):
    sizes = tuple(lax.axis_size(a) for a in axes)
    count, peers = len(arrays), sum(sizes) - len(sizes)
    return pl.pallas_call(
        functools.partial(share_kernel, axes, sizes, count),
        out_shape=[jax.ShapeDtypeStruct(sizes + a.shape, a.dtype) for a in arrays],
        in_specs=[pl.BlockSpec(memory_space=pltpu.VMEM)] * count,
        out_specs=[pl.BlockSpec(memory_space=pltpu.VMEM)] * count,
        scratch_shapes=[
            pltpu.SemaphoreType.DMA((count, peers)),
            pltpu.SemaphoreType.DMA((count, peers)),
            pltpu.SemaphoreType.DMA((count,)),
        ],
        compiler_params=pltpu.CompilerParams(
            collective_id=collective_id, has_side_effects=True
        ),
        name=f"share{collective_id}",
    )(*arrays)


def remote(src, dst, send, recv, device):
    return pltpu.make_async_remote_copy(
        src_ref=src, dst_ref=dst, send_sem=send, recv_sem=recv, device_id=device,
        device_id_type=MESH,
    )


def run_all(copies):
    for copy in copies:
        copy.start()
    for copy in copies:
        copy.wait()


def block_peer(sizes, step):
    nz, nx = sizes[:2]
    me = lax.axis_index("z") * nx + lax.axis_index("x")
    peer = lax.rem(me + step, nz * nx)
    return me, peer, {"z": peer // nx, "x": lax.rem(peer, nx)}


def fetch_kernel(sizes, in_ref, out_ref, from_c, from_y, half, total, sems_c, sems_y, sems_b):
    nz, nx, ny, nc = sizes
    blocks = nz * nx
    iy, ic = lax.axis_index("y"), lax.axis_index("c")
    along_y = [d for _, _, d in neighbours(("y",), (ny,))]
    along_c = [d for _, _, d in neighbours(("c",), (nc,))]
    along_b = [block_peer(sizes, step)[2] for step in range(1, blocks)]
    meet(along_c + along_y + along_b)
    run_all([
        remote(in_ref.at[:, d["c"]], from_c.at[i], sems_c.at[0, i], sems_c.at[1, i], d)
        for i, d in enumerate(along_c)
    ])

    @pl.loop(0, ny)
    def _(y):
        @pl.loop(0, blocks)
        def _(k):
            value = in_ref[y, ic, k]
            for i in range(nc - 1):
                value = value + from_c[i, y, k]
            half[y, k] = value

    run_all([
        remote(half.at[d["y"]], from_y.at[i], sems_y.at[0, i], sems_y.at[1, i], d)
        for i, d in enumerate(along_y)
    ])

    @pl.loop(0, blocks)
    def _(k):
        value = half[iy, k]
        for i in range(ny - 1):
            value = value + from_y[i, k]
        total[k] = value

    me = block_peer(sizes, 0)[0]
    copies = []
    for step in range(1, blocks):
        _, peer, device = block_peer(sizes, step)
        copies.append(
            remote(total.at[peer], out_ref.at[me], sems_b.at[0, step], sems_b.at[1, step], device)
        )
    for copy in copies:
        copy.start()
    out_ref[me] = total[me]
    for copy in copies:
        copy.wait()


def fetch_blocks(sizes, looked_up, collective_id):
    nz, nx, ny, nc = sizes
    block = looked_up.shape[3:]
    blocks = nz * nx
    return pl.pallas_call(
        functools.partial(fetch_kernel, sizes),
        out_shape=jax.ShapeDtypeStruct((blocks,) + block, BF),
        in_specs=[pl.BlockSpec(memory_space=pltpu.VMEM)],
        out_specs=pl.BlockSpec(memory_space=pltpu.VMEM),
        scratch_shapes=[
            pltpu.VMEM((nc - 1, ny, blocks) + block, BF),
            pltpu.VMEM((ny - 1, blocks) + block, BF),
            pltpu.VMEM((ny, blocks) + block, BF),
            pltpu.VMEM((blocks,) + block, BF),
            pltpu.SemaphoreType.DMA((2, nc - 1)),
            pltpu.SemaphoreType.DMA((2, ny - 1)),
            pltpu.SemaphoreType.DMA((2, blocks)),
        ],
        compiler_params=pltpu.CompilerParams(
            collective_id=collective_id, has_side_effects=True, vmem_limit_bytes=VMEM_LIMIT
        ),
        cost_estimate=pl.CostEstimate(flops=0, bytes_accessed=1 << 27, transcendentals=0),
        name="fetch_blocks",
    )(looked_up)


def spread_kernel(sizes, in_ref, small_ref, out_ref, all_ref, sems_c, sems_y, sems_b, sems_s, near):
    nz, nx, ny, nc = sizes
    blocks = nz * nx
    index = tuple(lax.axis_index(a) for a in ALL)
    iy, ic = index[2:]
    along_y = [d for _, _, d in neighbours(("y",), (ny,))]
    along_c = [d for _, _, d in neighbours(("c",), (nc,))]
    along_b = [block_peer(sizes, step)[2] for step in range(1, blocks)]
    meet(along_c + along_y + along_b)
    me = block_peer(sizes, 0)[0]
    peers = neighbours(ALL, sizes)

    def small(place):
        view = (slice(None),) * place + index[place:]
        return [
            remote(all_ref.at[view], all_ref.at[view], sems_s.at[0, i], sems_s.at[1, i], device)
            for i, (at, _, device) in enumerate(peers)
            if at == place
        ]

    def start(copies):
        for copy in copies:
            copy.start()
        return copies

    def wait(copies):
        for copy in copies:
            copy.wait()

    own = pltpu.make_async_copy(small_ref, all_ref.at[index], near.at[0])
    own.start()
    own.wait()
    along_z = start(small(0))
    columns = []
    for step in range(1, blocks):
        _, peer, device = block_peer(sizes, step)
        columns.append(
            remote(in_ref.at[peer], out_ref.at[iy, ic, me], sems_b.at[0, step],
                   sems_b.at[1, step], device)
        )
    start(columns)
    out_ref[iy, ic, me] = in_ref[me]
    wait(along_z)
    along_x = start(small(1))
    wait(along_x)
    small_y = start(small(2))
    wait(columns)
    rows_y = start([
        remote(out_ref.at[iy, ic], out_ref.at[iy, ic], sems_y.at[0, i], sems_y.at[1, i], d)
        for i, d in enumerate(along_y)
    ])
    wait(small_y)
    small_c = start(small(3))
    wait(rows_y)
    rows_c = start([
        remote(out_ref.at[:, ic], out_ref.at[:, ic], sems_c.at[0, i], sems_c.at[1, i], d)
        for i, d in enumerate(along_c)
    ])
    wait(small_c)
    wait(rows_c)


def spread_blocks(sizes, parts, small, collective_id):
    nz, nx, ny, nc = sizes
    return pl.pallas_call(
        functools.partial(spread_kernel, sizes),
        out_shape=[
            jax.ShapeDtypeStruct((ny, nc) + parts.shape, parts.dtype),
            jax.ShapeDtypeStruct(sizes + small.shape, small.dtype),
        ],
        in_specs=[pl.BlockSpec(memory_space=pltpu.VMEM)] * 2,
        out_specs=[pl.BlockSpec(memory_space=pltpu.VMEM)] * 2,
        scratch_shapes=[
            pltpu.SemaphoreType.DMA((2, nc - 1)),
            pltpu.SemaphoreType.DMA((2, ny - 1)),
            pltpu.SemaphoreType.DMA((2, nz * nx)),
            pltpu.SemaphoreType.DMA((2, sum(sizes) - 4)),
            pltpu.SemaphoreType.DMA((1,)),
        ],
        compiler_params=pltpu.CompilerParams(
            collective_id=collective_id, has_side_effects=True, vmem_limit_bytes=VMEM_LIMIT
        ),
        cost_estimate=pl.CostEstimate(flops=0, bytes_accessed=1 << 27, transcendentals=0),
        name="spread_blocks",
    )(parts, small)


def axis_place(axes):
    index, size = 0, 1
    for axis in axes:
        index = index * lax.axis_size(axis) + lax.axis_index(axis)
        size = size * lax.axis_size(axis)
    return index, size


def exchange(piece_for, axes):
    me, n = axis_place(axes)
    got = [(me, piece_for(me))]
    for step in range(1, n):
        piece = piece_for(lax.rem(me + step, n))
        moved = lax.ppermute(piece, axes, [(i, (i + step) % n) for i in range(n)])
        got.append((lax.rem(me + n - step, n), moved))
    return got


def in_order(got):
    out = jnp.zeros((len(got),) + got[0][1].shape, got[0][1].dtype)
    for sender, piece in got:
        out = lax.dynamic_update_index_in_dim(out, piece, sender, 0)
    return out


def together(*values):
    return lax.optimization_barrier(values)


def pick(values, index, dim=0):
    return lax.dynamic_index_in_dim(values, index, dim, keepdims=False)


def spread_parts(values, dim, axis):
    got = exchange(lambda k: pick(values, k, dim).astype(jnp.float16), (axis,))
    return pick(values, got[0][0], dim), [piece for _, piece in got[1:]]


def added(own, pieces):
    for piece in pieces:
        own = own + piece.astype(F32)
    return own


def gather_kernel(low_ref, high_ref, ids_ref, table_ref, out_ref, turned_ref, rows_ref):
    source = pl.program_id(0)

    @pl.when(source == 0)
    def _():
        @pl.loop(0, table_ref.shape[1] // LANES)
        def _(k):
            at = pl.multiple_of(k * LANES, LANES)
            turned_ref[pl.ds(at, LANES), :] = table_ref[:, pl.ds(at, LANES)].T

    low, high = low_ref[source], high_ref[source]
    rows_ref[...] = jnp.zeros_like(rows_ref)

    def chunk(k, carry):
        base = pl.multiple_of(k * 8, 8)
        rows = []
        for i in range(8):
            place = base + i
            valid = jnp.logical_and(place >= low, place < high)
            row = jnp.where(valid, ids_ref[source, place], 0)
            value = turned_ref[pl.ds(row, 1), :]
            rows.append(jnp.where(valid, value, 0.0))
        rows_ref[pl.ds(base, 8), :] = jnp.concatenate(rows, axis=0)
        return carry

    lax.fori_loop(low // 8, (high + 7) // 8, chunk, 0)
    out_ref[0] = rows_ref[...].T.astype(BF)


def gather_rows(table, ids, low, high):
    sources, count = ids.shape
    width = table.shape[0]
    return pl.pallas_call(
        gather_kernel,
        out_shape=jax.ShapeDtypeStruct((sources, width, count), BF),
        grid_spec=pltpu.PrefetchScalarGridSpec(
            num_scalar_prefetch=3,
            grid=(sources,),
            in_specs=[
                pl.BlockSpec(table.shape, lambda i, *_: (0, 0), pipeline_mode=pl.Buffered(1))
            ],
            out_specs=pl.BlockSpec((1, width, count), lambda i, *_: (i, 0, 0)),
            scratch_shapes=[
                pltpu.VMEM((table.shape[1], width), F32),
                pltpu.VMEM((count, width), F32),
            ],
        ),
        compiler_params=pltpu.CompilerParams(vmem_limit_bytes=VMEM_LIMIT),
        cost_estimate=pl.CostEstimate(flops=0, bytes_accessed=1 << 27, transcendentals=0),
        name="gather_rows",
    )(low, high, ids, table)


def scatter_kernel(low_ref, high_ref, ids_ref, rows_ref, out_ref, wide_ref, *totals):
    source = pl.program_id(0)

    @pl.when(source == 0)
    def _():
        for total_ref in totals:
            total_ref[...] = jnp.zeros_like(total_ref)

    low, high = low_ref[source], high_ref[source]
    wide_ref[...] = rows_ref[0].astype(F32).T

    def chunk(k, carry):
        base = pl.multiple_of(k * 8, 8)
        block = wide_ref[pl.ds(base, 8), :]
        for i in range(8):
            total_ref = totals[i % len(totals)]
            place = base + i
            valid = jnp.logical_and(place >= low, place < high)
            row = jnp.where(valid, ids_ref[source, place], 0)
            addend = jnp.where(valid, block[i : i + 1, :], 0.0)
            total_ref[pl.ds(row, 1), :] = total_ref[pl.ds(row, 1), :] + addend
        return carry

    lax.fori_loop(low // 8, (high + 7) // 8, chunk, 0)

    @pl.when(source == pl.num_programs(0) - 1)
    def _():
        @pl.loop(0, out_ref.shape[1] // LANES)
        def _(k):
            at = pl.multiple_of(k * LANES, LANES)
            value = totals[0][pl.ds(at, LANES), :]
            for total_ref in totals[1:]:
                value = value + total_ref[pl.ds(at, LANES), :]
            out_ref[:, pl.ds(at, LANES)] = value.T


def scatter_rows(rows, ids, low, high, table_rows):
    sources, width, count = rows.shape
    return pl.pallas_call(
        scatter_kernel,
        out_shape=jax.ShapeDtypeStruct((width, table_rows), F32),
        grid_spec=pltpu.PrefetchScalarGridSpec(
            num_scalar_prefetch=3,
            grid=(sources,),
            in_specs=[pl.BlockSpec((1, width, count), lambda i, *_: (i, 0, 0))],
            out_specs=pl.BlockSpec((width, table_rows), lambda i, *_: (0, 0)),
            scratch_shapes=[pltpu.VMEM((count, width), F32)]
            + [pltpu.VMEM((table_rows, width), F32)] * 4,
        ),
        compiler_params=pltpu.CompilerParams(vmem_limit_bytes=VMEM_LIMIT),
        cost_estimate=pl.CostEstimate(flops=0, bytes_accessed=1 << 27, transcendentals=0),
        name="scatter_rows",
    )(low, high, ids, rows)


def swap_halves(values):
    lane = lax.broadcasted_iota(jnp.int32, values.shape, 1)
    half = HD // 2
    up = pltpu.roll(values, LANES - half, 1)
    down = pltpu.roll(values, half, 1)
    return jnp.where(lax.rem(lane, HD) < half, up, down)


def turn(values, cosine, sine):
    return values * cosine + swap_halves(values) * sine


def turn_back(values, cosine, sine):
    return values * cosine - swap_halves(values) * sine


def attend_kernel(kv_ref, vv_ref, qm_ref, km_ref, vm_ref, cu_ref, su_ref, cm_ref, sm_ref,
                  mask_ref, q_out, ku_out, km_out, att_out, lse_out):
    rows = cm_ref.shape[0]
    wide = (rows, LANES)
    cm, sm = cm_ref[...], sm_ref[...]
    q = turn(jnp.broadcast_to(qm_ref[0:1, :], wide), cm, sm).astype(BF)
    k_m = turn(jnp.broadcast_to(km_ref[0:1, :], wide), cm, sm).astype(BF)
    k_u = turn(kv_ref[...], cu_ref[...], su_ref[...]).astype(BF)
    v_u = vv_ref[...].astype(BF)
    v_m = vm_ref[0:1, :].astype(BF).astype(F32)
    q_out[...] = q
    ku_out[...] = k_u
    km_out[...] = k_m
    mask = mask_ref[0:1, :]
    outs, totals = [], []
    for head in range(LANES // HD):
        part = slice(head * HD, (head + 1) * HD)
        s_u = matmul_nt(q[:, part], k_u[:, part]) * HD ** (-0.5) + mask
        s_m = matmul_nt(q[:, part], k_m[:, part]) * HD ** (-0.5)
        top = jnp.maximum(
            jnp.max(s_u, axis=1, keepdims=True), jnp.max(s_m, axis=1, keepdims=True)
        )
        e_u = jnp.exp(s_u - top)
        e_m = jnp.exp(s_m - top)
        total = jnp.sum(e_u, axis=1, keepdims=True) + jnp.sum(e_m, axis=1, keepdims=True)
        inverse = 1.0 / total
        p_u = (e_u * inverse).astype(BF)
        p_m = (e_m * inverse).astype(BF).astype(F32)
        mixed = matmul(p_u, v_u[:, part]) + jnp.sum(p_m, axis=1, keepdims=True) * v_m[:, part]
        outs.append(mixed)
        totals.append(top + jnp.log(total))
    att_out[...] = jnp.concatenate(outs, axis=1).astype(BF)
    lse_out[0] = jnp.concatenate(totals, axis=1)


def attend(kv_u, qkv_m, tables, mask):
    count, rows = kv_u.shape[0], tables[2].shape[0]
    blocks = D // LANES
    per = LANES // HD
    row = lambda offset: pl.BlockSpec((qkv_m.shape[0], LANES), lambda i: (0, offset * blocks + i))
    column = lambda n: pl.BlockSpec((n, LANES), lambda i: (0, i))
    whole = lambda a: pl.BlockSpec(a.shape, lambda i: (0, 0))
    return pl.pallas_call(
        attend_kernel,
        grid=(blocks,),
        out_shape=[
            jax.ShapeDtypeStruct((rows, D), BF),
            jax.ShapeDtypeStruct((count, D), BF),
            jax.ShapeDtypeStruct((rows, D), BF),
            jax.ShapeDtypeStruct((rows, D), BF),
            jax.ShapeDtypeStruct((blocks, rows, per), F32),
        ],
        in_specs=[
            pl.BlockSpec((count, LANES), lambda i: (0, i)),
            pl.BlockSpec((count, LANES), lambda i: (0, blocks + i)),
            row(0), row(1), row(2),
            *[whole(t) for t in tables],
            whole(mask),
        ],
        out_specs=[column(rows), column(count), column(rows), column(rows),
                   pl.BlockSpec((1, rows, per), lambda i: (i, 0, 0))],
        compiler_params=pltpu.CompilerParams(vmem_limit_bytes=VMEM_LIMIT),
        cost_estimate=pl.CostEstimate(
            flops=2 * 3 * rows * count * D, bytes_accessed=12 * rows * D,
            transcendentals=2 * rows * count * H,
        ),
        name="attend",
    )(kv_u, kv_u, qkv_m, qkv_m, qkv_m, *tables, mask)


def attend_back_kernel(q_ref, ku_ref, km_ref, vv_ref, vm_ref, cu_ref, su_ref, cm_ref, sm_ref,
                       mask_ref, lse_ref, datt_ref, dk_out, dv_out, dm_out):
    q, k_u, k_m, datt = q_ref[...], ku_ref[...], km_ref[...], datt_ref[...]
    v_u = vv_ref[...].astype(BF)
    v_m = vm_ref[0:1, :].astype(BF).astype(F32)
    datt_f = datt.astype(F32)
    mask = mask_ref[0:1, :]
    scale = HD ** (-0.5)
    dq, dk_u, dk_m, dv_u, dv_m = [], [], [], [], []
    for head in range(LANES // HD):
        part = slice(head * HD, (head + 1) * HD)
        lse = lse_ref[0, :, head : head + 1]
        p_u = jnp.exp(matmul_nt(q[:, part], k_u[:, part]) * scale + mask - lse)
        p_m = jnp.exp(matmul_nt(q[:, part], k_m[:, part]) * scale - lse)
        dp_u = matmul_nt(datt[:, part], v_u[:, part])
        dp_m = jnp.sum(datt_f[:, part] * v_m[:, part], axis=1, keepdims=True)
        inner = jnp.sum(p_u * dp_u, axis=1, keepdims=True) + dp_m * jnp.sum(
            p_m, axis=1, keepdims=True
        )
        ds_u = (p_u * (dp_u - inner) * scale).astype(BF)
        ds_m = (p_m * ((dp_m - inner) * scale)).astype(BF)
        dq.append(matmul(ds_u, k_u[:, part]) + matmul(ds_m, k_m[:, part]))
        dk_u.append(matmul_tn(ds_u, q[:, part]))
        dk_m.append(matmul_tn(ds_m, q[:, part]))
        dv_u.append(matmul_tn(p_u.astype(BF), datt[:, part]))
        mass = jnp.sum(p_m.astype(BF).astype(F32), axis=1, keepdims=True)
        dv_m.append(jnp.sum(mass * datt_f[:, part], axis=0, keepdims=True))
    cm, sm = cm_ref[...], sm_ref[...]
    join = lambda parts: jnp.concatenate(parts, axis=1)
    low = lambda a: a.astype(BF).astype(F32)
    dk_out[...] = turn_back(join(dk_u), cu_ref[...], su_ref[...]).astype(BF)
    dv_out[...] = join(dv_u).astype(BF)
    dq_sum = jnp.sum(low(turn_back(join(dq), cm, sm)), axis=0, keepdims=True)
    dk_sum = jnp.sum(low(turn_back(join(dk_m), cm, sm)), axis=0, keepdims=True)
    filler = jnp.zeros((5, LANES), F32)
    dm_out[...] = jnp.concatenate([dq_sum, dk_sum, join(dv_m), filler], axis=0)


def attend_back(q, k_u, k_m, kv_u, qkv_m, tables, mask, lse, datt):
    count, rows = kv_u.shape[0], q.shape[0]
    blocks = D // LANES
    per = LANES // HD
    column = lambda n: pl.BlockSpec((n, LANES), lambda i: (0, i))
    whole = lambda a: pl.BlockSpec(a.shape, lambda i: (0, 0))
    return pl.pallas_call(
        attend_back_kernel,
        grid=(blocks,),
        out_shape=[
            jax.ShapeDtypeStruct((count, D), BF),
            jax.ShapeDtypeStruct((count, D), BF),
            jax.ShapeDtypeStruct((8, D), F32),
        ],
        in_specs=[
            column(rows), column(count), column(rows),
            pl.BlockSpec((count, LANES), lambda i: (0, blocks + i)),
            pl.BlockSpec((qkv_m.shape[0], LANES), lambda i: (0, 2 * blocks + i)),
            *[whole(t) for t in tables],
            whole(mask),
            pl.BlockSpec((1, rows, per), lambda i: (i, 0, 0)),
            column(rows),
        ],
        out_specs=[column(count), column(count), column(8)],
        compiler_params=pltpu.CompilerParams(vmem_limit_bytes=VMEM_LIMIT),
        cost_estimate=pl.CostEstimate(
            flops=2 * 8 * rows * count * D, bytes_accessed=14 * rows * D,
            transcendentals=2 * rows * count * H,
        ),
        name="attend_back",
    )(q, k_u, k_m, kv_u, qkv_m, *tables, mask, lse, datt)


def tile_of(segments):
    return max(16, 1024 // segments)


def logits_kernel(places_ref, x_ref, w_ref, target_ref, e_ref, stats_ref, logits_ref):
    segments, _, width = w_ref.shape
    rows = x_ref.shape[0]
    x = x_ref[...]
    starts = list(range(0, width - width % 768 or width, 768))
    best = None
    for y in range(segments):
        for at, end in zip(starts, starts[1:] + [width]):
            logits = matmul(x, w_ref[y, :, at:end])
            logits_ref[:, y * width + at : y * width + end] = logits
            for g in range(0, end - at, LANES):
                part = logits[:, g : g + LANES]
                best = part if best is None else jnp.maximum(best, part)
    lane = lax.broadcasted_iota(jnp.int32, (ROWS, LANES), 1)
    peaks = jnp.max(best, axis=1, keepdims=True)
    for r in range(0, rows, ROWS):
        peak = peaks[r : r + ROWS]
        top = jnp.broadcast_to(peak, (ROWS, LANES))
        place = target_ref[r : r + ROWS, :] - lane
        total = jnp.zeros((ROWS, LANES), F32)
        chosen = jnp.zeros((ROWS, LANES), F32)
        for y in range(segments):
            for at in range(0, width, LANES):
                column = y * width + at
                logits = logits_ref[r : r + ROWS, column : column + LANES]
                e = jnp.exp(logits - top)
                total = total + e
                chosen = chosen + jnp.where(place == column, logits, 0.0)
                e_ref[y, r : r + ROWS, at : at + LANES] = e.astype(BF)
        sums = [jnp.sum(a, axis=1, keepdims=True) for a in (total, chosen)]
        stats_ref[r : r + ROWS, :] = jnp.concatenate([peak, *sums, peak], axis=1)


def head_logits(rows, weights, targets, places):
    count = rows.shape[0]
    segments, _, width = weights.shape
    tile = tile_of(segments)
    per = count // places.shape[0] // tile

    def placed(i, places):
        return (places[i // per] * per + lax.rem(i, per), 0)

    return pl.pallas_call(
        logits_kernel,
        out_shape=[
            jax.ShapeDtypeStruct((segments, count, width), BF),
            jax.ShapeDtypeStruct((count, 4), F32),
        ],
        grid_spec=pltpu.PrefetchScalarGridSpec(
            num_scalar_prefetch=1,
            grid=(count // tile,),
            in_specs=[
                pl.BlockSpec((tile, D), lambda i, p: (i, 0)),
                pl.BlockSpec(weights.shape, lambda i, p: (0, 0, 0), pipeline_mode=pl.Buffered(1)),
                pl.BlockSpec((tile, 1), placed),
            ],
            out_specs=[
                pl.BlockSpec((segments, tile, width), lambda i, p: (0, i, 0)),
                pl.BlockSpec((tile, 4), placed),
            ],
            scratch_shapes=[pltpu.VMEM((tile, segments * width), F32)],
        ),
        compiler_params=pltpu.CompilerParams(vmem_limit_bytes=VMEM_LIMIT),
        cost_estimate=pl.CostEstimate(
            flops=2 * count * D * segments * width,
            bytes_accessed=2 * count * segments * width,
            transcendentals=count * segments * width,
        ),
        name="head_logits",
    )(places, rows, weights, targets)


def rows_back_kernel(places_ref, e_ref, w_ref, target_ref, factor_ref, d_ref, dx_ref):
    segments, _, width = w_ref.shape
    rows = e_ref.shape[1]
    lane = lax.broadcasted_iota(jnp.int32, (ROWS, LANES), 1)
    wide = lambda a: jnp.broadcast_to(a, (ROWS, LANES))
    total = None
    for y in range(segments):
        for r in range(0, rows, ROWS):
            place = target_ref[r : r + ROWS, :] - (lane + y * width)
            factor = wide(factor_ref[r : r + ROWS, 0:1])
            special = wide(factor_ref[r : r + ROWS, 1:2])
            for at in range(0, width, LANES):
                e = e_ref[y, r : r + ROWS, at : at + LANES].astype(F32)
                d_ref[y, r : r + ROWS, at : at + LANES] = jnp.where(
                    place == at, special, e * factor).astype(BF)
        part = matmul_nt(d_ref[y], w_ref[y])
        total = part if total is None else total + part
    dx_ref[...] = total.astype(BF)


def head_rows_back(e, weights, targets, factors, places):
    segments, count, width = e.shape
    tile = tile_of(segments)
    per = count // places.shape[0] // tile

    def placed(i, places):
        return (places[i // per] * per + lax.rem(i, per), 0)

    return pl.pallas_call(
        rows_back_kernel,
        out_shape=[
            jax.ShapeDtypeStruct(e.shape, BF),
            jax.ShapeDtypeStruct((count, D), BF),
        ],
        grid_spec=pltpu.PrefetchScalarGridSpec(
            num_scalar_prefetch=1,
            grid=(count // tile,),
            in_specs=[
                pl.BlockSpec((segments, tile, width), lambda i, p: (0, i, 0)),
                pl.BlockSpec(weights.shape, lambda i, p: (0, 0, 0), pipeline_mode=pl.Buffered(1)),
                pl.BlockSpec((tile, 1), placed),
                pl.BlockSpec((tile, 2), placed),
            ],
            out_specs=[
                pl.BlockSpec((segments, tile, width), lambda i, p: (0, i, 0)),
                pl.BlockSpec((tile, D), placed),
            ],
        ),
        input_output_aliases={1: 0},
        compiler_params=pltpu.CompilerParams(vmem_limit_bytes=VMEM_LIMIT),
        cost_estimate=pl.CostEstimate(
            flops=2 * count * D * segments * width,
            bytes_accessed=4 * count * segments * width,
            transcendentals=0,
        ),
        name="head_rows_back",
    )(places, e, weights, targets, factors)


def layer_norm(values):
    center = values - jnp.mean(values, axis=-1, keepdims=True)
    spread = jnp.mean(center * center, axis=-1, keepdims=True)
    inv_std = lax.rsqrt(spread + NORM_EPS)
    return (center * inv_std, inv_std)


def norm_back(d_normed, normed, inv_std):
    return inv_std * (
        d_normed
        - jnp.mean(d_normed, axis=-1, keepdims=True)
        - normed * jnp.mean(d_normed * normed, axis=-1, keepdims=True)
    )


def time_features(time_index, width, steps):
    t_value = (time_index.astype(F32) + 1.0) / steps
    half_width = width // 2
    frequencies = jnp.exp(-math.log(10000.0) * jnp.arange(half_width, dtype=F32) / half_width)
    angles = 1000.0 * t_value[:, None] * frequencies[None, :]
    return jax.nn.silu(jnp.concatenate([jnp.cos(angles), jnp.sin(angles)], axis=1))


def rope_rows(positions):
    half = HD // 2
    inverse = jnp.exp(-math.log(10000.0) * jnp.arange(half, dtype=F32) * 2.0 / HD)
    angles = positions.astype(F32)[:, None] * inverse[None, :]
    cosine, sine = jnp.cos(angles), jnp.sin(angles)
    return (jnp.tile(cosine, (1, LANES // half)),
            jnp.tile(jnp.concatenate([-sine, sine], axis=1), (1, LANES // HD)))


def gelu_tanh(values):
    return jax.nn.gelu(values, approximate=True)


def adam_step(weight, first, second, ema_copy, gradient, step_value, learn_rate, decay_rate):
    first_new = BETA_ONE * first + (1.0 - BETA_ONE) * gradient
    second_new = BETA_TWO * second + (1.0 - BETA_TWO) * gradient * gradient
    first_hat = first_new / (1.0 - BETA_ONE**step_value)
    second_hat = second_new / (1.0 - BETA_TWO**step_value)
    weight_new = weight - learn_rate * (
        first_hat / (jnp.sqrt(second_hat) + ADAM_EPS) + decay_rate * weight
    )
    ema_rate = jnp.minimum(EMA_DECAY, (1.0 + step_value) / (10.0 + step_value))
    ema_new = ema_rate * ema_copy + (1.0 - ema_rate) * weight_new
    return (first_new, second_new, weight_new, ema_new)


def split3(row):
    parts, rest = [], row
    for _ in range(3):
        part = lax.reduce_precision(rest, 8, 7)
        parts.append(part.astype(BF))
        rest = rest - part
    return parts


def local(sizes, token_ids, scored, lengths, times, step_count, layer_w, layer_m, layer_v, layer_ema,
          ada_w, ada_m, ada_v, ada_ema, gains_w, gains_m, gains_v, gains_ema,
          embed_w, embed_m, embed_v, embed_ema, head_w, head_m, head_v, head_ema):
    nz, nx, ny, nc = sizes
    n = nz * nx * ny * nc
    length, score_count = token_ids.shape[1], scored.shape[1]
    free_count = length - score_count
    total_rows = n * score_count
    table_rows, table_width = embed_w.shape
    iz, ix, iy, ic = [lax.axis_index(a) for a in ALL]
    vocab_index = iy * nc + ic
    vocab_start = vocab_index * table_rows
    me = (iz * nx + ix) * (ny * nc) + vocab_index

    tokens, masked = token_ids[0], scored[0]
    positions = jnp.arange(length, dtype=jnp.int32)
    hits = masked[:, None] == positions[None, :]
    is_masked = jnp.any(hits, axis=0)
    targets = jnp.sum(jnp.where(hits, tokens[None, :], 0), axis=1)
    keys = jnp.where(is_masked, n * V, (tokens // table_rows) * length + positions)
    rank = jnp.sum((keys[None, :] < keys[:, None]).astype(jnp.int32), axis=1)
    rank = jnp.where(is_masked, length, rank)
    slots = rank[None, :] == jnp.arange(free_count, dtype=jnp.int32)[:, None]
    free_tokens = jnp.sum(jnp.where(slots, tokens[None, :], 0), axis=1)
    free_positions = jnp.sum(jnp.where(slots, positions[None, :], 0), axis=1)

    ints = jnp.concatenate([free_tokens.reshape(-1, LANES), targets.reshape(-1, LANES),
                            jnp.broadcast_to(times[:, None], (1, LANES))], axis=0)
    ints = jnp.pad(ints, ((0, -ints.shape[0] % 8), (0, 0)))
    gain_part = jnp.pad(gains_w.astype(BF).astype(F32),
                        ((0, 8 - gains_w.shape[0]), (0, LANES - gains_w.shape[1])))
    ints_all, gains_all = share(ALL, 0, ints, gain_part)
    ints_all = ints_all.reshape((n,) + ints.shape)
    gains_all = gains_all.reshape((n,) + gain_part.shape)

    block_low = jnp.concatenate(
        [layer_w.astype(BF), ada_w.astype(BF).reshape(layer_w.shape[0], -1)], axis=1)
    block_low, head_low, ints_all = together(block_low, head_w.astype(BF), ints_all)
    layer_all = lax.all_gather(block_low, ALL, axis=0, tiled=True)

    piece_for = lambda k: lax.dynamic_slice_in_dim(head_low, k * SEGMENT, SEGMENT, 1)
    head_parts = exchange(piece_for, ("z",))

    gains = jnp.moveaxis(gains_all[:, : gains_w.shape[0], : gains_w.shape[1]], 0, 1).reshape(4, D)
    free_rows = free_count // LANES
    score_rows = score_count // LANES
    all_tokens = ints_all[:, :free_rows].reshape(nz * nx, ny * nc, free_count)
    all_targets = ints_all[:, free_rows : free_rows + score_rows].reshape(
        nz, nx, ny, nc, score_count)
    all_times = ints_all[:, free_rows + score_rows, 0]

    wanted = jnp.swapaxes(all_tokens, 0, 1).reshape(n, free_count)
    owners = wanted // table_rows
    low = jnp.sum((owners < vocab_index).astype(jnp.int32), axis=1)
    high = jnp.sum((owners <= vocab_index).astype(jnp.int32), axis=1)
    local_ids = wanted - vocab_start
    looked_up = gather_rows(embed_w.T, local_ids, low, high)
    looked_up = looked_up.reshape((ny, nc, nz * nx) + looked_up.shape[1:])
    x0_u = fetch_blocks(sizes, looked_up, 3).reshape(D, free_count).T.astype(F32)
    senders = [sender for sender, _ in head_parts]
    x0_u, *pieces = together(x0_u, *[piece for _, piece in head_parts])
    head_part = in_order(list(zip(senders, pieces))).reshape(-1, SEGMENT)

    mask_row = gains[3:4]
    condition = time_features(times, C, TSTEPS).astype(BF)
    modulation = matmul(condition, layer_all[:, layer_w.shape[1] :].reshape(C, 6 * D))
    shift_a, scale_a, gate_a, shift_m, scale_m, gate_m = [
        modulation[:, i * D : (i + 1) * D] for i in range(6)]
    normed_u, inv_u = layer_norm(x0_u)
    a_u = (normed_u * gains[0:1] * (1.0 + scale_a) + shift_a).astype(BF)
    normed_0, inv_0 = layer_norm(mask_row)
    a_m = (normed_0 * gains[0:1] * (1.0 + scale_a) + shift_a).astype(BF)
    w_qkv, w_o = layer_all[:, : 3 * D], layer_all[:, 3 * D : 4 * D]
    w_up, w_down = layer_all[:, 4 * D : 4 * D + FF], layer_all[:, 4 * D + FF : 4 * D + 2 * FF]
    qkv_m = matmul(jnp.broadcast_to(a_m, (16, D)), w_qkv)
    kv_u = matmul(a_u, w_qkv[:, D:])
    tables = (*rope_rows(free_positions), *rope_rows(masked))
    mask = jnp.where(free_positions[None, :] < lengths[:, None], 0.0, -1e30)
    mask = jnp.broadcast_to(mask, (8, free_count)).astype(F32)
    q, k_u, k_m, att, lse_a = attend(kv_u, qkv_m, tables, mask)
    branch = matmul(att, w_o)
    x1 = mask_row + gate_a * branch
    normed_m, inv_m = layer_norm(x1)
    b = (normed_m * gains[1:2] * (1.0 + scale_m) + shift_m).astype(BF)
    pre = matmul(b, w_up)
    act = gelu_tanh(pre).astype(BF)
    mlp = matmul_nt(act, w_down)
    x2 = x1 + gate_m * mlp
    normed_f, inv_f = layer_norm(x2)
    final = (normed_f * gains[2:3]).astype(BF)

    final_turned = jnp.swapaxes(final.reshape(score_count, nz, nx, -1), 1, 2).reshape(score_count, D)
    head_all = lax.all_gather(head_part, ("y", "x"), axis=0, tiled=True).reshape(ny, D, SEGMENT)
    group = nz * nc * score_count
    blocks, places = [], []
    for sender, piece in exchange(lambda k: final_turned, ("z",)):
        for place, part in exchange(lambda k: piece, ("c",)):
            blocks.append(part)
            places.append(sender * nc + place)
    places = jnp.stack(places).astype(jnp.int32)
    row_targets = pick(jnp.moveaxis(jnp.moveaxis(all_targets, 3, 1), (2, 3), (0, 1)).reshape(
        nx * ny, group), ix * ny + iy)
    row_times = pick(jnp.moveaxis(jnp.moveaxis(all_times.reshape(nz, nx, ny, nc), 3, 1), (2, 3), (0, 1))
                     .reshape(nx * ny, nz * nc), ix * ny + iy)
    row_weights = jnp.repeat(TSTEPS / (row_times.astype(F32) + 1.0) / total_rows, score_count)
    owner, within = row_targets // table_rows, row_targets % table_rows
    owned = jnp.logical_and(owner % nc == ic, within // SEGMENT == iz)
    column_of = jnp.where(owned, (owner // nc) * SEGMENT + within % SEGMENT, -1)[:, None]
    rows = jnp.concatenate(blocks, axis=0)
    e, stats = head_logits(rows, head_all, column_of, places)
    top = stats[:, 0]
    every = share(("z", "c"), 4, stats.T.reshape(4, -1, LANES))[0].reshape(nz * nc, 4, group)
    best = jnp.max(every[:, 0], axis=0)
    log_total = best + jnp.log(jnp.sum(every[:, 1] * jnp.exp(every[:, 0] - best), axis=0))
    chosen = jnp.sum(every[:, 2], axis=0)
    own_start = (iz * nc + ic) * score_count
    own_terms = lax.dynamic_slice_in_dim(row_weights * (log_total - chosen), own_start, score_count)
    loss_part = jnp.sum(own_terms)
    factors = jnp.stack([row_weights * jnp.exp(top - log_total),
                         row_weights * (jnp.exp(chosen - log_total) - 1.0)], axis=1)
    d_logits, d_rows = head_rows_back(e, head_all, column_of, factors, places)
    d_final = lax.psum_scatter(d_rows, ("z", "c"), scatter_dimension=0, tiled=True)

    bound = D**0.5 * jnp.max(jnp.abs(gains[2])) * 1.02
    bound = bound * score_count * jnp.sum(TSTEPS / (all_times.astype(F32) + 1.0) / total_rows)
    enlarge = 60000.0 / jnp.maximum(bound, 1e-30)
    d_head = jnp.einsum("rd,yrv->ydv", rows, d_logits, preferred_element_type=F32) * enlarge
    d_final, d_head = together(d_final, d_head.reshape(ny, nx, nz, -1, SEGMENT))
    cut = nz // 2
    own_x, from_x = spread_parts(d_head[:, :, :cut], 1, "x")
    own_y, from_y = spread_parts(d_head[:, :, cut:], 0, "y")
    d_final = d_final.astype(F32)
    d_final = jnp.swapaxes(d_final.reshape(score_count, nx, nz, -1), 1, 2).reshape(score_count, D)

    d_gain_f = jnp.sum(d_final * normed_f, axis=0)
    d_x2 = norm_back(d_final * gains[2:3], normed_f, inv_f)
    d_gate_m = jnp.sum(d_x2 * mlp, axis=0)
    d_out = (d_x2 * gate_m).astype(BF)
    d_down = matmul_tn(d_out, act)
    d_act = matmul(d_out, w_down)
    d_pre = jax.vjp(gelu_tanh, pre)[1](d_act)[0].astype(BF)
    d_up = matmul_tn(b, d_pre)
    d_b = matmul_nt(d_pre, w_up)
    d_shift_m = jnp.sum(d_b, axis=0)
    product = jnp.sum(d_b * normed_m, axis=0)
    d_scale_m = product * gains[1]
    d_gain_m = product * (1.0 + scale_m[0])
    d_x1 = d_x2 + norm_back(d_b * ((1.0 + scale_m) * gains[1:2]), normed_m, inv_m)
    d_gate_a = jnp.sum(d_x1 * branch, axis=0)
    d_branch = (d_x1 * gate_a).astype(BF)
    d_wout = matmul_tn(att, d_branch)
    d_att, *from_xy = together(matmul_nt(d_branch, w_o).astype(BF), *from_x, *from_y)
    def over_cores(gradient):
        width = gradient.shape[1]
        parts = jnp.transpose(gradient.reshape(nz, nx, ny, nc, -1, width), (3, 1, 2, 0, 4, 5))
        parts = parts.reshape(nc, -1, width)
        got = exchange(lambda k: pick(parts, k), ("c",))
        return sum(piece.astype(F32) for _, piece in got).astype(BF)

    over_plane = lambda a: lax.psum_scatter(a, ("x", "y"), scatter_dimension=0, tiled=True)
    own_xy, from_xy = (
        spread_parts(added(own_x, from_xy[: nx - 1]), 0, "y"),
        spread_parts(added(own_y, from_xy[nx - 1 :]), 0, "x"),
    )
    mlp_sum = over_cores(jnp.concatenate([d_up.astype(BF), d_down.astype(BF)], axis=1))
    d_att, mlp_sum = together(d_att, mlp_sum)
    mlp_sum = over_plane(mlp_sum)
    d_k, d_v, d_qkv_m = attend_back(q, k_u, k_m, kv_u, qkv_m, tables, mask, lse_a, d_att)
    d_k, *arrivals = together(d_k, *own_xy[1], *from_xy[1])
    d_kv = jnp.concatenate([d_k, d_v], axis=1)
    d_wkv = matmul_tn(a_u, d_kv)
    d_row_m = d_qkv_m[:3].reshape(3 * D)
    d_a_u = matmul_nt(d_kv, w_qkv[:, D:])
    d_parts = matmul_nt(jnp.pad(jnp.stack(split3(d_row_m)), ((0, 13), (0, 0))), w_qkv)
    d_a_m = jnp.sum(d_parts[:3], axis=0, keepdims=True)
    d_shift_a = jnp.sum(d_a_u, axis=0) + d_a_m[0]
    product = jnp.sum(d_a_u * normed_u, axis=0) + (d_a_m * normed_0)[0]
    d_scale_a = product * gains[0]
    d_gain_a = product * (1.0 + scale_a[0])
    scaling = (1.0 + scale_a) * gains[0:1]
    d_x0_u = norm_back(d_a_u * scaling, normed_u, inv_u)
    d_mask = jnp.sum(d_x1, axis=0) + norm_back(d_a_m * scaling, normed_0, inv_0)[0]

    rest_sum = over_cores(jnp.concatenate([d_wkv.astype(BF), d_wout.astype(BF)], axis=1))

    small = jnp.concatenate([d_shift_a, d_scale_a, d_gate_a, d_shift_m, d_scale_m, d_gate_m,
                             d_gain_a, d_gain_m, d_gain_f, d_mask,
                             a_m[0].astype(F32), d_row_m, jnp.broadcast_to(loss_part, (LANES,))])
    small = small.reshape(-1, LANES)
    count_small = small.shape[0]
    small = jnp.pad(small, ((0, -count_small % 8), (0, 0)))

    sent, rest_sum = together(
        d_x0_u.astype(BF).T.reshape(nz * nx, table_width, free_count), rest_sum)
    rest_sum, mlp_sum = together(rest_sum, mlp_sum)
    rest_sum = over_plane(rest_sum)
    head_sum = jnp.concatenate(
        [added(own_xy[0], arrivals[: ny - 1]), added(from_xy[0], arrivals[ny - 1 :])], axis=0)
    sent, head_sum = together(sent, head_sum)
    head_own, head_parts = spread_parts(head_sum, 0, "z")

    arrived, small_all = spread_blocks(sizes, sent, small, 5)
    arrived, mlp_sum, rest_sum, *head_parts = together(arrived, mlp_sum, rest_sum, *head_parts)
    plane_sum = jnp.concatenate([rest_sum, mlp_sum], axis=1)
    plane_sum = plane_sum.reshape(nz, -1, plane_sum.shape[1])
    block_parts = [p for _, p in exchange(lambda k: pick(plane_sum, k), ("z",))]
    g_embed = scatter_rows(arrived.reshape(n, table_width, free_count), local_ids, low, high,
                           table_rows)
    together_now = together(g_embed, small_all, head_own, *head_parts, *block_parts)
    g_embed, small_all, head_own = together_now[:3]
    head_parts, block_parts = together_now[3 : 2 + nz], together_now[2 + nz :]
    small_all = small_all.reshape((n,) + small.shape)
    small_all = small_all[:, :count_small].reshape(n, -1)
    d_mod_all = small_all[:, : 6 * D]
    d_gains = jnp.sum(small_all[:, 6 * D : 10 * D], axis=0).reshape(4, D)
    g_gains = lax.dynamic_slice_in_dim(d_gains, me * gains_w.shape[1], gains_w.shape[1], 1)
    total_loss = jnp.sum(small_all[:, 14 * D])
    condition_all = time_features(all_times, C, TSTEPS).astype(BF).astype(F32)
    condition_rows = lax.dynamic_slice_in_dim(condition_all, me * ada_w.shape[0], ada_w.shape[0], 1)
    exact = lambda a, b: jnp.einsum("nr,nc->rc", a, b, precision=lax.Precision.HIGHEST)
    g_ada = exact(condition_rows, d_mod_all)
    a_rows = lax.dynamic_slice_in_dim(small_all[:, 10 * D : 11 * D], me * layer_w.shape[0],
                                      layer_w.shape[0], 1)
    g_outer = exact(a_rows, small_all[:, 11 * D : 14 * D])

    g_rest = sum(p.astype(F32) for p in block_parts)
    g_layer = jnp.concatenate(
        [g_outer[:, :D], g_outer[:, D:] + g_rest[:, : 2 * D], g_rest[:, 2 * D :]], axis=1)

    segments = []
    for k in range(nz):
        segment = head_own
        for step, piece in enumerate(head_parts, 1):
            segment = jnp.where(lax.rem(iz + nz - step, nz) == k, piece.astype(F32), segment)
        segments.append(segment)
    g_head = jnp.concatenate(segments, axis=1) / enlarge

    squares = sum(jnp.sum(g * g) for g in (g_layer, g_ada, g_gains, g_embed, g_head))
    squares_all = share(ALL, 2, jnp.broadcast_to(squares, (8, LANES)))[0]
    grad_norm = jnp.sqrt(jnp.sum(squares_all[..., 0, 0]))
    factor = jnp.minimum(1.0, CLIP_NORM / grad_norm)
    step_value = step_count[0].astype(F32)
    updates = (
        (layer_w, layer_m, layer_v, layer_ema, g_layer),
        (ada_w, ada_m, ada_v, ada_ema, g_ada),
        (gains_w, gains_m, gains_v, gains_ema, g_gains),
        (embed_w.T, embed_m.T, embed_v.T, embed_ema.T, g_embed),
        (head_w, head_m, head_v, head_ema, g_head),
    )
    results = []
    for (w, m, v, ema, g), rate, decay in zip(updates, LEARN_RATES, WEIGHT_DECAYS):
        results.extend(adam_step(w, m, v, ema, g * factor, step_value, rate, decay))
    results[12:16] = [a.T for a in results[12:16]]
    return (total_loss, grad_norm, *results)


def solution(mesh):
    dp, vocab = mesh.shape["dp"], mesh.shape["vocab"]
    nz, nc = V // vocab // SEGMENT, 2
    sizes = (nz, dp // nz, vocab // nc, nc)
    fine = Mesh(mesh.devices.reshape(sizes), ALL)
    rows_all, columns_all = P(ALL, None), P(None, ALL)
    table, head = P(("y", "c"), ("z", "x")), P(("z", "x"), ("y", "c"))
    weights = [rows_all] * 8 + [columns_all] * 4 + [table] * 4 + [head] * 4
    return jax.shard_map(
        functools.partial(local, sizes),
        mesh=fine,
        in_specs=(rows_all, rows_all, P(ALL), P(ALL), P(), *weights),
        out_specs=(P(), P(), *weights),
        check_vma=False,
    )
```

```python
import functools
import math

import jax
import jax.numpy as jnp
from jax import lax
from jax.experimental import pallas as pl
from jax.experimental.pallas import tpu as pltpu
from jax.sharding import Mesh, PartitionSpec as P

D = 768
H = 12
HD = 64
FF = 3072
V = 51200
C = 128
TSTEPS = 20
SEGMENT = 3200
LANES = 128
ROWS = 64

NORM_EPS = 1e-05
CLIP_NORM = 0.05
BETA_ONE = 0.9
BETA_TWO = 0.95
ADAM_EPS = 1e-08
EMA_DECAY = 0.9999
LEARN_RATES = (0.03, 0.1, 0.1, 0.5, 0.05)
WEIGHT_DECAYS = (0.01, 0.01, 0.0, 0.01, 0.01)

ALL = ("z", "x", "y", "c")
BF = jnp.bfloat16
F32 = jnp.float32
MESH = pl.DeviceIdType.MESH
VMEM_LIMIT = 60 * 1024 * 1024


def dot(a, b, contract):
    return lax.dot_general(a, b, ((contract[0], contract[1]), ((), ())), preferred_element_type=F32)


def matmul(a, b):
    return dot(a, b, ((1,), (0,)))


def matmul_nt(a, b):
    return dot(a, b, ((1,), (1,)))


def matmul_tn(a, b):
    return dot(a, b, ((0,), (0,)))


def neighbours(axes, sizes):
    found = []
    for place, (axis, size) in enumerate(zip(axes, sizes)):
        for step in range(1, size):
            found.append((place, step, {axis: lax.rem(lax.axis_index(axis) + step, size)}))
    return found


def meet(devices):
    barrier = pltpu.get_barrier_semaphore()
    for device in devices:
        pl.semaphore_signal(barrier, inc=1, device_id=device, device_id_type=MESH)
    pl.semaphore_wait(barrier, len(devices))


def share_kernel(axes, sizes, count, *refs):
    ins, outs = refs[:count], refs[count : 2 * count]
    send, recv, near = refs[2 * count :]
    index = tuple(lax.axis_index(a) for a in axes)
    peers = neighbours(axes, sizes)
    meet([device for _, _, device in peers])
    for i in range(count):
        pltpu.make_async_copy(ins[i], outs[i].at[index], near.at[i]).start()
    for i in range(count):
        pltpu.make_async_copy(ins[i], outs[i].at[index], near.at[i]).wait()
    for place in range(len(axes)):
        view = (slice(None),) * place + index[place:]
        copies = []
        for number, (at, _, device) in enumerate(peers):
            if at == place:
                for i in range(count):
                    copies.append(
                        pltpu.make_async_remote_copy(
                            src_ref=outs[i].at[view],
                            dst_ref=outs[i].at[view],
                            send_sem=send.at[i, number],
                            recv_sem=recv.at[i, number],
                            device_id=device,
                            device_id_type=MESH,
                        )
                    )
        for copy in copies:
            copy.start()
        for copy in copies:
            copy.wait()


def share(axes, collective_id, *arrays):
    sizes = tuple(lax.axis_size(a) for a in axes)
    count, peers = len(arrays), sum(sizes) - len(sizes)
    return pl.pallas_call(
        functools.partial(share_kernel, axes, sizes, count),
        out_shape=[jax.ShapeDtypeStruct(sizes + a.shape, a.dtype) for a in arrays],
        in_specs=[pl.BlockSpec(memory_space=pltpu.VMEM)] * count,
        out_specs=[pl.BlockSpec(memory_space=pltpu.VMEM)] * count,
        scratch_shapes=[
            pltpu.SemaphoreType.DMA((count, peers)),
            pltpu.SemaphoreType.DMA((count, peers)),
            pltpu.SemaphoreType.DMA((count,)),
        ],
        compiler_params=pltpu.CompilerParams(
            collective_id=collective_id, has_side_effects=True
        ),
        name=f"share{collective_id}",
    )(*arrays)


def remote(src, dst, send, recv, device):
    return pltpu.make_async_remote_copy(
        src_ref=src, dst_ref=dst, send_sem=send, recv_sem=recv, device_id=device,
        device_id_type=MESH,
    )


def run_all(copies):
    for copy in copies:
        copy.start()
    for copy in copies:
        copy.wait()


def block_peer(sizes, step):
    nz, nx = sizes[:2]
    me = lax.axis_index("z") * nx + lax.axis_index("x")
    peer = lax.rem(me + step, nz * nx)
    return me, peer, {"z": peer // nx, "x": lax.rem(peer, nx)}


def fetch_kernel(sizes, in_ref, out_ref, from_c, from_y, half, total, sems_c, sems_y, sems_b):
    nz, nx, ny, nc = sizes
    blocks = nz * nx
    iy, ic = lax.axis_index("y"), lax.axis_index("c")
    along_y = [d for _, _, d in neighbours(("y",), (ny,))]
    along_c = [d for _, _, d in neighbours(("c",), (nc,))]
    along_b = [block_peer(sizes, step)[2] for step in range(1, blocks)]
    meet(along_c + along_y + along_b)
    run_all([
        remote(in_ref.at[:, d["c"]], from_c.at[i], sems_c.at[0, i], sems_c.at[1, i], d)
        for i, d in enumerate(along_c)
    ])

    @pl.loop(0, ny)
    def _(y):
        @pl.loop(0, blocks)
        def _(k):
            value = in_ref[y, ic, k]
            for i in range(nc - 1):
                value = value + from_c[i, y, k]
            half[y, k] = value

    run_all([
        remote(half.at[d["y"]], from_y.at[i], sems_y.at[0, i], sems_y.at[1, i], d)
        for i, d in enumerate(along_y)
    ])

    @pl.loop(0, blocks)
    def _(k):
        value = half[iy, k]
        for i in range(ny - 1):
            value = value + from_y[i, k]
        total[k] = value

    me = block_peer(sizes, 0)[0]
    copies = []
    for step in range(1, blocks):
        _, peer, device = block_peer(sizes, step)
        copies.append(
            remote(total.at[peer], out_ref.at[me], sems_b.at[0, step], sems_b.at[1, step], device)
        )
    for copy in copies:
        copy.start()
    out_ref[me] = total[me]
    for copy in copies:
        copy.wait()


def fetch_blocks(sizes, looked_up, collective_id):
    nz, nx, ny, nc = sizes
    block = looked_up.shape[3:]
    blocks = nz * nx
    return pl.pallas_call(
        functools.partial(fetch_kernel, sizes),
        out_shape=jax.ShapeDtypeStruct((blocks,) + block, BF),
        in_specs=[pl.BlockSpec(memory_space=pltpu.VMEM)],
        out_specs=pl.BlockSpec(memory_space=pltpu.VMEM),
        scratch_shapes=[
            pltpu.VMEM((nc - 1, ny, blocks) + block, BF),
            pltpu.VMEM((ny - 1, blocks) + block, BF),
            pltpu.VMEM((ny, blocks) + block, BF),
            pltpu.VMEM((blocks,) + block, BF),
            pltpu.SemaphoreType.DMA((2, nc - 1)),
            pltpu.SemaphoreType.DMA((2, ny - 1)),
            pltpu.SemaphoreType.DMA((2, blocks)),
        ],
        compiler_params=pltpu.CompilerParams(
            collective_id=collective_id, has_side_effects=True, vmem_limit_bytes=VMEM_LIMIT
        ),
        cost_estimate=pl.CostEstimate(flops=0, bytes_accessed=1 << 27, transcendentals=0),
        name="fetch_blocks",
    )(looked_up)


def spread_kernel(sizes, in_ref, small_ref, out_ref, all_ref, sems_c, sems_y, sems_b, sems_s, near):
    nz, nx, ny, nc = sizes
    blocks = nz * nx
    index = tuple(lax.axis_index(a) for a in ALL)
    iy, ic = index[2:]
    along_y = [d for _, _, d in neighbours(("y",), (ny,))]
    along_c = [d for _, _, d in neighbours(("c",), (nc,))]
    along_b = [block_peer(sizes, step)[2] for step in range(1, blocks)]
    meet(along_c + along_y + along_b)
    me = block_peer(sizes, 0)[0]
    peers = neighbours(ALL, sizes)

    def small(place):
        view = (slice(None),) * place + index[place:]
        return [
            remote(all_ref.at[view], all_ref.at[view], sems_s.at[0, i], sems_s.at[1, i], device)
            for i, (at, _, device) in enumerate(peers)
            if at == place
        ]

    def start(copies):
        for copy in copies:
            copy.start()
        return copies

    def wait(copies):
        for copy in copies:
            copy.wait()

    own = pltpu.make_async_copy(small_ref, all_ref.at[index], near.at[0])
    own.start()
    own.wait()
    along_z = start(small(0))
    columns = []
    for step in range(1, blocks):
        _, peer, device = block_peer(sizes, step)
        columns.append(
            remote(in_ref.at[peer], out_ref.at[iy, ic, me], sems_b.at[0, step],
                   sems_b.at[1, step], device)
        )
    start(columns)
    out_ref[iy, ic, me] = in_ref[me]
    wait(along_z)
    along_x = start(small(1))
    wait(along_x)
    small_y = start(small(2))
    wait(columns)
    rows_y = start([
        remote(out_ref.at[iy, ic], out_ref.at[iy, ic], sems_y.at[0, i], sems_y.at[1, i], d)
        for i, d in enumerate(along_y)
    ])
    wait(small_y)
    small_c = start(small(3))
    wait(rows_y)
    rows_c = start([
        remote(out_ref.at[:, ic], out_ref.at[:, ic], sems_c.at[0, i], sems_c.at[1, i], d)
        for i, d in enumerate(along_c)
    ])
    wait(small_c)
    wait(rows_c)


def spread_blocks(sizes, parts, small, collective_id):
    nz, nx, ny, nc = sizes
    return pl.pallas_call(
        functools.partial(spread_kernel, sizes),
        out_shape=[
            jax.ShapeDtypeStruct((ny, nc) + parts.shape, parts.dtype),
            jax.ShapeDtypeStruct(sizes + small.shape, small.dtype),
        ],
        in_specs=[pl.BlockSpec(memory_space=pltpu.VMEM)] * 2,
        out_specs=[pl.BlockSpec(memory_space=pltpu.VMEM)] * 2,
        scratch_shapes=[
            pltpu.SemaphoreType.DMA((2, nc - 1)),
            pltpu.SemaphoreType.DMA((2, ny - 1)),
            pltpu.SemaphoreType.DMA((2, nz * nx)),
            pltpu.SemaphoreType.DMA((2, sum(sizes) - 4)),
            pltpu.SemaphoreType.DMA((1,)),
        ],
        compiler_params=pltpu.CompilerParams(
            collective_id=collective_id, has_side_effects=True, vmem_limit_bytes=VMEM_LIMIT
        ),
        cost_estimate=pl.CostEstimate(flops=0, bytes_accessed=1 << 27, transcendentals=0),
        name="spread_blocks",
    )(parts, small)


def axis_place(axes):
    index, size = 0, 1
    for axis in axes:
        index = index * lax.axis_size(axis) + lax.axis_index(axis)
        size = size * lax.axis_size(axis)
    return index, size


def exchange(piece_for, axes):
    me, n = axis_place(axes)
    got = [(me, piece_for(me))]
    for step in range(1, n):
        piece = piece_for(lax.rem(me + step, n))
        moved = lax.ppermute(piece, axes, [(i, (i + step) % n) for i in range(n)])
        got.append((lax.rem(me + n - step, n), moved))
    return got


def in_order(got):
    out = jnp.zeros((len(got),) + got[0][1].shape, got[0][1].dtype)
    for sender, piece in got:
        out = lax.dynamic_update_index_in_dim(out, piece, sender, 0)
    return out


def together(*values):
    return lax.optimization_barrier(values)


def pick(values, index, dim=0):
    return lax.dynamic_index_in_dim(values, index, dim, keepdims=False)


def spread_parts(values, dim, axis):
    got = exchange(lambda k: pick(values, k, dim).astype(jnp.float16), (axis,))
    return pick(values, got[0][0], dim), [piece for _, piece in got[1:]]


def added(own, pieces):
    for piece in pieces:
        own = own + piece.astype(F32)
    return own


def gather_kernel(low_ref, high_ref, ids_ref, table_ref, out_ref, turned_ref, rows_ref):
    source = pl.program_id(0)

    @pl.when(source == 0)
    def _():
        @pl.loop(0, table_ref.shape[1] // LANES)
        def _(k):
            at = pl.multiple_of(k * LANES, LANES)
            turned_ref[pl.ds(at, LANES), :] = table_ref[:, pl.ds(at, LANES)].T

    low, high = low_ref[source], high_ref[source]
    rows_ref[...] = jnp.zeros_like(rows_ref)

    first, last = low // 8, (high - 1) // 8

    def edge(k):
        base = pl.multiple_of(k * 8, 8)
        for i in range(8):
            place = base + i
            valid = jnp.logical_and(place >= low, place < high)
            row = jnp.where(valid, ids_ref[source, place], 0)
            value = turned_ref[pl.ds(row, 1), :]
            rows_ref[pl.ds(place, 1), :] = jnp.where(valid, value, 0.0)

    @pl.when(high > low)
    def _():
        edge(first)
        edge(last)

    def chunk(k, carry):
        base = pl.multiple_of(k * 8, 8)
        for i in range(8):
            row = ids_ref[source, base + i]
            rows_ref[pl.ds(base + i, 1), :] = turned_ref[pl.ds(row, 1), :]
        return carry

    lax.fori_loop(first + 1, last, chunk, 0)
    out_ref[0] = rows_ref[...].T.astype(BF)


def gather_rows(table, ids, low, high):
    sources, count = ids.shape
    width = table.shape[0]
    return pl.pallas_call(
        gather_kernel,
        out_shape=jax.ShapeDtypeStruct((sources, width, count), BF),
        grid_spec=pltpu.PrefetchScalarGridSpec(
            num_scalar_prefetch=3,
            grid=(sources,),
            in_specs=[
                pl.BlockSpec(table.shape, lambda i, *_: (0, 0), pipeline_mode=pl.Buffered(1))
            ],
            out_specs=pl.BlockSpec((1, width, count), lambda i, *_: (i, 0, 0)),
            scratch_shapes=[
                pltpu.VMEM((table.shape[1], width), F32),
                pltpu.VMEM((count, width), F32),
            ],
        ),
        compiler_params=pltpu.CompilerParams(vmem_limit_bytes=VMEM_LIMIT),
        cost_estimate=pl.CostEstimate(flops=0, bytes_accessed=1 << 27, transcendentals=0),
        name="gather_rows",
    )(low, high, ids, table)


def scatter_kernel(low_ref, high_ref, ids_ref, rows_ref, out_ref, wide_ref, *totals):
    source = pl.program_id(0)

    @pl.when(source == 0)
    def _():
        for total_ref in totals:
            total_ref[...] = jnp.zeros_like(total_ref)

    low, high = low_ref[source], high_ref[source]
    wide_ref[...] = rows_ref[0].astype(F32).T

    first, last = low // 8, (high - 1) // 8

    def edge(k):
        base = pl.multiple_of(k * 8, 8)
        for i in range(8):
            total_ref = totals[i % len(totals)]
            place = base + i
            valid = jnp.logical_and(place >= low, place < high)
            row = jnp.where(valid, ids_ref[source, place], 0)
            addend = jnp.where(valid, wide_ref[pl.ds(place, 1), :], 0.0)
            total_ref[pl.ds(row, 1), :] = total_ref[pl.ds(row, 1), :] + addend

    @pl.when(high > low)
    def _():
        edge(first)

    @pl.when(jnp.logical_and(high > low, last > first))
    def _():
        edge(last)

    def chunk(k, carry):
        base = pl.multiple_of(k * 8, 8)
        for i in range(8):
            total_ref = totals[i % len(totals)]
            row = ids_ref[source, base + i]
            addend = wide_ref[pl.ds(base + i, 1), :]
            total_ref[pl.ds(row, 1), :] = total_ref[pl.ds(row, 1), :] + addend
        return carry

    lax.fori_loop(first + 1, last, chunk, 0)

    @pl.when(source == pl.num_programs(0) - 1)
    def _():
        @pl.loop(0, out_ref.shape[1] // LANES)
        def _(k):
            at = pl.multiple_of(k * LANES, LANES)
            value = totals[0][pl.ds(at, LANES), :]
            for total_ref in totals[1:]:
                value = value + total_ref[pl.ds(at, LANES), :]
            out_ref[:, pl.ds(at, LANES)] = value.T


def scatter_rows(rows, ids, low, high, table_rows):
    sources, width, count = rows.shape
    return pl.pallas_call(
        scatter_kernel,
        out_shape=jax.ShapeDtypeStruct((width, table_rows), F32),
        grid_spec=pltpu.PrefetchScalarGridSpec(
            num_scalar_prefetch=3,
            grid=(sources,),
            in_specs=[pl.BlockSpec((1, width, count), lambda i, *_: (i, 0, 0))],
            out_specs=pl.BlockSpec((width, table_rows), lambda i, *_: (0, 0)),
            scratch_shapes=[pltpu.VMEM((count, width), F32)]
            + [pltpu.VMEM((table_rows, width), F32)] * 2,
        ),
        compiler_params=pltpu.CompilerParams(vmem_limit_bytes=VMEM_LIMIT),
        cost_estimate=pl.CostEstimate(flops=0, bytes_accessed=1 << 27, transcendentals=0),
        name="scatter_rows",
    )(low, high, ids, rows)


def swap_halves(values):
    lane = lax.broadcasted_iota(jnp.int32, values.shape, 1)
    half = HD // 2
    up = pltpu.roll(values, LANES - half, 1)
    down = pltpu.roll(values, half, 1)
    return jnp.where(lax.rem(lane, HD) < half, up, down)


def turn(values, cosine, sine):
    return values * cosine + swap_halves(values) * sine


def turn_back(values, cosine, sine):
    return values * cosine - swap_halves(values) * sine


def attend_kernel(kv_ref, vv_ref, qm_ref, km_ref, vm_ref, cu_ref, su_ref, cm_ref, sm_ref,
                  mask_ref, q_out, ku_out, km_out, att_out, lse_out):
    rows = cm_ref.shape[0]
    wide = (rows, LANES)
    cm, sm = cm_ref[...], sm_ref[...]
    q = turn(jnp.broadcast_to(qm_ref[0:1, :], wide), cm, sm).astype(BF)
    k_m = turn(jnp.broadcast_to(km_ref[0:1, :], wide), cm, sm).astype(BF)
    k_u = turn(kv_ref[...], cu_ref[...], su_ref[...]).astype(BF)
    v_u = vv_ref[...].astype(BF)
    v_m = vm_ref[0:1, :].astype(BF).astype(F32)
    q_out[...] = q
    ku_out[...] = k_u
    km_out[...] = k_m
    mask = mask_ref[0:1, :]
    outs, totals = [], []
    for head in range(LANES // HD):
        part = slice(head * HD, (head + 1) * HD)
        s_u = matmul_nt(q[:, part], k_u[:, part]) * HD ** (-0.5) + mask
        s_m = matmul_nt(q[:, part], k_m[:, part]) * HD ** (-0.5)
        top = jnp.maximum(
            jnp.max(s_u, axis=1, keepdims=True), jnp.max(s_m, axis=1, keepdims=True)
        )
        e_u = jnp.exp(s_u - top)
        e_m = jnp.exp(s_m - top)
        total = jnp.sum(e_u, axis=1, keepdims=True) + jnp.sum(e_m, axis=1, keepdims=True)
        inverse = 1.0 / total
        p_u = (e_u * inverse).astype(BF)
        p_m = (e_m * inverse).astype(BF).astype(F32)
        mixed = matmul(p_u, v_u[:, part]) + jnp.sum(p_m, axis=1, keepdims=True) * v_m[:, part]
        outs.append(mixed)
        totals.append(top + jnp.log(total))
    att_out[...] = jnp.concatenate(outs, axis=1).astype(BF)
    lse_out[0] = jnp.concatenate(totals, axis=1)


def attend(kv_u, qkv_m, tables, mask):
    count, rows = kv_u.shape[0], tables[2].shape[0]
    blocks = D // LANES
    per = LANES // HD
    row = lambda offset: pl.BlockSpec((qkv_m.shape[0], LANES), lambda i: (0, offset * blocks + i))
    column = lambda n: pl.BlockSpec((n, LANES), lambda i: (0, i))
    whole = lambda a: pl.BlockSpec(a.shape, lambda i: (0, 0))
    return pl.pallas_call(
        attend_kernel,
        grid=(blocks,),
        out_shape=[
            jax.ShapeDtypeStruct((rows, D), BF),
            jax.ShapeDtypeStruct((count, D), BF),
            jax.ShapeDtypeStruct((rows, D), BF),
            jax.ShapeDtypeStruct((rows, D), BF),
            jax.ShapeDtypeStruct((blocks, rows, per), F32),
        ],
        in_specs=[
            pl.BlockSpec((count, LANES), lambda i: (0, i)),
            pl.BlockSpec((count, LANES), lambda i: (0, blocks + i)),
            row(0), row(1), row(2),
            *[whole(t) for t in tables],
            whole(mask),
        ],
        out_specs=[column(rows), column(count), column(rows), column(rows),
                   pl.BlockSpec((1, rows, per), lambda i: (i, 0, 0))],
        compiler_params=pltpu.CompilerParams(vmem_limit_bytes=VMEM_LIMIT),
        cost_estimate=pl.CostEstimate(
            flops=2 * 3 * rows * count * D, bytes_accessed=12 * rows * D,
            transcendentals=2 * rows * count * H,
        ),
        name="attend",
    )(kv_u, kv_u, qkv_m, qkv_m, qkv_m, *tables, mask)


def attend_back_kernel(q_ref, ku_ref, km_ref, vv_ref, vm_ref, cu_ref, su_ref, cm_ref, sm_ref,
                       mask_ref, lse_ref, datt_ref, dk_out, dv_out, dm_out):
    q, k_u, k_m, datt = q_ref[...], ku_ref[...], km_ref[...], datt_ref[...]
    v_u = vv_ref[...].astype(BF)
    v_m = vm_ref[0:1, :].astype(BF).astype(F32)
    datt_f = datt.astype(F32)
    mask = mask_ref[0:1, :]
    scale = HD ** (-0.5)
    dq, dk_u, dk_m, dv_u, dv_m = [], [], [], [], []
    for head in range(LANES // HD):
        part = slice(head * HD, (head + 1) * HD)
        lse = lse_ref[0, :, head : head + 1]
        p_u = jnp.exp(matmul_nt(q[:, part], k_u[:, part]) * scale + mask - lse)
        p_m = jnp.exp(matmul_nt(q[:, part], k_m[:, part]) * scale - lse)
        dp_u = matmul_nt(datt[:, part], v_u[:, part])
        dp_m = jnp.sum(datt_f[:, part] * v_m[:, part], axis=1, keepdims=True)
        inner = jnp.sum(p_u * dp_u, axis=1, keepdims=True) + dp_m * jnp.sum(
            p_m, axis=1, keepdims=True
        )
        ds_u = (p_u * (dp_u - inner) * scale).astype(BF)
        ds_m = (p_m * ((dp_m - inner) * scale)).astype(BF)
        dq.append(matmul(ds_u, k_u[:, part]) + matmul(ds_m, k_m[:, part]))
        dk_u.append(matmul_tn(ds_u, q[:, part]))
        dk_m.append(matmul_tn(ds_m, q[:, part]))
        dv_u.append(matmul_tn(p_u.astype(BF), datt[:, part]))
        mass = jnp.sum(p_m.astype(BF).astype(F32), axis=1, keepdims=True)
        dv_m.append(jnp.sum(mass * datt_f[:, part], axis=0, keepdims=True))
    cm, sm = cm_ref[...], sm_ref[...]
    join = lambda parts: jnp.concatenate(parts, axis=1)
    low = lambda a: a.astype(BF).astype(F32)
    dk_out[...] = turn_back(join(dk_u), cu_ref[...], su_ref[...]).astype(BF)
    dv_out[...] = join(dv_u).astype(BF)
    dq_sum = jnp.sum(low(turn_back(join(dq), cm, sm)), axis=0, keepdims=True)
    dk_sum = jnp.sum(low(turn_back(join(dk_m), cm, sm)), axis=0, keepdims=True)
    filler = jnp.zeros((5, LANES), F32)
    dm_out[...] = jnp.concatenate([dq_sum, dk_sum, join(dv_m), filler], axis=0)


def attend_back(q, k_u, k_m, kv_u, qkv_m, tables, mask, lse, datt):
    count, rows = kv_u.shape[0], q.shape[0]
    blocks = D // LANES
    per = LANES // HD
    column = lambda n: pl.BlockSpec((n, LANES), lambda i: (0, i))
    whole = lambda a: pl.BlockSpec(a.shape, lambda i: (0, 0))
    return pl.pallas_call(
        attend_back_kernel,
        grid=(blocks,),
        out_shape=[
            jax.ShapeDtypeStruct((count, D), BF),
            jax.ShapeDtypeStruct((count, D), BF),
            jax.ShapeDtypeStruct((8, D), F32),
        ],
        in_specs=[
            column(rows), column(count), column(rows),
            pl.BlockSpec((count, LANES), lambda i: (0, blocks + i)),
            pl.BlockSpec((qkv_m.shape[0], LANES), lambda i: (0, 2 * blocks + i)),
            *[whole(t) for t in tables],
            whole(mask),
            pl.BlockSpec((1, rows, per), lambda i: (i, 0, 0)),
            column(rows),
        ],
        out_specs=[column(count), column(count), column(8)],
        compiler_params=pltpu.CompilerParams(vmem_limit_bytes=VMEM_LIMIT),
        cost_estimate=pl.CostEstimate(
            flops=2 * 8 * rows * count * D, bytes_accessed=14 * rows * D,
            transcendentals=2 * rows * count * H,
        ),
        name="attend_back",
    )(q, k_u, k_m, kv_u, qkv_m, *tables, mask, lse, datt)


def tile_of(segments):
    return max(16, 1024 // segments)


def logits_kernel(places_ref, w_ref, target_ref, *refs):
    blocks, (e_ref, stats_ref, x_ref, logits_ref) = refs[:-4], refs[-4:]
    segments, _, width = w_ref.shape
    rows = x_ref.shape[0]
    per = blocks[0].shape[0] // rows
    step = pl.program_id(0)
    for number, block in enumerate(blocks):

        @pl.when(step // per == number)
        def _(block=block):
            x_ref[...] = block[pl.ds(pl.multiple_of(lax.rem(step, per) * rows, rows), rows), :]

    x = x_ref[...]
    starts = list(range(0, width - width % 768 or width, 768))
    best = None
    for y in range(segments):
        for at, end in zip(starts, starts[1:] + [width]):
            logits = matmul(x, w_ref[y, :, at:end])
            logits_ref[:, y * width + at : y * width + end] = logits
            for g in range(0, end - at, LANES):
                part = logits[:, g : g + LANES]
                best = part if best is None else jnp.maximum(best, part)
    lane = lax.broadcasted_iota(jnp.int32, (ROWS, LANES), 1)
    peaks = jnp.max(best, axis=1, keepdims=True)
    for r in range(0, rows, ROWS):
        peak = peaks[r : r + ROWS]
        top = jnp.broadcast_to(peak, (ROWS, LANES))
        place = target_ref[r : r + ROWS, :] - lane
        total = jnp.zeros((ROWS, LANES), F32)
        chosen = jnp.zeros((ROWS, LANES), F32)
        for y in range(segments):
            for at in range(0, width, LANES):
                column = y * width + at
                logits = logits_ref[r : r + ROWS, column : column + LANES]
                e = jnp.exp(logits - top)
                total = total + e
                chosen = chosen + jnp.where(place == column, logits, 0.0)
                e_ref[y, r : r + ROWS, at : at + LANES] = e.astype(BF)
        sums = [jnp.sum(a, axis=1, keepdims=True) for a in (total, chosen)]
        stats_ref[r : r + ROWS, :] = jnp.concatenate([peak, *sums, peak], axis=1)


def head_logits(blocks, weights, targets, places):
    count = targets.shape[0]
    segments, _, width = weights.shape
    tile = tile_of(segments)
    per = blocks[0].shape[0] // tile

    def placed(i, places):
        return (places[i // per] * per + lax.rem(i, per), 0)

    return pl.pallas_call(
        logits_kernel,
        out_shape=[
            jax.ShapeDtypeStruct((segments, count, width), BF),
            jax.ShapeDtypeStruct((count, 4), F32),
            jax.ShapeDtypeStruct((count, D), BF),
        ],
        grid_spec=pltpu.PrefetchScalarGridSpec(
            num_scalar_prefetch=1,
            grid=(count // tile,),
            in_specs=[
                pl.BlockSpec(weights.shape, lambda i, p: (0, 0, 0), pipeline_mode=pl.Buffered(1)),
                pl.BlockSpec((tile, 1), placed),
            ] + [
                pl.BlockSpec(b.shape, lambda i, p: (0, 0), pipeline_mode=pl.Buffered(1))
                for b in blocks
            ],
            out_specs=[
                pl.BlockSpec((segments, tile, width), lambda i, p: (0, i, 0)),
                pl.BlockSpec((tile, 4), placed),
                pl.BlockSpec((tile, D), lambda i, p: (i, 0)),
            ],
            scratch_shapes=[pltpu.VMEM((tile, segments * width), F32)],
        ),
        compiler_params=pltpu.CompilerParams(vmem_limit_bytes=VMEM_LIMIT),
        cost_estimate=pl.CostEstimate(
            flops=2 * count * D * segments * width,
            bytes_accessed=2 * count * segments * width,
            transcendentals=count * segments * width,
        ),
        name="head_logits",
    )(places, weights, targets, *blocks)


def rows_back_kernel(places_ref, e_ref, w_ref, target_ref, factor_ref, d_ref, dx_ref):
    segments, _, width = w_ref.shape
    rows = e_ref.shape[1]
    lane = lax.broadcasted_iota(jnp.int32, (ROWS, LANES), 1)
    wide = lambda a: jnp.broadcast_to(a, (ROWS, LANES))
    total = None
    for y in range(segments):
        for r in range(0, rows, ROWS):
            place = target_ref[r : r + ROWS, :] - (lane + y * width)
            factor = wide(factor_ref[r : r + ROWS, 0:1])
            special = wide(factor_ref[r : r + ROWS, 1:2])
            for at in range(0, width, LANES):
                e = e_ref[y, r : r + ROWS, at : at + LANES].astype(F32)
                d_ref[y, r : r + ROWS, at : at + LANES] = jnp.where(
                    place == at, special, e * factor).astype(BF)
        part = matmul_nt(d_ref[y], w_ref[y])
        total = part if total is None else total + part
    dx_ref[...] = total.astype(BF)


def head_rows_back(e, weights, targets, factors, places):
    segments, count, width = e.shape
    tile = tile_of(segments)
    per = count // places.shape[0] // tile

    def placed(i, places):
        return (places[i // per] * per + lax.rem(i, per), 0)

    return pl.pallas_call(
        rows_back_kernel,
        out_shape=[
            jax.ShapeDtypeStruct(e.shape, BF),
            jax.ShapeDtypeStruct((count, D), BF),
        ],
        grid_spec=pltpu.PrefetchScalarGridSpec(
            num_scalar_prefetch=1,
            grid=(count // tile,),
            in_specs=[
                pl.BlockSpec((segments, tile, width), lambda i, p: (0, i, 0)),
                pl.BlockSpec(weights.shape, lambda i, p: (0, 0, 0), pipeline_mode=pl.Buffered(1)),
                pl.BlockSpec((tile, 1), placed),
                pl.BlockSpec((tile, 2), placed),
            ],
            out_specs=[
                pl.BlockSpec((segments, tile, width), lambda i, p: (0, i, 0)),
                pl.BlockSpec((tile, D), placed),
            ],
        ),
        input_output_aliases={1: 0},
        compiler_params=pltpu.CompilerParams(vmem_limit_bytes=VMEM_LIMIT),
        cost_estimate=pl.CostEstimate(
            flops=2 * count * D * segments * width,
            bytes_accessed=4 * count * segments * width,
            transcendentals=0,
        ),
        name="head_rows_back",
    )(places, e, weights, targets, factors)


def layer_norm(values):
    center = values - jnp.mean(values, axis=-1, keepdims=True)
    spread = jnp.mean(center * center, axis=-1, keepdims=True)
    inv_std = lax.rsqrt(spread + NORM_EPS)
    return (center * inv_std, inv_std)


def norm_back(d_normed, normed, inv_std):
    return inv_std * (
        d_normed
        - jnp.mean(d_normed, axis=-1, keepdims=True)
        - normed * jnp.mean(d_normed * normed, axis=-1, keepdims=True)
    )


def time_features(time_index, width, steps):
    t_value = (time_index.astype(F32) + 1.0) / steps
    half_width = width // 2
    frequencies = jnp.exp(-math.log(10000.0) * jnp.arange(half_width, dtype=F32) / half_width)
    angles = 1000.0 * t_value[:, None] * frequencies[None, :]
    return jax.nn.silu(jnp.concatenate([jnp.cos(angles), jnp.sin(angles)], axis=1))


def rope_rows(positions):
    half = HD // 2
    inverse = jnp.exp(-math.log(10000.0) * jnp.arange(half, dtype=F32) * 2.0 / HD)
    angles = positions.astype(F32)[:, None] * inverse[None, :]
    cosine, sine = jnp.cos(angles), jnp.sin(angles)
    return (jnp.tile(cosine, (1, LANES // half)),
            jnp.tile(jnp.concatenate([-sine, sine], axis=1), (1, LANES // HD)))


def gelu_tanh(values):
    return jax.nn.gelu(values, approximate=True)


def adam_step(weight, first, second, ema_copy, gradient, step_value, learn_rate, decay_rate):
    first_new = BETA_ONE * first + (1.0 - BETA_ONE) * gradient
    second_new = BETA_TWO * second + (1.0 - BETA_TWO) * gradient * gradient
    first_hat = first_new / (1.0 - BETA_ONE**step_value)
    second_hat = second_new / (1.0 - BETA_TWO**step_value)
    weight_new = weight - learn_rate * (
        first_hat / (jnp.sqrt(second_hat) + ADAM_EPS) + decay_rate * weight
    )
    ema_rate = jnp.minimum(EMA_DECAY, (1.0 + step_value) / (10.0 + step_value))
    ema_new = ema_rate * ema_copy + (1.0 - ema_rate) * weight_new
    return (first_new, second_new, weight_new, ema_new)


def split3(row):
    parts, rest = [], row
    for _ in range(3):
        part = lax.reduce_precision(rest, 8, 7)
        parts.append(part.astype(BF))
        rest = rest - part
    return parts


def local(sizes, token_ids, scored, lengths, times, step_count, layer_w, layer_m, layer_v, layer_ema,
          ada_w, ada_m, ada_v, ada_ema, gains_w, gains_m, gains_v, gains_ema,
          embed_w, embed_m, embed_v, embed_ema, head_w, head_m, head_v, head_ema):
    nz, nx, ny, nc = sizes
    n = nz * nx * ny * nc
    length, score_count = token_ids.shape[1], scored.shape[1]
    free_count = length - score_count
    total_rows = n * score_count
    table_rows, table_width = embed_w.shape
    iz, ix, iy, ic = [lax.axis_index(a) for a in ALL]
    vocab_index = iy * nc + ic
    vocab_start = vocab_index * table_rows
    me = (iz * nx + ix) * (ny * nc) + vocab_index

    tokens, masked = token_ids[0], scored[0]
    positions = jnp.arange(length, dtype=jnp.int32)
    hits = masked[:, None] == positions[None, :]
    is_masked = jnp.any(hits, axis=0)
    targets = jnp.sum(jnp.where(hits, tokens[None, :], 0), axis=1)
    keys = jnp.where(is_masked, n * V, (tokens // table_rows) * length + positions)
    rank = jnp.sum((keys[None, :] < keys[:, None]).astype(jnp.int32), axis=1)
    rank = jnp.where(is_masked, length, rank)
    slots = rank[None, :] == jnp.arange(free_count, dtype=jnp.int32)[:, None]
    free_tokens = jnp.sum(jnp.where(slots, tokens[None, :], 0), axis=1)
    free_positions = jnp.sum(jnp.where(slots, positions[None, :], 0), axis=1)

    ints = jnp.concatenate([free_tokens.reshape(-1, LANES), targets.reshape(-1, LANES),
                            jnp.broadcast_to(times[:, None], (1, LANES))], axis=0)
    ints = jnp.pad(ints, ((0, -ints.shape[0] % 8), (0, 0)))
    gain_part = jnp.pad(gains_w.astype(BF).astype(F32),
                        ((0, 8 - gains_w.shape[0]), (0, LANES - gains_w.shape[1])))
    ints_all, gains_all = share(ALL, 0, ints, gain_part)
    ints_all = ints_all.reshape((n,) + ints.shape)
    gains_all = gains_all.reshape((n,) + gain_part.shape)

    block_low = jnp.concatenate(
        [layer_w.astype(BF), ada_w.astype(BF).reshape(layer_w.shape[0], -1)], axis=1)
    block_low, head_low, ints_all = together(block_low, head_w.astype(BF), ints_all)
    layer_all = lax.all_gather(block_low, ALL, axis=0, tiled=True)

    piece_for = lambda k: lax.dynamic_slice_in_dim(head_low, k * SEGMENT, SEGMENT, 1)
    head_parts = exchange(piece_for, ("z",))

    gains = jnp.moveaxis(gains_all[:, : gains_w.shape[0], : gains_w.shape[1]], 0, 1).reshape(4, D)
    free_rows = free_count // LANES
    score_rows = score_count // LANES
    all_tokens = ints_all[:, :free_rows].reshape(nz * nx, ny * nc, free_count)
    all_targets = ints_all[:, free_rows : free_rows + score_rows].reshape(
        nz, nx, ny, nc, score_count)
    all_times = ints_all[:, free_rows + score_rows, 0]

    wanted = jnp.swapaxes(all_tokens, 0, 1).reshape(n, free_count)
    owners = wanted // table_rows
    low = jnp.sum((owners < vocab_index).astype(jnp.int32), axis=1)
    high = jnp.sum((owners <= vocab_index).astype(jnp.int32), axis=1)
    local_ids = wanted - vocab_start
    looked_up = gather_rows(embed_w.T, local_ids, low, high)
    looked_up = looked_up.reshape((ny, nc, nz * nx) + looked_up.shape[1:])
    x0_u = fetch_blocks(sizes, looked_up, 3).reshape(D, free_count).T.astype(F32)
    senders = [sender for sender, _ in head_parts]
    x0_u, *pieces = together(x0_u, *[piece for _, piece in head_parts])
    head_part = in_order(list(zip(senders, pieces))).reshape(-1, SEGMENT)

    mask_row = gains[3:4]
    condition = time_features(times, C, TSTEPS).astype(BF)
    modulation = matmul(condition, layer_all[:, layer_w.shape[1] :].reshape(C, 6 * D))
    shift_a, scale_a, gate_a, shift_m, scale_m, gate_m = [
        modulation[:, i * D : (i + 1) * D] for i in range(6)]
    normed_u, inv_u = layer_norm(x0_u)
    a_u = (normed_u * gains[0:1] * (1.0 + scale_a) + shift_a).astype(BF)
    normed_0, inv_0 = layer_norm(mask_row)
    a_m = (normed_0 * gains[0:1] * (1.0 + scale_a) + shift_a).astype(BF)
    w_qkv, w_o = layer_all[:, : 3 * D], layer_all[:, 3 * D : 4 * D]
    w_up, w_down = layer_all[:, 4 * D : 4 * D + FF], layer_all[:, 4 * D + FF : 4 * D + 2 * FF]
    qkv_m = matmul(jnp.broadcast_to(a_m, (16, D)), w_qkv)
    kv_u = matmul(a_u, w_qkv[:, D:])
    tables = (*rope_rows(free_positions), *rope_rows(masked))
    mask = jnp.where(free_positions[None, :] < lengths[:, None], 0.0, -1e30)
    mask = jnp.broadcast_to(mask, (8, free_count)).astype(F32)
    q, k_u, k_m, att, lse_a = attend(kv_u, qkv_m, tables, mask)
    branch = matmul(att, w_o)
    x1 = mask_row + gate_a * branch
    normed_m, inv_m = layer_norm(x1)
    b = (normed_m * gains[1:2] * (1.0 + scale_m) + shift_m).astype(BF)
    pre = matmul(b, w_up)
    act = gelu_tanh(pre).astype(BF)
    mlp = matmul_nt(act, w_down)
    x2 = x1 + gate_m * mlp
    normed_f, inv_f = layer_norm(x2)
    final = (normed_f * gains[2:3]).astype(BF)

    final_turned = jnp.swapaxes(final.reshape(score_count, nz, nx, -1), 1, 2).reshape(score_count, D)
    head_all = lax.all_gather(head_part, ("y", "x"), axis=0, tiled=True).reshape(ny, D, SEGMENT)
    group = nz * nc * score_count
    blocks, places = [], []
    for sender, piece in exchange(lambda k: final_turned, ("z",)):
        for place, part in exchange(lambda k: piece, ("c",)):
            blocks.append(part)
            places.append(sender * nc + place)
    places = jnp.stack(places).astype(jnp.int32)
    row_targets = pick(jnp.moveaxis(jnp.moveaxis(all_targets, 3, 1), (2, 3), (0, 1)).reshape(
        nx * ny, group), ix * ny + iy)
    row_times = pick(jnp.moveaxis(jnp.moveaxis(all_times.reshape(nz, nx, ny, nc), 3, 1), (2, 3), (0, 1))
                     .reshape(nx * ny, nz * nc), ix * ny + iy)
    row_weights = jnp.repeat(TSTEPS / (row_times.astype(F32) + 1.0) / total_rows, score_count)
    owner, within = row_targets // table_rows, row_targets % table_rows
    owned = jnp.logical_and(owner % nc == ic, within // SEGMENT == iz)
    column_of = jnp.where(owned, (owner // nc) * SEGMENT + within % SEGMENT, -1)[:, None]
    e, stats, rows = head_logits(blocks, head_all, column_of, places)
    top = stats[:, 0]
    every = share(("z", "c"), 4, stats.T.reshape(4, -1, LANES))[0].reshape(nz * nc, 4, group)
    best = jnp.max(every[:, 0], axis=0)
    log_total = best + jnp.log(jnp.sum(every[:, 1] * jnp.exp(every[:, 0] - best), axis=0))
    chosen = jnp.sum(every[:, 2], axis=0)
    own_start = (iz * nc + ic) * score_count
    own_terms = lax.dynamic_slice_in_dim(row_weights * (log_total - chosen), own_start, score_count)
    loss_part = jnp.sum(own_terms)
    factors = jnp.stack([row_weights * jnp.exp(top - log_total),
                         row_weights * (jnp.exp(chosen - log_total) - 1.0)], axis=1)
    d_logits, d_rows = head_rows_back(e, head_all, column_of, factors, places)
    d_final = lax.psum_scatter(d_rows, ("z", "c"), scatter_dimension=0, tiled=True)

    bound = D**0.5 * jnp.max(jnp.abs(gains[2])) * 1.02
    bound = bound * score_count * jnp.sum(TSTEPS / (all_times.astype(F32) + 1.0) / total_rows)
    enlarge = 60000.0 / jnp.maximum(bound, 1e-30)
    d_head = jnp.einsum("rd,yrv->ydv", rows, d_logits, preferred_element_type=F32) * enlarge
    d_final, d_head = together(d_final, d_head.reshape(ny, nx, nz, -1, SEGMENT))
    cut = nz // 2
    own_x, from_x = spread_parts(d_head[:, :, :cut], 1, "x")
    own_y, from_y = spread_parts(d_head[:, :, cut:], 0, "y")
    d_final = d_final.astype(F32)
    d_final = jnp.swapaxes(d_final.reshape(score_count, nx, nz, -1), 1, 2).reshape(score_count, D)

    d_gain_f = jnp.sum(d_final * normed_f, axis=0)
    d_x2 = norm_back(d_final * gains[2:3], normed_f, inv_f)
    d_gate_m = jnp.sum(d_x2 * mlp, axis=0)
    d_out = (d_x2 * gate_m).astype(BF)
    d_down = matmul_tn(d_out, act)
    d_act = matmul(d_out, w_down)
    d_pre = jax.vjp(gelu_tanh, pre)[1](d_act)[0].astype(BF)
    d_up = matmul_tn(b, d_pre)
    d_b = matmul_nt(d_pre, w_up)
    d_shift_m = jnp.sum(d_b, axis=0)
    product = jnp.sum(d_b * normed_m, axis=0)
    d_scale_m = product * gains[1]
    d_gain_m = product * (1.0 + scale_m[0])
    d_x1 = d_x2 + norm_back(d_b * ((1.0 + scale_m) * gains[1:2]), normed_m, inv_m)
    d_gate_a = jnp.sum(d_x1 * branch, axis=0)
    d_branch = (d_x1 * gate_a).astype(BF)
    d_wout = matmul_tn(att, d_branch)
    d_att, *from_xy = together(matmul_nt(d_branch, w_o).astype(BF), *from_x, *from_y)
    def over_cores(gradient):
        width = gradient.shape[1]
        parts = jnp.transpose(gradient.reshape(nz, nx, ny, nc, -1, width), (3, 1, 2, 0, 4, 5))
        parts = parts.reshape(nc, -1, width)
        got = exchange(lambda k: pick(parts, k), ("c",))
        return sum(piece.astype(F32) for _, piece in got).astype(BF)

    over_plane = lambda a: lax.psum_scatter(a, ("x", "y"), scatter_dimension=0, tiled=True)
    own_xy, from_xy = (
        spread_parts(added(own_x, from_xy[: nx - 1]), 0, "y"),
        spread_parts(added(own_y, from_xy[nx - 1 :]), 0, "x"),
    )
    d_k, d_v, d_qkv_m = attend_back(q, k_u, k_m, kv_u, qkv_m, tables, mask, lse_a, d_att)
    d_k, *arrivals = together(d_k, *own_xy[1], *from_xy[1])
    head_sum = jnp.concatenate(
        [added(own_xy[0], arrivals[: ny - 1]), added(from_xy[0], arrivals[ny - 1 :])], axis=0)
    d_k, head_sum = together(d_k, head_sum)
    head_own, head_parts = spread_parts(head_sum, 0, "z")
    d_kv = jnp.concatenate([d_k, d_v], axis=1)
    d_wkv = matmul_tn(a_u, d_kv)
    d_row_m = d_qkv_m[:3].reshape(3 * D)
    d_a_u = matmul_nt(d_kv, w_qkv[:, D:])
    d_parts = matmul_nt(jnp.pad(jnp.stack(split3(d_row_m)), ((0, 13), (0, 0))), w_qkv)
    d_a_m = jnp.sum(d_parts[:3], axis=0, keepdims=True)
    d_shift_a = jnp.sum(d_a_u, axis=0) + d_a_m[0]
    product = jnp.sum(d_a_u * normed_u, axis=0) + (d_a_m * normed_0)[0]
    d_scale_a = product * gains[0]
    d_gain_a = product * (1.0 + scale_a[0])
    scaling = (1.0 + scale_a) * gains[0:1]
    d_x0_u = norm_back(d_a_u * scaling, normed_u, inv_u)
    d_mask = jnp.sum(d_x1, axis=0) + norm_back(d_a_m * scaling, normed_0, inv_0)[0]

    chip_sum = over_cores(jnp.concatenate(
        [d_wkv.astype(BF), d_wout.astype(BF), d_up.astype(BF), d_down.astype(BF)], axis=1))

    small = jnp.concatenate([d_shift_a, d_scale_a, d_gate_a, d_shift_m, d_scale_m, d_gate_m,
                             d_gain_a, d_gain_m, d_gain_f, d_mask,
                             a_m[0].astype(F32), d_row_m, jnp.broadcast_to(loss_part, (LANES,))])
    small = small.reshape(-1, LANES)
    count_small = small.shape[0]
    small = jnp.pad(small, ((0, -count_small % 8), (0, 0)))

    sent = d_x0_u.astype(BF).T.reshape(nz * nx, table_width, free_count)
    sent, chip_sum = together(sent, chip_sum)
    plane_sum = over_plane(chip_sum)
    sent, *head_parts = together(sent, *head_parts)

    arrived, small_all = spread_blocks(sizes, sent, small, 5)
    arrived, plane_sum = together(arrived, plane_sum)
    plane_sum = plane_sum.reshape(nz, -1, plane_sum.shape[1])
    block_parts = [p for _, p in exchange(lambda k: pick(plane_sum, k), ("z",))]
    g_embed = scatter_rows(arrived.reshape(n, table_width, free_count), local_ids, low, high,
                           table_rows)
    together_now = together(g_embed, small_all, head_own, *head_parts, *block_parts)
    g_embed, small_all, head_own = together_now[:3]
    head_parts, block_parts = together_now[3 : 2 + nz], together_now[2 + nz :]
    small_all = small_all.reshape((n,) + small.shape)
    small_all = small_all[:, :count_small].reshape(n, -1)
    d_mod_all = small_all[:, : 6 * D]
    d_gains = jnp.sum(small_all[:, 6 * D : 10 * D], axis=0).reshape(4, D)
    g_gains = lax.dynamic_slice_in_dim(d_gains, me * gains_w.shape[1], gains_w.shape[1], 1)
    total_loss = jnp.sum(small_all[:, 14 * D])
    condition_all = time_features(all_times, C, TSTEPS).astype(BF).astype(F32)
    condition_rows = lax.dynamic_slice_in_dim(condition_all, me * ada_w.shape[0], ada_w.shape[0], 1)
    exact = lambda a, b: jnp.einsum("nr,nc->rc", a, b, precision=lax.Precision.HIGHEST)
    g_ada = exact(condition_rows, d_mod_all)
    a_rows = lax.dynamic_slice_in_dim(small_all[:, 10 * D : 11 * D], me * layer_w.shape[0],
                                      layer_w.shape[0], 1)
    g_outer = exact(a_rows, small_all[:, 11 * D : 14 * D])

    g_rest = sum(p.astype(F32) for p in block_parts)
    g_layer = jnp.concatenate(
        [g_outer[:, :D], g_outer[:, D:] + g_rest[:, : 2 * D], g_rest[:, 2 * D :]], axis=1)

    segments = []
    for k in range(nz):
        segment = head_own
        for step, piece in enumerate(head_parts, 1):
            segment = jnp.where(lax.rem(iz + nz - step, nz) == k, piece.astype(F32), segment)
        segments.append(segment)
    g_head = jnp.concatenate(segments, axis=1) / enlarge

    squares = sum(jnp.sum(g * g) for g in (g_layer, g_ada, g_gains, g_embed, g_head))
    squares_all = share(ALL, 2, jnp.broadcast_to(squares, (8, LANES)))[0]
    grad_norm = jnp.sqrt(jnp.sum(squares_all[..., 0, 0]))
    factor = jnp.minimum(1.0, CLIP_NORM / grad_norm)
    step_value = step_count[0].astype(F32)
    updates = (
        (layer_w, layer_m, layer_v, layer_ema, g_layer),
        (ada_w, ada_m, ada_v, ada_ema, g_ada),
        (gains_w, gains_m, gains_v, gains_ema, g_gains),
        (embed_w.T, embed_m.T, embed_v.T, embed_ema.T, g_embed),
        (head_w, head_m, head_v, head_ema, g_head),
    )
    results = []
    for (w, m, v, ema, g), rate, decay in zip(updates, LEARN_RATES, WEIGHT_DECAYS):
        results.extend(adam_step(w, m, v, ema, g * factor, step_value, rate, decay))
    results[12:16] = [a.T for a in results[12:16]]
    return (total_loss, grad_norm, *results)


def solution(mesh):
    dp, vocab = mesh.shape["dp"], mesh.shape["vocab"]
    nz, nc = V // vocab // SEGMENT, 2
    sizes = (nz, dp // nz, vocab // nc, nc)
    fine = Mesh(mesh.devices.reshape(sizes), ALL)
    rows_all, columns_all = P(ALL, None), P(None, ALL)
    table, head = P(("y", "c"), ("z", "x")), P(("z", "x"), ("y", "c"))
    weights = [rows_all] * 8 + [columns_all] * 4 + [table] * 4 + [head] * 4
    return jax.shard_map(
        functools.partial(local, sizes),
        mesh=fine,
        in_specs=(rows_all, rows_all, P(ALL), P(ALL), P(), *weights),
        out_specs=(P(), P(), *weights),
        check_vma=False,
    )
```

```python
import functools
import math

import jax
import jax.numpy as jnp
from jax import lax
from jax.experimental import pallas as pl
from jax.experimental.pallas import tpu as pltpu
from jax.sharding import Mesh, PartitionSpec as P

D = 768
H = 12
HD = 64
FF = 3072
V = 51200
C = 128
TSTEPS = 20
SEGMENT = 3200
LANES = 128
ROWS = 64

NORM_EPS = 1e-05
CLIP_NORM = 0.05
BETA_ONE = 0.9
BETA_TWO = 0.95
ADAM_EPS = 1e-08
EMA_DECAY = 0.9999
LEARN_RATES = (0.03, 0.1, 0.1, 0.5, 0.05)
WEIGHT_DECAYS = (0.01, 0.01, 0.0, 0.01, 0.01)

ALL = ("z", "x", "y", "c")
BF = jnp.bfloat16
F32 = jnp.float32
MESH = pl.DeviceIdType.MESH
VMEM_LIMIT = 60 * 1024 * 1024


def dot(a, b, contract):
    return lax.dot_general(a, b, ((contract[0], contract[1]), ((), ())), preferred_element_type=F32)


def matmul(a, b):
    return dot(a, b, ((1,), (0,)))


def matmul_nt(a, b):
    return dot(a, b, ((1,), (1,)))


def matmul_tn(a, b):
    return dot(a, b, ((0,), (0,)))


def neighbours(axes, sizes):
    found = []
    for place, (axis, size) in enumerate(zip(axes, sizes)):
        for step in range(1, size):
            found.append((place, step, {axis: lax.rem(lax.axis_index(axis) + step, size)}))
    return found


def meet(devices):
    barrier = pltpu.get_barrier_semaphore()
    for device in devices:
        pl.semaphore_signal(barrier, inc=1, device_id=device, device_id_type=MESH)
    pl.semaphore_wait(barrier, len(devices))


def share_kernel(axes, sizes, count, *refs):
    ins, outs = refs[:count], refs[count : 2 * count]
    send, recv, near = refs[2 * count :]
    index = tuple(lax.axis_index(a) for a in axes)
    peers = neighbours(axes, sizes)
    meet([device for _, _, device in peers])
    for i in range(count):
        pltpu.make_async_copy(ins[i], outs[i].at[index], near.at[i]).start()
    for i in range(count):
        pltpu.make_async_copy(ins[i], outs[i].at[index], near.at[i]).wait()
    for place in range(len(axes)):
        view = (slice(None),) * place + index[place:]
        copies = []
        for number, (at, _, device) in enumerate(peers):
            if at == place:
                for i in range(count):
                    copies.append(
                        pltpu.make_async_remote_copy(
                            src_ref=outs[i].at[view],
                            dst_ref=outs[i].at[view],
                            send_sem=send.at[i, number],
                            recv_sem=recv.at[i, number],
                            device_id=device,
                            device_id_type=MESH,
                        )
                    )
        for copy in copies:
            copy.start()
        for copy in copies:
            copy.wait()


def share(axes, collective_id, *arrays):
    sizes = tuple(lax.axis_size(a) for a in axes)
    count, peers = len(arrays), sum(sizes) - len(sizes)
    return pl.pallas_call(
        functools.partial(share_kernel, axes, sizes, count),
        out_shape=[jax.ShapeDtypeStruct(sizes + a.shape, a.dtype) for a in arrays],
        in_specs=[pl.BlockSpec(memory_space=pltpu.VMEM)] * count,
        out_specs=[pl.BlockSpec(memory_space=pltpu.VMEM)] * count,
        scratch_shapes=[
            pltpu.SemaphoreType.DMA((count, peers)),
            pltpu.SemaphoreType.DMA((count, peers)),
            pltpu.SemaphoreType.DMA((count,)),
        ],
        compiler_params=pltpu.CompilerParams(
            collective_id=collective_id, has_side_effects=True
        ),
        name=f"share{collective_id}",
    )(*arrays)


def remote(src, dst, send, recv, device):
    return pltpu.make_async_remote_copy(
        src_ref=src, dst_ref=dst, send_sem=send, recv_sem=recv, device_id=device,
        device_id_type=MESH,
    )


def run_all(copies):
    for copy in copies:
        copy.start()
    for copy in copies:
        copy.wait()


def block_peer(sizes, step):
    nz, nx = sizes[:2]
    me = lax.axis_index("z") * nx + lax.axis_index("x")
    peer = lax.rem(me + step, nz * nx)
    return me, peer, {"z": peer // nx, "x": lax.rem(peer, nx)}


def fetch_kernel(sizes, in_ref, out_ref, from_c, from_y, half, total, sems_c, sems_y, sems_b):
    nz, nx, ny, nc = sizes
    blocks = nz * nx
    iy, ic = lax.axis_index("y"), lax.axis_index("c")
    along_y = [d for _, _, d in neighbours(("y",), (ny,))]
    along_c = [d for _, _, d in neighbours(("c",), (nc,))]
    along_b = [block_peer(sizes, step)[2] for step in range(1, blocks)]
    meet(along_c + along_y + along_b)
    run_all([
        remote(in_ref.at[:, d["c"]], from_c.at[i], sems_c.at[0, i], sems_c.at[1, i], d)
        for i, d in enumerate(along_c)
    ])

    @pl.loop(0, ny)
    def _(y):
        @pl.loop(0, blocks)
        def _(k):
            value = in_ref[y, ic, k]
            for i in range(nc - 1):
                value = value + from_c[i, y, k]
            half[y, k] = value

    run_all([
        remote(half.at[d["y"]], from_y.at[i], sems_y.at[0, i], sems_y.at[1, i], d)
        for i, d in enumerate(along_y)
    ])

    @pl.loop(0, blocks)
    def _(k):
        value = half[iy, k]
        for i in range(ny - 1):
            value = value + from_y[i, k]
        total[k] = value

    me = block_peer(sizes, 0)[0]
    copies = []
    for step in range(1, blocks):
        _, peer, device = block_peer(sizes, step)
        copies.append(
            remote(total.at[peer], out_ref.at[me], sems_b.at[0, step], sems_b.at[1, step], device)
        )
    for copy in copies:
        copy.start()
    out_ref[me] = total[me]
    for copy in copies:
        copy.wait()


def fetch_blocks(sizes, looked_up, collective_id):
    nz, nx, ny, nc = sizes
    block = looked_up.shape[3:]
    blocks = nz * nx
    return pl.pallas_call(
        functools.partial(fetch_kernel, sizes),
        out_shape=jax.ShapeDtypeStruct((blocks,) + block, BF),
        in_specs=[pl.BlockSpec(memory_space=pltpu.VMEM)],
        out_specs=pl.BlockSpec(memory_space=pltpu.VMEM),
        scratch_shapes=[
            pltpu.VMEM((nc - 1, ny, blocks) + block, BF),
            pltpu.VMEM((ny - 1, blocks) + block, BF),
            pltpu.VMEM((ny, blocks) + block, BF),
            pltpu.VMEM((blocks,) + block, BF),
            pltpu.SemaphoreType.DMA((2, nc - 1)),
            pltpu.SemaphoreType.DMA((2, ny - 1)),
            pltpu.SemaphoreType.DMA((2, blocks)),
        ],
        compiler_params=pltpu.CompilerParams(
            collective_id=collective_id, has_side_effects=True, vmem_limit_bytes=VMEM_LIMIT
        ),
        cost_estimate=pl.CostEstimate(flops=0, bytes_accessed=1 << 27, transcendentals=0),
        name="fetch_blocks",
    )(looked_up)


def spread_kernel(sizes, in_ref, small_ref, out_ref, all_ref, sems_c, sems_y, sems_b, sems_s, near):
    nz, nx, ny, nc = sizes
    blocks = nz * nx
    index = tuple(lax.axis_index(a) for a in ALL)
    iy, ic = index[2:]
    along_y = [d for _, _, d in neighbours(("y",), (ny,))]
    along_c = [d for _, _, d in neighbours(("c",), (nc,))]
    along_b = [block_peer(sizes, step)[2] for step in range(1, blocks)]
    meet(along_c + along_y + along_b)
    me = block_peer(sizes, 0)[0]
    peers = neighbours(ALL, sizes)

    def small(place):
        view = (slice(None),) * place + index[place:]
        return [
            remote(all_ref.at[view], all_ref.at[view], sems_s.at[0, i], sems_s.at[1, i], device)
            for i, (at, _, device) in enumerate(peers)
            if at == place
        ]

    def start(copies):
        for copy in copies:
            copy.start()
        return copies

    def wait(copies):
        for copy in copies:
            copy.wait()

    own = pltpu.make_async_copy(small_ref, all_ref.at[index], near.at[0])
    own.start()
    own.wait()
    along_z = start(small(0))
    columns = []
    for step in range(1, blocks):
        _, peer, device = block_peer(sizes, step)
        columns.append(
            remote(in_ref.at[peer], out_ref.at[iy, ic, me], sems_b.at[0, step],
                   sems_b.at[1, step], device)
        )
    start(columns)
    out_ref[iy, ic, me] = in_ref[me]
    wait(along_z)
    along_x = start(small(1))
    wait(along_x)
    small_y = start(small(2))
    wait(columns)
    rows_y = start([
        remote(out_ref.at[iy, ic], out_ref.at[iy, ic], sems_y.at[0, i], sems_y.at[1, i], d)
        for i, d in enumerate(along_y)
    ])
    wait(small_y)
    small_c = start(small(3))
    wait(rows_y)
    rows_c = start([
        remote(out_ref.at[:, ic], out_ref.at[:, ic], sems_c.at[0, i], sems_c.at[1, i], d)
        for i, d in enumerate(along_c)
    ])
    wait(small_c)
    wait(rows_c)


def spread_blocks(sizes, parts, small, collective_id):
    nz, nx, ny, nc = sizes
    return pl.pallas_call(
        functools.partial(spread_kernel, sizes),
        out_shape=[
            jax.ShapeDtypeStruct((ny, nc) + parts.shape, parts.dtype),
            jax.ShapeDtypeStruct(sizes + small.shape, small.dtype),
        ],
        in_specs=[pl.BlockSpec(memory_space=pltpu.VMEM)] * 2,
        out_specs=[pl.BlockSpec(memory_space=pltpu.VMEM)] * 2,
        scratch_shapes=[
            pltpu.SemaphoreType.DMA((2, nc - 1)),
            pltpu.SemaphoreType.DMA((2, ny - 1)),
            pltpu.SemaphoreType.DMA((2, nz * nx)),
            pltpu.SemaphoreType.DMA((2, sum(sizes) - 4)),
            pltpu.SemaphoreType.DMA((1,)),
        ],
        compiler_params=pltpu.CompilerParams(
            collective_id=collective_id, has_side_effects=True, vmem_limit_bytes=VMEM_LIMIT
        ),
        cost_estimate=pl.CostEstimate(flops=0, bytes_accessed=1 << 27, transcendentals=0),
        name="spread_blocks",
    )(parts, small)


def axis_place(axes):
    index, size = 0, 1
    for axis in axes:
        index = index * lax.axis_size(axis) + lax.axis_index(axis)
        size = size * lax.axis_size(axis)
    return index, size


def exchange(piece_for, axes):
    me, n = axis_place(axes)
    got = [(me, piece_for(me))]
    for step in range(1, n):
        piece = piece_for(lax.rem(me + step, n))
        moved = lax.ppermute(piece, axes, [(i, (i + step) % n) for i in range(n)])
        got.append((lax.rem(me + n - step, n), moved))
    return got


def in_order(got):
    out = jnp.zeros((len(got),) + got[0][1].shape, got[0][1].dtype)
    for sender, piece in got:
        out = lax.dynamic_update_index_in_dim(out, piece, sender, 0)
    return out


def together(*values):
    return lax.optimization_barrier(values)


def pick(values, index, dim=0):
    return lax.dynamic_index_in_dim(values, index, dim, keepdims=False)


def cut_parts(values, dim, axis):
    me, n = lax.axis_index(axis), lax.axis_size(axis)
    return pick(values, me, dim), [
        pick(values, lax.rem(me + step, n), dim).astype(jnp.float16) for step in range(1, n)]


def send_parts(parts, axis):
    n = lax.axis_size(axis)
    return [lax.ppermute(part, axis, [(i, (i + step) % n) for i in range(n)])
            for step, part in enumerate(parts, 1)]


def spread_parts(values, dim, axis):
    own, parts = cut_parts(values, dim, axis)
    return own, send_parts(parts, axis)


def added(own, pieces):
    for piece in pieces:
        own = own + piece.astype(F32)
    return own


def gather_kernel(low_ref, high_ref, ids_ref, table_ref, out_ref, turned_ref, rows_ref):
    source = pl.program_id(0)

    @pl.when(source == 0)
    def _():
        @pl.loop(0, table_ref.shape[1] // LANES // 5)
        def _(k):
            for i in range(5):
                at = pl.multiple_of((k * 5 + i) * LANES, LANES)
                turned_ref[pl.ds(at, LANES), :] = table_ref[:, pl.ds(at, LANES)].T

    low, high = low_ref[source], high_ref[source]
    rows_ref[...] = jnp.zeros_like(rows_ref)

    first, last = low // 8, (high - 1) // 8

    def edge(k):
        base = pl.multiple_of(k * 8, 8)
        for i in range(8):
            place = base + i
            valid = jnp.logical_and(place >= low, place < high)
            row = jnp.where(valid, ids_ref[source, place], 0)
            value = turned_ref[pl.ds(row, 1), :]
            rows_ref[pl.ds(place, 1), :] = jnp.where(valid, value, 0.0)

    @pl.when(high > low)
    def _():
        edge(first)
        edge(last)

    def chunk(k, carry):
        base = pl.multiple_of(k * 8, 8)
        for i in range(8):
            row = ids_ref[source, base + i]
            rows_ref[pl.ds(base + i, 1), :] = turned_ref[pl.ds(row, 1), :]
        return carry

    lax.fori_loop(first + 1, last, chunk, 0)
    out_ref[0] = rows_ref[...].T.astype(BF)


def gather_rows(table, ids, low, high):
    sources, count = ids.shape
    width = table.shape[0]
    return pl.pallas_call(
        gather_kernel,
        out_shape=jax.ShapeDtypeStruct((sources, width, count), BF),
        grid_spec=pltpu.PrefetchScalarGridSpec(
            num_scalar_prefetch=3,
            grid=(sources,),
            in_specs=[
                pl.BlockSpec(table.shape, lambda i, *_: (0, 0), pipeline_mode=pl.Buffered(1))
            ],
            out_specs=pl.BlockSpec((1, width, count), lambda i, *_: (i, 0, 0)),
            scratch_shapes=[
                pltpu.VMEM((table.shape[1], width), F32),
                pltpu.VMEM((count, width), F32),
            ],
        ),
        compiler_params=pltpu.CompilerParams(vmem_limit_bytes=VMEM_LIMIT),
        cost_estimate=pl.CostEstimate(flops=0, bytes_accessed=1 << 27, transcendentals=0),
        name="gather_rows",
    )(low, high, ids, table)


def scatter_kernel(low_ref, high_ref, ids_ref, rows_ref, out_ref, wide_ref, *totals):
    source = pl.program_id(0)

    @pl.when(source == 0)
    def _():
        for total_ref in totals:
            total_ref[...] = jnp.zeros_like(total_ref)

    low, high = low_ref[source], high_ref[source]
    wide_ref[...] = rows_ref[0].astype(F32).T

    first, last = low // 8, (high - 1) // 8

    def edge(k):
        base = pl.multiple_of(k * 8, 8)
        for i in range(8):
            total_ref = totals[i % len(totals)]
            place = base + i
            valid = jnp.logical_and(place >= low, place < high)
            row = jnp.where(valid, ids_ref[source, place], 0)
            addend = jnp.where(valid, wide_ref[pl.ds(place, 1), :], 0.0)
            total_ref[pl.ds(row, 1), :] = total_ref[pl.ds(row, 1), :] + addend

    @pl.when(high > low)
    def _():
        edge(first)

    @pl.when(jnp.logical_and(high > low, last > first))
    def _():
        edge(last)

    def chunk(k, carry):
        base = pl.multiple_of(k * 8, 8)
        for i in range(8):
            total_ref = totals[i % len(totals)]
            row = ids_ref[source, base + i]
            addend = wide_ref[pl.ds(base + i, 1), :]
            total_ref[pl.ds(row, 1), :] = total_ref[pl.ds(row, 1), :] + addend
        return carry

    lax.fori_loop(first + 1, last, chunk, 0)

    @pl.when(source == pl.num_programs(0) - 1)
    def _():
        @pl.loop(0, out_ref.shape[1] // LANES // 5)
        def _(k):
            for i in range(5):
                at = pl.multiple_of((k * 5 + i) * LANES, LANES)
                value = totals[0][pl.ds(at, LANES), :]
                for total_ref in totals[1:]:
                    value = value + total_ref[pl.ds(at, LANES), :]
                out_ref[:, pl.ds(at, LANES)] = value.T


def scatter_rows(rows, ids, low, high, table_rows):
    sources, width, count = rows.shape
    return pl.pallas_call(
        scatter_kernel,
        out_shape=jax.ShapeDtypeStruct((width, table_rows), F32),
        grid_spec=pltpu.PrefetchScalarGridSpec(
            num_scalar_prefetch=3,
            grid=(sources,),
            in_specs=[pl.BlockSpec((1, width, count), lambda i, *_: (i, 0, 0))],
            out_specs=pl.BlockSpec((width, table_rows), lambda i, *_: (0, 0)),
            scratch_shapes=[pltpu.VMEM((count, width), F32)]
            + [pltpu.VMEM((table_rows, width), F32)] * 2,
        ),
        compiler_params=pltpu.CompilerParams(vmem_limit_bytes=VMEM_LIMIT),
        cost_estimate=pl.CostEstimate(flops=0, bytes_accessed=1 << 27, transcendentals=0),
        name="scatter_rows",
    )(low, high, ids, rows)


def swap_halves(values):
    lane = lax.broadcasted_iota(jnp.int32, values.shape, 1)
    half = HD // 2
    up = pltpu.roll(values, LANES - half, 1)
    down = pltpu.roll(values, half, 1)
    return jnp.where(lax.rem(lane, HD) < half, up, down)


def turn(values, cosine, sine):
    return values * cosine + swap_halves(values) * sine


def turn_back(values, cosine, sine):
    return values * cosine - swap_halves(values) * sine


def attend_kernel(kv_ref, vv_ref, qm_ref, km_ref, vm_ref, cu_ref, su_ref, cm_ref, sm_ref,
                  mask_ref, q_out, ku_out, km_out, att_out, lse_out):
    rows = cm_ref.shape[0]
    wide = (rows, LANES)
    cm, sm = cm_ref[...], sm_ref[...]
    q = turn(jnp.broadcast_to(qm_ref[0:1, :], wide), cm, sm).astype(BF)
    k_m = turn(jnp.broadcast_to(km_ref[0:1, :], wide), cm, sm).astype(BF)
    k_u = turn(kv_ref[...], cu_ref[...], su_ref[...]).astype(BF)
    v_u = vv_ref[...].astype(BF)
    v_m = vm_ref[0:1, :].astype(BF).astype(F32)
    q_out[...] = q
    ku_out[...] = k_u
    km_out[...] = k_m
    mask = mask_ref[0:1, :]
    outs, totals = [], []
    for head in range(LANES // HD):
        part = slice(head * HD, (head + 1) * HD)
        s_u = matmul_nt(q[:, part], k_u[:, part]) * HD ** (-0.5) + mask
        s_m = matmul_nt(q[:, part], k_m[:, part]) * HD ** (-0.5)
        top = jnp.maximum(
            jnp.max(s_u, axis=1, keepdims=True), jnp.max(s_m, axis=1, keepdims=True)
        )
        e_u = jnp.exp(s_u - top)
        e_m = jnp.exp(s_m - top)
        total = jnp.sum(e_u, axis=1, keepdims=True) + jnp.sum(e_m, axis=1, keepdims=True)
        inverse = 1.0 / total
        p_u = (e_u * inverse).astype(BF)
        p_m = (e_m * inverse).astype(BF).astype(F32)
        mixed = matmul(p_u, v_u[:, part]) + jnp.sum(p_m, axis=1, keepdims=True) * v_m[:, part]
        outs.append(mixed)
        totals.append(top + jnp.log(total))
    att_out[...] = jnp.concatenate(outs, axis=1).astype(BF)
    lse_out[0] = jnp.concatenate(totals, axis=1)


def attend(kv_u, qkv_m, tables, mask):
    count, rows = kv_u.shape[0], tables[2].shape[0]
    blocks = D // LANES
    per = LANES // HD
    row = lambda offset: pl.BlockSpec((qkv_m.shape[0], LANES), lambda i: (0, offset * blocks + i))
    column = lambda n: pl.BlockSpec((n, LANES), lambda i: (0, i))
    whole = lambda a: pl.BlockSpec(a.shape, lambda i: (0, 0))
    return pl.pallas_call(
        attend_kernel,
        grid=(blocks,),
        out_shape=[
            jax.ShapeDtypeStruct((rows, D), BF),
            jax.ShapeDtypeStruct((count, D), BF),
            jax.ShapeDtypeStruct((rows, D), BF),
            jax.ShapeDtypeStruct((rows, D), BF),
            jax.ShapeDtypeStruct((blocks, rows, per), F32),
        ],
        in_specs=[
            pl.BlockSpec((count, LANES), lambda i: (0, i)),
            pl.BlockSpec((count, LANES), lambda i: (0, blocks + i)),
            row(0), row(1), row(2),
            *[whole(t) for t in tables],
            whole(mask),
        ],
        out_specs=[column(rows), column(count), column(rows), column(rows),
                   pl.BlockSpec((1, rows, per), lambda i: (i, 0, 0))],
        compiler_params=pltpu.CompilerParams(vmem_limit_bytes=VMEM_LIMIT),
        cost_estimate=pl.CostEstimate(
            flops=2 * 3 * rows * count * D, bytes_accessed=12 * rows * D,
            transcendentals=2 * rows * count * H,
        ),
        name="attend",
    )(kv_u, kv_u, qkv_m, qkv_m, qkv_m, *tables, mask)


def attend_back_kernel(q_ref, ku_ref, km_ref, vv_ref, vm_ref, cu_ref, su_ref, cm_ref, sm_ref,
                       mask_ref, lse_ref, datt_ref, dk_out, dv_out, dm_out):
    q, k_u, k_m, datt = q_ref[...], ku_ref[...], km_ref[...], datt_ref[...]
    v_u = vv_ref[...].astype(BF)
    v_m = vm_ref[0:1, :].astype(BF).astype(F32)
    datt_f = datt.astype(F32)
    mask = mask_ref[0:1, :]
    scale = HD ** (-0.5)
    dq, dk_u, dk_m, dv_u, dv_m = [], [], [], [], []
    for head in range(LANES // HD):
        part = slice(head * HD, (head + 1) * HD)
        lse = lse_ref[0, :, head : head + 1]
        p_u = jnp.exp(matmul_nt(q[:, part], k_u[:, part]) * scale + mask - lse)
        p_m = jnp.exp(matmul_nt(q[:, part], k_m[:, part]) * scale - lse)
        dp_u = matmul_nt(datt[:, part], v_u[:, part])
        dp_m = jnp.sum(datt_f[:, part] * v_m[:, part], axis=1, keepdims=True)
        inner = jnp.sum(p_u * dp_u, axis=1, keepdims=True) + dp_m * jnp.sum(
            p_m, axis=1, keepdims=True
        )
        ds_u = (p_u * (dp_u - inner) * scale).astype(BF)
        ds_m = (p_m * ((dp_m - inner) * scale)).astype(BF)
        dq.append(matmul(ds_u, k_u[:, part]) + matmul(ds_m, k_m[:, part]))
        dk_u.append(matmul_tn(ds_u, q[:, part]))
        dk_m.append(matmul_tn(ds_m, q[:, part]))
        dv_u.append(matmul_tn(p_u.astype(BF), datt[:, part]))
        mass = jnp.sum(p_m.astype(BF).astype(F32), axis=1, keepdims=True)
        dv_m.append(jnp.sum(mass * datt_f[:, part], axis=0, keepdims=True))
    cm, sm = cm_ref[...], sm_ref[...]
    join = lambda parts: jnp.concatenate(parts, axis=1)
    low = lambda a: a.astype(BF).astype(F32)
    dk_out[...] = turn_back(join(dk_u), cu_ref[...], su_ref[...]).astype(BF)
    dv_out[...] = join(dv_u).astype(BF)
    dq_sum = jnp.sum(low(turn_back(join(dq), cm, sm)), axis=0, keepdims=True)
    dk_sum = jnp.sum(low(turn_back(join(dk_m), cm, sm)), axis=0, keepdims=True)
    filler = jnp.zeros((5, LANES), F32)
    dm_out[...] = jnp.concatenate([dq_sum, dk_sum, join(dv_m), filler], axis=0)


def attend_back(q, k_u, k_m, kv_u, qkv_m, tables, mask, lse, datt):
    count, rows = kv_u.shape[0], q.shape[0]
    blocks = D // LANES
    per = LANES // HD
    column = lambda n: pl.BlockSpec((n, LANES), lambda i: (0, i))
    whole = lambda a: pl.BlockSpec(a.shape, lambda i: (0, 0))
    return pl.pallas_call(
        attend_back_kernel,
        grid=(blocks,),
        out_shape=[
            jax.ShapeDtypeStruct((count, D), BF),
            jax.ShapeDtypeStruct((count, D), BF),
            jax.ShapeDtypeStruct((8, D), F32),
        ],
        in_specs=[
            column(rows), column(count), column(rows),
            pl.BlockSpec((count, LANES), lambda i: (0, blocks + i)),
            pl.BlockSpec((qkv_m.shape[0], LANES), lambda i: (0, 2 * blocks + i)),
            *[whole(t) for t in tables],
            whole(mask),
            pl.BlockSpec((1, rows, per), lambda i: (i, 0, 0)),
            column(rows),
        ],
        out_specs=[column(count), column(count), column(8)],
        compiler_params=pltpu.CompilerParams(vmem_limit_bytes=VMEM_LIMIT),
        cost_estimate=pl.CostEstimate(
            flops=2 * 8 * rows * count * D, bytes_accessed=14 * rows * D,
            transcendentals=2 * rows * count * H,
        ),
        name="attend_back",
    )(q, k_u, k_m, kv_u, qkv_m, *tables, mask, lse, datt)


def tile_of(segments):
    return max(16, 1024 // segments)


def logits_kernel(places_ref, w_ref, target_ref, *refs):
    blocks, (e_ref, stats_ref, x_ref, logits_ref) = refs[:-4], refs[-4:]
    segments, _, width = w_ref.shape
    rows = x_ref.shape[0]
    per = blocks[0].shape[0] // rows
    step = pl.program_id(0)
    for number, block in enumerate(blocks):

        @pl.when(step // per == number)
        def _(block=block):
            x_ref[...] = block[pl.ds(pl.multiple_of(lax.rem(step, per) * rows, rows), rows), :]

    x = x_ref[...]
    starts = list(range(0, width - width % 768 or width, 768))
    best = None
    for y in range(segments):
        for at, end in zip(starts, starts[1:] + [width]):
            logits = matmul(x, w_ref[y, :, at:end])
            logits_ref[:, y * width + at : y * width + end] = logits
            for g in range(0, end - at, LANES):
                part = logits[:, g : g + LANES]
                best = part if best is None else jnp.maximum(best, part)
    lane = lax.broadcasted_iota(jnp.int32, (ROWS, LANES), 1)
    peaks = jnp.max(best, axis=1, keepdims=True)
    for r in range(0, rows, ROWS):
        peak = peaks[r : r + ROWS]
        top = jnp.broadcast_to(peak, (ROWS, LANES))
        place = target_ref[r : r + ROWS, :] - lane
        total = jnp.zeros((ROWS, LANES), F32)
        chosen = jnp.zeros((ROWS, LANES), F32)
        for y in range(segments):
            for at in range(0, width, LANES):
                column = y * width + at
                logits = logits_ref[r : r + ROWS, column : column + LANES]
                e = jnp.exp(logits - top)
                total = total + e
                chosen = chosen + jnp.where(place == column, logits, 0.0)
                e_ref[y, r : r + ROWS, at : at + LANES] = e.astype(BF)
        sums = [jnp.sum(a, axis=1, keepdims=True) for a in (total, chosen)]
        stats_ref[r : r + ROWS, :] = jnp.concatenate([peak, *sums, peak], axis=1)


def head_logits(blocks, weights, targets, places):
    count = targets.shape[0]
    segments, _, width = weights.shape
    tile = tile_of(segments)
    per = blocks[0].shape[0] // tile

    def placed(i, places):
        return (places[i // per] * per + lax.rem(i, per), 0)

    return pl.pallas_call(
        logits_kernel,
        out_shape=[
            jax.ShapeDtypeStruct((segments, count, width), BF),
            jax.ShapeDtypeStruct((count, 4), F32),
            jax.ShapeDtypeStruct((count, D), BF),
        ],
        grid_spec=pltpu.PrefetchScalarGridSpec(
            num_scalar_prefetch=1,
            grid=(count // tile,),
            in_specs=[
                pl.BlockSpec(weights.shape, lambda i, p: (0, 0, 0), pipeline_mode=pl.Buffered(1)),
                pl.BlockSpec((tile, 1), placed),
            ] + [
                pl.BlockSpec(b.shape, lambda i, p: (0, 0), pipeline_mode=pl.Buffered(1))
                for b in blocks
            ],
            out_specs=[
                pl.BlockSpec((segments, tile, width), lambda i, p: (0, i, 0)),
                pl.BlockSpec((tile, 4), placed),
                pl.BlockSpec((tile, D), lambda i, p: (i, 0)),
            ],
            scratch_shapes=[pltpu.VMEM((tile, segments * width), F32)],
        ),
        compiler_params=pltpu.CompilerParams(vmem_limit_bytes=VMEM_LIMIT),
        cost_estimate=pl.CostEstimate(
            flops=2 * count * D * segments * width,
            bytes_accessed=2 * count * segments * width,
            transcendentals=count * segments * width,
        ),
        name="head_logits",
    )(places, weights, targets, *blocks)


def rows_back_kernel(places_ref, e_ref, w_ref, target_ref, factor_ref, d_ref, dx_ref):
    segments, _, width = w_ref.shape
    rows = e_ref.shape[1]
    lane = lax.broadcasted_iota(jnp.int32, (ROWS, LANES), 1)
    wide = lambda a: jnp.broadcast_to(a, (ROWS, LANES))
    total = None
    for y in range(segments):
        for r in range(0, rows, ROWS):
            place = target_ref[r : r + ROWS, :] - (lane + y * width)
            factor = wide(factor_ref[r : r + ROWS, 0:1])
            special = wide(factor_ref[r : r + ROWS, 1:2])
            for at in range(0, width, LANES):
                e = e_ref[y, r : r + ROWS, at : at + LANES].astype(F32)
                d_ref[y, r : r + ROWS, at : at + LANES] = jnp.where(
                    place == at, special, e * factor).astype(BF)
        part = matmul_nt(d_ref[y], w_ref[y])
        total = part if total is None else total + part
    dx_ref[...] = total.astype(BF)


def head_rows_back(e, weights, targets, factors, places):
    segments, count, width = e.shape
    tile = tile_of(segments)
    per = count // places.shape[0] // tile

    def placed(i, places):
        return (places[i // per] * per + lax.rem(i, per), 0)

    return pl.pallas_call(
        rows_back_kernel,
        out_shape=[
            jax.ShapeDtypeStruct(e.shape, BF),
            jax.ShapeDtypeStruct((count, D), BF),
        ],
        grid_spec=pltpu.PrefetchScalarGridSpec(
            num_scalar_prefetch=1,
            grid=(count // tile,),
            in_specs=[
                pl.BlockSpec((segments, tile, width), lambda i, p: (0, i, 0)),
                pl.BlockSpec(weights.shape, lambda i, p: (0, 0, 0), pipeline_mode=pl.Buffered(1)),
                pl.BlockSpec((tile, 1), placed),
                pl.BlockSpec((tile, 2), placed),
            ],
            out_specs=[
                pl.BlockSpec((segments, tile, width), lambda i, p: (0, i, 0)),
                pl.BlockSpec((tile, D), placed),
            ],
        ),
        input_output_aliases={1: 0},
        compiler_params=pltpu.CompilerParams(vmem_limit_bytes=VMEM_LIMIT),
        cost_estimate=pl.CostEstimate(
            flops=2 * count * D * segments * width,
            bytes_accessed=4 * count * segments * width,
            transcendentals=0,
        ),
        name="head_rows_back",
    )(places, e, weights, targets, factors)


def layer_norm(values):
    center = values - jnp.mean(values, axis=-1, keepdims=True)
    spread = jnp.mean(center * center, axis=-1, keepdims=True)
    inv_std = lax.rsqrt(spread + NORM_EPS)
    return (center * inv_std, inv_std)


def norm_back(d_normed, normed, inv_std):
    return inv_std * (
        d_normed
        - jnp.mean(d_normed, axis=-1, keepdims=True)
        - normed * jnp.mean(d_normed * normed, axis=-1, keepdims=True)
    )


def time_features(time_index, width, steps):
    t_value = (time_index.astype(F32) + 1.0) / steps
    half_width = width // 2
    frequencies = jnp.exp(-math.log(10000.0) * jnp.arange(half_width, dtype=F32) / half_width)
    angles = 1000.0 * t_value[:, None] * frequencies[None, :]
    return jax.nn.silu(jnp.concatenate([jnp.cos(angles), jnp.sin(angles)], axis=1))


def rope_rows(positions):
    half = HD // 2
    inverse = jnp.exp(-math.log(10000.0) * jnp.arange(half, dtype=F32) * 2.0 / HD)
    angles = positions.astype(F32)[:, None] * inverse[None, :]
    cosine, sine = jnp.cos(angles), jnp.sin(angles)
    return (jnp.tile(cosine, (1, LANES // half)),
            jnp.tile(jnp.concatenate([-sine, sine], axis=1), (1, LANES // HD)))


def gelu_tanh(values):
    return jax.nn.gelu(values, approximate=True)


def adam_step(weight, first, second, ema_copy, gradient, step_value, learn_rate, decay_rate):
    first_new = BETA_ONE * first + (1.0 - BETA_ONE) * gradient
    second_new = BETA_TWO * second + (1.0 - BETA_TWO) * gradient * gradient
    first_hat = first_new / (1.0 - BETA_ONE**step_value)
    second_hat = second_new / (1.0 - BETA_TWO**step_value)
    weight_new = weight - learn_rate * (
        first_hat / (jnp.sqrt(second_hat) + ADAM_EPS) + decay_rate * weight
    )
    ema_rate = jnp.minimum(EMA_DECAY, (1.0 + step_value) / (10.0 + step_value))
    ema_new = ema_rate * ema_copy + (1.0 - ema_rate) * weight_new
    return (first_new, second_new, weight_new, ema_new)


def split3(row):
    parts, rest = [], row
    for _ in range(3):
        part = lax.reduce_precision(rest, 8, 7)
        parts.append(part.astype(BF))
        rest = rest - part
    return parts


def local(sizes, token_ids, scored, lengths, times, step_count, layer_w, layer_m, layer_v, layer_ema,
          ada_w, ada_m, ada_v, ada_ema, gains_w, gains_m, gains_v, gains_ema,
          embed_w, embed_m, embed_v, embed_ema, head_w, head_m, head_v, head_ema):
    nz, nx, ny, nc = sizes
    n = nz * nx * ny * nc
    length, score_count = token_ids.shape[1], scored.shape[1]
    free_count = length - score_count
    total_rows = n * score_count
    table_rows, table_width = embed_w.shape
    iz, ix, iy, ic = [lax.axis_index(a) for a in ALL]
    vocab_index = iy * nc + ic
    vocab_start = vocab_index * table_rows
    me = (iz * nx + ix) * (ny * nc) + vocab_index

    tokens, masked = token_ids[0], scored[0]
    positions = jnp.arange(length, dtype=jnp.int32)
    hits = masked[:, None] == positions[None, :]
    is_masked = jnp.any(hits, axis=0)
    targets = jnp.sum(jnp.where(hits, tokens[None, :], 0), axis=1)
    keys = jnp.where(is_masked, n * V, (tokens // table_rows) * length + positions)
    rank = jnp.sum((keys[None, :] < keys[:, None]).astype(jnp.int32), axis=1)
    rank = jnp.where(is_masked, length, rank)
    slots = rank[None, :] == jnp.arange(free_count, dtype=jnp.int32)[:, None]
    free_tokens = jnp.sum(jnp.where(slots, tokens[None, :], 0), axis=1)
    free_positions = jnp.sum(jnp.where(slots, positions[None, :], 0), axis=1)

    ints = jnp.concatenate([free_tokens.reshape(-1, LANES), targets.reshape(-1, LANES),
                            jnp.broadcast_to(times[:, None], (1, LANES))], axis=0)
    ints = jnp.pad(ints, ((0, -ints.shape[0] % 8), (0, 0)))
    gain_part = jnp.pad(gains_w.astype(BF).astype(F32),
                        ((0, 8 - gains_w.shape[0]), (0, LANES - gains_w.shape[1])))
    ints_all, gains_all = share(ALL, 0, ints, gain_part)
    ints_all = ints_all.reshape((n,) + ints.shape)
    gains_all = gains_all.reshape((n,) + gain_part.shape)

    block_low = jnp.concatenate(
        [layer_w.astype(BF), ada_w.astype(BF).reshape(layer_w.shape[0], -1)], axis=1)
    block_low, head_low, ints_all = together(block_low, head_w.astype(BF), ints_all)
    layer_all = lax.all_gather(block_low, ALL, axis=0, tiled=True)

    piece_for = lambda k: lax.dynamic_slice_in_dim(head_low, k * SEGMENT, SEGMENT, 1)
    head_parts = exchange(piece_for, ("z",))

    gains = jnp.moveaxis(gains_all[:, : gains_w.shape[0], : gains_w.shape[1]], 0, 1).reshape(4, D)
    free_rows = free_count // LANES
    score_rows = score_count // LANES
    all_tokens = ints_all[:, :free_rows].reshape(nz * nx, ny * nc, free_count)
    all_targets = ints_all[:, free_rows : free_rows + score_rows].reshape(
        nz, nx, ny, nc, score_count)
    all_times = ints_all[:, free_rows + score_rows, 0]

    wanted = jnp.swapaxes(all_tokens, 0, 1).reshape(n, free_count)
    owners = wanted // table_rows
    low = jnp.sum((owners < vocab_index).astype(jnp.int32), axis=1)
    high = jnp.sum((owners <= vocab_index).astype(jnp.int32), axis=1)
    local_ids = wanted - vocab_start
    looked_up = gather_rows(embed_w.T, local_ids, low, high)
    looked_up = looked_up.reshape((ny, nc, nz * nx) + looked_up.shape[1:])
    x0_u = fetch_blocks(sizes, looked_up, 3).reshape(D, free_count).T.astype(F32)
    group = nz * nc * score_count
    row_targets = pick(jnp.moveaxis(jnp.moveaxis(all_targets, 3, 1), (2, 3), (0, 1)).reshape(
        nx * ny, group), ix * ny + iy)
    row_times = pick(jnp.moveaxis(jnp.moveaxis(all_times.reshape(nz, nx, ny, nc), 3, 1), (2, 3), (0, 1))
                     .reshape(nx * ny, nz * nc), ix * ny + iy)
    row_weights = jnp.repeat(TSTEPS / (row_times.astype(F32) + 1.0) / total_rows, score_count)
    owner, within = row_targets // table_rows, row_targets % table_rows
    owned = jnp.logical_and(owner % nc == ic, within // SEGMENT == iz)
    column_of = jnp.where(owned, (owner // nc) * SEGMENT + within % SEGMENT, -1)[:, None]
    x0_u, column_of, row_weights = together(x0_u, column_of, row_weights)
    senders = [sender for sender, _ in head_parts]
    x0_u, *pieces = together(x0_u, *[piece for _, piece in head_parts])
    head_part = in_order(list(zip(senders, pieces))).reshape(-1, SEGMENT)

    mask_row = gains[3:4]
    condition = time_features(times, C, TSTEPS).astype(BF)
    modulation = matmul(condition, layer_all[:, layer_w.shape[1] :].reshape(C, 6 * D))
    shift_a, scale_a, gate_a, shift_m, scale_m, gate_m = [
        modulation[:, i * D : (i + 1) * D] for i in range(6)]
    normed_u, inv_u = layer_norm(x0_u)
    a_u = (normed_u * gains[0:1] * (1.0 + scale_a) + shift_a).astype(BF)
    normed_0, inv_0 = layer_norm(mask_row)
    a_m = (normed_0 * gains[0:1] * (1.0 + scale_a) + shift_a).astype(BF)
    w_qkv, w_o = layer_all[:, : 3 * D], layer_all[:, 3 * D : 4 * D]
    w_up, w_down = layer_all[:, 4 * D : 4 * D + FF], layer_all[:, 4 * D + FF : 4 * D + 2 * FF]
    qkv_m = matmul(jnp.broadcast_to(a_m, (16, D)), w_qkv)
    kv_u = matmul(a_u, w_qkv[:, D:])
    tables = (*rope_rows(free_positions), *rope_rows(masked))
    mask = jnp.where(free_positions[None, :] < lengths[:, None], 0.0, -1e30)
    mask = jnp.broadcast_to(mask, (8, free_count)).astype(F32)
    q, k_u, k_m, att, lse_a = attend(kv_u, qkv_m, tables, mask)
    branch = matmul(att, w_o)
    x1 = mask_row + gate_a * branch
    normed_m, inv_m = layer_norm(x1)
    b = (normed_m * gains[1:2] * (1.0 + scale_m) + shift_m).astype(BF)
    pre = matmul(b, w_up)
    act = gelu_tanh(pre).astype(BF)
    mlp = matmul_nt(act, w_down)
    x2 = x1 + gate_m * mlp
    normed_f, inv_f = layer_norm(x2)
    final = (normed_f * gains[2:3]).astype(BF)

    final_turned = jnp.swapaxes(final.reshape(score_count, nz, nx, -1), 1, 2).reshape(score_count, D)
    head_all = lax.all_gather(head_part, ("y", "x"), axis=0, tiled=True).reshape(ny, D, SEGMENT)
    blocks, places = [], []
    for sender, piece in exchange(lambda k: final_turned, ("z",)):
        for place, part in exchange(lambda k: piece, ("c",)):
            blocks.append(part)
            places.append(sender * nc + place)
    places = jnp.stack(places).astype(jnp.int32)
    e, stats, rows = head_logits(blocks, head_all, column_of, places)
    top = stats[:, 0]
    every = share(("z", "c"), 4, stats.T.reshape(4, -1, LANES))[0].reshape(nz * nc, 4, group)
    best = jnp.max(every[:, 0], axis=0)
    log_total = best + jnp.log(jnp.sum(every[:, 1] * jnp.exp(every[:, 0] - best), axis=0))
    chosen = jnp.sum(every[:, 2], axis=0)
    own_start = (iz * nc + ic) * score_count
    own_terms = lax.dynamic_slice_in_dim(row_weights * (log_total - chosen), own_start, score_count)
    loss_part = jnp.sum(own_terms)
    factors = jnp.stack([row_weights * jnp.exp(top - log_total),
                         row_weights * (jnp.exp(chosen - log_total) - 1.0)], axis=1)
    d_logits, d_rows = head_rows_back(e, head_all, column_of, factors, places)
    d_final = lax.psum_scatter(d_rows, ("z", "c"), scatter_dimension=0, tiled=True)

    bound = D**0.5 * jnp.max(jnp.abs(gains[2])) * 1.02
    bound = bound * score_count * jnp.sum(TSTEPS / (all_times.astype(F32) + 1.0) / total_rows)
    enlarge = 60000.0 / jnp.maximum(bound, 1e-30)
    d_head = jnp.einsum("rd,yrv->ydv", rows, d_logits, preferred_element_type=F32) * enlarge
    d_head = d_head.reshape(ny, nx, nz, -1, SEGMENT)
    cut = nz // 2
    own_x, to_x = cut_parts(d_head[:, :, :cut], 1, "x")
    own_y, to_y = cut_parts(d_head[:, :, cut:], 0, "y")
    d_final, *to_xy = together(d_final, *to_x, *to_y)
    from_x, from_y = send_parts(to_xy[: nx - 1], "x"), send_parts(to_xy[nx - 1 :], "y")
    d_final = d_final.astype(F32)
    d_final = jnp.swapaxes(d_final.reshape(score_count, nx, nz, -1), 1, 2).reshape(score_count, D)

    d_gain_f = jnp.sum(d_final * normed_f, axis=0)
    d_x2 = norm_back(d_final * gains[2:3], normed_f, inv_f)
    d_gate_m = jnp.sum(d_x2 * mlp, axis=0)
    d_out = (d_x2 * gate_m).astype(BF)
    d_down = matmul_tn(d_out, act)
    d_act = matmul(d_out, w_down)
    d_pre = jax.vjp(gelu_tanh, pre)[1](d_act)[0].astype(BF)
    d_up = matmul_tn(b, d_pre)
    d_b = matmul_nt(d_pre, w_up)
    d_shift_m = jnp.sum(d_b, axis=0)
    product = jnp.sum(d_b * normed_m, axis=0)
    d_scale_m = product * gains[1]
    d_gain_m = product * (1.0 + scale_m[0])
    d_x1 = d_x2 + norm_back(d_b * ((1.0 + scale_m) * gains[1:2]), normed_m, inv_m)
    d_gate_a = jnp.sum(d_x1 * branch, axis=0)
    d_branch = (d_x1 * gate_a).astype(BF)
    d_wout = matmul_tn(att, d_branch)
    d_att, *from_xy = together(matmul_nt(d_branch, w_o).astype(BF), *from_x, *from_y)
    def over_cores(gradient):
        width = gradient.shape[1]
        parts = jnp.transpose(gradient.reshape(nz, nx, ny, nc, -1, width), (3, 1, 2, 0, 4, 5))
        parts = parts.reshape(nc, -1, width)
        got = exchange(lambda k: pick(parts, k), ("c",))
        return sum(piece.astype(F32) for _, piece in got).astype(BF)

    over_plane = lambda a: lax.psum_scatter(a, ("x", "y"), scatter_dimension=0, tiled=True)
    own_xy, from_xy = (
        spread_parts(added(own_x, from_xy[: nx - 1]), 0, "y"),
        spread_parts(added(own_y, from_xy[nx - 1 :]), 0, "x"),
    )
    d_k, d_v, d_qkv_m = attend_back(q, k_u, k_m, kv_u, qkv_m, tables, mask, lse_a, d_att)
    d_k, *arrivals = together(d_k, *own_xy[1], *from_xy[1])
    head_sum = jnp.concatenate(
        [added(own_xy[0], arrivals[: ny - 1]), added(from_xy[0], arrivals[ny - 1 :])], axis=0)
    d_k, head_sum = together(d_k, head_sum)
    head_own, head_parts = spread_parts(head_sum, 0, "z")
    d_kv = jnp.concatenate([d_k, d_v], axis=1)
    d_wkv = matmul_tn(a_u, d_kv)
    d_row_m = d_qkv_m[:3].reshape(3 * D)
    d_a_u = matmul_nt(d_kv, w_qkv[:, D:])
    d_parts = matmul_nt(jnp.pad(jnp.stack(split3(d_row_m)), ((0, 13), (0, 0))), w_qkv)
    d_a_m = jnp.sum(d_parts[:3], axis=0, keepdims=True)
    d_shift_a = jnp.sum(d_a_u, axis=0) + d_a_m[0]
    product = jnp.sum(d_a_u * normed_u, axis=0) + (d_a_m * normed_0)[0]
    d_scale_a = product * gains[0]
    d_gain_a = product * (1.0 + scale_a[0])
    scaling = (1.0 + scale_a) * gains[0:1]
    d_x0_u = norm_back(d_a_u * scaling, normed_u, inv_u)
    d_mask = jnp.sum(d_x1, axis=0) + norm_back(d_a_m * scaling, normed_0, inv_0)[0]

    chip_sum = over_cores(jnp.concatenate(
        [d_wkv.astype(BF), d_wout.astype(BF), d_up.astype(BF), d_down.astype(BF)], axis=1))

    small = jnp.concatenate([d_shift_a, d_scale_a, d_gate_a, d_shift_m, d_scale_m, d_gate_m,
                             d_gain_a, d_gain_m, d_gain_f, d_mask,
                             a_m[0].astype(F32), d_row_m, jnp.broadcast_to(loss_part, (LANES,))])
    small = small.reshape(-1, LANES)
    count_small = small.shape[0]
    small = jnp.pad(small, ((0, -count_small % 8), (0, 0)))

    sent = d_x0_u.astype(BF).T.reshape(nz * nx, table_width, free_count)
    sent, chip_sum = together(sent, chip_sum)
    plane_sum = over_plane(chip_sum)
    sent, *head_parts = together(sent, *head_parts)

    arrived, small_all = spread_blocks(sizes, sent, small, 5)
    arrived, plane_sum = together(arrived, plane_sum)
    plane_sum = plane_sum.reshape(nz, -1, plane_sum.shape[1])
    block_parts = [p for _, p in exchange(lambda k: pick(plane_sum, k), ("z",))]
    g_embed = scatter_rows(arrived.reshape(n, table_width, free_count), local_ids, low, high,
                           table_rows)
    together_now = together(g_embed, small_all, head_own, *head_parts, *block_parts)
    g_embed, small_all, head_own = together_now[:3]
    head_parts, block_parts = together_now[3 : 2 + nz], together_now[2 + nz :]
    small_all = small_all.reshape((n,) + small.shape)
    small_all = small_all[:, :count_small].reshape(n, -1)
    d_mod_all = small_all[:, : 6 * D]
    d_gains = jnp.sum(small_all[:, 6 * D : 10 * D], axis=0).reshape(4, D)
    g_gains = lax.dynamic_slice_in_dim(d_gains, me * gains_w.shape[1], gains_w.shape[1], 1)
    total_loss = jnp.sum(small_all[:, 14 * D])
    condition_all = time_features(all_times, C, TSTEPS).astype(BF).astype(F32)
    condition_rows = lax.dynamic_slice_in_dim(condition_all, me * ada_w.shape[0], ada_w.shape[0], 1)
    exact = lambda a, b: jnp.einsum("nr,nc->rc", a, b, precision=lax.Precision.HIGHEST)
    g_ada = exact(condition_rows, d_mod_all)
    a_rows = lax.dynamic_slice_in_dim(small_all[:, 10 * D : 11 * D], me * layer_w.shape[0],
                                      layer_w.shape[0], 1)
    g_outer = exact(a_rows, small_all[:, 11 * D : 14 * D])

    g_rest = sum(p.astype(F32) for p in block_parts)
    g_layer = jnp.concatenate(
        [g_outer[:, :D], g_outer[:, D:] + g_rest[:, : 2 * D], g_rest[:, 2 * D :]], axis=1)

    segments = []
    for k in range(nz):
        segment = head_own
        for step, piece in enumerate(head_parts, 1):
            segment = jnp.where(lax.rem(iz + nz - step, nz) == k, piece.astype(F32), segment)
        segments.append(segment)
    g_head = jnp.concatenate(segments, axis=1) / enlarge

    squares = sum(jnp.sum(g * g) for g in (g_layer, g_ada, g_gains, g_embed, g_head))
    squares_all = share(ALL, 2, jnp.broadcast_to(squares, (8, LANES)))[0]
    grad_norm = jnp.sqrt(jnp.sum(squares_all[..., 0, 0]))
    factor = jnp.minimum(1.0, CLIP_NORM / grad_norm)
    step_value = step_count[0].astype(F32)
    updates = (
        (layer_w, layer_m, layer_v, layer_ema, g_layer),
        (ada_w, ada_m, ada_v, ada_ema, g_ada),
        (gains_w, gains_m, gains_v, gains_ema, g_gains),
        (embed_w.T, embed_m.T, embed_v.T, embed_ema.T, g_embed),
        (head_w, head_m, head_v, head_ema, g_head),
    )
    results = []
    for (w, m, v, ema, g), rate, decay in zip(updates, LEARN_RATES, WEIGHT_DECAYS):
        results.extend(adam_step(w, m, v, ema, g * factor, step_value, rate, decay))
    results[12:16] = [a.T for a in results[12:16]]
    return (total_loss, grad_norm, *results)


def solution(mesh):
    dp, vocab = mesh.shape["dp"], mesh.shape["vocab"]
    nz, nc = V // vocab // SEGMENT, 2
    sizes = (nz, dp // nz, vocab // nc, nc)
    fine = Mesh(mesh.devices.reshape(sizes), ALL)
    rows_all, columns_all = P(ALL, None), P(None, ALL)
    table, head = P(("y", "c"), ("z", "x")), P(("z", "x"), ("y", "c"))
    weights = [rows_all] * 8 + [columns_all] * 4 + [table] * 4 + [head] * 4
    return jax.shard_map(
        functools.partial(local, sizes),
        mesh=fine,
        in_specs=(rows_all, rows_all, P(ALL), P(ALL), P(), *weights),
        out_specs=(P(), P(), *weights),
        check_vma=False,
    )
```

```python
import functools
import math

import jax
import jax.numpy as jnp
from jax import lax
from jax.experimental import pallas as pl
from jax.experimental.pallas import tpu as pltpu
from jax.sharding import Mesh, PartitionSpec as P

D = 768
H = 12
HD = 64
FF = 3072
V = 51200
C = 128
TSTEPS = 20
SEGMENT = 3200
LANES = 128
ROWS = 64

NORM_EPS = 1e-05
CLIP_NORM = 0.05
BETA_ONE = 0.9
BETA_TWO = 0.95
ADAM_EPS = 1e-08
EMA_DECAY = 0.9999
LEARN_RATES = (0.03, 0.1, 0.1, 0.5, 0.05)
WEIGHT_DECAYS = (0.01, 0.01, 0.0, 0.01, 0.01)

ALL = ("z", "x", "y", "c")
BF = jnp.bfloat16
F32 = jnp.float32
MESH = pl.DeviceIdType.MESH
VMEM_LIMIT = 60 * 1024 * 1024


def dot(a, b, contract):
    return lax.dot_general(a, b, ((contract[0], contract[1]), ((), ())), preferred_element_type=F32)


def matmul(a, b):
    return dot(a, b, ((1,), (0,)))


def matmul_nt(a, b):
    return dot(a, b, ((1,), (1,)))


def matmul_tn(a, b):
    return dot(a, b, ((0,), (0,)))


def neighbours(axes, sizes):
    found = []
    for place, (axis, size) in enumerate(zip(axes, sizes)):
        for step in range(1, size):
            found.append((place, step, {axis: lax.rem(lax.axis_index(axis) + step, size)}))
    return found


def meet(devices):
    barrier = pltpu.get_barrier_semaphore()
    for device in devices:
        pl.semaphore_signal(barrier, inc=1, device_id=device, device_id_type=MESH)
    pl.semaphore_wait(barrier, len(devices))


def share_kernel(axes, sizes, count, *refs):
    ins, outs = refs[:count], refs[count : 2 * count]
    send, recv, near = refs[2 * count :]
    index = tuple(lax.axis_index(a) for a in axes)
    peers = neighbours(axes, sizes)
    meet([device for _, _, device in peers])
    for i in range(count):
        pltpu.make_async_copy(ins[i], outs[i].at[index], near.at[i]).start()
    for i in range(count):
        pltpu.make_async_copy(ins[i], outs[i].at[index], near.at[i]).wait()
    for place in range(len(axes)):
        view = (slice(None),) * place + index[place:]
        copies = []
        for number, (at, _, device) in enumerate(peers):
            if at == place:
                for i in range(count):
                    copies.append(
                        pltpu.make_async_remote_copy(
                            src_ref=outs[i].at[view],
                            dst_ref=outs[i].at[view],
                            send_sem=send.at[i, number],
                            recv_sem=recv.at[i, number],
                            device_id=device,
                            device_id_type=MESH,
                        )
                    )
        for copy in copies:
            copy.start()
        for copy in copies:
            copy.wait()


def share(axes, collective_id, *arrays):
    sizes = tuple(lax.axis_size(a) for a in axes)
    count, peers = len(arrays), sum(sizes) - len(sizes)
    return pl.pallas_call(
        functools.partial(share_kernel, axes, sizes, count),
        out_shape=[jax.ShapeDtypeStruct(sizes + a.shape, a.dtype) for a in arrays],
        in_specs=[pl.BlockSpec(memory_space=pltpu.VMEM)] * count,
        out_specs=[pl.BlockSpec(memory_space=pltpu.VMEM)] * count,
        scratch_shapes=[
            pltpu.SemaphoreType.DMA((count, peers)),
            pltpu.SemaphoreType.DMA((count, peers)),
            pltpu.SemaphoreType.DMA((count,)),
        ],
        compiler_params=pltpu.CompilerParams(
            collective_id=collective_id, has_side_effects=True
        ),
        name=f"share{collective_id}",
    )(*arrays)


def remote(src, dst, send, recv, device):
    return pltpu.make_async_remote_copy(
        src_ref=src, dst_ref=dst, send_sem=send, recv_sem=recv, device_id=device,
        device_id_type=MESH,
    )


def run_all(copies):
    for copy in copies:
        copy.start()
    for copy in copies:
        copy.wait()


def block_peer(sizes, step):
    nz, nx = sizes[:2]
    me = lax.axis_index("z") * nx + lax.axis_index("x")
    peer = lax.rem(me + step, nz * nx)
    return me, peer, {"z": peer // nx, "x": lax.rem(peer, nx)}


def fetch_kernel(sizes, in_ref, out_ref, from_c, from_y, half, total, sems_c, sems_y, sems_b):
    nz, nx, ny, nc = sizes
    blocks = nz * nx
    iy, ic = lax.axis_index("y"), lax.axis_index("c")
    along_y = [d for _, _, d in neighbours(("y",), (ny,))]
    along_c = [d for _, _, d in neighbours(("c",), (nc,))]
    along_b = [block_peer(sizes, step)[2] for step in range(1, blocks)]
    meet(along_c + along_y + along_b)
    run_all([
        remote(in_ref.at[:, d["c"]], from_c.at[i], sems_c.at[0, i], sems_c.at[1, i], d)
        for i, d in enumerate(along_c)
    ])

    @pl.loop(0, ny)
    def _(y):
        @pl.loop(0, blocks)
        def _(k):
            value = in_ref[y, ic, k]
            for i in range(nc - 1):
                value = value + from_c[i, y, k]
            half[y, k] = value

    run_all([
        remote(half.at[d["y"]], from_y.at[i], sems_y.at[0, i], sems_y.at[1, i], d)
        for i, d in enumerate(along_y)
    ])

    @pl.loop(0, blocks)
    def _(k):
        value = half[iy, k]
        for i in range(ny - 1):
            value = value + from_y[i, k]
        total[k] = value

    me = block_peer(sizes, 0)[0]
    copies = []
    for step in range(1, blocks):
        _, peer, device = block_peer(sizes, step)
        copies.append(
            remote(total.at[peer], out_ref.at[me], sems_b.at[0, step], sems_b.at[1, step], device)
        )
    for copy in copies:
        copy.start()
    out_ref[me] = total[me]
    for copy in copies:
        copy.wait()


def fetch_blocks(sizes, looked_up, collective_id):
    nz, nx, ny, nc = sizes
    block = looked_up.shape[3:]
    blocks = nz * nx
    return pl.pallas_call(
        functools.partial(fetch_kernel, sizes),
        out_shape=jax.ShapeDtypeStruct((blocks,) + block, BF),
        in_specs=[pl.BlockSpec(memory_space=pltpu.VMEM)],
        out_specs=pl.BlockSpec(memory_space=pltpu.VMEM),
        scratch_shapes=[
            pltpu.VMEM((nc - 1, ny, blocks) + block, BF),
            pltpu.VMEM((ny - 1, blocks) + block, BF),
            pltpu.VMEM((ny, blocks) + block, BF),
            pltpu.VMEM((blocks,) + block, BF),
            pltpu.SemaphoreType.DMA((2, nc - 1)),
            pltpu.SemaphoreType.DMA((2, ny - 1)),
            pltpu.SemaphoreType.DMA((2, blocks)),
        ],
        compiler_params=pltpu.CompilerParams(
            collective_id=collective_id, has_side_effects=True, vmem_limit_bytes=VMEM_LIMIT
        ),
        cost_estimate=pl.CostEstimate(flops=0, bytes_accessed=1 << 27, transcendentals=0),
        name="fetch_blocks",
    )(looked_up)


def spread_kernel(sizes, in_ref, small_ref, out_ref, all_ref, sems_c, sems_y, sems_b, sems_s, near):
    nz, nx, ny, nc = sizes
    blocks = nz * nx
    index = tuple(lax.axis_index(a) for a in ALL)
    iy, ic = index[2:]
    along_y = [d for _, _, d in neighbours(("y",), (ny,))]
    along_c = [d for _, _, d in neighbours(("c",), (nc,))]
    along_b = [block_peer(sizes, step)[2] for step in range(1, blocks)]
    meet(along_c + along_y + along_b)
    me = block_peer(sizes, 0)[0]
    peers = neighbours(ALL, sizes)

    def small(place):
        view = (slice(None),) * place + index[place:]
        return [
            remote(all_ref.at[view], all_ref.at[view], sems_s.at[0, i], sems_s.at[1, i], device)
            for i, (at, _, device) in enumerate(peers)
            if at == place
        ]

    def start(copies):
        for copy in copies:
            copy.start()
        return copies

    def wait(copies):
        for copy in copies:
            copy.wait()

    own = pltpu.make_async_copy(small_ref, all_ref.at[index], near.at[0])
    own.start()
    own.wait()
    along_z = start(small(0))
    columns = []
    for step in range(1, blocks):
        _, peer, device = block_peer(sizes, step)
        columns.append(
            remote(in_ref.at[peer], out_ref.at[iy, ic, me], sems_b.at[0, step],
                   sems_b.at[1, step], device)
        )
    start(columns)
    out_ref[iy, ic, me] = in_ref[me]
    wait(along_z)
    along_x = start(small(1))
    wait(along_x)
    small_y = start(small(2))
    wait(columns)
    rows_y = start([
        remote(out_ref.at[iy, ic], out_ref.at[iy, ic], sems_y.at[0, i], sems_y.at[1, i], d)
        for i, d in enumerate(along_y)
    ])
    wait(small_y)
    small_c = start(small(3))
    wait(rows_y)
    rows_c = start([
        remote(out_ref.at[:, ic], out_ref.at[:, ic], sems_c.at[0, i], sems_c.at[1, i], d)
        for i, d in enumerate(along_c)
    ])
    wait(small_c)
    wait(rows_c)


def spread_blocks(sizes, parts, small, collective_id):
    nz, nx, ny, nc = sizes
    return pl.pallas_call(
        functools.partial(spread_kernel, sizes),
        out_shape=[
            jax.ShapeDtypeStruct((ny, nc) + parts.shape, parts.dtype),
            jax.ShapeDtypeStruct(sizes + small.shape, small.dtype),
        ],
        in_specs=[pl.BlockSpec(memory_space=pltpu.VMEM)] * 2,
        out_specs=[pl.BlockSpec(memory_space=pltpu.VMEM)] * 2,
        scratch_shapes=[
            pltpu.SemaphoreType.DMA((2, nc - 1)),
            pltpu.SemaphoreType.DMA((2, ny - 1)),
            pltpu.SemaphoreType.DMA((2, nz * nx)),
            pltpu.SemaphoreType.DMA((2, sum(sizes) - 4)),
            pltpu.SemaphoreType.DMA((1,)),
        ],
        compiler_params=pltpu.CompilerParams(
            collective_id=collective_id, has_side_effects=True, vmem_limit_bytes=VMEM_LIMIT
        ),
        cost_estimate=pl.CostEstimate(flops=0, bytes_accessed=1 << 27, transcendentals=0),
        name="spread_blocks",
    )(parts, small)


def axis_place(axes):
    index, size = 0, 1
    for axis in axes:
        index = index * lax.axis_size(axis) + lax.axis_index(axis)
        size = size * lax.axis_size(axis)
    return index, size


def exchange(piece_for, axes):
    me, n = axis_place(axes)
    got = [(me, piece_for(me))]
    for step in range(1, n):
        piece = piece_for(lax.rem(me + step, n))
        moved = lax.ppermute(piece, axes, [(i, (i + step) % n) for i in range(n)])
        got.append((lax.rem(me + n - step, n), moved))
    return got


def in_order(got):
    out = jnp.zeros((len(got),) + got[0][1].shape, got[0][1].dtype)
    for sender, piece in got:
        out = lax.dynamic_update_index_in_dim(out, piece, sender, 0)
    return out


def together(*values):
    return lax.optimization_barrier(values)


def pick(values, index, dim=0):
    return lax.dynamic_index_in_dim(values, index, dim, keepdims=False)


def cut_parts(values, dim, axis):
    me, n = lax.axis_index(axis), lax.axis_size(axis)
    return pick(values, me, dim), [
        pick(values, lax.rem(me + step, n), dim).astype(jnp.float16) for step in range(1, n)]


def send_parts(parts, axis):
    n = lax.axis_size(axis)
    return [lax.ppermute(part, axis, [(i, (i + step) % n) for i in range(n)])
            for step, part in enumerate(parts, 1)]


def spread_parts(values, dim, axis):
    own, parts = cut_parts(values, dim, axis)
    return own, send_parts(parts, axis)


def added(own, pieces):
    for piece in pieces:
        own = own + piece.astype(F32)
    return own


def gather_kernel(low_ref, high_ref, ids_ref, table_ref, out_ref, turned_ref, rows_ref):
    source = pl.program_id(0)

    @pl.when(source == 0)
    def _():
        @pl.loop(0, table_ref.shape[1] // LANES // 5)
        def _(k):
            for i in range(5):
                at = pl.multiple_of((k * 5 + i) * LANES, LANES)
                turned_ref[pl.ds(at, LANES), :] = table_ref[:, pl.ds(at, LANES)].T

    low, high = low_ref[source], high_ref[source]
    rows_ref[...] = jnp.zeros_like(rows_ref)

    first, last = low // 8, (high - 1) // 8

    def edge(k):
        base = pl.multiple_of(k * 8, 8)
        for i in range(8):
            place = base + i
            valid = jnp.logical_and(place >= low, place < high)
            row = jnp.where(valid, ids_ref[source, place], 0)
            value = turned_ref[pl.ds(row, 1), :]
            rows_ref[pl.ds(place, 1), :] = jnp.where(valid, value, 0.0)

    @pl.when(high > low)
    def _():
        edge(first)
        edge(last)

    def chunk(k, carry):
        base = pl.multiple_of(k * 8, 8)
        for i in range(8):
            row = ids_ref[source, base + i]
            rows_ref[pl.ds(base + i, 1), :] = turned_ref[pl.ds(row, 1), :]
        return carry

    lax.fori_loop(first + 1, last, chunk, 0)
    out_ref[0] = rows_ref[...].T.astype(BF)


def gather_rows(table, ids, low, high):
    sources, count = ids.shape
    width = table.shape[0]
    return pl.pallas_call(
        gather_kernel,
        out_shape=jax.ShapeDtypeStruct((sources, width, count), BF),
        grid_spec=pltpu.PrefetchScalarGridSpec(
            num_scalar_prefetch=3,
            grid=(sources,),
            in_specs=[
                pl.BlockSpec(table.shape, lambda i, *_: (0, 0), pipeline_mode=pl.Buffered(1))
            ],
            out_specs=pl.BlockSpec((1, width, count), lambda i, *_: (i, 0, 0)),
            scratch_shapes=[
                pltpu.VMEM((table.shape[1], width), F32),
                pltpu.VMEM((count, width), F32),
            ],
        ),
        compiler_params=pltpu.CompilerParams(vmem_limit_bytes=VMEM_LIMIT),
        cost_estimate=pl.CostEstimate(flops=0, bytes_accessed=1 << 27, transcendentals=0),
        name="gather_rows",
    )(low, high, ids, table)


def scatter_kernel(low_ref, high_ref, ids_ref, rows_ref, out_ref, wide_ref, *totals):
    source = pl.program_id(0)

    @pl.when(source == 0)
    def _():
        for total_ref in totals:
            total_ref[...] = jnp.zeros_like(total_ref)

    low, high = low_ref[source], high_ref[source]
    wide_ref[...] = rows_ref[0].astype(F32).T

    first, last = low // 8, (high - 1) // 8

    def edge(k):
        base = pl.multiple_of(k * 8, 8)
        for i in range(8):
            total_ref = totals[i % len(totals)]
            place = base + i
            valid = jnp.logical_and(place >= low, place < high)
            row = jnp.where(valid, ids_ref[source, place], 0)
            addend = jnp.where(valid, wide_ref[pl.ds(place, 1), :], 0.0)
            total_ref[pl.ds(row, 1), :] = total_ref[pl.ds(row, 1), :] + addend

    @pl.when(high > low)
    def _():
        edge(first)

    @pl.when(jnp.logical_and(high > low, last > first))
    def _():
        edge(last)

    def chunk(k, carry):
        base = pl.multiple_of(k * 8, 8)
        for i in range(8):
            total_ref = totals[i % len(totals)]
            row = ids_ref[source, base + i]
            addend = wide_ref[pl.ds(base + i, 1), :]
            total_ref[pl.ds(row, 1), :] = total_ref[pl.ds(row, 1), :] + addend
        return carry

    lax.fori_loop(first + 1, last, chunk, 0)

    @pl.when(source == pl.num_programs(0) - 1)
    def _():
        @pl.loop(0, out_ref.shape[1] // LANES // 5)
        def _(k):
            for i in range(5):
                at = pl.multiple_of((k * 5 + i) * LANES, LANES)
                value = totals[0][pl.ds(at, LANES), :]
                for total_ref in totals[1:]:
                    value = value + total_ref[pl.ds(at, LANES), :]
                out_ref[:, pl.ds(at, LANES)] = value.T


def scatter_rows(rows, ids, low, high, table_rows):
    sources, width, count = rows.shape
    return pl.pallas_call(
        scatter_kernel,
        out_shape=jax.ShapeDtypeStruct((width, table_rows), F32),
        grid_spec=pltpu.PrefetchScalarGridSpec(
            num_scalar_prefetch=3,
            grid=(sources,),
            in_specs=[pl.BlockSpec((1, width, count), lambda i, *_: (i, 0, 0))],
            out_specs=pl.BlockSpec((width, table_rows), lambda i, *_: (0, 0)),
            scratch_shapes=[pltpu.VMEM((count, width), F32)]
            + [pltpu.VMEM((table_rows, width), F32)] * 2,
        ),
        compiler_params=pltpu.CompilerParams(vmem_limit_bytes=VMEM_LIMIT),
        cost_estimate=pl.CostEstimate(flops=0, bytes_accessed=1 << 27, transcendentals=0),
        name="scatter_rows",
    )(low, high, ids, rows)


def swap_halves(values):
    lane = lax.broadcasted_iota(jnp.int32, values.shape, 1)
    half = HD // 2
    up = pltpu.roll(values, LANES - half, 1)
    down = pltpu.roll(values, half, 1)
    return jnp.where(lax.rem(lane, HD) < half, up, down)


def turn(values, cosine, sine):
    return values * cosine + swap_halves(values) * sine


def turn_back(values, cosine, sine):
    return values * cosine - swap_halves(values) * sine


def attend_kernel(kv_ref, vv_ref, qm_ref, km_ref, vm_ref, cu_ref, su_ref, cm_ref, sm_ref,
                  mask_ref, q_out, ku_out, km_out, att_out, lse_out):
    rows = cm_ref.shape[0]
    wide = (rows, LANES)
    cm, sm = cm_ref[...], sm_ref[...]
    q = turn(jnp.broadcast_to(qm_ref[0:1, :], wide), cm, sm).astype(BF)
    k_m = turn(jnp.broadcast_to(km_ref[0:1, :], wide), cm, sm).astype(BF)
    k_u = turn(kv_ref[...], cu_ref[...], su_ref[...]).astype(BF)
    v_u = vv_ref[...].astype(BF)
    v_m = vm_ref[0:1, :].astype(BF).astype(F32)
    q_out[...] = q
    ku_out[...] = k_u
    km_out[...] = k_m
    mask = mask_ref[0:1, :]
    outs, totals = [], []
    for head in range(LANES // HD):
        part = slice(head * HD, (head + 1) * HD)
        s_u = matmul_nt(q[:, part], k_u[:, part]) * HD ** (-0.5) + mask
        s_m = matmul_nt(q[:, part], k_m[:, part]) * HD ** (-0.5)
        top = jnp.maximum(
            jnp.max(s_u, axis=1, keepdims=True), jnp.max(s_m, axis=1, keepdims=True)
        )
        e_u = jnp.exp(s_u - top)
        e_m = jnp.exp(s_m - top)
        total = jnp.sum(e_u, axis=1, keepdims=True) + jnp.sum(e_m, axis=1, keepdims=True)
        inverse = 1.0 / total
        p_u = (e_u * inverse).astype(BF)
        p_m = (e_m * inverse).astype(BF).astype(F32)
        mixed = matmul(p_u, v_u[:, part]) + jnp.sum(p_m, axis=1, keepdims=True) * v_m[:, part]
        outs.append(mixed)
        totals.append(top + jnp.log(total))
    att_out[...] = jnp.concatenate(outs, axis=1).astype(BF)
    lse_out[0] = jnp.concatenate(totals, axis=1)


def attend(kv_u, qkv_m, tables, mask):
    count, rows = kv_u.shape[0], tables[2].shape[0]
    blocks = D // LANES
    per = LANES // HD
    row = lambda offset: pl.BlockSpec((qkv_m.shape[0], LANES), lambda i: (0, offset * blocks + i))
    column = lambda n: pl.BlockSpec((n, LANES), lambda i: (0, i))
    whole = lambda a: pl.BlockSpec(a.shape, lambda i: (0, 0))
    return pl.pallas_call(
        attend_kernel,
        grid=(blocks,),
        out_shape=[
            jax.ShapeDtypeStruct((rows, D), BF),
            jax.ShapeDtypeStruct((count, D), BF),
            jax.ShapeDtypeStruct((rows, D), BF),
            jax.ShapeDtypeStruct((rows, D), BF),
            jax.ShapeDtypeStruct((blocks, rows, per), F32),
        ],
        in_specs=[
            pl.BlockSpec((count, LANES), lambda i: (0, i)),
            pl.BlockSpec((count, LANES), lambda i: (0, blocks + i)),
            row(0), row(1), row(2),
            *[whole(t) for t in tables],
            whole(mask),
        ],
        out_specs=[column(rows), column(count), column(rows), column(rows),
                   pl.BlockSpec((1, rows, per), lambda i: (i, 0, 0))],
        compiler_params=pltpu.CompilerParams(vmem_limit_bytes=VMEM_LIMIT),
        cost_estimate=pl.CostEstimate(
            flops=2 * 3 * rows * count * D, bytes_accessed=12 * rows * D,
            transcendentals=2 * rows * count * H,
        ),
        name="attend",
    )(kv_u, kv_u, qkv_m, qkv_m, qkv_m, *tables, mask)


def attend_back_kernel(q_ref, ku_ref, km_ref, vv_ref, vm_ref, cu_ref, su_ref, cm_ref, sm_ref,
                       mask_ref, lse_ref, datt_ref, dk_out, dv_out, dm_out):
    q, k_u, k_m, datt = q_ref[...], ku_ref[...], km_ref[...], datt_ref[...]
    v_u = vv_ref[...].astype(BF)
    v_m = vm_ref[0:1, :].astype(BF).astype(F32)
    datt_f = datt.astype(F32)
    mask = mask_ref[0:1, :]
    scale = HD ** (-0.5)
    dq, dk_u, dk_m, dv_u, dv_m = [], [], [], [], []
    for head in range(LANES // HD):
        part = slice(head * HD, (head + 1) * HD)
        lse = lse_ref[0, :, head : head + 1]
        p_u = jnp.exp(matmul_nt(q[:, part], k_u[:, part]) * scale + mask - lse)
        p_m = jnp.exp(matmul_nt(q[:, part], k_m[:, part]) * scale - lse)
        dp_u = matmul_nt(datt[:, part], v_u[:, part])
        dp_m = jnp.sum(datt_f[:, part] * v_m[:, part], axis=1, keepdims=True)
        inner = jnp.sum(p_u * dp_u, axis=1, keepdims=True) + dp_m * jnp.sum(
            p_m, axis=1, keepdims=True
        )
        ds_u = (p_u * (dp_u - inner) * scale).astype(BF)
        ds_m = (p_m * ((dp_m - inner) * scale)).astype(BF)
        dq.append(matmul(ds_u, k_u[:, part]) + matmul(ds_m, k_m[:, part]))
        dk_u.append(matmul_tn(ds_u, q[:, part]))
        dk_m.append(matmul_tn(ds_m, q[:, part]))
        dv_u.append(matmul_tn(p_u.astype(BF), datt[:, part]))
        mass = jnp.sum(p_m.astype(BF).astype(F32), axis=1, keepdims=True)
        dv_m.append(jnp.sum(mass * datt_f[:, part], axis=0, keepdims=True))
    cm, sm = cm_ref[...], sm_ref[...]
    join = lambda parts: jnp.concatenate(parts, axis=1)
    low = lambda a: a.astype(BF).astype(F32)
    dk_out[...] = turn_back(join(dk_u), cu_ref[...], su_ref[...]).astype(BF)
    dv_out[...] = join(dv_u).astype(BF)
    dq_sum = jnp.sum(low(turn_back(join(dq), cm, sm)), axis=0, keepdims=True)
    dk_sum = jnp.sum(low(turn_back(join(dk_m), cm, sm)), axis=0, keepdims=True)
    filler = jnp.zeros((5, LANES), F32)
    dm_out[...] = jnp.concatenate([dq_sum, dk_sum, join(dv_m), filler], axis=0)


def attend_back(q, k_u, k_m, kv_u, qkv_m, tables, mask, lse, datt):
    count, rows = kv_u.shape[0], q.shape[0]
    blocks = D // LANES
    per = LANES // HD
    column = lambda n: pl.BlockSpec((n, LANES), lambda i: (0, i))
    whole = lambda a: pl.BlockSpec(a.shape, lambda i: (0, 0))
    return pl.pallas_call(
        attend_back_kernel,
        grid=(blocks,),
        out_shape=[
            jax.ShapeDtypeStruct((count, D), BF),
            jax.ShapeDtypeStruct((count, D), BF),
            jax.ShapeDtypeStruct((8, D), F32),
        ],
        in_specs=[
            column(rows), column(count), column(rows),
            pl.BlockSpec((count, LANES), lambda i: (0, blocks + i)),
            pl.BlockSpec((qkv_m.shape[0], LANES), lambda i: (0, 2 * blocks + i)),
            *[whole(t) for t in tables],
            whole(mask),
            pl.BlockSpec((1, rows, per), lambda i: (i, 0, 0)),
            column(rows),
        ],
        out_specs=[column(count), column(count), column(8)],
        compiler_params=pltpu.CompilerParams(vmem_limit_bytes=VMEM_LIMIT),
        cost_estimate=pl.CostEstimate(
            flops=2 * 8 * rows * count * D, bytes_accessed=14 * rows * D,
            transcendentals=2 * rows * count * H,
        ),
        name="attend_back",
    )(q, k_u, k_m, kv_u, qkv_m, *tables, mask, lse, datt)


def tile_of(segments):
    return max(16, 1024 // segments)


def logits_kernel(places_ref, w_ref, target_ref, *refs):
    blocks, (e_ref, stats_ref, x_ref, logits_ref) = refs[:-4], refs[-4:]
    segments, _, width = w_ref.shape
    rows = x_ref.shape[0]
    per = blocks[0].shape[0] // rows
    step = pl.program_id(0)
    for number, block in enumerate(blocks):

        @pl.when(step // per == number)
        def _(block=block):
            x_ref[...] = block[pl.ds(pl.multiple_of(lax.rem(step, per) * rows, rows), rows), :]

    x = x_ref[...]
    starts = list(range(0, width - width % 768 or width, 768))
    best = None
    for y in range(segments):
        for at, end in zip(starts, starts[1:] + [width]):
            logits = matmul(x, w_ref[y, :, at:end])
            logits_ref[:, y * width + at : y * width + end] = logits
            for g in range(0, end - at, LANES):
                part = logits[:, g : g + LANES]
                best = part if best is None else jnp.maximum(best, part)
    lane = lax.broadcasted_iota(jnp.int32, (ROWS, LANES), 1)
    peaks = jnp.max(best, axis=1, keepdims=True)
    for r in range(0, rows, ROWS):
        peak = peaks[r : r + ROWS]
        top = jnp.broadcast_to(peak, (ROWS, LANES))
        place = target_ref[r : r + ROWS, :] - lane
        total = jnp.zeros((ROWS, LANES), F32)
        chosen = jnp.zeros((ROWS, LANES), F32)
        for y in range(segments):
            for at in range(0, width, LANES):
                column = y * width + at
                logits = logits_ref[r : r + ROWS, column : column + LANES]
                e = jnp.exp(logits - top)
                total = total + e
                chosen = chosen + jnp.where(place == column, logits, 0.0)
                e_ref[y, r : r + ROWS, at : at + LANES] = e.astype(BF)
        sums = [jnp.sum(a, axis=1, keepdims=True) for a in (total, chosen)]
        stats_ref[r : r + ROWS, :] = jnp.concatenate([peak, *sums, peak], axis=1)


def head_logits(blocks, weights, targets, places):
    count = targets.shape[0]
    segments, _, width = weights.shape
    tile = tile_of(segments)
    per = blocks[0].shape[0] // tile

    def placed(i, places):
        return (places[i // per] * per + lax.rem(i, per), 0)

    return pl.pallas_call(
        logits_kernel,
        out_shape=[
            jax.ShapeDtypeStruct((segments, count, width), BF),
            jax.ShapeDtypeStruct((count, 4), F32),
            jax.ShapeDtypeStruct((count, D), BF),
        ],
        grid_spec=pltpu.PrefetchScalarGridSpec(
            num_scalar_prefetch=1,
            grid=(count // tile,),
            in_specs=[
                pl.BlockSpec(weights.shape, lambda i, p: (0, 0, 0), pipeline_mode=pl.Buffered(1)),
                pl.BlockSpec((tile, 1), placed),
            ] + [
                pl.BlockSpec(b.shape, lambda i, p: (0, 0), pipeline_mode=pl.Buffered(1))
                for b in blocks
            ],
            out_specs=[
                pl.BlockSpec((segments, tile, width), lambda i, p: (0, i, 0)),
                pl.BlockSpec((tile, 4), placed),
                pl.BlockSpec((tile, D), lambda i, p: (i, 0)),
            ],
            scratch_shapes=[pltpu.VMEM((tile, segments * width), F32)],
        ),
        compiler_params=pltpu.CompilerParams(vmem_limit_bytes=VMEM_LIMIT),
        cost_estimate=pl.CostEstimate(
            flops=2 * count * D * segments * width,
            bytes_accessed=2 * count * segments * width,
            transcendentals=count * segments * width,
        ),
        name="head_logits",
    )(places, weights, targets, *blocks)


def rows_back_kernel(places_ref, e_ref, w_ref, target_ref, factor_ref, d_ref, dx_ref):
    segments, _, width = w_ref.shape
    rows = e_ref.shape[1]
    lane = lax.broadcasted_iota(jnp.int32, (ROWS, LANES), 1)
    wide = lambda a: jnp.broadcast_to(a, (ROWS, LANES))
    total = None
    for y in range(segments):
        for r in range(0, rows, ROWS):
            place = target_ref[r : r + ROWS, :] - (lane + y * width)
            factor = wide(factor_ref[r : r + ROWS, 0:1])
            special = wide(factor_ref[r : r + ROWS, 1:2])
            for at in range(0, width, LANES):
                e = e_ref[y, r : r + ROWS, at : at + LANES].astype(F32)
                d_ref[y, r : r + ROWS, at : at + LANES] = jnp.where(
                    place == at, special, e * factor).astype(BF)
        part = matmul_nt(d_ref[y], w_ref[y])
        total = part if total is None else total + part
    dx_ref[...] = total.astype(BF)


def head_rows_back(e, weights, targets, factors, places):
    segments, count, width = e.shape
    tile = tile_of(segments)
    per = count // places.shape[0] // tile

    def placed(i, places):
        return (places[i // per] * per + lax.rem(i, per), 0)

    return pl.pallas_call(
        rows_back_kernel,
        out_shape=[
            jax.ShapeDtypeStruct(e.shape, BF),
            jax.ShapeDtypeStruct((count, D), BF),
        ],
        grid_spec=pltpu.PrefetchScalarGridSpec(
            num_scalar_prefetch=1,
            grid=(count // tile,),
            in_specs=[
                pl.BlockSpec((segments, tile, width), lambda i, p: (0, i, 0)),
                pl.BlockSpec(weights.shape, lambda i, p: (0, 0, 0), pipeline_mode=pl.Buffered(1)),
                pl.BlockSpec((tile, 1), placed),
                pl.BlockSpec((tile, 2), placed),
            ],
            out_specs=[
                pl.BlockSpec((segments, tile, width), lambda i, p: (0, i, 0)),
                pl.BlockSpec((tile, D), placed),
            ],
        ),
        input_output_aliases={1: 0},
        compiler_params=pltpu.CompilerParams(vmem_limit_bytes=VMEM_LIMIT),
        cost_estimate=pl.CostEstimate(
            flops=2 * count * D * segments * width,
            bytes_accessed=4 * count * segments * width,
            transcendentals=0,
        ),
        name="head_rows_back",
    )(places, e, weights, targets, factors)


def layer_norm(values):
    center = values - jnp.mean(values, axis=-1, keepdims=True)
    spread = jnp.mean(center * center, axis=-1, keepdims=True)
    inv_std = lax.rsqrt(spread + NORM_EPS)
    return (center * inv_std, inv_std)


def norm_back(d_normed, normed, inv_std):
    return inv_std * (
        d_normed
        - jnp.mean(d_normed, axis=-1, keepdims=True)
        - normed * jnp.mean(d_normed * normed, axis=-1, keepdims=True)
    )


def time_features(time_index, width, steps):
    t_value = (time_index.astype(F32) + 1.0) / steps
    half_width = width // 2
    frequencies = jnp.exp(-math.log(10000.0) * jnp.arange(half_width, dtype=F32) / half_width)
    angles = 1000.0 * t_value[:, None] * frequencies[None, :]
    return jax.nn.silu(jnp.concatenate([jnp.cos(angles), jnp.sin(angles)], axis=1))


def rope_rows(positions):
    half = HD // 2
    inverse = jnp.exp(-math.log(10000.0) * jnp.arange(half, dtype=F32) * 2.0 / HD)
    angles = positions.astype(F32)[:, None] * inverse[None, :]
    cosine, sine = jnp.cos(angles), jnp.sin(angles)
    return (jnp.tile(cosine, (1, LANES // half)),
            jnp.tile(jnp.concatenate([-sine, sine], axis=1), (1, LANES // HD)))


def gelu_tanh(values):
    return jax.nn.gelu(values, approximate=True)


def adam_step(weight, first, second, ema_copy, gradient, step_value, learn_rate, decay_rate):
    first_new = BETA_ONE * first + (1.0 - BETA_ONE) * gradient
    second_new = BETA_TWO * second + (1.0 - BETA_TWO) * gradient * gradient
    first_hat = first_new / (1.0 - BETA_ONE**step_value)
    second_hat = second_new / (1.0 - BETA_TWO**step_value)
    weight_new = weight - learn_rate * (
        first_hat / (jnp.sqrt(second_hat) + ADAM_EPS) + decay_rate * weight
    )
    ema_rate = jnp.minimum(EMA_DECAY, (1.0 + step_value) / (10.0 + step_value))
    ema_new = ema_rate * ema_copy + (1.0 - ema_rate) * weight_new
    return (first_new, second_new, weight_new, ema_new)


def split3(row):
    parts, rest = [], row
    for _ in range(3):
        part = lax.reduce_precision(rest, 8, 7)
        parts.append(part.astype(BF))
        rest = rest - part
    return parts


def local(sizes, token_ids, scored, lengths, times, step_count, layer_w, layer_m, layer_v, layer_ema,
          ada_w, ada_m, ada_v, ada_ema, gains_w, gains_m, gains_v, gains_ema,
          embed_w, embed_m, embed_v, embed_ema, head_w, head_m, head_v, head_ema):
    nz, nx, ny, nc = sizes
    n = nz * nx * ny * nc
    length, score_count = token_ids.shape[1], scored.shape[1]
    free_count = length - score_count
    total_rows = n * score_count
    table_rows, table_width = embed_w.shape
    iz, ix, iy, ic = [lax.axis_index(a) for a in ALL]
    vocab_index = iy * nc + ic
    vocab_start = vocab_index * table_rows
    me = (iz * nx + ix) * (ny * nc) + vocab_index

    tokens, masked = token_ids[0], scored[0]
    positions = jnp.arange(length, dtype=jnp.int32)
    hits = masked[:, None] == positions[None, :]
    is_masked = jnp.any(hits, axis=0)
    targets = jnp.sum(jnp.where(hits, tokens[None, :], 0), axis=1)
    keys = jnp.where(is_masked, n * V, (tokens // table_rows) * length + positions)
    rank = jnp.sum((keys[None, :] < keys[:, None]).astype(jnp.int32), axis=1)
    rank = jnp.where(is_masked, length, rank)
    slots = rank[None, :] == jnp.arange(free_count, dtype=jnp.int32)[:, None]
    free_tokens = jnp.sum(jnp.where(slots, tokens[None, :], 0), axis=1)
    free_positions = jnp.sum(jnp.where(slots, positions[None, :], 0), axis=1)

    ints = jnp.concatenate([free_tokens.reshape(-1, LANES), targets.reshape(-1, LANES),
                            jnp.broadcast_to(times[:, None], (1, LANES))], axis=0)
    ints = jnp.pad(ints, ((0, -ints.shape[0] % 8), (0, 0)))
    gain_part = jnp.pad(gains_w.astype(BF).astype(F32),
                        ((0, 8 - gains_w.shape[0]), (0, LANES - gains_w.shape[1])))
    ints_all, gains_all = share(ALL, 0, ints, gain_part)
    ints_all = ints_all.reshape((n,) + ints.shape)
    gains_all = gains_all.reshape((n,) + gain_part.shape)

    block_low = jnp.concatenate(
        [layer_w.astype(BF), ada_w.astype(BF).reshape(layer_w.shape[0], -1)], axis=1)
    head_low, ints_all = together(head_w.astype(BF), ints_all)
    layer_all = lax.all_gather(block_low, ALL, axis=0, tiled=True)

    piece_for = lambda k: lax.dynamic_slice_in_dim(head_low, k * SEGMENT, SEGMENT, 1)
    head_parts = exchange(piece_for, ("z",))

    gains = jnp.moveaxis(gains_all[:, : gains_w.shape[0], : gains_w.shape[1]], 0, 1).reshape(4, D)
    free_rows = free_count // LANES
    score_rows = score_count // LANES
    all_tokens = ints_all[:, :free_rows].reshape(nz * nx, ny * nc, free_count)
    all_targets = ints_all[:, free_rows : free_rows + score_rows].reshape(
        nz, nx, ny, nc, score_count)
    all_times = ints_all[:, free_rows + score_rows, 0]

    wanted = jnp.swapaxes(all_tokens, 0, 1).reshape(n, free_count)
    owners = wanted // table_rows
    low = jnp.sum((owners < vocab_index).astype(jnp.int32), axis=1)
    high = jnp.sum((owners <= vocab_index).astype(jnp.int32), axis=1)
    local_ids = wanted - vocab_start
    looked_up = gather_rows(embed_w.T, local_ids, low, high)
    looked_up = looked_up.reshape((ny, nc, nz * nx) + looked_up.shape[1:])
    x0_u = fetch_blocks(sizes, looked_up, 3).reshape(D, free_count).T.astype(F32)
    group = nz * nc * score_count
    row_targets = pick(jnp.moveaxis(jnp.moveaxis(all_targets, 3, 1), (2, 3), (0, 1)).reshape(
        nx * ny, group), ix * ny + iy)
    row_times = pick(jnp.moveaxis(jnp.moveaxis(all_times.reshape(nz, nx, ny, nc), 3, 1), (2, 3), (0, 1))
                     .reshape(nx * ny, nz * nc), ix * ny + iy)
    row_weights = jnp.repeat(TSTEPS / (row_times.astype(F32) + 1.0) / total_rows, score_count)
    owner, within = row_targets // table_rows, row_targets % table_rows
    owned = jnp.logical_and(owner % nc == ic, within // SEGMENT == iz)
    column_of = jnp.where(owned, (owner // nc) * SEGMENT + within % SEGMENT, -1)[:, None]
    x0_u, column_of, row_weights = together(x0_u, column_of, row_weights)
    senders = [sender for sender, _ in head_parts]
    x0_u, *pieces = together(x0_u, *[piece for _, piece in head_parts])
    head_part = in_order(list(zip(senders, pieces))).reshape(-1, SEGMENT)

    mask_row = gains[3:4]
    condition = time_features(times, C, TSTEPS).astype(BF)
    modulation = matmul(condition, layer_all[:, layer_w.shape[1] :].reshape(C, 6 * D))
    shift_a, scale_a, gate_a, shift_m, scale_m, gate_m = [
        modulation[:, i * D : (i + 1) * D] for i in range(6)]
    normed_u, inv_u = layer_norm(x0_u)
    a_u = (normed_u * gains[0:1] * (1.0 + scale_a) + shift_a).astype(BF)
    normed_0, inv_0 = layer_norm(mask_row)
    a_m = (normed_0 * gains[0:1] * (1.0 + scale_a) + shift_a).astype(BF)
    w_qkv, w_o = layer_all[:, : 3 * D], layer_all[:, 3 * D : 4 * D]
    w_up, w_down = layer_all[:, 4 * D : 4 * D + FF], layer_all[:, 4 * D + FF : 4 * D + 2 * FF]
    qkv_m = matmul(jnp.broadcast_to(a_m, (16, D)), w_qkv)
    kv_u = matmul(a_u, w_qkv[:, D:])
    tables = (*rope_rows(free_positions), *rope_rows(masked))
    mask = jnp.where(free_positions[None, :] < lengths[:, None], 0.0, -1e30)
    mask = jnp.broadcast_to(mask, (8, free_count)).astype(F32)
    q, k_u, k_m, att, lse_a = attend(kv_u, qkv_m, tables, mask)
    branch = matmul(att, w_o)
    x1 = mask_row + gate_a * branch
    normed_m, inv_m = layer_norm(x1)
    b = (normed_m * gains[1:2] * (1.0 + scale_m) + shift_m).astype(BF)
    pre = matmul(b, w_up)
    act = gelu_tanh(pre).astype(BF)
    mlp = matmul_nt(act, w_down)
    x2 = x1 + gate_m * mlp
    normed_f, inv_f = layer_norm(x2)
    final = (normed_f * gains[2:3]).astype(BF)

    final_turned = jnp.swapaxes(final.reshape(score_count, nz, nx, -1), 1, 2).reshape(score_count, D)
    head_all = lax.all_gather(head_part, ("y", "x"), axis=0, tiled=True).reshape(ny, D, SEGMENT)
    blocks, places = [], []
    for sender, piece in exchange(lambda k: final_turned, ("z",)):
        for place, part in exchange(lambda k: piece, ("c",)):
            blocks.append(part)
            places.append(sender * nc + place)
    places = jnp.stack(places).astype(jnp.int32)
    e, stats, rows = head_logits(blocks, head_all, column_of, places)
    top = stats[:, 0]
    every = share(("z", "c"), 4, stats.T.reshape(4, -1, LANES))[0].reshape(nz * nc, 4, group)
    best = jnp.max(every[:, 0], axis=0)
    log_total = best + jnp.log(jnp.sum(every[:, 1] * jnp.exp(every[:, 0] - best), axis=0))
    chosen = jnp.sum(every[:, 2], axis=0)
    own_start = (iz * nc + ic) * score_count
    own_terms = lax.dynamic_slice_in_dim(row_weights * (log_total - chosen), own_start, score_count)
    loss_part = jnp.sum(own_terms)
    factors = jnp.stack([row_weights * jnp.exp(top - log_total),
                         row_weights * (jnp.exp(chosen - log_total) - 1.0)], axis=1)
    d_logits, d_rows = head_rows_back(e, head_all, column_of, factors, places)
    d_final = lax.psum_scatter(d_rows, ("z", "c"), scatter_dimension=0, tiled=True)

    bound = D**0.5 * jnp.max(jnp.abs(gains[2])) * 1.02
    bound = bound * score_count * jnp.sum(TSTEPS / (all_times.astype(F32) + 1.0) / total_rows)
    enlarge = 60000.0 / jnp.maximum(bound, 1e-30)
    d_head = jnp.einsum("rd,yrv->ydv", rows, d_logits, preferred_element_type=F32) * enlarge
    d_head = d_head.reshape(ny, nx, nz, -1, SEGMENT)
    cut = nz // 2
    own_x, to_x = cut_parts(d_head[:, :, :cut], 1, "x")
    own_y, to_y = cut_parts(d_head[:, :, cut:], 0, "y")
    d_final, *to_xy = together(d_final, *to_x, *to_y)
    from_x, from_y = send_parts(to_xy[: nx - 1], "x"), send_parts(to_xy[nx - 1 :], "y")
    d_final = d_final.astype(F32)
    d_final = jnp.swapaxes(d_final.reshape(score_count, nx, nz, -1), 1, 2).reshape(score_count, D)

    d_gain_f = jnp.sum(d_final * normed_f, axis=0)
    d_x2 = norm_back(d_final * gains[2:3], normed_f, inv_f)
    d_gate_m = jnp.sum(d_x2 * mlp, axis=0)
    d_out = (d_x2 * gate_m).astype(BF)
    d_down = matmul_tn(d_out, act)
    d_act = matmul(d_out, w_down)
    d_pre = jax.vjp(gelu_tanh, pre)[1](d_act)[0].astype(BF)
    d_up = matmul_tn(b, d_pre)
    d_b = matmul_nt(d_pre, w_up)
    d_shift_m = jnp.sum(d_b, axis=0)
    product = jnp.sum(d_b * normed_m, axis=0)
    d_scale_m = product * gains[1]
    d_gain_m = product * (1.0 + scale_m[0])
    d_x1 = d_x2 + norm_back(d_b * ((1.0 + scale_m) * gains[1:2]), normed_m, inv_m)
    d_gate_a = jnp.sum(d_x1 * branch, axis=0)
    d_branch = (d_x1 * gate_a).astype(BF)
    d_wout = matmul_tn(att, d_branch)
    d_att = matmul_nt(d_branch, w_o).astype(BF)
    d_k, d_v, d_qkv_m = attend_back(q, k_u, k_m, kv_u, qkv_m, tables, mask, lse_a, d_att)
    d_k, *from_xy = together(d_k, *from_x, *from_y)

    over_plane = lambda a: lax.psum_scatter(a, ("x", "y"), scatter_dimension=0, tiled=True)
    own_xy, from_xy = (
        spread_parts(added(own_x, from_xy[: nx - 1]), 0, "y"),
        spread_parts(added(own_y, from_xy[nx - 1 :]), 0, "x"),
    )
    d_kv = jnp.concatenate([d_k, d_v], axis=1)
    d_wkv = matmul_tn(a_u, d_kv)
    d_row_m = d_qkv_m[:3].reshape(3 * D)
    d_a_u = matmul_nt(d_kv, w_qkv[:, D:])
    d_parts = matmul_nt(jnp.pad(jnp.stack(split3(d_row_m)), ((0, 13), (0, 0))), w_qkv)
    d_a_m = jnp.sum(d_parts[:3], axis=0, keepdims=True)
    d_shift_a = jnp.sum(d_a_u, axis=0) + d_a_m[0]
    product = jnp.sum(d_a_u * normed_u, axis=0) + (d_a_m * normed_0)[0]
    d_scale_a = product * gains[0]
    d_gain_a = product * (1.0 + scale_a[0])
    scaling = (1.0 + scale_a) * gains[0:1]
    d_x0_u = norm_back(d_a_u * scaling, normed_u, inv_u)
    d_mask = jnp.sum(d_x1, axis=0) + norm_back(d_a_m * scaling, normed_0, inv_0)[0]

    d_block = jnp.concatenate(
        [d_wkv.astype(BF), d_wout.astype(BF), d_up.astype(BF), d_down.astype(BF)], axis=1)
    width = d_block.shape[1]
    d_block = jnp.transpose(d_block.reshape(nz, nx, ny, nc, -1, width), (3, 1, 2, 0, 4, 5))
    d_block, *arrivals = together(d_block.reshape(nc, -1, width), *own_xy[1], *from_xy[1])
    head_sum = jnp.concatenate(
        [added(own_xy[0], arrivals[: ny - 1]), added(from_xy[0], arrivals[ny - 1 :])], axis=0)
    head_own, head_parts = spread_parts(head_sum, 0, "z")
    got = exchange(lambda k: pick(d_block, k), ("c",))
    chip_sum = sum(piece.astype(F32) for _, piece in got).astype(BF)

    small = jnp.concatenate([d_shift_a, d_scale_a, d_gate_a, d_shift_m, d_scale_m, d_gate_m,
                             d_gain_a, d_gain_m, d_gain_f, d_mask,
                             a_m[0].astype(F32), d_row_m, jnp.broadcast_to(loss_part, (LANES,))])
    small = small.reshape(-1, LANES)
    count_small = small.shape[0]
    small = jnp.pad(small, ((0, -count_small % 8), (0, 0)))

    sent = d_x0_u.astype(BF).T.reshape(nz * nx, table_width, free_count)
    plane_sum = over_plane(chip_sum)
    sent, *head_parts = together(sent, *head_parts)

    arrived, small_all = spread_blocks(sizes, sent, small, 5)
    arrived, plane_sum = together(arrived, plane_sum)
    plane_sum = plane_sum.reshape(nz, -1, plane_sum.shape[1])
    block_parts = [p for _, p in exchange(lambda k: pick(plane_sum, k), ("z",))]
    g_embed = scatter_rows(arrived.reshape(n, table_width, free_count), local_ids, low, high,
                           table_rows)
    together_now = together(g_embed, small_all, head_own, *head_parts, *block_parts)
    g_embed, small_all, head_own = together_now[:3]
    head_parts, block_parts = together_now[3 : 2 + nz], together_now[2 + nz :]
    small_all = small_all.reshape((n,) + small.shape)
    small_all = small_all[:, :count_small].reshape(n, -1)
    d_mod_all = small_all[:, : 6 * D]
    d_gains = jnp.sum(small_all[:, 6 * D : 10 * D], axis=0).reshape(4, D)
    g_gains = lax.dynamic_slice_in_dim(d_gains, me * gains_w.shape[1], gains_w.shape[1], 1)
    total_loss = jnp.sum(small_all[:, 14 * D])
    condition_all = time_features(all_times, C, TSTEPS).astype(BF).astype(F32)
    condition_rows = lax.dynamic_slice_in_dim(condition_all, me * ada_w.shape[0], ada_w.shape[0], 1)
    exact = lambda a, b: jnp.einsum("nr,nc->rc", a, b, precision=lax.Precision.HIGHEST)
    g_ada = exact(condition_rows, d_mod_all)
    a_rows = lax.dynamic_slice_in_dim(small_all[:, 10 * D : 11 * D], me * layer_w.shape[0],
                                      layer_w.shape[0], 1)
    g_outer = exact(a_rows, small_all[:, 11 * D : 14 * D])

    g_rest = sum(p.astype(F32) for p in block_parts)
    g_layer = jnp.concatenate(
        [g_outer[:, :D], g_outer[:, D:] + g_rest[:, : 2 * D], g_rest[:, 2 * D :]], axis=1)

    segments = []
    for k in range(nz):
        segment = head_own
        for step, piece in enumerate(head_parts, 1):
            segment = jnp.where(lax.rem(iz + nz - step, nz) == k, piece.astype(F32), segment)
        segments.append(segment)
    g_head = jnp.concatenate(segments, axis=1) / enlarge

    squares = sum(jnp.sum(g * g) for g in (g_layer, g_ada, g_gains, g_embed, g_head))
    squares_all = share(ALL, 2, jnp.broadcast_to(squares, (8, LANES)))[0]
    grad_norm = jnp.sqrt(jnp.sum(squares_all[..., 0, 0]))
    factor = jnp.minimum(1.0, CLIP_NORM / grad_norm)
    step_value = step_count[0].astype(F32)
    updates = (
        (layer_w, layer_m, layer_v, layer_ema, g_layer),
        (ada_w, ada_m, ada_v, ada_ema, g_ada),
        (gains_w, gains_m, gains_v, gains_ema, g_gains),
        (embed_w.T, embed_m.T, embed_v.T, embed_ema.T, g_embed),
        (head_w, head_m, head_v, head_ema, g_head),
    )
    results = []
    for (w, m, v, ema, g), rate, decay in zip(updates, LEARN_RATES, WEIGHT_DECAYS):
        results.extend(adam_step(w, m, v, ema, g * factor, step_value, rate, decay))
    results[12:16] = [a.T for a in results[12:16]]
    return (total_loss, grad_norm, *results)


def solution(mesh):
    dp, vocab = mesh.shape["dp"], mesh.shape["vocab"]
    nz, nc = V // vocab // SEGMENT, 2
    sizes = (nz, dp // nz, vocab // nc, nc)
    fine = Mesh(mesh.devices.reshape(sizes), ALL)
    rows_all, columns_all = P(ALL, None), P(None, ALL)
    table, head = P(("y", "c"), ("z", "x")), P(("z", "x"), ("y", "c"))
    weights = [rows_all] * 8 + [columns_all] * 4 + [table] * 4 + [head] * 4
    return jax.shard_map(
        functools.partial(local, sizes),
        mesh=fine,
        in_specs=(rows_all, rows_all, P(ALL), P(ALL), P(), *weights),
        out_specs=(P(), P(), *weights),
        check_vma=False,
    )
```
